128 devices in a mesh: dp: 4 (over z), context: 4 (over x_lo, core), expert: 8 (over x_hi, y).
Axes of the slice: x: 4 (x_hi: 2, x_lo: 2; x = x_hi * 2 + x_lo), y: 4, z: 4, core: 2. Of those that a mesh axis runs over, the one named last changes fastest.
Arguments:
- inputs: bfloat16 [4, 4096, 1024], P('dp', ('context', 'expert')), may hold values from -6 to 6
- prenorm_gain: float32 [1024], replicated, may hold values from 0.1 to 1.9
- query_weight: bfloat16 [1024, 512], replicated, may hold values from -4 to 4
- key_weight: bfloat16 [1024, 256], replicated, may hold values from -4 to 4
- value_weight: bfloat16 [1024, 256], replicated, may hold values from -0.1875 to 0.1875
- output_weight: bfloat16 [512, 1024], replicated, may hold values from -0.75 to 0.75
- midnorm_gain: float32 [1024], replicated, may hold values from 0.1 to 1.9
- router_weight: bfloat16 [1024, 32], replicated, may hold values from -0.1875 to 0.1875
- gate_weight: bfloat16 [32, 1024, 512], P('expert'), may hold values from -0.1875 to 0.1875
- up_weight: bfloat16 [32, 1024, 512], P('expert'), may hold values from -0.1875 to 0.1875
- down_weight: bfloat16 [32, 512, 1024], P('expert'), may hold values from -0.25 to 0.25
- expert_ids: int32 [4, 4096, 8], P('dp', ('context', 'expert')), may hold values from 0 to 31, all different within a row; in each aligned block of 128 rows (0 to 127, 128 to 255, ..., all dimensions but the last counted through in order) at most 64 rows name the same one
- cotangent: bfloat16 [4, 4096, 1024], P('dp', ('context', 'expert')), may hold values from -6 to 6
Outputs:
- outputs: bfloat16 [4, 4096, 1024], P('dp', ('context', 'expert'))
- input_gradient: float32 [4, 4096, 1024], P('dp', ('context', 'expert'))
- prenorm_gradient: float32 [1024], replicated
- query_gradient: float32 [1024, 512], replicated
- key_gradient: float32 [1024, 256], replicated
- value_gradient: float32 [1024, 256], replicated
- output_gradient: float32 [512, 1024], replicated
- midnorm_gradient: float32 [1024], replicated
- router_gradient: float32 [1024, 32], replicated
- gate_gradient: float32 [32, 1024, 512], P('expert', ('dp', 'context'))
- up_gradient: float32 [32, 1024, 512], P('expert', ('dp', 'context'))
- down_gradient: float32 [32, 512, 1024], P('expert', ('dp', 'context'))
The draws below stay inside these ranges and needn't reach their ends.
Inputs may be any that keep to these rules, and one draw needn't show every extreme that they name: `expert_ids`: in each aligned block of 128 positions of a sequence (the tokens of one device) no expert is named by more than 64 tokens, a bound that some block reaches; the 8 experts of a token are distinct.
All inputs are finite; a program needn't handle non-finite values.
Results may differ from the reference program's by a relative error of at most 0.023.
The reference program's roundings to bfloat16 on the way count: a program that leaves them out, or rounds other values in their place, can miss the bound.
Values may be sent and summed in bfloat16 or wider, within the bound.
A program may use at most 192 MiB of HBM per device.

```python
import math
import jax
import jax.numpy as jnp
import numpy as np
from jax import lax

D = 1024
HEADS = 8
KV_HEADS = 4
HEAD_DIM = 64
FF = 512
EXPERTS = 32
TOP = 8
TOK_DEV = 128
QW = 512
KW = 256
LEN = 4096
SEQS = 4
CAP = 64


def draw_query_weight(key, part):
    return jnp.clip(jax.random.normal(jax.random.fold_in(key, 11), (D, QW), jnp.float32) / math.sqrt(D), -4.0, 4.0).astype(jnp.bfloat16)


def draw_key_weight(key, part):
    return jnp.clip(jax.random.normal(jax.random.fold_in(key, 21), (D, KW), jnp.float32) / math.sqrt(D), -4.0, 4.0).astype(jnp.bfloat16)


def shard_levels(own_key, dims, shards, least, top_value):
    gain, own = 1.0, jax.random.fold_in(own_key, 6)
    for position, parts in shards:
        draws = jnp.exp(jax.random.uniform(jax.random.fold_in(own, position), (parts,), jnp.float32, least / len(shards), top_value / len(shards)))
        gain = gain * jnp.repeat(draws, dims[position] // parts).reshape([-1 if axis == position else 1 for axis in range(len(dims))])
    return gain


def deal_out(key, own, number, rows, count, top, reach, slope):
    order = jax.random.permutation(key, count)
    crowded, ordinary = load_shares(count, rows * top, reach, slope, True), load_shares(count, rows * top, reach, slope, False)
    places = jnp.arange(count)

    def named(tallies, offset_by):
        used = int((tallies > 0).sum())
        fixed = max(1, used // 4)
        passed = fixed + (places - fixed + offset_by * (used - fixed)) % max(1, count - fixed)
        return jnp.zeros((count,), jnp.int32).at[order[jnp.where(places < fixed, places, passed)]].set(jnp.asarray(tallies, jnp.int32))

    tallies = jnp.where(number % 4 == 0, named(crowded, number // 4), named(ordinary, number - number // 4 - 1))
    mixed = jax.random.permutation(jax.random.fold_in(own, 3), count)
    source_of, receiver = mixed[0:count // 2 * 2:2], mixed[1:count // 2 * 2:2]
    margin = jnp.minimum(tallies[source_of] - 1, reach - tallies[receiver]) // 2
    margin = jnp.where((source_of == order[0]) | (receiver == order[0]) | (tallies[receiver] == 0), 0, jnp.maximum(margin, 0))
    passed = jax.random.randint(jax.random.fold_in(own, 4), (count // 2,), 0, 1 << 20) % (margin + 1)
    tallies = tallies.at[source_of].add(-passed).at[receiver].add(passed)
    labels = jnp.searchsorted(jnp.cumsum(tallies), jnp.arange(rows * top), side="right").astype(jnp.int32)
    table = labels.reshape(top, rows).T
    table = table[jax.random.permutation(jax.random.fold_in(own, 1), rows)]
    offset_by = jax.random.randint(jax.random.fold_in(own, 2), (rows, 1), 0, top)
    return jnp.take_along_axis(table, (jnp.arange(top)[None, :] + offset_by) % top, axis=1)


def load_shares(amount, total, limit, lean, full):
    weights = [(1 << 20) // math.isqrt(rank ** lean) + 1 for rank in range(1, amount + 1)]
    largest = limit if full else min(limit, max(-(-total // amount), total * weights[0] // sum(weights)))
    least = 1 if total - largest >= amount - 1 else 0
    holding, rest = [largest] + [least] * (amount - 1), total - largest - least * (amount - 1)
    while rest > 0:
        free = [i for i in range(1, amount) if holding[i] < largest] or [i for i in range(1, amount) if holding[i] < limit]
        whole, remaining = sum([weights[i] for i in free]), rest
        for i in free:
            more = min(limit - holding[i], max(1, remaining * weights[i] // whole), rest)
            holding[i] = holding[i] + more
            rest = rest - more
    return np.array(holding)


def noise(rng, extent, spread, bound, cuts=(), kind=jnp.bfloat16):
    result = spread * jax.random.normal(rng, extent, jnp.float32)
    if cuts:
        result = result * shard_levels(rng, extent, cuts, -0.22, 0.18)
    return jnp.clip(result, -bound, bound).astype(kind)


def setup_inputs(seed: int = 0) -> dict:
    splits = jax.random.split(jax.random.key(seed), 14)
    inputs = noise(splits[0], (SEQS, LEN, D), 1.0, 6.0, ((0, 4), (1, 32)))
    prenorm_gain = jnp.clip(1.0 + 0.18 * jax.random.normal(splits[1], (D,), jnp.float32), 0.1, 1.9)
    query_weight = draw_query_weight(jax.random.fold_in(splits[13], 71), 0)
    key_weight = draw_key_weight(jax.random.fold_in(splits[13], 71), 0)
    value_weight = noise(splits[4], (D, KW), D ** -0.5, 0.1875)
    output_weight = noise(splits[5], (QW, D), (QW // 8) ** -0.5, 0.75)
    midnorm_gain = jnp.clip(1.0 + 0.18 * jax.random.normal(splits[6], (D,), jnp.float32), 0.1, 1.9)
    router_weight = noise(splits[7], (D, EXPERTS), D ** -0.5, 0.1875)
    gate_weight = noise(splits[8], (EXPERTS, D, FF), D ** -0.5, 0.1875, ((0, 8),))
    up_weight = noise(splits[9], (EXPERTS, D, FF), D ** -0.5, 0.1875, ((0, 8),))
    down_weight = noise(splits[10], (EXPERTS, FF, D), FF ** -0.5, 0.25, ((0, 8),))
    expert_ids_keys = jax.random.split(jax.random.fold_in(splits[11], 1), SEQS * LEN // TOK_DEV)
    expert_ids_turns = jax.random.permutation(jax.random.fold_in(splits[11], 3), SEQS * LEN // TOK_DEV)
    expert_ids = jax.vmap(lambda own, number: deal_out(jax.random.fold_in(splits[11], 2), own, number, TOK_DEV, EXPERTS, TOP, CAP, 2))(expert_ids_keys, expert_ids_turns).reshape((SEQS, LEN, TOP))
    cotangent = noise(splits[12], (SEQS, LEN, D), 1.0, 6.0, ((0, 4), (1, 32)))
    return {"inputs": inputs, "prenorm_gain": prenorm_gain, "query_weight": query_weight, "key_weight": key_weight, "value_weight": value_weight, "output_weight": output_weight, "midnorm_gain": midnorm_gain, "router_weight": router_weight, "gate_weight": gate_weight, "up_weight": up_weight, "down_weight": down_weight, "expert_ids": expert_ids, "cotangent": cotangent}


EPSILON = 1e-06
ROPE_BASE = 10000.0

def product(form, left, right):
    return jnp.einsum(form, left.astype(jnp.float32), right.astype(jnp.float32))

def rope_tables(positions, head_size):
    half_dim = head_size // 2
    frequency = ROPE_BASE ** (-2.0 * jnp.arange(half_dim, dtype=jnp.float32) / head_size)
    angles = positions.astype(jnp.float32)[:, None] * frequency[None, :]
    angles = jnp.concatenate([angles, angles], axis=1)
    return (jnp.cos(angles), jnp.sin(angles))

def rotate(values, cosine, sine_table):
    half_dim = values.shape[-1] // 2
    turned = jnp.concatenate([-values[..., half_dim:], values[..., :half_dim]], axis=-1)
    return values * cosine[:, None, :] + turned * sine_table[:, None, :]

def rotate_back(grads, cosine, sine_table):
    half_dim = grads.shape[-1] // 2
    scaled = grads * sine_table[:, None, :]
    turned = jnp.concatenate([scaled[..., half_dim:], -scaled[..., :half_dim]], axis=-1)
    return grads * cosine[:, None, :] + turned

def norm_forward(values, gain_vec):
    inverse = lax.rsqrt(lax.optimization_barrier(jnp.mean(values * values, axis=-1, keepdims=True)) + EPSILON)
    normed = values * inverse
    return (inverse, normed, (normed * gain_vec).astype(jnp.bfloat16))

def norm_backward(grad_out, normed, inverse, gain_vec):
    gain_grad = lax.optimization_barrier(jnp.sum(grad_out * normed, axis=0))
    scaled = grad_out * gain_vec
    inner = lax.optimization_barrier(jnp.mean(scaled * normed, axis=-1, keepdims=True))
    return (gain_grad, inverse * (scaled - normed * inner))

def score_table(queries, keys_all, query_pos, key_pos):
    factor = queries.shape[-1] ** (-0.5)
    scores = product('tkgd,skd->kgts', queries, keys_all) * factor
    allowed = key_pos[None, :] <= query_pos[:, None]
    return jnp.where(allowed, scores, -jnp.inf)

def attention_forward(queries, keys_all, values_all, query_pos, key_pos):
    scores = score_table(queries, keys_all, query_pos, key_pos)
    maximum = lax.optimization_barrier(jnp.max(scores, axis=-1, keepdims=True))
    logsum = maximum + jnp.log(lax.optimization_barrier(jnp.sum(jnp.exp(scores - maximum), axis=-1, keepdims=True)))
    soft_round = jnp.exp(scores - logsum).astype(jnp.bfloat16)
    mixture = product('kgts,skd->tkgd', soft_round, values_all)
    return (logsum, mixture.astype(jnp.bfloat16))

def score_grads(queries, keys_all, values_all, query_pos, key_pos, logsum, delta, grad_mix):
    scores = score_table(queries, keys_all, query_pos, key_pos)
    soft_exact = jnp.exp(scores - logsum)
    soft_round = soft_exact.astype(jnp.bfloat16)
    grad_soft = product('tkgd,skd->kgts', grad_mix, values_all)
    grad_score = (soft_exact * (grad_soft - delta)).astype(jnp.bfloat16)
    return (soft_round, grad_score)

def slot_targets(ids_block):
    flat_ids = ids_block.reshape(-1)
    onehot = (flat_ids[:, None] == jnp.arange(EXPERTS, dtype=jnp.int32)[None, :]).astype(jnp.int32)
    before = jnp.cumsum(onehot, axis=0) - onehot
    slot_index = lax.optimization_barrier(jnp.sum(before * onehot, axis=1))
    return (flat_ids * CAP + slot_index).astype(jnp.int32)

def fill_slots(pair_rows, targets):
    empty = jnp.zeros((EXPERTS * CAP, pair_rows.shape[1]), pair_rows.dtype)
    return empty.at[targets].set(pair_rows)

def take_slots(table, targets):
    return table[targets]

def sequence_pass(params, seq_inputs, seq_ids, seq_cotangent):
    prenorm_gain, query_weight, key_weight, value_weight, output_weight, midnorm_gain, router_weight, gate_weight, up_weight, down_weight = params
    groups = HEADS // KV_HEADS
    factor = HEAD_DIM ** (-0.5)
    positions = jnp.arange(LEN, dtype=jnp.int32)
    cosine, sine_table = rope_tables(positions, HEAD_DIM)
    input_float = seq_inputs.astype(jnp.float32)
    inverse_first, normed_first, attn_input = norm_forward(input_float, prenorm_gain)
    query_raw = jnp.dot(attn_input, query_weight, preferred_element_type=jnp.float32).reshape(LEN, HEADS, HEAD_DIM)
    key_raw = jnp.dot(attn_input, key_weight, preferred_element_type=jnp.float32).reshape(LEN, KV_HEADS, HEAD_DIM)
    value_raw = jnp.dot(attn_input, value_weight, preferred_element_type=jnp.float32).reshape(LEN, KV_HEADS, HEAD_DIM)
    query_rot = rotate(query_raw, cosine, sine_table).astype(jnp.bfloat16).reshape(LEN, KV_HEADS, groups, HEAD_DIM)
    key_rot = rotate(key_raw, cosine, sine_table).astype(jnp.bfloat16)
    value_half = value_raw.astype(jnp.bfloat16)
    logsum, mixture = attention_forward(query_rot, key_rot, value_half, positions, positions)
    mixture_flat = mixture.reshape(LEN, QW)
    after_attn = input_float + jnp.dot(mixture_flat, output_weight, preferred_element_type=jnp.float32)
    inverse_second, normed_second, moe_input = norm_forward(after_attn, midnorm_gain)
    logits = jnp.dot(moe_input, router_weight, preferred_element_type=jnp.float32)
    chosen = jnp.take_along_axis(logits, seq_ids, axis=1)
    gate_probs = jax.nn.softmax(chosen, axis=-1)
    blocks = LEN // TOK_DEV
    ids_blocks = seq_ids.reshape(blocks, TOK_DEV, TOP)
    targets = jax.vmap(slot_targets)(ids_blocks)
    pair_inputs = jnp.repeat(moe_input, TOP, axis=0).reshape(blocks, TOK_DEV * TOP, D)
    buffer = jax.vmap(fill_slots)(pair_inputs, targets).reshape(blocks, EXPERTS, CAP, D)
    gate_act = product('becd,edf->becf', buffer, gate_weight)
    up_act = product('becd,edf->becf', buffer, up_weight)
    silu_gate = jax.nn.silu(gate_act)
    hidden = (silu_gate * up_act).astype(jnp.bfloat16)
    expert_out = product('becf,efd->becd', hidden, down_weight).astype(jnp.bfloat16)
    picked = jax.vmap(take_slots)(expert_out.reshape(blocks, EXPERTS * CAP, D), targets).reshape(LEN, TOP, D)
    moe_out = lax.optimization_barrier(jnp.sum(gate_probs[:, :, None] * picked.astype(jnp.float32), axis=1))
    outputs = (after_attn + moe_out).astype(jnp.bfloat16)
    grad_out = seq_cotangent.astype(jnp.float32)
    grad_gates = lax.optimization_barrier(jnp.sum(grad_out[:, None, :] * picked.astype(jnp.float32), axis=-1))
    grad_pairs = (gate_probs[:, :, None] * grad_out[:, None, :]).astype(jnp.bfloat16)
    grad_expert = jax.vmap(fill_slots)(grad_pairs.reshape(blocks, TOK_DEV * TOP, D), targets).reshape(blocks, EXPERTS, CAP, D)
    grad_hidden = product('becd,efd->becf', grad_expert, down_weight)
    down_grad = product('becf,becd->efd', hidden, grad_expert)
    sigmoid_gate = jax.nn.sigmoid(gate_act)
    silu_slope = sigmoid_gate * (1.0 + gate_act * (1.0 - sigmoid_gate))
    grad_gate = (grad_hidden * up_act * silu_slope).astype(jnp.bfloat16)
    grad_up = (grad_hidden * silu_gate).astype(jnp.bfloat16)
    gate_grad = product('becd,becf->edf', buffer, grad_gate)
    up_grad = product('becd,becf->edf', buffer, grad_up)
    grad_buffer = (product('becf,edf->becd', grad_gate, gate_weight) + product('becf,edf->becd', grad_up, up_weight)).astype(jnp.bfloat16)
    grad_back = jax.vmap(take_slots)(grad_buffer.reshape(blocks, EXPERTS * CAP, D), targets).reshape(LEN, TOP, D)
    grad_moe_in = lax.optimization_barrier(jnp.sum(grad_back.astype(jnp.float32), axis=1))
    grad_chosen = gate_probs * (grad_gates - lax.optimization_barrier(jnp.sum(gate_probs * grad_gates, axis=-1, keepdims=True)))
    onehot = (seq_ids[:, :, None] == jnp.arange(EXPERTS, dtype=jnp.int32)[None, None, :]).astype(jnp.float32)
    grad_logits = jnp.einsum('tk,tke->te', grad_chosen, onehot)
    router_grad = jnp.dot(moe_input.astype(jnp.float32).T, grad_logits, precision=lax.Precision.HIGHEST)
    grad_moe_in = grad_moe_in + jnp.dot(grad_logits, router_weight.astype(jnp.float32).T, precision=lax.Precision.HIGHEST)
    midnorm_grad, grad_after = norm_backward(grad_moe_in, normed_second, inverse_second, midnorm_gain)
    grad_after = grad_out + grad_after
    grad_after_half = grad_after.astype(jnp.bfloat16)
    output_grad = jnp.dot(mixture_flat.T, grad_after_half, preferred_element_type=jnp.float32)
    grad_mix = jnp.dot(grad_after_half, output_weight.T, preferred_element_type=jnp.float32).astype(jnp.bfloat16)
    grad_mix = grad_mix.reshape(LEN, KV_HEADS, groups, HEAD_DIM)
    delta = product('tkgd,tkgd->kgt', grad_mix, mixture)[..., None]
    soft_round, grad_score = score_grads(query_rot, key_rot, value_half, positions, positions, logsum, delta, grad_mix)
    grad_query = product('kgts,skd->tkgd', grad_score, key_rot) * factor
    grad_keys = product('kgts,tkgd->skd', grad_score, query_rot) * factor
    grad_values = product('kgts,tkgd->skd', soft_round, grad_mix)
    query_back = rotate_back(grad_query.reshape(LEN, HEADS, HEAD_DIM), cosine, sine_table).reshape(LEN, QW).astype(jnp.bfloat16)
    key_back = rotate_back(grad_keys, cosine, sine_table).reshape(LEN, KW).astype(jnp.bfloat16)
    value_back = grad_values.reshape(LEN, KW).astype(jnp.bfloat16)
    query_grad = jnp.dot(attn_input.T, query_back, preferred_element_type=jnp.float32)
    key_grad = jnp.dot(attn_input.T, key_back, preferred_element_type=jnp.float32)
    value_grad = jnp.dot(attn_input.T, value_back, preferred_element_type=jnp.float32)
    grad_attn_in = jnp.dot(query_back, query_weight.T, preferred_element_type=jnp.float32) + jnp.dot(key_back, key_weight.T, preferred_element_type=jnp.float32) + jnp.dot(value_back, value_weight.T, preferred_element_type=jnp.float32)
    prenorm_grad, grad_inputs = norm_backward(grad_attn_in, normed_first, inverse_first, prenorm_gain)
    grad_inputs = grad_after + grad_inputs
    sums = (prenorm_grad, query_grad, key_grad, value_grad, output_grad, midnorm_grad, router_grad, gate_grad, up_grad, down_grad)
    return (outputs, grad_inputs, sums)

def reference(inputs, prenorm_gain, query_weight, key_weight, value_weight, output_weight, midnorm_gain, router_weight, gate_weight, up_weight, down_weight, expert_ids, cotangent):
    params = (prenorm_gain, query_weight, key_weight, value_weight, output_weight, midnorm_gain, router_weight, gate_weight, up_weight, down_weight)
    start = (jnp.zeros((D,), jnp.float32), jnp.zeros((D, QW), jnp.float32), jnp.zeros((D, KW), jnp.float32), jnp.zeros((D, KW), jnp.float32), jnp.zeros((QW, D), jnp.float32), jnp.zeros((D,), jnp.float32), jnp.zeros((D, EXPERTS), jnp.float32), jnp.zeros((EXPERTS, D, FF), jnp.float32), jnp.zeros((EXPERTS, D, FF), jnp.float32), jnp.zeros((EXPERTS, FF, D), jnp.float32))

    def step_fn(carry, items):
        seq_inputs, seq_ids, seq_cotangent = items
        outputs, grad_inputs, sums = sequence_pass(params, seq_inputs, seq_ids, seq_cotangent)
        carry = tuple((accum + term for accum, term in zip(carry, sums)))
        return (carry, (outputs, grad_inputs))
    totals, (outputs, grad_inputs) = lax.scan(step_fn, start, (inputs, expert_ids, cotangent))
    return (outputs, grad_inputs, totals[0], totals[1], totals[2], totals[3], totals[4], totals[5], totals[6], totals[7], totals[8], totals[9])
```

```python
import functools

import jax
import jax.numpy as jnp
from jax import lax
from jax.experimental import pallas as pl
from jax.experimental.pallas import tpu as pltpu
from jax.sharding import PartitionSpec as P

HEADS = 8
KV_HEADS = 4
HEAD_DIM = 64
EXPERTS = 32
TOP = 8
CAP = 64
EPSILON = 1e-06
ROPE_BASE = 10000.0
F32 = jnp.float32
BF16 = jnp.bfloat16
MESH_ID = pl.DeviceIdType.MESH
SEQ_AXES = ("context", "expert")


def dot(left, right):
    return jnp.dot(left, right, preferred_element_type=F32)


def dot_t(left, right):
    return lax.dot_general(left, right, (((1,), (1,)), ((), ())), preferred_element_type=F32)


def t_dot(left, right):
    return lax.dot_general(left, right, (((0,), (0,)), ((), ())), preferred_element_type=F32)


def coords_of(axes, sizes, index):
    out = {}
    for name in reversed(axes):
        out[name] = lax.rem(index, sizes[name])
        index = index // sizes[name]
    return out


def exchange_body(items, sizes, *refs):
    count = len(items)
    ins, outs, sems = refs[:count], refs[count : 2 * count], refs[2 * count :]
    widest = max((item[0] for item in items), key=len)

    def own_index(axes):
        index = 0
        for name in axes:
            index = index * sizes[name] + lax.axis_index(name)
        return index

    def group_size(axes):
        total = 1
        for name in axes:
            total *= sizes[name]
        return total

    barrier = pltpu.get_barrier_semaphore()
    me, total = own_index(widest), group_size(widest)
    for step in range(1, total):
        peer = coords_of(widest, sizes, lax.rem(me + step, total))
        pl.semaphore_signal(barrier, inc=1, device_id=peer, device_id_type=MESH_ID)
    pl.semaphore_wait(barrier, total - 1)

    waits = []
    for number, (axes, pick) in enumerate(items):
        me, total = own_index(axes), group_size(axes)
        send, recv = sems[2 * number], sems[2 * number + 1]
        for step in range(1, total):
            target = lax.rem(me + step, total)
            peer = coords_of(axes, sizes, target)
            copy = pltpu.make_async_remote_copy(
                src_ref=pick(ins[number], target, peer),
                dst_ref=outs[number].at[me],
                send_sem=send.at[step],
                recv_sem=recv.at[step],
                device_id=peer,
                device_id_type=MESH_ID,
            )
            copy.start()
            waits.append(copy)
        own = pltpu.make_async_copy(
            pick(ins[number], me, coords_of(axes, sizes, me)), outs[number].at[me], send.at[0]
        )
        own.start()
        waits.append(own)
    for copy in waits:
        copy.wait()


def pick_whole(ref, target, peer):
    return ref


def pick_target(ref, target, peer):
    return ref.at[target]


def pick_context(ref, target, peer):
    return ref.at[peer["context"]]


def exchange(cid, sizes, name, *specs):
    arrays = [spec[0] for spec in specs]
    items = [(spec[1], spec[2]) for spec in specs]
    shapes, scratch = [], []
    for array, axes, pick in specs:
        total = 1
        for axis in axes:
            total *= sizes[axis]
        chunk = array.shape if pick is pick_whole else array.shape[1:]
        shapes.append(jax.ShapeDtypeStruct((total, *chunk), array.dtype))
        scratch += [pltpu.SemaphoreType.DMA((total,)), pltpu.SemaphoreType.DMA((total,))]
    space = pl.BlockSpec(memory_space=pltpu.VMEM)
    return pl.pallas_call(
        functools.partial(exchange_body, items, sizes),
        out_shape=shapes,
        in_specs=[space] * len(specs),
        out_specs=[space] * len(specs),
        scratch_shapes=scratch,
        name=name,
        compiler_params=pltpu.CompilerParams(collective_id=cid, has_side_effects=True),
    )(*arrays)


def shift(array, axes, sizes, step):
    total = 1
    for name in axes:
        total *= sizes[name]
    return lax.ppermute(array, axes, [(i, (i + step) % total) for i in range(total)])


def flip(array, axis, size, bit):
    return lax.ppermute(array, axis, [(i, i ^ bit) for i in range(size)])


def rope_tables(positions, head_size):
    half_dim = head_size // 2
    frequency = ROPE_BASE ** (-2.0 * jnp.arange(half_dim, dtype=F32) / head_size)
    angles = positions.astype(F32)[:, None] * frequency[None, :]
    angles = jnp.concatenate([angles, angles], axis=1)
    return (jnp.cos(angles), jnp.sin(angles))


def rotate(values, cosine, sine_table):
    half_dim = values.shape[-1] // 2
    turned = jnp.concatenate([-values[..., half_dim:], values[..., :half_dim]], axis=-1)
    return values * cosine[:, None, :] + turned * sine_table[:, None, :]


def rotate_back(grads, cosine, sine_table):
    half_dim = grads.shape[-1] // 2
    scaled = grads * sine_table[:, None, :]
    turned = jnp.concatenate([scaled[..., half_dim:], -scaled[..., :half_dim]], axis=-1)
    return grads * cosine[:, None, :] + turned


def norm_forward(values, gain_vec):
    inverse = lax.rsqrt(jnp.mean(values * values, axis=-1, keepdims=True) + EPSILON)
    normed = values * inverse
    return (inverse, normed, (normed * gain_vec).astype(BF16))


def norm_backward(grad_out, normed, inverse, gain_vec):
    gain_grad = jnp.sum(grad_out * normed, axis=0)
    scaled = grad_out * gain_vec
    inner = jnp.mean(scaled * normed, axis=-1, keepdims=True)
    return (gain_grad, inverse * (scaled - normed * inner))


def stack_heads(block):
    return jnp.concatenate([block[:, :HEAD_DIM], block[:, HEAD_DIM:]], axis=0)


def side_heads(rows):
    half = rows.shape[0] // 2
    return jnp.concatenate([rows[:half], rows[half:]], axis=1)


def chunk_scores(rows, keys, number, offset):
    tokens = rows.shape[0] // 2
    scores = dot_t(rows, keys) * (HEAD_DIM ** (-0.5))
    last = scores[:, number * 8 * tokens :]
    row_pos = offset * tokens + lax.rem(lax.broadcasted_iota(jnp.int32, last.shape, 0), tokens)
    key_pos = lax.broadcasted_iota(jnp.int32, last.shape, 1)
    last = jnp.where(key_pos <= row_pos, last, -jnp.inf)
    return jnp.concatenate([scores[:, : number * 8 * tokens], last], axis=1)


def attention_forward(queries, kv_all, offset):
    blocks, tokens = queries.shape[:2]
    outs, sums = [], []
    for number in range(blocks):
        width = (number + 1) * 8 * tokens
        rows = stack_heads(queries[number])
        scores = chunk_scores(rows, kv_all[:width, :HEAD_DIM], number, offset)
        maximum = jnp.max(scores, axis=-1, keepdims=True)
        logsum = maximum + jnp.log(jnp.sum(jnp.exp(scores - maximum), axis=-1, keepdims=True))
        soft = jnp.exp(scores - logsum).astype(BF16)
        outs.append(side_heads(dot(soft, kv_all[:width, HEAD_DIM:]).astype(BF16)))
        sums.append(logsum)
    return jnp.stack(outs), sums


def attention_backward(queries, kv_all, mixtures, grad_mix, sums, offset):
    blocks, tokens = queries.shape[:2]
    factor = HEAD_DIM ** (-0.5)
    grad_queries, key_terms, value_terms = [], 0.0, 0.0
    for number in range(blocks):
        width = (number + 1) * 8 * tokens
        rows = stack_heads(queries[number])
        grads = stack_heads(grad_mix[number])
        mixed = stack_heads(mixtures[number])
        keys, values = kv_all[:width, :HEAD_DIM], kv_all[:width, HEAD_DIM:]
        delta = jnp.sum(grads.astype(F32) * mixed.astype(F32), axis=-1, keepdims=True)
        soft = jnp.exp(chunk_scores(rows, keys, number, offset) - sums[number])
        grad_soft = dot_t(grads, values)
        grad_score = (soft * (grad_soft - delta)).astype(BF16)
        soft_round = soft.astype(BF16)
        grad_queries.append(side_heads(dot(grad_score, keys) * factor))
        pad = ((0, blocks * 8 * tokens - width), (0, 0))
        key_terms = key_terms + jnp.pad(t_dot(grad_score, rows) * factor, pad)
        value_terms = value_terms + jnp.pad(t_dot(soft_round, grads), pad)
    return jnp.stack(grad_queries), jnp.concatenate([key_terms, value_terms], axis=1)


def reduce_experts(grads, sizes):
    dp, context = lax.axis_index("dp"), lax.axis_index("context")
    core, side = lax.rem(context, 2), context // 2
    experts, rows, columns = grads.shape
    part = rows // 16
    grads = grads.reshape(experts, 4, 2, 2, part, columns)

    def take(array, index, axis):
        return lax.dynamic_index_in_dim(array, index, axis, keepdims=False)

    other = flip(take(grads, 1 - core, 3).astype(BF16), "context", 4, 1)
    held = take(grads, core, 3) + other.astype(F32)

    def over_dp(array):
        total = take(array, dp, 1)
        for step in range(1, 4):
            sent = take(array, lax.rem(dp + step, 4), 1).astype(BF16)
            total = total + shift(sent, ("dp",), sizes, step).astype(F32)
        return total

    def over_side(array, axis):
        sent = take(array, 1 - side, axis).astype(BF16)
        return take(array, side, axis) + flip(sent, "context", 4, 2).astype(F32)

    half = experts // 2
    first = over_side(over_dp(held[:half]), 1)
    second = over_dp(over_side(held[half:], 2))
    return jnp.concatenate([first, second], axis=0)


def local(
    sizes,
    inputs,
    prenorm_gain,
    query_weight,
    key_weight,
    value_weight,
    output_weight,
    midnorm_gain,
    router_weight,
    gate_weight,
    up_weight,
    down_weight,
    expert_ids,
    cotangent,
):
    tokens, width = inputs.shape[1:]
    owners = sizes["expert"]
    mine = gate_weight.shape[0]
    context, owner = lax.axis_index("context"), lax.axis_index("expert")
    block = context * owners + owner
    positions = block * tokens + jnp.arange(tokens, dtype=jnp.int32)
    cosine, sine_table = rope_tables(positions, HEAD_DIM)

    sent = [shift(cotangent[0], ("expert",), sizes, step) for step in range(1, owners)]
    grad_group = jnp.stack([cotangent[0]] + sent)

    input_float = inputs[0].astype(F32)
    inverse_first, normed_first, attn_input = norm_forward(input_float, prenorm_gain)
    query_raw = dot(attn_input, query_weight).reshape(tokens, HEADS, HEAD_DIM)
    key_raw = dot(attn_input, key_weight).reshape(tokens, KV_HEADS, HEAD_DIM)
    value_raw = dot(attn_input, value_weight).reshape(tokens, KV_HEADS, HEAD_DIM)
    query_rot = rotate(query_raw, cosine, sine_table).astype(BF16)
    key_rot = rotate(key_raw, cosine, sine_table).astype(BF16)
    query_send = query_rot.reshape(tokens, KV_HEADS, 2 * HEAD_DIM).transpose(1, 0, 2)
    kv_send = jnp.concatenate([key_rot, value_raw.astype(BF16)], axis=2).transpose(1, 0, 2)
    kv_all, queries = exchange(
        0, sizes, "send_qkv", (kv_send, SEQ_AXES, pick_context), (query_send, ("context",), pick_target)
    )
    kv_all = kv_all.reshape(-1, 2 * HEAD_DIM)
    mixtures, sums = attention_forward(queries, kv_all, owner)
    (mixture,) = exchange(1, sizes, "send_mixture", (mixtures, ("context",), pick_target))
    mixture_flat = mixture.transpose(1, 0, 2).reshape(tokens, HEADS * HEAD_DIM)

    after_attn = input_float + dot(mixture_flat, output_weight)
    inverse_second, normed_second, moe_input = norm_forward(after_attn, midnorm_gain)
    logits = lax.dot_general(
        router_weight, moe_input, (((0,), (1,)), ((), ())), preferred_element_type=F32
    )
    numbers = jnp.arange(EXPERTS, dtype=jnp.int32)[:, None, None]
    chosen = jnp.any(expert_ids[0].T[None] == numbers, axis=1)
    masked = jnp.where(chosen, logits, -jnp.inf)
    powers = jnp.exp(masked - jnp.max(masked, axis=0, keepdims=True))
    gates = powers / jnp.sum(powers, axis=0, keepdims=True)
    gate_table = jnp.where(chosen, gates, -1.0)

    moe_all, table_all = exchange(
        2, sizes, "send_tokens", (moe_input, ("expert",), pick_whole), (gate_table, ("expert",), pick_whole)
    )
    order = lax.rem(owner - jnp.arange(owners) + owners, owners)
    grad_all = jnp.zeros_like(grad_group).at[order].set(grad_group)
    table = lax.dynamic_slice_in_dim(table_all, owner * mine, mine, axis=1)
    named = table >= 0.0
    before = jnp.triu(jnp.ones((tokens, tokens), BF16), 1)
    slots = jnp.einsum("skt,tu->sku", named.astype(BF16), before, preferred_element_type=F32)
    places = jnp.arange(CAP, dtype=F32)[None, None, :, None]
    pick = named[:, :, None, :] & (slots[:, :, None, :] == places)
    onehot = pick.astype(BF16)
    slot_gates = jnp.sum(jnp.where(pick, table[:, :, None, :], 0.0), axis=3)

    received = jnp.einsum("skct,std->skcd", onehot, moe_all)
    grad_slots = jnp.einsum("skct,std->skcd", onehot, grad_all)

    def product(form, left, right):
        return jnp.einsum(form, left, right, preferred_element_type=F32)

    gate_act = product("secd,edf->secf", received, gate_weight)
    up_act = product("secd,edf->secf", received, up_weight)
    silu_gate = jax.nn.silu(gate_act)
    hidden = (silu_gate * up_act).astype(BF16)
    expert_out = product("secf,efd->secd", hidden, down_weight).astype(BF16)
    grad_expert = (slot_gates[..., None] * grad_slots.astype(F32)).astype(BF16)
    slot_dots = jnp.sum(grad_slots.astype(F32) * expert_out.astype(F32), axis=-1)
    grad_hidden = product("secd,efd->secf", grad_expert, down_weight)
    down_grad = product("secf,secd->efd", hidden, grad_expert)
    sigmoid_gate = jax.nn.sigmoid(gate_act)
    silu_slope = sigmoid_gate * (1.0 + gate_act * (1.0 - sigmoid_gate))
    grad_gate = (grad_hidden * up_act * silu_slope).astype(BF16)
    grad_up = (grad_hidden * silu_gate).astype(BF16)
    gate_grad = product("secd,secf->edf", received, grad_gate)
    up_grad = product("secd,secf->edf", received, grad_up)
    grad_buffer = (
        product("secf,edf->secd", grad_gate, gate_weight)
        + product("secf,edf->secd", grad_up, up_weight)
    ).astype(BF16)

    weights = jnp.where(pick, table[:, :, None, :], 0.0)
    high = weights.astype(BF16)
    low = (weights - high.astype(F32)).astype(BF16)
    moe_terms = (
        product("skct,skcd->std", high, expert_out) + product("skct,skcd->std", low, expert_out)
    ).astype(BF16)
    grad_terms = product("skct,skcd->std", onehot, grad_buffer).astype(BF16)
    dot_terms = jnp.sum(jnp.where(pick, slot_dots[..., None], 0.0), axis=2)
    dot_terms = jnp.concatenate([dot_terms, jnp.zeros_like(dot_terms)], axis=1)
    moe_back, grad_back, dot_back = exchange(
        3,
        sizes,
        "send_results",
        (moe_terms, ("expert",), pick_target),
        (grad_terms, ("expert",), pick_target),
        (dot_terms, ("expert",), pick_target),
    )
    gate_sum, up_sum, down_sum = (
        reduce_experts(gate_grad, sizes),
        reduce_experts(up_grad, sizes),
        reduce_experts(down_grad, sizes),
    )

    outputs = (after_attn + jnp.sum(moe_back.astype(F32), axis=0)).astype(BF16)
    grad_gates = dot_back[:, :mine].reshape(EXPERTS, tokens)
    grad_logits = gates * (grad_gates - jnp.sum(gates * grad_gates, axis=0, keepdims=True))
    router_grad = jnp.einsum(
        "td,et->de", moe_input.astype(F32), grad_logits, precision=lax.Precision.HIGHEST
    )
    grad_moe_in = jnp.sum(grad_back.astype(F32), axis=0) + jnp.einsum(
        "et,de->td", grad_logits, router_weight.astype(F32), precision=lax.Precision.HIGHEST
    )
    grad_out = cotangent[0].astype(F32)
    midnorm_grad, grad_after = norm_backward(grad_moe_in, normed_second, inverse_second, midnorm_gain)
    grad_after = grad_out + grad_after
    grad_after_half = grad_after.astype(BF16)
    output_grad = t_dot(mixture_flat, grad_after_half)
    grad_mix = dot_t(grad_after_half, output_weight).astype(BF16)
    grad_mix = grad_mix.reshape(tokens, KV_HEADS, 2 * HEAD_DIM).transpose(1, 0, 2)
    (grad_mixtures,) = exchange(4, sizes, "send_grad_mixture", (grad_mix, ("context",), pick_target))
    grad_queries, kv_terms = attention_backward(queries, kv_all, mixtures, grad_mixtures, sums, owner)
    kv_terms = kv_terms.astype(BF16).reshape(-1, tokens, 2 * HEAD_DIM)
    kv_back, grad_query = exchange(
        5, sizes, "send_grad_qkv", (kv_terms, SEQ_AXES, pick_target), (grad_queries, ("context",), pick_target)
    )
    grad_kv = jnp.sum(kv_back.astype(F32).reshape(KV_HEADS, owners, tokens, 2 * HEAD_DIM), axis=1)
    grad_kv = grad_kv.transpose(1, 0, 2)
    grad_query = grad_query.transpose(1, 0, 2).reshape(tokens, HEADS, HEAD_DIM)
    query_back = rotate_back(grad_query, cosine, sine_table).reshape(tokens, -1).astype(BF16)
    key_back = rotate_back(grad_kv[..., :HEAD_DIM], cosine, sine_table).reshape(tokens, -1).astype(BF16)
    value_back = grad_kv[..., HEAD_DIM:].reshape(tokens, -1).astype(BF16)
    query_grad = t_dot(attn_input, query_back)
    key_grad = t_dot(attn_input, key_back)
    value_grad = t_dot(attn_input, value_back)
    grad_attn_in = (
        dot_t(query_back, query_weight) + dot_t(key_back, key_weight) + dot_t(value_back, value_weight)
    )
    prenorm_grad, grad_inputs = norm_backward(grad_attn_in, normed_first, inverse_first, prenorm_gain)
    grad_inputs = grad_after + grad_inputs
    dense = lax.psum(
        (prenorm_grad, query_grad, key_grad, value_grad, output_grad, midnorm_grad, router_grad),
        ("dp", "context", "expert"),
    )
    return (outputs[None], grad_inputs[None], *dense, gate_sum, up_sum, down_sum)


def solution(mesh):
    split = P("dp", ("context", "expert"), None)
    owned = P("expert", None, None)
    summed = P("expert", ("dp", "context"), None)
    in_specs = (split, *([P()] * 7), owned, owned, owned, split, split)
    out_specs = (split, split, *([P()] * 7), summed, summed, summed)
    return jax.shard_map(
        functools.partial(local, dict(mesh.shape)),
        mesh=mesh,
        in_specs=in_specs,
        out_specs=out_specs,
        check_vma=False,
    )
```

```python
import functools

import jax
import jax.numpy as jnp
from jax import lax
from jax.experimental import pallas as pl
from jax.experimental.pallas import tpu as pltpu
from jax.sharding import PartitionSpec as P

HEADS = 8
KV_HEADS = 4
HEAD_DIM = 64
EXPERTS = 32
TOP = 8
CAP = 64
EPSILON = 1e-06
ROPE_BASE = 10000.0
F32 = jnp.float32
BF16 = jnp.bfloat16
MESH_ID = pl.DeviceIdType.MESH
SEQ_AXES = ("context", "expert")


def dot(left, right):
    return jnp.dot(left, right, preferred_element_type=F32)


def dot_t(left, right):
    return lax.dot_general(left, right, (((1,), (1,)), ((), ())), preferred_element_type=F32)


def t_dot(left, right):
    return lax.dot_general(left, right, (((0,), (0,)), ((), ())), preferred_element_type=F32)


def coords_of(axes, sizes, index):
    out = {}
    for name in reversed(axes):
        out[name] = lax.rem(index, sizes[name])
        index = index // sizes[name]
    return out


def exchange_body(items, sizes, *refs):
    count = len(items)
    ins, outs, sems = refs[:count], refs[count : 2 * count], refs[2 * count :]
    widest = max((item[0] for item in items), key=len)

    def own_index(axes):
        index = 0
        for name in axes:
            index = index * sizes[name] + lax.axis_index(name)
        return index

    def group_size(axes):
        total = 1
        for name in axes:
            total *= sizes[name]
        return total

    barrier = pltpu.get_barrier_semaphore()
    me, total = own_index(widest), group_size(widest)
    for step in range(1, total):
        peer = coords_of(widest, sizes, lax.rem(me + step, total))
        pl.semaphore_signal(barrier, inc=1, device_id=peer, device_id_type=MESH_ID)
    pl.semaphore_wait(barrier, total - 1)

    waits = []
    for number, (axes, pick) in enumerate(items):
        me, total = own_index(axes), group_size(axes)
        send, recv = sems[2 * number], sems[2 * number + 1]
        for step in range(1, total):
            target = lax.rem(me + step, total)
            peer = coords_of(axes, sizes, target)
            copy = pltpu.make_async_remote_copy(
                src_ref=pick(ins[number], target, peer),
                dst_ref=outs[number].at[me],
                send_sem=send.at[step],
                recv_sem=recv.at[step],
                device_id=peer,
                device_id_type=MESH_ID,
            )
            copy.start()
            waits.append(copy)
        own = pltpu.make_async_copy(
            pick(ins[number], me, coords_of(axes, sizes, me)), outs[number].at[me], send.at[0]
        )
        own.start()
        waits.append(own)
    for copy in waits:
        copy.wait()


def pick_whole(ref, target, peer):
    return ref


def pick_target(ref, target, peer):
    return ref.at[target]


def pick_context(ref, target, peer):
    return ref.at[peer["context"]]


def exchange(cid, sizes, name, *specs):
    arrays = [spec[0] for spec in specs]
    items = [(spec[1], spec[2]) for spec in specs]
    shapes, scratch = [], []
    for array, axes, pick in specs:
        total = 1
        for axis in axes:
            total *= sizes[axis]
        chunk = array.shape if pick is pick_whole else array.shape[1:]
        shapes.append(jax.ShapeDtypeStruct((total, *chunk), array.dtype))
        scratch += [pltpu.SemaphoreType.DMA((total,)), pltpu.SemaphoreType.DMA((total,))]
    space = pl.BlockSpec(memory_space=pltpu.VMEM)
    return pl.pallas_call(
        functools.partial(exchange_body, items, sizes),
        out_shape=shapes,
        in_specs=[space] * len(specs),
        out_specs=[space] * len(specs),
        scratch_shapes=scratch,
        name=name,
        compiler_params=pltpu.CompilerParams(collective_id=cid, has_side_effects=True),
    )(*arrays)


def shift(array, axes, sizes, step):
    total = 1
    for name in axes:
        total *= sizes[name]
    return lax.ppermute(array, axes, [(i, (i + step) % total) for i in range(total)])


def flip(array, axis, size, bit):
    return lax.ppermute(array, axis, [(i, i ^ bit) for i in range(size)])


def moe_copies(sizes, refs):
    d_send, d_back, dots, dot_back, g_sends, g_backs, sems = refs
    owners = sizes["expert"]
    owner, context = lax.axis_index("expert"), lax.axis_index("context")

    def results(step):
        target = lax.rem(owner + step, owners)
        pairs = ((d_send, d_back, sems[0], sems[1]), (dots, dot_back, sems[2], sems[3]))
        return [
            pltpu.make_async_remote_copy(
                src_ref=src.at[target],
                dst_ref=dst.at[owner],
                send_sem=send.at[step],
                recv_sem=recv.at[step],
                device_id={"expert": target},
                device_id_type=MESH_ID,
            )
            for src, dst, send, recv in pairs
        ]

    def own_results():
        return [
            pltpu.make_async_copy(d_send.at[owner], d_back.at[owner], sems[0].at[0]),
            pltpu.make_async_copy(dots.at[owner], dot_back.at[owner], sems[2].at[0]),
        ]

    def halves(number):
        partner = context + 1 - 2 * lax.rem(context, 2)
        return [
            pltpu.make_async_remote_copy(
                src_ref=g_sends[i].at[number],
                dst_ref=g_backs[i].at[number],
                send_sem=sems[4].at[3 * number + i],
                recv_sem=sems[5].at[3 * number + i],
                device_id={"context": partner},
                device_id_type=MESH_ID,
            )
            for i in range(3)
        ]

    return results, own_results, halves


def moe_body(
    sizes,
    moe_ref,
    grad_ref,
    table_ref,
    wg_ref,
    wu_ref,
    wd_ref,
    own_g,
    own_u,
    own_d,
    back_g,
    back_u,
    back_d,
    y_out,
    d_back,
    dot_back,
    x_all,
    g_now,
    deo_all,
    dgu_all,
    eh_all,
    eo_all,
    dbuf_all,
    picks,
    highs,
    lows,
    gate_col,
    dot_col,
    dots,
    y_send,
    d_send,
    send_g,
    send_u,
    send_d,
    *sems,
):
    step = pl.program_id(0)
    owners = sizes["expert"]
    owner, context = lax.axis_index("expert"), lax.axis_index("context")
    core = lax.rem(context, 2)
    mine = 4
    tokens, width = moe_ref.shape[1:]
    hidden_width = wg_ref.shape[2]
    rows = owners * CAP
    tile = rows // 2
    barrier = pltpu.get_barrier_semaphore()
    results, own_results, halves = moe_copies(
        sizes, (d_send, d_back, dots, dot_back, (send_g, send_u, send_d), (back_g, back_u, back_d), sems)
    )

    @pl.when(step == 0)
    def _():
        for shift_by in range(1, owners):
            pl.semaphore_signal(
                barrier,
                inc=1,
                device_id={"expert": lax.rem(owner + shift_by, owners)},
                device_id_type=MESH_ID,
            )
        pl.semaphore_signal(
            barrier, inc=1, device_id={"context": context + 1 - 2 * core}, device_id_type=MESH_ID
        )
        dots[...] = jnp.zeros_like(dots)

    @pl.when(step == 4)
    def _():
        pl.semaphore_wait(barrier, owners)
        for shift_by in range(1, owners):
            for copy in results(shift_by):
                copy.start()
        for copy in own_results():
            copy.start()
        pltpu.make_async_copy(y_send, y_out, sems[6].at[0]).start()

    for number in range(mine):

        @pl.when(step == 5 + number)
        def _(number=number):
            for copy in halves(number):
                copy.start()

    @pl.when(step < mine)
    def _():
        place = pl.multiple_of(step * CAP, CAP)
        table = jnp.concatenate(
            [table_ref[s, pl.ds(owner * mine + step, 1), :] for s in range(owners)], axis=0
        )
        named = table >= 0.0
        above = lax.broadcasted_iota(jnp.int32, (tokens, tokens), 0)
        beside = lax.broadcasted_iota(jnp.int32, (tokens, tokens), 1)
        before = (above < beside).astype(F32).astype(BF16)
        slots = dot(named.astype(F32).astype(BF16), before)
        slots = jnp.where(named, slots, -1.0)
        counts = lax.broadcasted_iota(jnp.int32, (CAP, tokens), 0).astype(F32)
        for s in range(owners):
            chosen = counts == slots[s : s + 1]
            onehot = jnp.where(chosen, 1.0, 0.0).astype(BF16)
            weight = jnp.where(chosen, table[s : s + 1], 0.0)
            high = weight.astype(BF16)
            picks[s, pl.ds(place, CAP), :] = onehot
            highs[s, pl.ds(place, CAP), :] = high
            lows[s, pl.ds(place, CAP), :] = (weight - high.astype(F32)).astype(BF16)
            gate_col[s * CAP : (s + 1) * CAP, :] = jnp.sum(weight, axis=1, keepdims=True)
            x_all[step, s * CAP : (s + 1) * CAP, :] = dot(onehot, moe_ref[s]).astype(BF16)
            g_now[s * CAP : (s + 1) * CAP, :] = dot(onehot, grad_ref[s]).astype(BF16)

        def run_tile(r, carry):
            here = pl.ds(pl.multiple_of(r * tile, tile), tile)
            part = pl.ds(r * (owners // 2), owners // 2)
            spot = pl.ds(place, CAP)
            rows_in = x_all[step, here, :]
            gate_act = dot(rows_in, wg_ref[0])
            up_act = dot(rows_in, wu_ref[0])
            sigma = jax.nn.sigmoid(gate_act)
            silu = gate_act * sigma
            hidden = (silu * up_act).astype(BF16)
            eh_all[step, here, :] = hidden
            expert_out = dot(hidden, wd_ref[0]).astype(BF16)
            eo_all[part, spot, :] = expert_out.reshape(owners // 2, CAP, width)
            grads = g_now[here, :].astype(F32)
            dot_col[here, :] = jnp.sum(grads * expert_out.astype(F32), axis=1, keepdims=True)
            grad_expert = (gate_col[here, :] * grads).astype(BF16)
            deo_all[step, here, :] = grad_expert
            grad_hidden = dot_t(grad_expert, wd_ref[0])
            slope = sigma * (1.0 + gate_act * (1.0 - sigma))
            grad_gate = (grad_hidden * up_act * slope).astype(BF16)
            grad_up = (grad_hidden * silu).astype(BF16)
            dgu_all[step, here, :hidden_width] = grad_gate
            dgu_all[step, here, hidden_width:] = grad_up
            grad_buffer = (dot_t(grad_gate, wg_ref[0]) + dot_t(grad_up, wu_ref[0])).astype(BF16)
            dbuf_all[part, spot, :] = grad_buffer.reshape(owners // 2, CAP, width)
            return carry

        lax.fori_loop(0, 2, run_tile, 0)
        for s in range(owners):
            onehot = picks[s, pl.ds(place, CAP), :].astype(F32)
            line = jnp.sum(onehot * dot_col[s * CAP : (s + 1) * CAP, :], axis=0, keepdims=True)
            dots[s, pl.ds(step, 1), :] = line

    @pl.when(step == mine - 1)
    def _():
        def combine(s, carry):
            moved = t_dot(highs[s], eo_all[s]) + t_dot(lows[s], eo_all[s])
            y_send[s] = moved.astype(BF16)
            d_send[s] = t_dot(picks[s], dbuf_all[s]).astype(BF16)
            return carry

        lax.fori_loop(0, owners, combine, 0)

    @pl.when((step >= mine) & (step < 2 * mine))
    def _():
        number = step - mine
        blocks = width // 256
        per = width // 16

        def gate_rows(j, carry):
            columns = pl.ds(pl.multiple_of(j * 256, 256), 256)
            rows_in = x_all[number, :, columns]
            for half, own, send in ((0, own_g, send_g), (1, own_u, send_u)):
                grads = dgu_all[number, :, half * hidden_width : (half + 1) * hidden_width]
                terms = t_dot(rows_in, grads).reshape(128 // per, 2, per, hidden_width)
                first, second = terms[:, 0], terms[:, 1]
                group = pl.ds(j * (128 // per), 128 // per)
                own[0, group] = jnp.where(core == 0, first, second)
                send[number, group] = jnp.where(core == 0, second, first).astype(BF16)
            return carry

        lax.fori_loop(0, blocks, gate_rows, 0)
        less = hidden_width // 16

        def down_rows(j, carry):
            columns = pl.ds(pl.multiple_of(j * 256, 256), 256)
            terms = t_dot(eh_all[number, :, columns], deo_all[number])
            terms = terms.reshape(128 // less, 2, less, width)
            first, second = terms[:, 0], terms[:, 1]
            group = pl.ds(j * (128 // less), 128 // less)
            own_d[0, group] = jnp.where(core == 0, first, second)
            send_d[number, group] = jnp.where(core == 0, second, first).astype(BF16)
            return carry

        lax.fori_loop(0, hidden_width // 256, down_rows, 0)

    @pl.when(step == 2 * mine)
    def _():
        for shift_by in range(1, owners):
            for copy in results(shift_by):
                copy.wait()
        for copy in own_results():
            copy.wait()
        pltpu.make_async_copy(y_send, y_out, sems[6].at[0]).wait()
        for number in range(mine):
            for copy in halves(number):
                copy.wait()


def run_experts(cid, sizes, moe_all, grad_all, table_all, gate_weight, up_weight, down_weight):
    owners, tokens, width = moe_all.shape
    mine, _, inner = gate_weight.shape
    rows = owners * CAP
    part, less = width // 16, inner // 16

    def fixed(array):
        return pl.BlockSpec(array.shape, lambda i: (0, 0, 0), pipeline_mode=pl.Buffered(1))

    def expert_block(array):
        return pl.BlockSpec((1, *array.shape[1:]), lambda i: (jnp.minimum(i, mine - 1), 0, 0))

    def own_block(*shape):
        return pl.BlockSpec((1, *shape), lambda i: (jnp.clip(i - mine, 0, mine - 1), 0, 0, 0))

    anywhere = pl.BlockSpec(memory_space=pl.ANY)
    wide, tall = (8, part, inner), (8, less, width)
    dma = pltpu.SemaphoreType.DMA
    return pl.pallas_call(
        functools.partial(moe_body, sizes),
        grid=(2 * mine + 1,),
        out_shape=[
            jax.ShapeDtypeStruct((mine, *wide), F32),
            jax.ShapeDtypeStruct((mine, *wide), F32),
            jax.ShapeDtypeStruct((mine, *tall), F32),
            jax.ShapeDtypeStruct((mine, *wide), BF16),
            jax.ShapeDtypeStruct((mine, *wide), BF16),
            jax.ShapeDtypeStruct((mine, *tall), BF16),
            jax.ShapeDtypeStruct((owners, tokens, width), BF16),
            jax.ShapeDtypeStruct((owners, tokens, width), BF16),
            jax.ShapeDtypeStruct((owners, 8, tokens), F32),
        ],
        in_specs=[
            fixed(moe_all),
            fixed(grad_all),
            fixed(table_all),
            expert_block(gate_weight),
            expert_block(up_weight),
            expert_block(down_weight),
        ],
        out_specs=[own_block(*wide), own_block(*wide), own_block(*tall), *([anywhere] * 6)],
        scratch_shapes=[
            pltpu.VMEM((mine, rows, width), BF16),
            pltpu.VMEM((rows, width), BF16),
            pltpu.VMEM((mine, rows, width), BF16),
            pltpu.VMEM((mine, rows, 2 * inner), BF16),
            pltpu.VMEM((mine, rows, inner), BF16),
            pltpu.VMEM((owners, mine * CAP, width), BF16),
            pltpu.VMEM((owners, mine * CAP, width), BF16),
            pltpu.VMEM((owners, mine * CAP, tokens), BF16),
            pltpu.VMEM((owners, mine * CAP, tokens), BF16),
            pltpu.VMEM((owners, mine * CAP, tokens), BF16),
            pltpu.VMEM((rows, 1), F32),
            pltpu.VMEM((rows, 1), F32),
            pltpu.VMEM((owners, 8, tokens), F32),
            pltpu.VMEM((owners, tokens, width), BF16),
            pltpu.VMEM((owners, tokens, width), BF16),
            pltpu.VMEM((mine, *wide), BF16),
            pltpu.VMEM((mine, *wide), BF16),
            pltpu.VMEM((mine, *tall), BF16),
            dma((owners,)),
            dma((owners,)),
            dma((owners,)),
            dma((owners,)),
            dma((3 * mine,)),
            dma((3 * mine,)),
            dma((1,)),
        ],
        name="run_experts",
        compiler_params=pltpu.CompilerParams(
            collective_id=cid, has_side_effects=True, vmem_limit_bytes=67_043_328
        ),
    )(moe_all, grad_all, table_all, gate_weight, up_weight, down_weight)


def rope_tables(positions, head_size):
    half_dim = head_size // 2
    frequency = ROPE_BASE ** (-2.0 * jnp.arange(half_dim, dtype=F32) / head_size)
    angles = positions.astype(F32)[:, None] * frequency[None, :]
    angles = jnp.concatenate([angles, angles], axis=1)
    return (jnp.cos(angles), jnp.sin(angles))


def rotate(values, cosine, sine_table):
    half_dim = values.shape[-1] // 2
    turned = jnp.concatenate([-values[..., half_dim:], values[..., :half_dim]], axis=-1)
    return values * cosine[:, None, :] + turned * sine_table[:, None, :]


def rotate_back(grads, cosine, sine_table):
    half_dim = grads.shape[-1] // 2
    scaled = grads * sine_table[:, None, :]
    turned = jnp.concatenate([scaled[..., half_dim:], -scaled[..., :half_dim]], axis=-1)
    return grads * cosine[:, None, :] + turned


def norm_forward(values, gain_vec):
    inverse = lax.rsqrt(jnp.mean(values * values, axis=-1, keepdims=True) + EPSILON)
    normed = values * inverse
    return (inverse, normed, (normed * gain_vec).astype(BF16))


def norm_backward(grad_out, normed, inverse, gain_vec):
    gain_grad = jnp.sum(grad_out * normed, axis=0)
    scaled = grad_out * gain_vec
    inner = jnp.mean(scaled * normed, axis=-1, keepdims=True)
    return (gain_grad, inverse * (scaled - normed * inner))


def stack_heads(block):
    return jnp.concatenate([block[:, :HEAD_DIM], block[:, HEAD_DIM:]], axis=0)


def side_heads(rows):
    half = rows.shape[0] // 2
    return jnp.concatenate([rows[:half], rows[half:]], axis=1)


def chunk_scores(rows, keys, number, offset):
    tokens = rows.shape[0] // 2
    scores = dot_t(rows, keys) * (HEAD_DIM ** (-0.5))
    last = scores[:, number * 8 * tokens :]
    row_pos = offset * tokens + lax.rem(lax.broadcasted_iota(jnp.int32, last.shape, 0), tokens)
    key_pos = lax.broadcasted_iota(jnp.int32, last.shape, 1)
    last = jnp.where(key_pos <= row_pos, last, -jnp.inf)
    return jnp.concatenate([scores[:, : number * 8 * tokens], last], axis=1)


def attention_forward(queries, kv_all, offset):
    blocks, tokens = queries.shape[:2]
    outs, sums = [], []
    for number in range(blocks):
        width = (number + 1) * 8 * tokens
        rows = stack_heads(queries[number])
        scores = chunk_scores(rows, kv_all[:width, :HEAD_DIM], number, offset)
        maximum = jnp.max(scores, axis=-1, keepdims=True)
        logsum = maximum + jnp.log(jnp.sum(jnp.exp(scores - maximum), axis=-1, keepdims=True))
        soft = jnp.exp(scores - logsum).astype(BF16)
        outs.append(side_heads(dot(soft, kv_all[:width, HEAD_DIM:]).astype(BF16)))
        sums.append(logsum)
    return jnp.stack(outs), sums


def attention_backward(queries, kv_all, mixtures, grad_mix, sums, offset):
    blocks, tokens = queries.shape[:2]
    factor = HEAD_DIM ** (-0.5)
    grad_queries, key_terms, value_terms = [], 0.0, 0.0
    for number in range(blocks):
        width = (number + 1) * 8 * tokens
        rows = stack_heads(queries[number])
        grads = stack_heads(grad_mix[number])
        mixed = stack_heads(mixtures[number])
        keys, values = kv_all[:width, :HEAD_DIM], kv_all[:width, HEAD_DIM:]
        delta = jnp.sum(grads.astype(F32) * mixed.astype(F32), axis=-1, keepdims=True)
        soft = jnp.exp(chunk_scores(rows, keys, number, offset) - sums[number])
        grad_soft = dot_t(grads, values)
        grad_score = (soft * (grad_soft - delta)).astype(BF16)
        soft_round = soft.astype(BF16)
        grad_queries.append(side_heads(dot(grad_score, keys) * factor))
        pad = ((0, blocks * 8 * tokens - width), (0, 0))
        key_terms = key_terms + jnp.pad(t_dot(grad_score, rows) * factor, pad)
        value_terms = value_terms + jnp.pad(t_dot(soft_round, grads), pad)
    return jnp.stack(grad_queries), jnp.concatenate([key_terms, value_terms], axis=1)


def reduce_experts(own, other, sizes):
    dp, side = lax.axis_index("dp"), lax.axis_index("context") // 2
    experts, _, part, columns = own.shape
    held = (own + other.astype(F32)).reshape(experts, 4, 2, part, columns)

    def take(array, index, axis):
        return lax.dynamic_index_in_dim(array, index, axis, keepdims=False)

    def over_dp(array):
        total = take(array, dp, 1)
        for step in range(1, 4):
            sent = take(array, lax.rem(dp + step, 4), 1).astype(BF16)
            total = total + shift(sent, ("dp",), sizes, step).astype(F32)
        return total

    def over_side(array, axis):
        sent = take(array, 1 - side, axis).astype(BF16)
        return take(array, side, axis) + flip(sent, "context", 4, 2).astype(F32)

    half = experts // 2
    first = over_side(over_dp(held[:half]), 1)
    second = over_dp(over_side(held[half:], 2))
    return jnp.concatenate([first, second], axis=0)


def local(
    sizes,
    inputs,
    prenorm_gain,
    query_weight,
    key_weight,
    value_weight,
    output_weight,
    midnorm_gain,
    router_weight,
    gate_weight,
    up_weight,
    down_weight,
    expert_ids,
    cotangent,
):
    tokens, width = inputs.shape[1:]
    owners = sizes["expert"]
    mine = gate_weight.shape[0]
    context, owner = lax.axis_index("context"), lax.axis_index("expert")
    block = context * owners + owner
    positions = block * tokens + jnp.arange(tokens, dtype=jnp.int32)
    cosine, sine_table = rope_tables(positions, HEAD_DIM)

    input_float = inputs[0].astype(F32)
    inverse_first, normed_first, attn_input = norm_forward(input_float, prenorm_gain)
    query_raw = dot(attn_input, query_weight).reshape(tokens, HEADS, HEAD_DIM)
    key_raw = dot(attn_input, key_weight).reshape(tokens, KV_HEADS, HEAD_DIM)
    value_raw = dot(attn_input, value_weight).reshape(tokens, KV_HEADS, HEAD_DIM)
    query_rot = rotate(query_raw, cosine, sine_table).astype(BF16)
    key_rot = rotate(key_raw, cosine, sine_table).astype(BF16)
    query_send = query_rot.reshape(tokens, KV_HEADS, 2 * HEAD_DIM).transpose(1, 0, 2)
    kv_send = jnp.concatenate([key_rot, value_raw.astype(BF16)], axis=2).transpose(1, 0, 2)
    kv_all, queries, grad_all = exchange(
        0,
        sizes,
        "send_qkv",
        (kv_send, SEQ_AXES, pick_context),
        (query_send, ("context",), pick_target),
        (cotangent[0], ("expert",), pick_whole),
    )
    kv_all = kv_all.reshape(-1, 2 * HEAD_DIM)
    mixtures, sums = attention_forward(queries, kv_all, owner)
    (mixture,) = exchange(1, sizes, "send_mixture", (mixtures, ("context",), pick_target))
    mixture_flat = mixture.transpose(1, 0, 2).reshape(tokens, HEADS * HEAD_DIM)

    after_attn = input_float + dot(mixture_flat, output_weight)
    inverse_second, normed_second, moe_input = norm_forward(after_attn, midnorm_gain)
    logits = lax.dot_general(
        router_weight, moe_input, (((0,), (1,)), ((), ())), preferred_element_type=F32
    )
    numbers = jnp.arange(EXPERTS, dtype=jnp.int32)[:, None, None]
    chosen = jnp.any(expert_ids[0].T[None] == numbers, axis=1)
    masked = jnp.where(chosen, logits, -jnp.inf)
    powers = jnp.exp(masked - jnp.max(masked, axis=0, keepdims=True))
    gates = powers / jnp.sum(powers, axis=0, keepdims=True)
    gate_table = jnp.where(chosen, gates, -1.0)

    moe_all, table_all = exchange(
        2, sizes, "send_tokens", (moe_input, ("expert",), pick_whole), (gate_table, ("expert",), pick_whole)
    )
    own_g, own_u, own_d, other_g, other_u, other_d, moe_terms, grad_back, dot_back = run_experts(
        3, sizes, moe_all, grad_all, table_all, gate_weight, up_weight, down_weight
    )
    (moe_back,) = exchange(6, sizes, "send_outputs", (moe_terms, ("expert",), pick_target))
    gate_sum, up_sum, down_sum = (
        reduce_experts(own_g, other_g, sizes),
        reduce_experts(own_u, other_u, sizes),
        reduce_experts(own_d, other_d, sizes),
    )

    outputs = (after_attn + jnp.sum(moe_back.astype(F32), axis=0)).astype(BF16)
    grad_gates = dot_back[:, :mine].reshape(EXPERTS, tokens)
    grad_logits = gates * (grad_gates - jnp.sum(gates * grad_gates, axis=0, keepdims=True))
    router_grad = jnp.einsum(
        "td,et->de", moe_input.astype(F32), grad_logits, precision=lax.Precision.HIGHEST
    )
    grad_moe_in = jnp.sum(grad_back.astype(F32), axis=0) + jnp.einsum(
        "et,de->td", grad_logits, router_weight.astype(F32), precision=lax.Precision.HIGHEST
    )
    grad_out = cotangent[0].astype(F32)
    midnorm_grad, grad_after = norm_backward(grad_moe_in, normed_second, inverse_second, midnorm_gain)
    grad_after = grad_out + grad_after
    grad_after_half = grad_after.astype(BF16)
    output_grad = t_dot(mixture_flat, grad_after_half)
    grad_mix = dot_t(grad_after_half, output_weight).astype(BF16)
    grad_mix = grad_mix.reshape(tokens, KV_HEADS, 2 * HEAD_DIM).transpose(1, 0, 2)
    (grad_mixtures,) = exchange(4, sizes, "send_grad_mixture", (grad_mix, ("context",), pick_target))
    grad_queries, kv_terms = attention_backward(queries, kv_all, mixtures, grad_mixtures, sums, owner)
    kv_terms = kv_terms.astype(BF16).reshape(-1, tokens, 2 * HEAD_DIM)
    kv_back, grad_query = exchange(
        5, sizes, "send_grad_qkv", (kv_terms, SEQ_AXES, pick_target), (grad_queries, ("context",), pick_target)
    )
    grad_kv = jnp.sum(kv_back.astype(F32).reshape(KV_HEADS, owners, tokens, 2 * HEAD_DIM), axis=1)
    grad_kv = grad_kv.transpose(1, 0, 2)
    grad_query = grad_query.transpose(1, 0, 2).reshape(tokens, HEADS, HEAD_DIM)
    query_back = rotate_back(grad_query, cosine, sine_table).reshape(tokens, -1).astype(BF16)
    key_back = rotate_back(grad_kv[..., :HEAD_DIM], cosine, sine_table).reshape(tokens, -1).astype(BF16)
    value_back = grad_kv[..., HEAD_DIM:].reshape(tokens, -1).astype(BF16)
    query_grad = t_dot(attn_input, query_back)
    key_grad = t_dot(attn_input, key_back)
    value_grad = t_dot(attn_input, value_back)
    grad_attn_in = (
        dot_t(query_back, query_weight) + dot_t(key_back, key_weight) + dot_t(value_back, value_weight)
    )
    prenorm_grad, grad_inputs = norm_backward(grad_attn_in, normed_first, inverse_first, prenorm_gain)
    grad_inputs = grad_after + grad_inputs
    narrow = jnp.concatenate([router_grad, prenorm_grad[:, None], midnorm_grad[:, None]], axis=1)
    query_grad, key_grad, value_grad, output_grad, narrow = lax.psum(
        (query_grad, key_grad, value_grad, output_grad, narrow), ("dp", "context", "expert")
    )
    dense = (
        narrow[:, EXPERTS],
        query_grad,
        key_grad,
        value_grad,
        output_grad,
        narrow[:, EXPERTS + 1],
        narrow[:, :EXPERTS],
    )
    return (outputs[None], grad_inputs[None], *dense, gate_sum, up_sum, down_sum)


def solution(mesh):
    split = P("dp", ("context", "expert"), None)
    owned = P("expert", None, None)
    summed = P("expert", ("dp", "context"), None)
    in_specs = (split, *([P()] * 7), owned, owned, owned, split, split)
    out_specs = (split, split, *([P()] * 7), summed, summed, summed)
    return jax.shard_map(
        functools.partial(local, dict(mesh.shape)),
        mesh=mesh,
        in_specs=in_specs,
        out_specs=out_specs,
        check_vma=False,
    )
```

```python
import functools

import jax
import jax.numpy as jnp
from jax import lax
from jax.experimental import pallas as pl
from jax.experimental.pallas import tpu as pltpu
from jax.sharding import PartitionSpec as P

HEADS = 8
KV_HEADS = 4
HEAD_DIM = 64
EXPERTS = 32
TOP = 8
CAP = 64
EPSILON = 1e-06
ROPE_BASE = 10000.0
F32 = jnp.float32
BF16 = jnp.bfloat16
MESH_ID = pl.DeviceIdType.MESH
SEQ_AXES = ("context", "expert")
EVERY = ("dp", "context", "expert")


def dot(left, right):
    return jnp.dot(left, right, preferred_element_type=F32)


def dot_t(left, right):
    return lax.dot_general(left, right, (((1,), (1,)), ((), ())), preferred_element_type=F32)


def t_dot(left, right):
    return lax.dot_general(left, right, (((0,), (0,)), ((), ())), preferred_element_type=F32)


def axis_size(sizes, name):
    return 2 if name == "side" else sizes[name]


def group_size(axes, sizes):
    total = 1
    for name in axes:
        total *= axis_size(sizes, name)
    return total


def own_index(axes, sizes):
    index = 0
    for name in axes:
        own = lax.axis_index("context") // 2 if name == "side" else lax.axis_index(name)
        index = index * axis_size(sizes, name) + own
    return index


def coords_of(axes, sizes, index):
    out = {}
    for name in reversed(axes):
        place = lax.rem(index, axis_size(sizes, name))
        if name == "side":
            out["context"] = place * 2 + lax.rem(lax.axis_index("context"), 2)
        else:
            out[name] = place
        index = index // axis_size(sizes, name)
    return out


def pick_whole(ref, target, peer):
    return ref


def pick_target(ref, target, peer):
    return ref.at[target]


def pick_context(ref, target, peer):
    return ref.at[peer["context"]]


def exchange_body(items, sizes, compute, more_ins, more_outs, *refs):
    count = len(items)
    ins, refs = refs[:count], refs[count:]
    data_ins, refs = refs[:more_ins], refs[more_ins:]
    outs, refs = refs[:count], refs[count:]
    data_outs, refs = refs[:more_outs], refs[more_outs:]
    sems, scratch = refs[: 2 * count], refs[2 * count :]

    barrier = pltpu.get_barrier_semaphore()
    groups = []
    for axes, _, _ in items:
        if not any(set(axes) <= set(other) for other in groups):
            groups = [other for other in groups if not set(other) <= set(axes)] + [axes]
    signals = 0
    for axes in groups:
        me, total = own_index(axes, sizes), group_size(axes, sizes)
        for step in range(1, total):
            peer = coords_of(axes, sizes, lax.rem(me + step, total))
            pl.semaphore_signal(barrier, inc=1, device_id=peer, device_id_type=MESH_ID)
        signals += total - 1
    pl.semaphore_wait(barrier, signals)

    waits = []
    for number, (axes, pick, keep) in enumerate(items):
        me, total = own_index(axes, sizes), group_size(axes, sizes)
        send, recv = sems[2 * number], sems[2 * number + 1]
        for step in range(1, total):
            target = lax.rem(me + step, total)
            peer = coords_of(axes, sizes, target)
            copy = pltpu.make_async_remote_copy(
                src_ref=pick(ins[number], target, peer),
                dst_ref=outs[number].at[me],
                send_sem=send.at[step],
                recv_sem=recv.at[step],
                device_id=peer,
                device_id_type=MESH_ID,
            )
            copy.start()
            waits.append(copy)
        if keep:
            own = pltpu.make_async_copy(
                pick(ins[number], me, coords_of(axes, sizes, me)), outs[number].at[me], send.at[0]
            )
            own.start()
            waits.append(own)
    if compute is not None:
        compute(data_ins, data_outs, scratch)
    for copy in waits:
        copy.wait()


def exchange(cid, sizes, name, *specs, compute=None, data=(), results=(), scratch=(), cost=None):
    vmem, hbm = pl.BlockSpec(memory_space=pltpu.VMEM), pl.BlockSpec(memory_space=pl.ANY)
    items, shapes, spaces, sems = [], [], [], []
    for array, axes, pick, *large in specs:
        total = group_size(axes, sizes)
        chunk = array.shape if pick is pick_whole else array.shape[1:]
        shapes.append(jax.ShapeDtypeStruct((total, *chunk), array.dtype))
        spaces.append(hbm if large else vmem)
        items.append((axes, pick, not large))
        sems += [pltpu.SemaphoreType.DMA((total,)), pltpu.SemaphoreType.DMA((total,))]
    return pl.pallas_call(
        functools.partial(exchange_body, items, sizes, compute, len(data), len(results)),
        out_shape=[*shapes, *results],
        in_specs=[*spaces, *([vmem] * len(data))],
        out_specs=[*spaces, *([vmem] * len(results))],
        scratch_shapes=[*sems, *scratch],
        name=name,
        compiler_params=pltpu.CompilerParams(
            collective_id=cid, has_side_effects=True, vmem_limit_bytes=60_000_000
        ),
    )(*[spec[0] for spec in specs], *data)


def stack_heads(block, low):
    tokens = block.shape[0]
    zero = jnp.zeros((tokens, HEAD_DIM), block.dtype)
    parts = [block[:, :HEAD_DIM], block[:, HEAD_DIM:]]
    return jnp.concatenate(
        [jnp.concatenate([part, zero] if low else [zero, part], axis=1) for part in parts], axis=0
    )


def causal(shape, tokens):
    keys = lax.broadcasted_iota(jnp.int32, shape, 0)
    queries = lax.rem(lax.broadcasted_iota(jnp.int32, shape, 1), tokens)
    return keys - queries <= lax.axis_index("expert") * tokens


def identity(size):
    shape = (size, size)
    return lax.broadcasted_iota(jnp.int32, shape, 0) == lax.broadcasted_iota(jnp.int32, shape, 1)


def attention_forward(data, results, scratch):
    query_ref, kv_ref = data
    out_ref, sum_ref = results
    (score_ref,) = scratch
    blocks, tokens = query_ref.shape[:2]
    chunk, columns = 8 * tokens, 2 * tokens

    def block(number, carry):
        rows = stack_heads(query_ref[number], True) * (HEAD_DIM ** (-0.5))
        rows = rows.astype(BF16)

        def keys_of(j):
            return pl.ds(pl.multiple_of(j * chunk, chunk), chunk)

        def first(j, top):
            scores = dot_t(kv_ref[keys_of(j), :], rows)
            score_ref[keys_of(j), :] = scores
            return jnp.maximum(top, jnp.max(scores, axis=0, keepdims=True))

        top = lax.fori_loop(0, number, first, jnp.full((1, columns), -jnp.inf, F32))
        scores = dot_t(kv_ref[keys_of(number), :], rows)
        scores = jnp.where(causal(scores.shape, tokens), scores, -jnp.inf)
        score_ref[keys_of(number), :] = scores
        top = jnp.maximum(top, jnp.max(scores, axis=0, keepdims=True))

        def second(j, held):
            total, mixed = held
            powers = jnp.exp(score_ref[keys_of(j), :] - top)
            total = total + jnp.sum(powers, axis=0, keepdims=True)
            return total, mixed + t_dot(powers.astype(BF16), kv_ref[keys_of(j), :])

        start = (jnp.zeros((1, columns), F32), jnp.zeros((columns, 2 * HEAD_DIM), F32))
        total, mixed = lax.fori_loop(0, number + 1, second, start)
        sum_ref[number] = top + jnp.log(total)
        inverse = jnp.sum(jnp.where(identity(columns), 1.0 / total, 0.0), axis=1, keepdims=True)
        mixed = (mixed * inverse)[:, HEAD_DIM:]
        out_ref[number] = jnp.concatenate([mixed[:tokens], mixed[tokens:]], axis=1).astype(BF16)
        return carry

    lax.fori_loop(0, blocks, block, 0)


def attention_backward(data, results, scratch):
    query_ref, kv_ref, mix_ref, grad_ref, sum_ref = data
    grad_query_ref, terms_ref = results
    (sum_kv,) = scratch
    blocks, tokens = query_ref.shape[:2]
    chunk, columns = 8 * tokens, 2 * tokens
    factor = HEAD_DIM ** (-0.5)
    sum_kv[...] = jnp.zeros_like(sum_kv)

    def block(number, carry):
        rows = (stack_heads(query_ref[number], True) * factor).astype(BF16)
        grads = stack_heads(grad_ref[number], False)
        both = jnp.concatenate([rows, grads], axis=0)
        pairs = dot_t(stack_heads(mix_ref[number], False), grads)
        delta = jnp.sum(jnp.where(identity(columns), pairs, 0.0), axis=0, keepdims=True)
        logsum = sum_ref[number]

        def unit(j, total, masked):
            keys = pl.ds(pl.multiple_of(j * chunk, chunk), chunk)
            kv = kv_ref[keys, :]
            products = dot_t(kv, both)
            soft = jnp.exp(products[:, :columns] - logsum)
            if masked:
                soft = jnp.where(causal(soft.shape, tokens), soft, 0.0)
            scores = (soft * (products[:, columns:] - delta)).astype(BF16)
            sum_kv[keys, :] += dot(jnp.concatenate([scores, soft.astype(BF16)], axis=1), both)
            return total + t_dot(scores, kv)

        total = lax.fori_loop(
            0, number, lambda j, held: unit(j, held, False), jnp.zeros((columns, 2 * HEAD_DIM), F32)
        )
        total = unit(number, total, True)[:, :HEAD_DIM] * factor
        grad_query_ref[number] = jnp.concatenate([total[:tokens], total[tokens:]], axis=1)
        return carry

    lax.fori_loop(0, blocks, block, 0)
    terms_ref[...] = sum_kv[...].astype(BF16)


def moe_copies(sizes, refs):
    d_send, d_back, dots, dot_back, g_sends, g_backs, sems = refs
    owners = sizes["expert"]
    owner, context = lax.axis_index("expert"), lax.axis_index("context")

    def results(step):
        target = lax.rem(owner + step, owners)
        pairs = ((d_send, d_back, sems[0], sems[1]), (dots, dot_back, sems[2], sems[3]))
        return [
            pltpu.make_async_remote_copy(
                src_ref=src.at[target],
                dst_ref=dst.at[owner],
                send_sem=send.at[step],
                recv_sem=recv.at[step],
                device_id={"expert": target},
                device_id_type=MESH_ID,
            )
            for src, dst, send, recv in pairs
        ]

    def own_results():
        return [
            pltpu.make_async_copy(d_send.at[owner], d_back.at[owner], sems[0].at[0]),
            pltpu.make_async_copy(dots.at[owner], dot_back.at[owner], sems[2].at[0]),
        ]

    def halves(number):
        partner = context + 1 - 2 * lax.rem(context, 2)
        return [
            pltpu.make_async_remote_copy(
                src_ref=g_sends[i].at[number],
                dst_ref=g_backs[i].at[number],
                send_sem=sems[4].at[3 * number + i],
                recv_sem=sems[5].at[3 * number + i],
                device_id={"context": partner},
                device_id_type=MESH_ID,
            )
            for i in range(3)
        ]

    return results, own_results, halves


def moe_body(
    sizes,
    moe_ref,
    grad_ref,
    table_ref,
    wg_ref,
    wu_ref,
    wd_ref,
    own_g,
    own_u,
    own_d,
    back_g,
    back_u,
    back_d,
    y_out,
    d_back,
    dot_back,
    x_all,
    g_now,
    deo_all,
    dgu_all,
    eh_all,
    eo_all,
    dbuf_all,
    picks,
    highs,
    lows,
    gate_col,
    dot_col,
    dots,
    y_send,
    d_send,
    send_g,
    send_u,
    send_d,
    *sems,
):
    step = pl.program_id(0)
    owners = sizes["expert"]
    owner, context = lax.axis_index("expert"), lax.axis_index("context")
    core = lax.rem(context, 2)
    mine = 4
    tokens, width = moe_ref.shape[1:]
    hidden_width = wg_ref.shape[2]
    rows = owners * CAP
    tile = rows // 2
    barrier = pltpu.get_barrier_semaphore()
    results, own_results, halves = moe_copies(
        sizes, (d_send, d_back, dots, dot_back, (send_g, send_u, send_d), (back_g, back_u, back_d), sems)
    )

    @pl.when(step == 0)
    def _():
        for shift_by in range(1, owners):
            pl.semaphore_signal(
                barrier,
                inc=1,
                device_id={"expert": lax.rem(owner + shift_by, owners)},
                device_id_type=MESH_ID,
            )
        pl.semaphore_signal(
            barrier, inc=1, device_id={"context": context + 1 - 2 * core}, device_id_type=MESH_ID
        )
        dots[...] = jnp.zeros_like(dots)

    @pl.when(step == 4)
    def _():
        pl.semaphore_wait(barrier, owners)
        for shift_by in range(1, owners):
            for copy in results(shift_by):
                copy.start()
        for copy in own_results():
            copy.start()
        pltpu.make_async_copy(y_send, y_out, sems[6].at[0]).start()

    for number in range(mine):

        @pl.when(step == 5 + number)
        def _(number=number):
            for copy in halves(number):
                copy.start()

    @pl.when(step < mine)
    def _():
        place = pl.multiple_of(step * CAP, CAP)
        table = jnp.concatenate(
            [table_ref[s, pl.ds(owner * mine + step, 1), :] for s in range(owners)], axis=0
        )
        named = table >= 0.0
        above = lax.broadcasted_iota(jnp.int32, (tokens, tokens), 0)
        beside = lax.broadcasted_iota(jnp.int32, (tokens, tokens), 1)
        before = (above < beside).astype(F32).astype(BF16)
        slots = dot(named.astype(F32).astype(BF16), before)
        slots = jnp.where(named, slots, -1.0)
        counts = lax.broadcasted_iota(jnp.int32, (CAP, tokens), 0).astype(F32)
        for s in range(owners):
            chosen = counts == slots[s : s + 1]
            onehot = jnp.where(chosen, 1.0, 0.0).astype(BF16)
            weight = jnp.where(chosen, table[s : s + 1], 0.0)
            high = weight.astype(BF16)
            picks[s, pl.ds(place, CAP), :] = onehot
            highs[s, pl.ds(place, CAP), :] = high
            lows[s, pl.ds(place, CAP), :] = (weight - high.astype(F32)).astype(BF16)
            gate_col[s * CAP : (s + 1) * CAP, :] = jnp.sum(weight, axis=1, keepdims=True)
            x_all[step, s * CAP : (s + 1) * CAP, :] = dot(onehot, moe_ref[s]).astype(BF16)
            g_now[s * CAP : (s + 1) * CAP, :] = dot(onehot, grad_ref[s]).astype(BF16)

        def run_tile(r, carry):
            here = pl.ds(pl.multiple_of(r * tile, tile), tile)
            part = pl.ds(r * (owners // 2), owners // 2)
            spot = pl.ds(place, CAP)
            rows_in = x_all[step, here, :]
            gate_act = dot(rows_in, wg_ref[0])
            up_act = dot(rows_in, wu_ref[0])
            sigma = jax.nn.sigmoid(gate_act)
            silu = gate_act * sigma
            hidden = (silu * up_act).astype(BF16)
            eh_all[step, here, :] = hidden
            expert_out = dot(hidden, wd_ref[0]).astype(BF16)
            eo_all[part, spot, :] = expert_out.reshape(owners // 2, CAP, width)
            grads = g_now[here, :].astype(F32)
            dot_col[here, :] = jnp.sum(grads * expert_out.astype(F32), axis=1, keepdims=True)
            grad_expert = (gate_col[here, :] * grads).astype(BF16)
            deo_all[step, here, :] = grad_expert
            grad_hidden = dot_t(grad_expert, wd_ref[0])
            slope = sigma * (1.0 + gate_act * (1.0 - sigma))
            grad_gate = (grad_hidden * up_act * slope).astype(BF16)
            grad_up = (grad_hidden * silu).astype(BF16)
            dgu_all[step, here, :hidden_width] = grad_gate
            dgu_all[step, here, hidden_width:] = grad_up
            grad_buffer = (dot_t(grad_gate, wg_ref[0]) + dot_t(grad_up, wu_ref[0])).astype(BF16)
            dbuf_all[part, spot, :] = grad_buffer.reshape(owners // 2, CAP, width)
            return carry

        lax.fori_loop(0, 2, run_tile, 0)
        for s in range(owners):
            onehot = picks[s, pl.ds(place, CAP), :].astype(F32)
            line = jnp.sum(onehot * dot_col[s * CAP : (s + 1) * CAP, :], axis=0, keepdims=True)
            dots[s, pl.ds(step, 1), :] = line

    @pl.when(step == mine - 1)
    def _():
        def combine(s, carry):
            moved = t_dot(highs[s], eo_all[s]) + t_dot(lows[s], eo_all[s])
            y_send[s] = moved.astype(BF16)
            d_send[s] = t_dot(picks[s], dbuf_all[s]).astype(BF16)
            return carry

        lax.fori_loop(0, owners, combine, 0)

    @pl.when((step >= mine) & (step < 2 * mine))
    def _():
        number = step - mine
        blocks = width // 256
        per = width // 16

        def gate_rows(j, carry):
            columns = pl.ds(pl.multiple_of(j * 256, 256), 256)
            rows_in = x_all[number, :, columns]
            for half, own, send in ((0, own_g, send_g), (1, own_u, send_u)):
                grads = dgu_all[number, :, half * hidden_width : (half + 1) * hidden_width]
                terms = t_dot(rows_in, grads).reshape(128 // per, 2, per, hidden_width)
                first, second = terms[:, 0], terms[:, 1]
                group = pl.ds(j * (128 // per), 128 // per)
                own[0, group] = jnp.where(core == 0, first, second)
                send[number, group] = jnp.where(core == 0, second, first).astype(BF16)
            return carry

        lax.fori_loop(0, blocks, gate_rows, 0)
        less = hidden_width // 16

        def down_rows(j, carry):
            columns = pl.ds(pl.multiple_of(j * 256, 256), 256)
            terms = t_dot(eh_all[number, :, columns], deo_all[number])
            terms = terms.reshape(128 // less, 2, less, width)
            first, second = terms[:, 0], terms[:, 1]
            group = pl.ds(j * (128 // less), 128 // less)
            own_d[0, group] = jnp.where(core == 0, first, second)
            send_d[number, group] = jnp.where(core == 0, second, first).astype(BF16)
            return carry

        lax.fori_loop(0, hidden_width // 256, down_rows, 0)

    @pl.when(step == 2 * mine)
    def _():
        for shift_by in range(1, owners):
            for copy in results(shift_by):
                copy.wait()
        for copy in own_results():
            copy.wait()
        pltpu.make_async_copy(y_send, y_out, sems[6].at[0]).wait()
        for number in range(mine):
            for copy in halves(number):
                copy.wait()


def run_experts(cid, sizes, moe_all, grad_all, table_all, gate_weight, up_weight, down_weight):
    owners, tokens, width = moe_all.shape
    mine, _, inner = gate_weight.shape
    rows = owners * CAP
    part, less = width // 16, inner // 16

    def fixed(array):
        return pl.BlockSpec(array.shape, lambda i: (0, 0, 0), pipeline_mode=pl.Buffered(1))

    def expert_block(array):
        return pl.BlockSpec((1, *array.shape[1:]), lambda i: (jnp.minimum(i, mine - 1), 0, 0))

    def own_block(*shape):
        return pl.BlockSpec((1, *shape), lambda i: (jnp.clip(i - mine, 0, mine - 1), 0, 0, 0))

    anywhere = pl.BlockSpec(memory_space=pl.ANY)
    wide, tall = (8, part, inner), (8, less, width)
    dma = pltpu.SemaphoreType.DMA
    return pl.pallas_call(
        functools.partial(moe_body, sizes),
        grid=(2 * mine + 1,),
        out_shape=[
            jax.ShapeDtypeStruct((mine, *wide), F32),
            jax.ShapeDtypeStruct((mine, *wide), F32),
            jax.ShapeDtypeStruct((mine, *tall), F32),
            jax.ShapeDtypeStruct((mine, *wide), BF16),
            jax.ShapeDtypeStruct((mine, *wide), BF16),
            jax.ShapeDtypeStruct((mine, *tall), BF16),
            jax.ShapeDtypeStruct((owners, tokens, width), BF16),
            jax.ShapeDtypeStruct((owners, tokens, width), BF16),
            jax.ShapeDtypeStruct((owners, 8, tokens), F32),
        ],
        in_specs=[
            fixed(moe_all),
            fixed(grad_all),
            fixed(table_all),
            expert_block(gate_weight),
            expert_block(up_weight),
            expert_block(down_weight),
        ],
        out_specs=[own_block(*wide), own_block(*wide), own_block(*tall), *([anywhere] * 6)],
        scratch_shapes=[
            pltpu.VMEM((mine, rows, width), BF16),
            pltpu.VMEM((rows, width), BF16),
            pltpu.VMEM((mine, rows, width), BF16),
            pltpu.VMEM((mine, rows, 2 * inner), BF16),
            pltpu.VMEM((mine, rows, inner), BF16),
            pltpu.VMEM((owners, mine * CAP, width), BF16),
            pltpu.VMEM((owners, mine * CAP, width), BF16),
            pltpu.VMEM((owners, mine * CAP, tokens), BF16),
            pltpu.VMEM((owners, mine * CAP, tokens), BF16),
            pltpu.VMEM((owners, mine * CAP, tokens), BF16),
            pltpu.VMEM((rows, 1), F32),
            pltpu.VMEM((rows, 1), F32),
            pltpu.VMEM((owners, 8, tokens), F32),
            pltpu.VMEM((owners, tokens, width), BF16),
            pltpu.VMEM((owners, tokens, width), BF16),
            pltpu.VMEM((mine, *wide), BF16),
            pltpu.VMEM((mine, *wide), BF16),
            pltpu.VMEM((mine, *tall), BF16),
            dma((owners,)),
            dma((owners,)),
            dma((owners,)),
            dma((owners,)),
            dma((3 * mine,)),
            dma((3 * mine,)),
            dma((1,)),
        ],
        name="run_experts",
        compiler_params=pltpu.CompilerParams(
            collective_id=cid, has_side_effects=True, vmem_limit_bytes=67_043_328
        ),
    )(moe_all, grad_all, table_all, gate_weight, up_weight, down_weight)


def rope_tables(positions, head_size):
    half_dim = head_size // 2
    frequency = ROPE_BASE ** (-2.0 * jnp.arange(half_dim, dtype=F32) / head_size)
    angles = positions.astype(F32)[:, None] * frequency[None, :]
    angles = jnp.concatenate([angles, angles], axis=1)
    return (jnp.cos(angles), jnp.sin(angles))


def rotate(values, cosine, sine_table):
    half_dim = values.shape[-1] // 2
    turned = jnp.concatenate([-values[..., half_dim:], values[..., :half_dim]], axis=-1)
    return values * cosine[:, None, :] + turned * sine_table[:, None, :]


def rotate_back(grads, cosine, sine_table):
    half_dim = grads.shape[-1] // 2
    scaled = grads * sine_table[:, None, :]
    turned = jnp.concatenate([scaled[..., half_dim:], -scaled[..., :half_dim]], axis=-1)
    return grads * cosine[:, None, :] + turned


def norm_forward(values, gain_vec):
    inverse = lax.rsqrt(jnp.mean(values * values, axis=-1, keepdims=True) + EPSILON)
    normed = values * inverse
    return (inverse, normed, (normed * gain_vec).astype(BF16))


def norm_backward(grad_out, normed, inverse, gain_vec):
    gain_grad = jnp.sum(grad_out * normed, axis=0)
    scaled = grad_out * gain_vec
    inner = jnp.mean(scaled * normed, axis=-1, keepdims=True)
    return (gain_grad, inverse * (scaled - normed * inner))


def sum_others(received, own, index):
    numbers = jnp.arange(received.shape[0]).reshape(-1, *([1] * own.ndim))
    return own + jnp.sum(jnp.where(numbers == index, 0.0, received.astype(F32)), axis=0)


def own_part(array, index):
    return lax.dynamic_index_in_dim(array, index, 0, keepdims=False)


def local(
    sizes,
    inputs,
    prenorm_gain,
    query_weight,
    key_weight,
    value_weight,
    output_weight,
    midnorm_gain,
    router_weight,
    gate_weight,
    up_weight,
    down_weight,
    expert_ids,
    cotangent,
):
    tokens, width = inputs.shape[1:]
    owners = sizes["expert"]
    mine = gate_weight.shape[0]
    context, owner = lax.axis_index("context"), lax.axis_index("expert")
    block = context * owners + owner
    positions = block * tokens + jnp.arange(tokens, dtype=jnp.int32)
    cosine, sine_table = rope_tables(positions, HEAD_DIM)

    input_float = inputs[0].astype(F32)
    inverse_first, normed_first, attn_input = norm_forward(input_float, prenorm_gain)
    query_raw = dot(attn_input, query_weight).reshape(tokens, HEADS, HEAD_DIM)
    key_raw = dot(attn_input, key_weight).reshape(tokens, KV_HEADS, HEAD_DIM)
    value_raw = dot(attn_input, value_weight).reshape(tokens, KV_HEADS, HEAD_DIM)
    query_rot = rotate(query_raw, cosine, sine_table).astype(BF16)
    key_rot = rotate(key_raw, cosine, sine_table).astype(BF16)
    query_send = query_rot.reshape(tokens, KV_HEADS, 2 * HEAD_DIM).transpose(1, 0, 2)
    kv_send = jnp.concatenate([key_rot, value_raw.astype(BF16)], axis=2).transpose(1, 0, 2)
    kv_all, queries = exchange(
        0, sizes, "send_qkv", (kv_send, SEQ_AXES, pick_context), (query_send, ("context",), pick_target)
    )
    kv_all = kv_all.reshape(-1, 2 * HEAD_DIM)
    columns = 2 * tokens
    grad_all, mixtures, sums = exchange(
        7,
        sizes,
        "attention_forward",
        (cotangent[0], ("expert",), pick_whole),
        compute=attention_forward,
        data=(queries, kv_all),
        results=(
            jax.ShapeDtypeStruct(queries.shape, BF16),
            jax.ShapeDtypeStruct((KV_HEADS, 1, columns), F32),
        ),
        scratch=(pltpu.VMEM((kv_all.shape[0], columns), F32),),
    )
    (mixture,) = exchange(1, sizes, "send_mixture", (mixtures, ("context",), pick_target))
    mixture_flat = mixture.transpose(1, 0, 2).reshape(tokens, HEADS * HEAD_DIM)

    after_attn = input_float + dot(mixture_flat, output_weight)
    inverse_second, normed_second, moe_input = norm_forward(after_attn, midnorm_gain)
    logits = lax.dot_general(
        router_weight, moe_input, (((0,), (1,)), ((), ())), preferred_element_type=F32
    )
    numbers = jnp.arange(EXPERTS, dtype=jnp.int32)[:, None, None]
    chosen = jnp.any(expert_ids[0].T[None] == numbers, axis=1)
    masked = jnp.where(chosen, logits, -jnp.inf)
    powers = jnp.exp(masked - jnp.max(masked, axis=0, keepdims=True))
    gates = powers / jnp.sum(powers, axis=0, keepdims=True)
    gate_table = jnp.where(chosen, gates, -1.0)

    moe_all, table_all = exchange(
        2, sizes, "send_tokens", (moe_input, ("expert",), pick_whole), (gate_table, ("expert",), pick_whole)
    )
    own_g, own_u, own_d, other_g, other_u, other_d, moe_terms, grad_back, dot_back = run_experts(
        3, sizes, moe_all, grad_all, table_all, gate_weight, up_weight, down_weight
    )
    dp, side = lax.axis_index("dp"), context // 2

    def chip_sum(own, other):
        held = own + other.astype(F32)
        return held.reshape(mine, sizes["dp"], 2, *held.shape[2:])

    held_g = chip_sum(own_g, other_g).transpose(1, 0, 2, 3, 4)
    held_u = chip_sum(own_u, other_u).transpose(1, 0, 2, 3, 4)
    held_d = chip_sum(own_d, other_d).transpose(2, 0, 1, 3, 4)
    grad_gates = dot_back[:, :mine].reshape(EXPERTS, tokens)
    grad_logits = gates * (grad_gates - jnp.sum(gates * grad_gates, axis=0, keepdims=True))
    router_grad = jnp.einsum(
        "td,et->de", moe_input.astype(F32), grad_logits, precision=lax.Precision.HIGHEST
    )
    grad_moe_in = jnp.sum(grad_back.astype(F32), axis=0) + jnp.einsum(
        "et,de->td", grad_logits, router_weight.astype(F32), precision=lax.Precision.HIGHEST
    )
    grad_out = cotangent[0].astype(F32)
    midnorm_grad, grad_after = norm_backward(grad_moe_in, normed_second, inverse_second, midnorm_gain)
    grad_after = grad_out + grad_after
    grad_after_half = grad_after.astype(BF16)
    output_grad = t_dot(mixture_flat, grad_after_half)
    grad_mix = dot_t(grad_after_half, output_weight).astype(BF16)
    grad_mix = grad_mix.reshape(tokens, KV_HEADS, 2 * HEAD_DIM).transpose(1, 0, 2)
    (grad_mixtures,) = exchange(4, sizes, "send_grad_mixture", (grad_mix, ("context",), pick_target))
    got_g, got_u, got_d, moe_back, grad_queries, kv_terms = exchange(
        8,
        sizes,
        "attention_backward",
        (held_g.astype(BF16), ("dp",), pick_target, True),
        (held_u.astype(BF16), ("dp",), pick_target, True),
        (held_d.astype(BF16), ("side",), pick_target, True),
        (moe_terms, ("expert",), pick_target),
        compute=attention_backward,
        data=(queries, kv_all, mixtures, grad_mixtures, sums),
        results=(
            jax.ShapeDtypeStruct(queries.shape, F32),
            jax.ShapeDtypeStruct(kv_all.shape, BF16),
        ),
        scratch=(pltpu.VMEM(kv_all.shape, F32),),
    )
    outputs = (after_attn + jnp.sum(moe_back.astype(F32), axis=0)).astype(BF16)
    half_g = sum_others(got_g, own_part(held_g, dp), dp).transpose(1, 0, 2, 3)
    half_u = sum_others(got_u, own_part(held_u, dp), dp).transpose(1, 0, 2, 3)
    half_d = sum_others(got_d, own_part(held_d, side), side).transpose(1, 0, 2, 3)
    kv_terms = kv_terms.reshape(-1, tokens, 2 * HEAD_DIM)
    output_grad, narrow = lax.psum(
        (output_grad, jnp.concatenate([router_grad, midnorm_grad[:, None]], axis=1)), EVERY
    )
    kv_terms, output_grad, narrow = lax.optimization_barrier((kv_terms, output_grad, narrow))
    kv_back, grad_query, got_g, got_u, got_d = exchange(
        5,
        sizes,
        "send_grad_qkv",
        (kv_terms, SEQ_AXES, pick_target),
        (grad_queries, ("context",), pick_target),
        (half_g.astype(BF16), ("side",), pick_target, True),
        (half_u.astype(BF16), ("side",), pick_target, True),
        (half_d.astype(BF16), ("dp",), pick_target, True),
    )
    gate_sum = sum_others(got_g, own_part(half_g, side), side)
    up_sum = sum_others(got_u, own_part(half_u, side), side)
    down_sum = sum_others(got_d, own_part(half_d, dp), dp)
    grad_kv = jnp.sum(kv_back.astype(F32).reshape(KV_HEADS, owners, tokens, 2 * HEAD_DIM), axis=1)
    grad_kv = grad_kv.transpose(1, 0, 2)
    grad_query = grad_query.transpose(1, 0, 2).reshape(tokens, HEADS, HEAD_DIM)
    query_back = rotate_back(grad_query, cosine, sine_table).reshape(tokens, -1).astype(BF16)
    key_back = rotate_back(grad_kv[..., :HEAD_DIM], cosine, sine_table).reshape(tokens, -1).astype(BF16)
    value_back = grad_kv[..., HEAD_DIM:].reshape(tokens, -1).astype(BF16)
    query_grad = t_dot(attn_input, query_back)
    key_grad = t_dot(attn_input, key_back)
    value_grad = t_dot(attn_input, value_back)
    grad_attn_in = (
        dot_t(query_back, query_weight) + dot_t(key_back, key_weight) + dot_t(value_back, value_weight)
    )
    prenorm_grad, grad_inputs = norm_backward(grad_attn_in, normed_first, inverse_first, prenorm_gain)
    grad_inputs = grad_after + grad_inputs
    query_grad, key_grad, value_grad, prenorm_grad = lax.psum(
        (query_grad, key_grad, value_grad, jnp.pad(prenorm_grad[:, None], ((0, 0), (0, EXPERTS)))), EVERY
    )
    dense = (
        prenorm_grad[:, 0],
        query_grad,
        key_grad,
        value_grad,
        output_grad,
        narrow[:, EXPERTS],
        narrow[:, :EXPERTS],
    )
    return (outputs[None], grad_inputs[None], *dense, gate_sum, up_sum, down_sum)


def solution(mesh):
    split = P("dp", ("context", "expert"), None)
    owned = P("expert", None, None)
    summed = P("expert", ("dp", "context"), None)
    in_specs = (split, *([P()] * 7), owned, owned, owned, split, split)
    out_specs = (split, split, *([P()] * 7), summed, summed, summed)
    return jax.shard_map(
        functools.partial(local, dict(mesh.shape)),
        mesh=mesh,
        in_specs=in_specs,
        out_specs=out_specs,
        check_vma=False,
    )
```

```python
import functools

import jax
import jax.numpy as jnp
from jax import lax
from jax.experimental import pallas as pl
from jax.experimental.pallas import tpu as pltpu
from jax.sharding import PartitionSpec as P

HEADS = 8
KV_HEADS = 4
HEAD_DIM = 64
EXPERTS = 32
TOP = 8
CAP = 64
EPSILON = 1e-06
ROPE_BASE = 10000.0
F32 = jnp.float32
BF16 = jnp.bfloat16
MESH_ID = pl.DeviceIdType.MESH
SEQ_AXES = ("context", "expert")


def dot(left, right):
    return jnp.dot(left, right, preferred_element_type=F32)


def dot_t(left, right):
    return lax.dot_general(left, right, (((1,), (1,)), ((), ())), preferred_element_type=F32)


def t_dot(left, right):
    return lax.dot_general(left, right, (((0,), (0,)), ((), ())), preferred_element_type=F32)


def axis_size(sizes, name):
    return 2 if name == "side" else sizes[name]


def group_size(axes, sizes):
    total = 1
    for name in axes:
        total *= axis_size(sizes, name)
    return total


def own_index(axes, sizes):
    index = 0
    for name in axes:
        own = lax.axis_index("context") // 2 if name == "side" else lax.axis_index(name)
        index = index * axis_size(sizes, name) + own
    return index


def coords_of(axes, sizes, index):
    out = {}
    for name in reversed(axes):
        place = lax.rem(index, axis_size(sizes, name))
        if name == "side":
            out["context"] = place * 2 + lax.rem(lax.axis_index("context"), 2)
        else:
            out[name] = place
        index = index // axis_size(sizes, name)
    return out


def pick_whole(ref, target, peer):
    return ref


def pick_target(ref, target, peer):
    return ref.at[target]


def pick_context(ref, target, peer):
    return ref.at[peer["context"]]


def exchange_body(items, sizes, compute, more_ins, more_outs, *refs):
    count = len(items)
    ins, refs = refs[:count], refs[count:]
    data_ins, refs = refs[:more_ins], refs[more_ins:]
    outs, refs = refs[:count], refs[count:]
    data_outs, refs = refs[:more_outs], refs[more_outs:]
    sems, scratch = refs[: 2 * count], refs[2 * count :]

    barrier = pltpu.get_barrier_semaphore()
    groups = []
    for axes, _, _ in items:
        if not any(set(axes) <= set(other) for other in groups):
            groups = [other for other in groups if not set(other) <= set(axes)] + [axes]
    signals = 0
    for axes in groups:
        me, total = own_index(axes, sizes), group_size(axes, sizes)
        for step in range(1, total):
            peer = coords_of(axes, sizes, lax.rem(me + step, total))
            pl.semaphore_signal(barrier, inc=1, device_id=peer, device_id_type=MESH_ID)
        signals += total - 1
    pl.semaphore_wait(barrier, signals)

    waits = []
    for number, (axes, pick, keep) in enumerate(items):
        me, total = own_index(axes, sizes), group_size(axes, sizes)
        send, recv = sems[2 * number], sems[2 * number + 1]
        for step in range(1, total):
            target = lax.rem(me + step, total)
            peer = coords_of(axes, sizes, target)
            copy = pltpu.make_async_remote_copy(
                src_ref=pick(ins[number], target, peer),
                dst_ref=outs[number].at[me],
                send_sem=send.at[step],
                recv_sem=recv.at[step],
                device_id=peer,
                device_id_type=MESH_ID,
            )
            copy.start()
            waits.append(copy)
        if keep:
            own = pltpu.make_async_copy(
                pick(ins[number], me, coords_of(axes, sizes, me)), outs[number].at[me], send.at[0]
            )
            own.start()
            waits.append(own)
    if compute is not None:
        compute(data_ins, data_outs, scratch)
    for copy in waits:
        copy.wait()


def exchange(cid, sizes, name, *specs, compute=None, data=(), results=(), scratch=(), cost=None):
    vmem, hbm = pl.BlockSpec(memory_space=pltpu.VMEM), pl.BlockSpec(memory_space=pl.ANY)
    items, shapes, spaces, sems = [], [], [], []
    for array, axes, pick, *large in specs:
        total = group_size(axes, sizes)
        chunk = array.shape if pick is pick_whole else array.shape[1:]
        shapes.append(jax.ShapeDtypeStruct((total, *chunk), array.dtype))
        spaces.append(hbm if large else vmem)
        items.append((axes, pick, not large))
        sems += [pltpu.SemaphoreType.DMA((total,)), pltpu.SemaphoreType.DMA((total,))]
    return pl.pallas_call(
        functools.partial(exchange_body, items, sizes, compute, len(data), len(results)),
        out_shape=[*shapes, *results],
        in_specs=[*spaces, *([vmem] * len(data))],
        out_specs=[*spaces, *([vmem] * len(results))],
        scratch_shapes=[*sems, *scratch],
        name=name,
        compiler_params=pltpu.CompilerParams(
            collective_id=cid, has_side_effects=True, vmem_limit_bytes=60_000_000
        ),
    )(*[spec[0] for spec in specs], *data)


def stack_heads(block, low):
    tokens = block.shape[0]
    zero = jnp.zeros((tokens, HEAD_DIM), block.dtype)
    parts = [block[:, :HEAD_DIM], block[:, HEAD_DIM:]]
    return jnp.concatenate(
        [jnp.concatenate([part, zero] if low else [zero, part], axis=1) for part in parts], axis=0
    )


def causal(shape, tokens):
    keys = lax.broadcasted_iota(jnp.int32, shape, 0)
    queries = lax.rem(lax.broadcasted_iota(jnp.int32, shape, 1), tokens)
    return keys - queries <= lax.axis_index("expert") * tokens


def identity(size):
    shape = (size, size)
    return lax.broadcasted_iota(jnp.int32, shape, 0) == lax.broadcasted_iota(jnp.int32, shape, 1)


def attention_forward(data, results, scratch):
    query_ref, kv_ref = data
    out_ref, sum_ref = results
    (score_ref,) = scratch
    blocks, tokens = query_ref.shape[:2]
    chunk, columns = 8 * tokens, 2 * tokens

    def block(number, carry):
        rows = stack_heads(query_ref[number], True) * (HEAD_DIM ** (-0.5))
        rows = rows.astype(BF16)

        def keys_of(j):
            return pl.ds(pl.multiple_of(j * chunk, chunk), chunk)

        def first(j, top):
            scores = dot_t(kv_ref[keys_of(j), :], rows)
            score_ref[keys_of(j), :] = scores
            return jnp.maximum(top, jnp.max(scores, axis=0, keepdims=True))

        top = lax.fori_loop(0, number, first, jnp.full((1, columns), -jnp.inf, F32))
        scores = dot_t(kv_ref[keys_of(number), :], rows)
        scores = jnp.where(causal(scores.shape, tokens), scores, -jnp.inf)
        score_ref[keys_of(number), :] = scores
        top = jnp.maximum(top, jnp.max(scores, axis=0, keepdims=True))

        def second(j, held):
            total, mixed = held
            powers = jnp.exp(score_ref[keys_of(j), :] - top)
            total = total + jnp.sum(powers, axis=0, keepdims=True)
            return total, mixed + t_dot(powers.astype(BF16), kv_ref[keys_of(j), :])

        start = (jnp.zeros((1, columns), F32), jnp.zeros((columns, 2 * HEAD_DIM), F32))
        total, mixed = lax.fori_loop(0, number + 1, second, start)
        sum_ref[number] = top + jnp.log(total)
        inverse = jnp.sum(jnp.where(identity(columns), 1.0 / total, 0.0), axis=1, keepdims=True)
        mixed = (mixed * inverse)[:, HEAD_DIM:]
        out_ref[number] = jnp.concatenate([mixed[:tokens], mixed[tokens:]], axis=1).astype(BF16)
        return carry

    lax.fori_loop(0, blocks, block, 0)


def attention_backward(data, results, scratch):
    query_ref, kv_ref, mix_ref, grad_ref, sum_ref = data
    grad_query_ref, terms_ref = results
    (sum_kv,) = scratch
    blocks, tokens = query_ref.shape[:2]
    chunk, columns = 8 * tokens, 2 * tokens
    factor = HEAD_DIM ** (-0.5)
    sum_kv[...] = jnp.zeros_like(sum_kv)

    def block(number, carry):
        rows = (stack_heads(query_ref[number], True) * factor).astype(BF16)
        grads = stack_heads(grad_ref[number], False)
        both = jnp.concatenate([rows, grads], axis=0)
        pairs = dot_t(stack_heads(mix_ref[number], False), grads)
        delta = jnp.sum(jnp.where(identity(columns), pairs, 0.0), axis=0, keepdims=True)
        logsum = sum_ref[number]

        def unit(j, total, masked):
            keys = pl.ds(pl.multiple_of(j * chunk, chunk), chunk)
            kv = kv_ref[keys, :]
            products = dot_t(kv, both)
            soft = jnp.exp(products[:, :columns] - logsum)
            if masked:
                soft = jnp.where(causal(soft.shape, tokens), soft, 0.0)
            scores = (soft * (products[:, columns:] - delta)).astype(BF16)
            sum_kv[keys, :] += dot(jnp.concatenate([scores, soft.astype(BF16)], axis=1), both)
            return total + t_dot(scores, kv)

        total = lax.fori_loop(
            0, number, lambda j, held: unit(j, held, False), jnp.zeros((columns, 2 * HEAD_DIM), F32)
        )
        total = unit(number, total, True)[:, :HEAD_DIM] * factor
        grad_query_ref[number] = jnp.concatenate([total[:tokens], total[tokens:]], axis=1)
        return carry

    lax.fori_loop(0, blocks, block, 0)
    terms_ref[...] = sum_kv[...].astype(BF16)


def moe_copies(sizes, refs):
    d_send, d_back, dots, dot_back, g_sends, g_backs, sems = refs
    owners = sizes["expert"]
    owner, context = lax.axis_index("expert"), lax.axis_index("context")

    def results(step):
        target = lax.rem(owner + step, owners)
        pairs = ((d_send, d_back, sems[0], sems[1]), (dots, dot_back, sems[2], sems[3]))
        return [
            pltpu.make_async_remote_copy(
                src_ref=src.at[target],
                dst_ref=dst.at[owner],
                send_sem=send.at[step],
                recv_sem=recv.at[step],
                device_id={"expert": target},
                device_id_type=MESH_ID,
            )
            for src, dst, send, recv in pairs
        ]

    def own_results():
        return [
            pltpu.make_async_copy(d_send.at[owner], d_back.at[owner], sems[0].at[0]),
            pltpu.make_async_copy(dots.at[owner], dot_back.at[owner], sems[2].at[0]),
        ]

    def halves(number):
        partner = context + 1 - 2 * lax.rem(context, 2)
        return [
            pltpu.make_async_remote_copy(
                src_ref=g_sends[i].at[number],
                dst_ref=g_backs[i].at[number],
                send_sem=sems[4].at[3 * number + i],
                recv_sem=sems[5].at[3 * number + i],
                device_id={"context": partner},
                device_id_type=MESH_ID,
            )
            for i in range(3)
        ]

    return results, own_results, halves


def moe_body(
    sizes,
    moe_ref,
    grad_ref,
    table_ref,
    wg_ref,
    wu_ref,
    wd_ref,
    own_g,
    own_u,
    own_d,
    back_g,
    back_u,
    back_d,
    y_out,
    d_back,
    dot_back,
    x_all,
    g_now,
    deo_all,
    dgu_all,
    eh_all,
    eo_all,
    dbuf_all,
    picks,
    highs,
    lows,
    gate_col,
    dot_col,
    dots,
    y_send,
    d_send,
    send_g,
    send_u,
    send_d,
    *sems,
):
    step = pl.program_id(0)
    owners = sizes["expert"]
    owner, context = lax.axis_index("expert"), lax.axis_index("context")
    core = lax.rem(context, 2)
    mine = 4
    tokens, width = moe_ref.shape[1:]
    hidden_width = wg_ref.shape[2]
    rows = owners * CAP
    tile = rows // 2
    barrier = pltpu.get_barrier_semaphore()
    results, own_results, halves = moe_copies(
        sizes, (d_send, d_back, dots, dot_back, (send_g, send_u, send_d), (back_g, back_u, back_d), sems)
    )

    @pl.when(step == 0)
    def _():
        for shift_by in range(1, owners):
            pl.semaphore_signal(
                barrier,
                inc=1,
                device_id={"expert": lax.rem(owner + shift_by, owners)},
                device_id_type=MESH_ID,
            )
        pl.semaphore_signal(
            barrier, inc=1, device_id={"context": context + 1 - 2 * core}, device_id_type=MESH_ID
        )
        dots[...] = jnp.zeros_like(dots)

    @pl.when(step == 4)
    def _():
        pl.semaphore_wait(barrier, owners)
        for shift_by in range(1, owners):
            for copy in results(shift_by):
                copy.start()
        for copy in own_results():
            copy.start()
        pltpu.make_async_copy(y_send, y_out, sems[6].at[0]).start()

    for number in range(mine):

        @pl.when(step == 5 + number)
        def _(number=number):
            for copy in halves(number):
                copy.start()

    @pl.when(step < mine)
    def _():
        place = pl.multiple_of(step * CAP, CAP)
        table = jnp.concatenate(
            [table_ref[s, pl.ds(owner * mine + step, 1), :] for s in range(owners)], axis=0
        )
        named = table >= 0.0
        above = lax.broadcasted_iota(jnp.int32, (tokens, tokens), 0)
        beside = lax.broadcasted_iota(jnp.int32, (tokens, tokens), 1)
        before = (above < beside).astype(F32).astype(BF16)
        slots = dot(named.astype(F32).astype(BF16), before)
        slots = jnp.where(named, slots, -1.0)
        counts = lax.broadcasted_iota(jnp.int32, (CAP, tokens), 0).astype(F32)
        for s in range(owners):
            chosen = counts == slots[s : s + 1]
            onehot = jnp.where(chosen, 1.0, 0.0).astype(BF16)
            weight = jnp.where(chosen, table[s : s + 1], 0.0)
            high = weight.astype(BF16)
            picks[s, pl.ds(place, CAP), :] = onehot
            highs[s, pl.ds(place, CAP), :] = high
            lows[s, pl.ds(place, CAP), :] = (weight - high.astype(F32)).astype(BF16)
            gate_col[s * CAP : (s + 1) * CAP, :] = jnp.sum(weight, axis=1, keepdims=True)
            x_all[step, s * CAP : (s + 1) * CAP, :] = dot(onehot, moe_ref[s]).astype(BF16)
            g_now[s * CAP : (s + 1) * CAP, :] = dot(onehot, grad_ref[s]).astype(BF16)

        def run_tile(r, carry):
            here = pl.ds(pl.multiple_of(r * tile, tile), tile)
            part = pl.ds(r * (owners // 2), owners // 2)
            spot = pl.ds(place, CAP)
            rows_in = x_all[step, here, :]
            gate_act = dot(rows_in, wg_ref[0])
            up_act = dot(rows_in, wu_ref[0])
            sigma = jax.nn.sigmoid(gate_act)
            silu = gate_act * sigma
            hidden = (silu * up_act).astype(BF16)
            eh_all[step, here, :] = hidden
            expert_out = dot(hidden, wd_ref[0]).astype(BF16)
            eo_all[part, spot, :] = expert_out.reshape(owners // 2, CAP, width)
            grads = g_now[here, :].astype(F32)
            dot_col[here, :] = jnp.sum(grads * expert_out.astype(F32), axis=1, keepdims=True)
            grad_expert = (gate_col[here, :] * grads).astype(BF16)
            deo_all[step, here, :] = grad_expert
            grad_hidden = dot_t(grad_expert, wd_ref[0])
            slope = sigma * (1.0 + gate_act * (1.0 - sigma))
            grad_gate = (grad_hidden * up_act * slope).astype(BF16)
            grad_up = (grad_hidden * silu).astype(BF16)
            dgu_all[step, here, :hidden_width] = grad_gate
            dgu_all[step, here, hidden_width:] = grad_up
            grad_buffer = (dot_t(grad_gate, wg_ref[0]) + dot_t(grad_up, wu_ref[0])).astype(BF16)
            dbuf_all[part, spot, :] = grad_buffer.reshape(owners // 2, CAP, width)
            return carry

        lax.fori_loop(0, 2, run_tile, 0)
        for s in range(owners):
            onehot = picks[s, pl.ds(place, CAP), :].astype(F32)
            line = jnp.sum(onehot * dot_col[s * CAP : (s + 1) * CAP, :], axis=0, keepdims=True)
            dots[s, pl.ds(step, 1), :] = line

    @pl.when(step == mine - 1)
    def _():
        def combine(s, carry):
            moved = t_dot(highs[s], eo_all[s]) + t_dot(lows[s], eo_all[s])
            y_send[s] = moved.astype(BF16)
            d_send[s] = t_dot(picks[s], dbuf_all[s]).astype(BF16)
            return carry

        lax.fori_loop(0, owners, combine, 0)

    @pl.when((step >= mine) & (step < 2 * mine))
    def _():
        number = step - mine
        blocks = width // 256
        per = width // 16

        def gate_rows(j, carry):
            columns = pl.ds(pl.multiple_of(j * 256, 256), 256)
            rows_in = x_all[number, :, columns]
            for half, own, send in ((0, own_g, send_g), (1, own_u, send_u)):
                grads = dgu_all[number, :, half * hidden_width : (half + 1) * hidden_width]
                terms = t_dot(rows_in, grads).reshape(128 // per, 2, per, hidden_width)
                first, second = terms[:, 0], terms[:, 1]
                group = pl.ds(j * (128 // per), 128 // per)
                own[0, group] = jnp.where(core == 0, first, second)
                send[number, group] = jnp.where(core == 0, second, first).astype(BF16)
            return carry

        lax.fori_loop(0, blocks, gate_rows, 0)
        less = hidden_width // 16

        def down_rows(j, carry):
            columns = pl.ds(pl.multiple_of(j * 256, 256), 256)
            terms = t_dot(eh_all[number, :, columns], deo_all[number])
            terms = terms.reshape(128 // less, 2, less, width)
            first, second = terms[:, 0], terms[:, 1]
            group = pl.ds(j * (128 // less), 128 // less)
            own_d[0, group] = jnp.where(core == 0, first, second)
            send_d[number, group] = jnp.where(core == 0, second, first).astype(BF16)
            return carry

        lax.fori_loop(0, hidden_width // 256, down_rows, 0)

    @pl.when(step == 2 * mine)
    def _():
        for shift_by in range(1, owners):
            for copy in results(shift_by):
                copy.wait()
        for copy in own_results():
            copy.wait()
        pltpu.make_async_copy(y_send, y_out, sems[6].at[0]).wait()
        for number in range(mine):
            for copy in halves(number):
                copy.wait()


def run_experts(cid, sizes, moe_all, grad_all, table_all, gate_weight, up_weight, down_weight):
    owners, tokens, width = moe_all.shape
    mine, _, inner = gate_weight.shape
    rows = owners * CAP
    part, less = width // 16, inner // 16

    def fixed(array):
        return pl.BlockSpec(array.shape, lambda i: (0, 0, 0), pipeline_mode=pl.Buffered(1))

    def expert_block(array):
        return pl.BlockSpec((1, *array.shape[1:]), lambda i: (jnp.minimum(i, mine - 1), 0, 0))

    def own_block(*shape):
        return pl.BlockSpec((1, *shape), lambda i: (jnp.clip(i - mine, 0, mine - 1), 0, 0, 0))

    anywhere = pl.BlockSpec(memory_space=pl.ANY)
    wide, tall = (8, part, inner), (8, less, width)
    dma = pltpu.SemaphoreType.DMA
    return pl.pallas_call(
        functools.partial(moe_body, sizes),
        grid=(2 * mine + 1,),
        out_shape=[
            jax.ShapeDtypeStruct((mine, *wide), F32),
            jax.ShapeDtypeStruct((mine, *wide), F32),
            jax.ShapeDtypeStruct((mine, *tall), F32),
            jax.ShapeDtypeStruct((mine, *wide), BF16),
            jax.ShapeDtypeStruct((mine, *wide), BF16),
            jax.ShapeDtypeStruct((mine, *tall), BF16),
            jax.ShapeDtypeStruct((owners, tokens, width), BF16),
            jax.ShapeDtypeStruct((owners, tokens, width), BF16),
            jax.ShapeDtypeStruct((owners, 8, tokens), F32),
        ],
        in_specs=[
            fixed(moe_all),
            fixed(grad_all),
            fixed(table_all),
            expert_block(gate_weight),
            expert_block(up_weight),
            expert_block(down_weight),
        ],
        out_specs=[own_block(*wide), own_block(*wide), own_block(*tall), *([anywhere] * 6)],
        scratch_shapes=[
            pltpu.VMEM((mine, rows, width), BF16),
            pltpu.VMEM((rows, width), BF16),
            pltpu.VMEM((mine, rows, width), BF16),
            pltpu.VMEM((mine, rows, 2 * inner), BF16),
            pltpu.VMEM((mine, rows, inner), BF16),
            pltpu.VMEM((owners, mine * CAP, width), BF16),
            pltpu.VMEM((owners, mine * CAP, width), BF16),
            pltpu.VMEM((owners, mine * CAP, tokens), BF16),
            pltpu.VMEM((owners, mine * CAP, tokens), BF16),
            pltpu.VMEM((owners, mine * CAP, tokens), BF16),
            pltpu.VMEM((rows, 1), F32),
            pltpu.VMEM((rows, 1), F32),
            pltpu.VMEM((owners, 8, tokens), F32),
            pltpu.VMEM((owners, tokens, width), BF16),
            pltpu.VMEM((owners, tokens, width), BF16),
            pltpu.VMEM((mine, *wide), BF16),
            pltpu.VMEM((mine, *wide), BF16),
            pltpu.VMEM((mine, *tall), BF16),
            dma((owners,)),
            dma((owners,)),
            dma((owners,)),
            dma((owners,)),
            dma((3 * mine,)),
            dma((3 * mine,)),
            dma((1,)),
        ],
        name="run_experts",
        compiler_params=pltpu.CompilerParams(
            collective_id=cid, has_side_effects=True, vmem_limit_bytes=67_043_328
        ),
    )(moe_all, grad_all, table_all, gate_weight, up_weight, down_weight)


CHIP_AXES = ("dp", "side", "expert")


def sum_body(sizes, load_ref, out_ref, near, sums, got, *sems):
    near_sems, send_sems, recv_sems, give_sems, take_sems, pass_sems, land_sems = sems
    core = lax.rem(lax.axis_index("context"), 2)
    partner = {"context": lax.axis_index("context") + 1 - 2 * core}
    me, total = own_index(CHIP_AXES, sizes), group_size(CHIP_AXES, sizes)

    def place(step):
        target = lax.rem(me + step, total)
        return target, coords_of(CHIP_AXES, sizes, target)

    def remote(src, dst, send, recv, peer):
        return pltpu.make_async_remote_copy(
            src_ref=src, dst_ref=dst, send_sem=send, recv_sem=recv, device_id=peer, device_id_type=MESH_ID
        )

    def reduce_copy(step):
        target, peer = place(step)
        return remote(sums.at[target], got.at[me], send_sems.at[step], recv_sems.at[step], peer)

    def gather_copy(step):
        _, peer = place(step)
        own = out_ref.at[core, me]
        return remote(own, own, give_sems.at[step], take_sems.at[step], peer)

    def pass_copy(step):
        source = out_ref.at[core, lax.rem(me - step + total, total)]
        return remote(source, source, pass_sems.at[step], land_sems.at[step], partner)

    def each(start, body):
        def run(step, carry):
            body(step)
            return carry

        lax.fori_loop(start, total, run, 0)

    barrier = pltpu.get_barrier_semaphore()
    pl.semaphore_signal(barrier, inc=1, device_id=partner, device_id_type=MESH_ID)
    each(
        1,
        lambda step: pl.semaphore_signal(
            barrier, inc=1, device_id=place(step)[1], device_id_type=MESH_ID
        ),
    )
    pl.semaphore_wait(barrier, total)

    first = remote(load_ref.at[1 - core], near, near_sems.at[0], near_sems.at[1], partner)
    first.start()
    first.wait()

    def add(chunk):
        sums[chunk] = (load_ref[core, chunk].astype(F32) + near[chunk].astype(F32)).astype(BF16)

    each(0, add)
    got[me] = sums[me]
    each(1, lambda step: reduce_copy(step).start())
    each(1, lambda step: reduce_copy(step).wait())
    whole = lax.fori_loop(
        0, total, lambda i, held: held + got[i].astype(F32), jnp.zeros(got.shape[1:], F32)
    )
    out_ref[core, me] = whole.astype(BF16)
    each(1, lambda step: gather_copy(step).start())
    pass_copy(0).start()

    def forward(step):
        gather_copy(step).wait_recv()
        pass_copy(step).start()

    each(1, forward)
    each(1, lambda step: gather_copy(step).wait_send())
    each(0, lambda step: pass_copy(step).wait())


def sum_everywhere(cid, sizes, payload):
    total = payload.shape[1]
    half = payload.shape[1:]
    dma = pltpu.SemaphoreType.DMA
    vmem = pl.BlockSpec(memory_space=pltpu.VMEM)
    return pl.pallas_call(
        functools.partial(sum_body, sizes),
        out_shape=jax.ShapeDtypeStruct(payload.shape, payload.dtype),
        in_specs=[vmem],
        out_specs=vmem,
        scratch_shapes=[pltpu.VMEM(half, BF16)] * 3 + [dma((2,))] + [dma((total,))] * 6,
        name="sum_everywhere",
        compiler_params=pltpu.CompilerParams(collective_id=cid, has_side_effects=True),
    )(payload)


def rope_tables(positions, head_size):
    half_dim = head_size // 2
    frequency = ROPE_BASE ** (-2.0 * jnp.arange(half_dim, dtype=F32) / head_size)
    angles = positions.astype(F32)[:, None] * frequency[None, :]
    angles = jnp.concatenate([angles, angles], axis=1)
    return (jnp.cos(angles), jnp.sin(angles))


def rotate(values, cosine, sine_table):
    half_dim = values.shape[-1] // 2
    turned = jnp.concatenate([-values[..., half_dim:], values[..., :half_dim]], axis=-1)
    return values * cosine[:, None, :] + turned * sine_table[:, None, :]


def rotate_back(grads, cosine, sine_table):
    half_dim = grads.shape[-1] // 2
    scaled = grads * sine_table[:, None, :]
    turned = jnp.concatenate([scaled[..., half_dim:], -scaled[..., :half_dim]], axis=-1)
    return grads * cosine[:, None, :] + turned


def norm_forward(values, gain_vec):
    inverse = lax.rsqrt(jnp.mean(values * values, axis=-1, keepdims=True) + EPSILON)
    normed = values * inverse
    return (inverse, normed, (normed * gain_vec).astype(BF16))


def norm_backward(grad_out, normed, inverse, gain_vec):
    gain_grad = jnp.sum(grad_out * normed, axis=0)
    scaled = grad_out * gain_vec
    inner = jnp.mean(scaled * normed, axis=-1, keepdims=True)
    return (gain_grad, inverse * (scaled - normed * inner))


def sum_others(received, own, index):
    numbers = jnp.arange(received.shape[0]).reshape(-1, *([1] * own.ndim))
    return own + jnp.sum(jnp.where(numbers == index, 0.0, received.astype(F32)), axis=0)


def own_part(array, index):
    return lax.dynamic_index_in_dim(array, index, 0, keepdims=False)


def local(
    sizes,
    inputs,
    prenorm_gain,
    query_weight,
    key_weight,
    value_weight,
    output_weight,
    midnorm_gain,
    router_weight,
    gate_weight,
    up_weight,
    down_weight,
    expert_ids,
    cotangent,
):
    tokens, width = inputs.shape[1:]
    owners = sizes["expert"]
    mine = gate_weight.shape[0]
    context, owner = lax.axis_index("context"), lax.axis_index("expert")
    block = context * owners + owner
    positions = block * tokens + jnp.arange(tokens, dtype=jnp.int32)
    cosine, sine_table = rope_tables(positions, HEAD_DIM)

    input_float = inputs[0].astype(F32)
    inverse_first, normed_first, attn_input = norm_forward(input_float, prenorm_gain)
    query_raw = dot(attn_input, query_weight).reshape(tokens, HEADS, HEAD_DIM)
    key_raw = dot(attn_input, key_weight).reshape(tokens, KV_HEADS, HEAD_DIM)
    value_raw = dot(attn_input, value_weight).reshape(tokens, KV_HEADS, HEAD_DIM)
    query_rot = rotate(query_raw, cosine, sine_table).astype(BF16)
    key_rot = rotate(key_raw, cosine, sine_table).astype(BF16)
    query_send = query_rot.reshape(tokens, KV_HEADS, 2 * HEAD_DIM).transpose(1, 0, 2)
    kv_send = jnp.concatenate([key_rot, value_raw.astype(BF16)], axis=2).transpose(1, 0, 2)
    kv_all, queries = exchange(
        0, sizes, "send_qkv", (kv_send, SEQ_AXES, pick_context), (query_send, ("context",), pick_target)
    )
    kv_all = kv_all.reshape(-1, 2 * HEAD_DIM)
    columns = 2 * tokens
    grad_all, mixtures, sums = exchange(
        7,
        sizes,
        "attention_forward",
        (cotangent[0], ("expert",), pick_whole),
        compute=attention_forward,
        data=(queries, kv_all),
        results=(
            jax.ShapeDtypeStruct(queries.shape, BF16),
            jax.ShapeDtypeStruct((KV_HEADS, 1, columns), F32),
        ),
        scratch=(pltpu.VMEM((kv_all.shape[0], columns), F32),),
    )
    (mixture,) = exchange(1, sizes, "send_mixture", (mixtures, ("context",), pick_target))
    mixture_flat = mixture.transpose(1, 0, 2).reshape(tokens, HEADS * HEAD_DIM)

    after_attn = input_float + dot(mixture_flat, output_weight)
    inverse_second, normed_second, moe_input = norm_forward(after_attn, midnorm_gain)
    logits = lax.dot_general(
        router_weight, moe_input, (((0,), (1,)), ((), ())), preferred_element_type=F32
    )
    numbers = jnp.arange(EXPERTS, dtype=jnp.int32)[:, None, None]
    chosen = jnp.any(expert_ids[0].T[None] == numbers, axis=1)
    masked = jnp.where(chosen, logits, -jnp.inf)
    powers = jnp.exp(masked - jnp.max(masked, axis=0, keepdims=True))
    gates = powers / jnp.sum(powers, axis=0, keepdims=True)
    gate_table = jnp.where(chosen, gates, -1.0)

    moe_all, table_all = exchange(
        2, sizes, "send_tokens", (moe_input, ("expert",), pick_whole), (gate_table, ("expert",), pick_whole)
    )
    own_g, own_u, own_d, other_g, other_u, other_d, moe_terms, grad_back, dot_back = run_experts(
        3, sizes, moe_all, grad_all, table_all, gate_weight, up_weight, down_weight
    )
    dp, side = lax.axis_index("dp"), context // 2

    def chip_sum(own, other):
        held = own + other.astype(F32)
        return held.reshape(mine, sizes["dp"], 2, *held.shape[2:])

    held_g = chip_sum(own_g, other_g).transpose(1, 0, 2, 3, 4)
    held_u = chip_sum(own_u, other_u).transpose(1, 0, 2, 3, 4)
    held_d = chip_sum(own_d, other_d).transpose(2, 0, 1, 3, 4)
    grad_gates = dot_back[:, :mine].reshape(EXPERTS, tokens)
    grad_logits = gates * (grad_gates - jnp.sum(gates * grad_gates, axis=0, keepdims=True))
    router_grad = jnp.einsum(
        "td,et->de", moe_input.astype(F32), grad_logits, precision=lax.Precision.HIGHEST
    )
    grad_moe_in = jnp.sum(grad_back.astype(F32), axis=0) + jnp.einsum(
        "et,de->td", grad_logits, router_weight.astype(F32), precision=lax.Precision.HIGHEST
    )
    grad_out = cotangent[0].astype(F32)
    midnorm_grad, grad_after = norm_backward(grad_moe_in, normed_second, inverse_second, midnorm_gain)
    grad_after = grad_out + grad_after
    grad_after_half = grad_after.astype(BF16)
    output_grad = t_dot(grad_after_half, mixture_flat)
    grad_mix = dot_t(grad_after_half, output_weight).astype(BF16)
    grad_mix = grad_mix.reshape(tokens, KV_HEADS, 2 * HEAD_DIM).transpose(1, 0, 2)
    (grad_mixtures,) = exchange(4, sizes, "send_grad_mixture", (grad_mix, ("context",), pick_target))
    got_g, got_u, got_d, moe_back, grad_queries, kv_terms = exchange(
        8,
        sizes,
        "attention_backward",
        (held_g.astype(BF16), ("dp",), pick_target, True),
        (held_u.astype(BF16), ("dp",), pick_target, True),
        (held_d.astype(BF16), ("side",), pick_target, True),
        (moe_terms, ("expert",), pick_target),
        compute=attention_backward,
        data=(queries, kv_all, mixtures, grad_mixtures, sums),
        results=(
            jax.ShapeDtypeStruct(queries.shape, F32),
            jax.ShapeDtypeStruct(kv_all.shape, BF16),
        ),
        scratch=(pltpu.VMEM(kv_all.shape, F32),),
    )
    outputs = (after_attn + jnp.sum(moe_back.astype(F32), axis=0)).astype(BF16)
    half_g = sum_others(got_g, own_part(held_g, dp), dp).transpose(1, 0, 2, 3)
    half_u = sum_others(got_u, own_part(held_u, dp), dp).transpose(1, 0, 2, 3)
    half_d = sum_others(got_d, own_part(held_d, side), side).transpose(1, 0, 2, 3)
    kv_terms = kv_terms.reshape(-1, tokens, 2 * HEAD_DIM)
    kv_back, grad_query, got_g, got_u, got_d = exchange(
        5,
        sizes,
        "send_grad_qkv",
        (kv_terms, SEQ_AXES, pick_target),
        (grad_queries, ("context",), pick_target),
        (half_g.astype(BF16), ("side",), pick_target, True),
        (half_u.astype(BF16), ("side",), pick_target, True),
        (half_d.astype(BF16), ("dp",), pick_target, True),
    )
    gate_sum = sum_others(got_g, own_part(half_g, side), side)
    up_sum = sum_others(got_u, own_part(half_u, side), side)
    down_sum = sum_others(got_d, own_part(half_d, dp), dp)
    grad_kv = jnp.sum(kv_back.astype(F32).reshape(KV_HEADS, owners, tokens, 2 * HEAD_DIM), axis=1)
    grad_kv = grad_kv.transpose(1, 0, 2)
    grad_query = grad_query.transpose(1, 0, 2).reshape(tokens, HEADS, HEAD_DIM)
    query_back = rotate_back(grad_query, cosine, sine_table).reshape(tokens, -1).astype(BF16)
    key_back = rotate_back(grad_kv[..., :HEAD_DIM], cosine, sine_table).reshape(tokens, -1).astype(BF16)
    value_back = grad_kv[..., HEAD_DIM:].reshape(tokens, -1).astype(BF16)
    query_grad = t_dot(attn_input, query_back)
    key_grad = t_dot(attn_input, key_back)
    value_grad = t_dot(attn_input, value_back)
    grad_attn_in = (
        dot_t(query_back, query_weight) + dot_t(key_back, key_weight) + dot_t(value_back, value_weight)
    )
    prenorm_grad, grad_inputs = norm_backward(grad_attn_in, normed_first, inverse_first, prenorm_gain)
    grad_inputs = grad_after + grad_inputs
    half, part = HEADS * HEAD_DIM // 2, EXPERTS // 2
    blank = jnp.zeros((width, 128 - part - 1), F32)
    payload = jnp.stack(
        [
            jnp.concatenate(
                [query_grad, output_grad[:, :half], router_grad[:, :part], prenorm_grad[:, None], blank],
                axis=1,
            ),
            jnp.concatenate(
                [key_grad, value_grad, output_grad[:, half:], router_grad[:, part:], midnorm_grad[:, None], blank],
                axis=1,
            ),
        ]
    ).astype(BF16)
    chips = group_size(CHIP_AXES, sizes)
    summed = sum_everywhere(9, sizes, payload.reshape(2, chips, width // chips, -1))
    first, second = summed.reshape(payload.shape).astype(F32)
    columns = 2 * half
    dense = (
        first[:, columns + half + part],
        first[:, :columns],
        second[:, :half],
        second[:, half:columns],
        jnp.concatenate([first[:, columns : columns + half], second[:, columns : columns + half]], axis=1).T,
        second[:, columns + half + part],
        jnp.concatenate(
            [table[:, columns + half : columns + half + part] for table in (first, second)], axis=1
        ),
    )
    return (outputs[None], grad_inputs[None], *dense, gate_sum, up_sum, down_sum)


def solution(mesh):
    split = P("dp", ("context", "expert"), None)
    owned = P("expert", None, None)
    summed = P("expert", ("dp", "context"), None)
    in_specs = (split, *([P()] * 7), owned, owned, owned, split, split)
    out_specs = (split, split, *([P()] * 7), summed, summed, summed)
    return jax.shard_map(
        functools.partial(local, dict(mesh.shape)),
        mesh=mesh,
        in_specs=in_specs,
        out_specs=out_specs,
        check_vma=False,
    )
```

```python
import functools

import jax
import jax.numpy as jnp
from jax import lax
from jax.experimental import pallas as pl
from jax.experimental.pallas import tpu as pltpu
from jax.sharding import PartitionSpec as P

HEADS = 8
KV_HEADS = 4
HEAD_DIM = 64
EXPERTS = 32
TOP = 8
CAP = 64
EPSILON = 1e-06
ROPE_BASE = 10000.0
F32 = jnp.float32
BF16 = jnp.bfloat16
MESH_ID = pl.DeviceIdType.MESH
SEQ_AXES = ("context", "expert")


def dot(left, right):
    return jnp.dot(left, right, preferred_element_type=F32)


def dot_t(left, right):
    return lax.dot_general(left, right, (((1,), (1,)), ((), ())), preferred_element_type=F32)


def t_dot(left, right):
    return lax.dot_general(left, right, (((0,), (0,)), ((), ())), preferred_element_type=F32)


def axis_size(sizes, name):
    return 2 if name == "side" else sizes[name]


def group_size(axes, sizes):
    total = 1
    for name in axes:
        total *= axis_size(sizes, name)
    return total


def own_index(axes, sizes):
    index = 0
    for name in axes:
        own = lax.axis_index("context") // 2 if name == "side" else lax.axis_index(name)
        index = index * axis_size(sizes, name) + own
    return index


def coords_of(axes, sizes, index):
    out = {}
    for name in reversed(axes):
        place = lax.rem(index, axis_size(sizes, name))
        if name == "side":
            out["context"] = place * 2 + lax.rem(lax.axis_index("context"), 2)
        else:
            out[name] = place
        index = index // axis_size(sizes, name)
    return out


def pick_whole(ref, target, peer):
    return ref


def pick_target(ref, target, peer):
    return ref.at[target]


def pick_context(ref, target, peer):
    return ref.at[peer["context"]]


def greet(all_axes, sizes):
    barrier = pltpu.get_barrier_semaphore()
    groups = []
    for axes in all_axes:
        if not any(set(axes) <= set(other) for other in groups):
            groups = [other for other in groups if not set(other) <= set(axes)] + [axes]
    signals = 0
    for axes in groups:
        me, total = own_index(axes, sizes), group_size(axes, sizes)
        for step in range(1, total):
            peer = coords_of(axes, sizes, lax.rem(me + step, total))
            pl.semaphore_signal(barrier, inc=1, device_id=peer, device_id_type=MESH_ID)
        signals += total - 1
    pl.semaphore_wait(barrier, signals)


def launch(sizes, axes, pick, keep, source, landing, send, recv):
    started = []
    me, total = own_index(axes, sizes), group_size(axes, sizes)
    for step in range(1, total):
        target = lax.rem(me + step, total)
        peer = coords_of(axes, sizes, target)
        copy = pltpu.make_async_remote_copy(
            src_ref=pick(source, target, peer),
            dst_ref=landing.at[me],
            send_sem=send.at[step],
            recv_sem=recv.at[step],
            device_id=peer,
            device_id_type=MESH_ID,
        )
        copy.start()
        started.append(copy)
    if keep:
        own = pltpu.make_async_copy(
            pick(source, me, coords_of(axes, sizes, me)), landing.at[me], send.at[0]
        )
        own.start()
        started.append(own)
    return started


def exchange_body(items, sizes, compute, more_ins, more_outs, *refs):
    count = len(items)
    ins, refs = refs[:count], refs[count:]
    data_ins, refs = refs[:more_ins], refs[more_ins:]
    outs, refs = refs[:count], refs[count:]
    data_outs, refs = refs[:more_outs], refs[more_outs:]
    sems, scratch = refs[: 2 * count], refs[2 * count :]

    greet([item[0] for item in items], sizes)
    waits = []
    for number, item in enumerate(items):
        pair = sems[2 * number : 2 * number + 2]
        waits += launch(sizes, *item, ins[number], outs[number], *pair)
    if compute is not None:
        compute(data_ins, data_outs, scratch)
    for copy in waits:
        copy.wait()


def exchange(cid, sizes, name, *specs, compute=None, data=(), results=(), scratch=(), cost=None):
    vmem, hbm = pl.BlockSpec(memory_space=pltpu.VMEM), pl.BlockSpec(memory_space=pl.ANY)
    items, shapes, spaces, sems = [], [], [], []
    for array, axes, pick, *large in specs:
        total = group_size(axes, sizes)
        chunk = array.shape if pick is pick_whole else array.shape[1:]
        shapes.append(jax.ShapeDtypeStruct((total, *chunk), array.dtype))
        spaces.append(hbm if large else vmem)
        items.append((axes, pick, not large))
        sems += [pltpu.SemaphoreType.DMA((total,)), pltpu.SemaphoreType.DMA((total,))]
    return pl.pallas_call(
        functools.partial(exchange_body, items, sizes, compute, len(data), len(results)),
        out_shape=[*shapes, *results],
        in_specs=[*spaces, *([vmem] * len(data))],
        out_specs=[*spaces, *([vmem] * len(results))],
        scratch_shapes=[*sems, *scratch],
        name=name,
        compiler_params=pltpu.CompilerParams(
            collective_id=cid, has_side_effects=True, vmem_limit_bytes=60_000_000
        ),
    )(*[spec[0] for spec in specs], *data)


def stack_heads(block, low):
    tokens = block.shape[0]
    zero = jnp.zeros((tokens, HEAD_DIM), block.dtype)
    parts = [block[:, :HEAD_DIM], block[:, HEAD_DIM:]]
    return jnp.concatenate(
        [jnp.concatenate([part, zero] if low else [zero, part], axis=1) for part in parts], axis=0
    )


def causal(shape, tokens):
    keys = lax.broadcasted_iota(jnp.int32, shape, 0)
    queries = lax.rem(lax.broadcasted_iota(jnp.int32, shape, 1), tokens)
    return keys - queries <= lax.axis_index("expert") * tokens


def identity(size):
    shape = (size, size)
    return lax.broadcasted_iota(jnp.int32, shape, 0) == lax.broadcasted_iota(jnp.int32, shape, 1)


def attention_forward(data, results, scratch):
    query_ref, kv_ref = data
    out_ref, sum_ref = results
    (score_ref,) = scratch
    blocks, tokens = query_ref.shape[:2]
    chunk, columns = 8 * tokens, 2 * tokens

    def block(number, carry):
        rows = stack_heads(query_ref[number], True) * (HEAD_DIM ** (-0.5))
        rows = rows.astype(BF16)

        def keys_of(j):
            return pl.ds(pl.multiple_of(j * chunk, chunk), chunk)

        def first(j, top):
            scores = dot_t(kv_ref[keys_of(j), :], rows)
            score_ref[keys_of(j), :] = scores
            return jnp.maximum(top, jnp.max(scores, axis=0, keepdims=True))

        top = lax.fori_loop(0, number, first, jnp.full((1, columns), -jnp.inf, F32))
        scores = dot_t(kv_ref[keys_of(number), :], rows)
        scores = jnp.where(causal(scores.shape, tokens), scores, -jnp.inf)
        score_ref[keys_of(number), :] = scores
        top = jnp.maximum(top, jnp.max(scores, axis=0, keepdims=True))

        def second(j, held):
            total, mixed = held
            powers = jnp.exp(score_ref[keys_of(j), :] - top)
            total = total + jnp.sum(powers, axis=0, keepdims=True)
            return total, mixed + t_dot(powers.astype(BF16), kv_ref[keys_of(j), :])

        start = (jnp.zeros((1, columns), F32), jnp.zeros((columns, 2 * HEAD_DIM), F32))
        total, mixed = lax.fori_loop(0, number + 1, second, start)
        sum_ref[number] = top + jnp.log(total)
        inverse = jnp.sum(jnp.where(identity(columns), 1.0 / total, 0.0), axis=1, keepdims=True)
        mixed = (mixed * inverse)[:, HEAD_DIM:]
        out_ref[number] = jnp.concatenate([mixed[:tokens], mixed[tokens:]], axis=1).astype(BF16)
        return carry

    lax.fori_loop(0, blocks, block, 0)


def attention_backward(data, results, scratch):
    query_ref, kv_ref, mix_ref, grad_ref, sum_ref = data
    grad_query_ref, terms_ref = results
    (sum_kv,) = scratch
    blocks, tokens = query_ref.shape[:2]
    chunk, columns = 8 * tokens, 2 * tokens
    factor = HEAD_DIM ** (-0.5)
    sum_kv[...] = jnp.zeros_like(sum_kv)

    def block(number, carry):
        rows = (stack_heads(query_ref[number], True) * factor).astype(BF16)
        grads = stack_heads(grad_ref[number], False)
        both = jnp.concatenate([rows, grads], axis=0)
        pairs = dot_t(stack_heads(mix_ref[number], False), grads)
        delta = jnp.sum(jnp.where(identity(columns), pairs, 0.0), axis=0, keepdims=True)
        logsum = sum_ref[number]

        def unit(j, total, masked):
            keys = pl.ds(pl.multiple_of(j * chunk, chunk), chunk)
            kv = kv_ref[keys, :]
            products = dot_t(kv, both)
            soft = jnp.exp(products[:, :columns] - logsum)
            if masked:
                soft = jnp.where(causal(soft.shape, tokens), soft, 0.0)
            scores = (soft * (products[:, columns:] - delta)).astype(BF16)
            sum_kv[keys, :] += dot(jnp.concatenate([scores, soft.astype(BF16)], axis=1), both)
            return total + t_dot(scores, kv)

        total = lax.fori_loop(
            0, number, lambda j, held: unit(j, held, False), jnp.zeros((columns, 2 * HEAD_DIM), F32)
        )
        total = unit(number, total, True)[:, :HEAD_DIM] * factor
        grad_query_ref[number] = jnp.concatenate([total[:tokens], total[tokens:]], axis=1)
        return carry

    lax.fori_loop(0, blocks, block, 0)
    terms_ref[...] = sum_kv[...].astype(BF16).reshape(terms_ref.shape)


def backward_body(sizes, *refs):
    owns, others, y_ref, data, refs = refs[:3], refs[3:6], refs[6], refs[7:12], refs[12:]
    y_back, kv_back, query_back, *totals = refs[:6]
    sends, gots, sends_2, gots_2 = refs[6:9], refs[9:12], refs[12:15], refs[15:18]
    grad_query, terms, sum_kv = refs[18:21]
    sems = refs[21:]
    dp, side = lax.axis_index("dp"), lax.axis_index("context") // 2
    experts = owns[0].shape[0]
    firsts = (("dp",), ("dp",), ("side",))
    seconds = (("side",), ("side",), ("dp",))

    def chip_sum(i, expert, place):
        return owns[i][expert, place] + others[i][expert, place].astype(F32)

    for i, axes in enumerate(firsts):

        def fill(expert, carry, i=i, axes=axes):
            for d in range(4):
                for v in range(2):
                    terms_now = chip_sum(i, expert, 2 * d + v).astype(BF16)
                    if axes == ("dp",):
                        sends[i][d, expert, v] = terms_now
                    else:
                        sends[i][v, expert, d] = terms_now
            return carry

        lax.fori_loop(0, experts, fill, 0)
    greet([SEQ_AXES, ("dp",)], sizes)
    stage_1 = []
    for i, axes in enumerate(firsts):
        stage_1 += launch(sizes, axes, pick_target, False, sends[i], gots[i], *sems[2 * i : 2 * i + 2])
    rest = launch(sizes, ("expert",), pick_target, True, y_ref, y_back, *sems[6:8])

    attention_backward(data, (grad_query, terms), (sum_kv,))
    rest += launch(sizes, SEQ_AXES, pick_target, True, terms, kv_back, *sems[8:10])
    rest += launch(sizes, ("context",), pick_target, True, grad_query, query_back, *sems[10:12])
    for copy in stage_1:
        copy.wait()

    def part(i, expert, place):
        if firsts[i] == ("dp",):
            total = chip_sum(i, expert, 2 * dp + place)
            for step in range(1, 4):
                total = total + gots[i][lax.rem(dp + step, 4), expert, place].astype(F32)
            return total
        return chip_sum(i, expert, 2 * place + side) + gots[i][1 - side, expert, place].astype(F32)

    for i, axes in enumerate(seconds):

        def refill(expert, carry, i=i, axes=axes):
            for place in range(group_size(axes, sizes)):
                sends_2[i][place, expert] = part(i, expert, place).astype(BF16)
            return carry

        lax.fori_loop(0, experts, refill, 0)
    stage_2 = []
    for i, axes in enumerate(seconds):
        stage_2 += launch(
            sizes, axes, pick_target, False, sends_2[i], gots_2[i], *sems[12 + 2 * i : 14 + 2 * i]
        )
    for copy in stage_2:
        copy.wait()
    for i, axes in enumerate(seconds):
        me, total = own_index(axes, sizes), group_size(axes, sizes)

        def close(expert, carry, i=i, me=me, total=total):
            held = part(i, expert, me)
            for step in range(1, total):
                held = held + gots_2[i][lax.rem(me + step, total), expert].astype(F32)
            totals[i][expert] = held
            return carry

        lax.fori_loop(0, experts, close, 0)
    for copy in rest:
        copy.wait()


def run_backward(cid, sizes, owns, others, y_terms, data):
    queries, kv_all = data[:2]
    tokens = queries.shape[1]
    experts = owns[0].shape[0]
    vmem = pl.BlockSpec(memory_space=pltpu.VMEM)
    tiles = [own.shape[2:] for own in owns]
    stage_1 = [(4, experts, 2, *tiles[0]), (4, experts, 2, *tiles[1]), (2, experts, 4, *tiles[2])]
    stage_2 = [(2, experts, *tiles[0]), (2, experts, *tiles[1]), (4, experts, *tiles[2])]
    sizes_of = [4, 4, 2, sizes["expert"], group_size(SEQ_AXES, sizes), sizes["context"], 2, 2, 4]
    dma = pltpu.SemaphoreType.DMA
    return pl.pallas_call(
        functools.partial(backward_body, sizes),
        out_shape=[
            jax.ShapeDtypeStruct(y_terms.shape, BF16),
            jax.ShapeDtypeStruct((kv_all.shape[0] // tokens, tokens, 2 * HEAD_DIM), BF16),
            jax.ShapeDtypeStruct(queries.shape, F32),
            *[jax.ShapeDtypeStruct((experts, *tile), F32) for tile in tiles],
        ],
        in_specs=[vmem] * 12,
        out_specs=[vmem] * 6,
        scratch_shapes=[
            *[pltpu.VMEM(shape, BF16) for shape in stage_1 * 2 + stage_2 * 2],
            pltpu.VMEM(queries.shape, F32),
            pltpu.VMEM((kv_all.shape[0] // tokens, tokens, 2 * HEAD_DIM), BF16),
            pltpu.VMEM(kv_all.shape, F32),
            *[dma((n,)) for n in sizes_of for _ in range(2)],
        ],
        name="attention_backward",
        compiler_params=pltpu.CompilerParams(
            collective_id=cid, has_side_effects=True, vmem_limit_bytes=67_043_328
        ),
    )(*owns, *others, y_terms, *data)


def moe_copies(sizes, refs):
    d_send, d_back, dots, dot_back, g_sends, g_backs, sems = refs
    owners = sizes["expert"]
    owner, context = lax.axis_index("expert"), lax.axis_index("context")

    def results(step):
        target = lax.rem(owner + step, owners)
        pairs = ((d_send, d_back, sems[0], sems[1]), (dots, dot_back, sems[2], sems[3]))
        return [
            pltpu.make_async_remote_copy(
                src_ref=src.at[target],
                dst_ref=dst.at[owner],
                send_sem=send.at[step],
                recv_sem=recv.at[step],
                device_id={"expert": target},
                device_id_type=MESH_ID,
            )
            for src, dst, send, recv in pairs
        ]

    def own_results():
        return [
            pltpu.make_async_copy(d_send.at[owner], d_back.at[owner], sems[0].at[0]),
            pltpu.make_async_copy(dots.at[owner], dot_back.at[owner], sems[2].at[0]),
        ]

    def halves(number):
        partner = context + 1 - 2 * lax.rem(context, 2)
        return [
            pltpu.make_async_remote_copy(
                src_ref=g_sends[i].at[number],
                dst_ref=g_backs[i].at[number],
                send_sem=sems[4].at[3 * number + i],
                recv_sem=sems[5].at[3 * number + i],
                device_id={"context": partner},
                device_id_type=MESH_ID,
            )
            for i in range(3)
        ]

    return results, own_results, halves


def moe_body(
    sizes,
    moe_ref,
    grad_ref,
    table_ref,
    wg_ref,
    wu_ref,
    wd_ref,
    own_g,
    own_u,
    own_d,
    back_g,
    back_u,
    back_d,
    y_out,
    d_back,
    dot_back,
    x_all,
    g_now,
    deo_all,
    dgu_all,
    eh_all,
    eo_all,
    dbuf_all,
    picks,
    highs,
    lows,
    gate_col,
    dot_col,
    dots,
    y_send,
    d_send,
    send_g,
    send_u,
    send_d,
    *sems,
):
    step = pl.program_id(0)
    owners = sizes["expert"]
    owner, context = lax.axis_index("expert"), lax.axis_index("context")
    core = lax.rem(context, 2)
    mine = 4
    tokens, width = moe_ref.shape[1:]
    hidden_width = wg_ref.shape[2]
    rows = owners * CAP
    tile = rows // 2
    barrier = pltpu.get_barrier_semaphore()
    results, own_results, halves = moe_copies(
        sizes, (d_send, d_back, dots, dot_back, (send_g, send_u, send_d), (back_g, back_u, back_d), sems)
    )

    @pl.when(step == 0)
    def _():
        for shift_by in range(1, owners):
            pl.semaphore_signal(
                barrier,
                inc=1,
                device_id={"expert": lax.rem(owner + shift_by, owners)},
                device_id_type=MESH_ID,
            )
        pl.semaphore_signal(
            barrier, inc=1, device_id={"context": context + 1 - 2 * core}, device_id_type=MESH_ID
        )
        dots[...] = jnp.zeros_like(dots)

    @pl.when(step == 4)
    def _():
        pl.semaphore_wait(barrier, owners)
        for shift_by in range(1, owners):
            for copy in results(shift_by):
                copy.start()
        for copy in own_results():
            copy.start()
        pltpu.make_async_copy(y_send, y_out, sems[6].at[0]).start()

    for number in range(mine):

        @pl.when(step == 5 + number)
        def _(number=number):
            for copy in halves(number):
                copy.start()

    @pl.when(step < mine)
    def _():
        place = pl.multiple_of(step * CAP, CAP)
        table = jnp.concatenate(
            [table_ref[s, pl.ds(owner * mine + step, 1), :] for s in range(owners)], axis=0
        )
        named = table >= 0.0
        above = lax.broadcasted_iota(jnp.int32, (tokens, tokens), 0)
        beside = lax.broadcasted_iota(jnp.int32, (tokens, tokens), 1)
        before = (above < beside).astype(F32).astype(BF16)
        slots = dot(named.astype(F32).astype(BF16), before)
        slots = jnp.where(named, slots, -1.0)
        counts = lax.broadcasted_iota(jnp.int32, (CAP, tokens), 0).astype(F32)
        for s in range(owners):
            chosen = counts == slots[s : s + 1]
            onehot = jnp.where(chosen, 1.0, 0.0).astype(BF16)
            weight = jnp.where(chosen, table[s : s + 1], 0.0)
            high = weight.astype(BF16)
            picks[s, pl.ds(place, CAP), :] = onehot
            highs[s, pl.ds(place, CAP), :] = high
            lows[s, pl.ds(place, CAP), :] = (weight - high.astype(F32)).astype(BF16)
            gate_col[s * CAP : (s + 1) * CAP, :] = jnp.sum(weight, axis=1, keepdims=True)
            x_all[step, s * CAP : (s + 1) * CAP, :] = dot(onehot, moe_ref[s]).astype(BF16)
            g_now[s * CAP : (s + 1) * CAP, :] = dot(onehot, grad_ref[s]).astype(BF16)

        def run_tile(r, carry):
            here = pl.ds(pl.multiple_of(r * tile, tile), tile)
            part = pl.ds(r * (owners // 2), owners // 2)
            spot = pl.ds(place, CAP)
            rows_in = x_all[step, here, :]
            gate_act = dot(rows_in, wg_ref[0])
            up_act = dot(rows_in, wu_ref[0])
            sigma = jax.nn.sigmoid(gate_act)
            silu = gate_act * sigma
            hidden = (silu * up_act).astype(BF16)
            eh_all[step, here, :] = hidden
            expert_out = dot(hidden, wd_ref[0]).astype(BF16)
            eo_all[part, spot, :] = expert_out.reshape(owners // 2, CAP, width)
            grads = g_now[here, :].astype(F32)
            dot_col[here, :] = jnp.sum(grads * expert_out.astype(F32), axis=1, keepdims=True)
            grad_expert = (gate_col[here, :] * grads).astype(BF16)
            deo_all[step, here, :] = grad_expert
            grad_hidden = dot_t(grad_expert, wd_ref[0])
            slope = sigma * (1.0 + gate_act * (1.0 - sigma))
            grad_gate = (grad_hidden * up_act * slope).astype(BF16)
            grad_up = (grad_hidden * silu).astype(BF16)
            dgu_all[step, here, :hidden_width] = grad_gate
            dgu_all[step, here, hidden_width:] = grad_up
            grad_buffer = (dot_t(grad_gate, wg_ref[0]) + dot_t(grad_up, wu_ref[0])).astype(BF16)
            dbuf_all[part, spot, :] = grad_buffer.reshape(owners // 2, CAP, width)
            return carry

        lax.fori_loop(0, 2, run_tile, 0)
        for s in range(owners):
            onehot = picks[s, pl.ds(place, CAP), :].astype(F32)
            line = jnp.sum(onehot * dot_col[s * CAP : (s + 1) * CAP, :], axis=0, keepdims=True)
            dots[s, pl.ds(step, 1), :] = line

    @pl.when(step == mine - 1)
    def _():
        def combine(s, carry):
            moved = t_dot(highs[s], eo_all[s]) + t_dot(lows[s], eo_all[s])
            y_send[s] = moved.astype(BF16)
            d_send[s] = t_dot(picks[s], dbuf_all[s]).astype(BF16)
            return carry

        lax.fori_loop(0, owners, combine, 0)

    @pl.when((step >= mine) & (step < 2 * mine))
    def _():
        number = step - mine
        blocks = width // 256
        per = width // 16

        def gate_rows(j, carry):
            columns = pl.ds(pl.multiple_of(j * 256, 256), 256)
            rows_in = x_all[number, :, columns]
            for half, own, send in ((0, own_g, send_g), (1, own_u, send_u)):
                grads = dgu_all[number, :, half * hidden_width : (half + 1) * hidden_width]
                terms = t_dot(rows_in, grads).reshape(128 // per, 2, per, hidden_width)
                first, second = terms[:, 0], terms[:, 1]
                group = pl.ds(j * (128 // per), 128 // per)
                own[0, group] = jnp.where(core == 0, first, second)
                send[number, group] = jnp.where(core == 0, second, first).astype(BF16)
            return carry

        lax.fori_loop(0, blocks, gate_rows, 0)
        less = hidden_width // 16

        def down_rows(j, carry):
            columns = pl.ds(pl.multiple_of(j * 256, 256), 256)
            terms = t_dot(eh_all[number, :, columns], deo_all[number])
            terms = terms.reshape(128 // less, 2, less, width)
            first, second = terms[:, 0], terms[:, 1]
            group = pl.ds(j * (128 // less), 128 // less)
            own_d[0, group] = jnp.where(core == 0, first, second)
            send_d[number, group] = jnp.where(core == 0, second, first).astype(BF16)
            return carry

        lax.fori_loop(0, hidden_width // 256, down_rows, 0)

    @pl.when(step == 2 * mine)
    def _():
        for shift_by in range(1, owners):
            for copy in results(shift_by):
                copy.wait()
        for copy in own_results():
            copy.wait()
        pltpu.make_async_copy(y_send, y_out, sems[6].at[0]).wait()
        for number in range(mine):
            for copy in halves(number):
                copy.wait()


def run_experts(cid, sizes, moe_all, grad_all, table_all, gate_weight, up_weight, down_weight):
    owners, tokens, width = moe_all.shape
    mine, _, inner = gate_weight.shape
    rows = owners * CAP
    part, less = width // 16, inner // 16

    def fixed(array):
        return pl.BlockSpec(array.shape, lambda i: (0, 0, 0), pipeline_mode=pl.Buffered(1))

    def expert_block(array):
        return pl.BlockSpec((1, *array.shape[1:]), lambda i: (jnp.minimum(i, mine - 1), 0, 0))

    def own_block(*shape):
        return pl.BlockSpec((1, *shape), lambda i: (jnp.clip(i - mine, 0, mine - 1), 0, 0, 0))

    anywhere = pl.BlockSpec(memory_space=pl.ANY)
    wide, tall = (8, part, inner), (8, less, width)
    dma = pltpu.SemaphoreType.DMA
    return pl.pallas_call(
        functools.partial(moe_body, sizes),
        grid=(2 * mine + 1,),
        out_shape=[
            jax.ShapeDtypeStruct((mine, *wide), F32),
            jax.ShapeDtypeStruct((mine, *wide), F32),
            jax.ShapeDtypeStruct((mine, *tall), F32),
            jax.ShapeDtypeStruct((mine, *wide), BF16),
            jax.ShapeDtypeStruct((mine, *wide), BF16),
            jax.ShapeDtypeStruct((mine, *tall), BF16),
            jax.ShapeDtypeStruct((owners, tokens, width), BF16),
            jax.ShapeDtypeStruct((owners, tokens, width), BF16),
            jax.ShapeDtypeStruct((owners, 8, tokens), F32),
        ],
        in_specs=[
            fixed(moe_all),
            fixed(grad_all),
            fixed(table_all),
            expert_block(gate_weight),
            expert_block(up_weight),
            expert_block(down_weight),
        ],
        out_specs=[own_block(*wide), own_block(*wide), own_block(*tall), *([anywhere] * 6)],
        scratch_shapes=[
            pltpu.VMEM((mine, rows, width), BF16),
            pltpu.VMEM((rows, width), BF16),
            pltpu.VMEM((mine, rows, width), BF16),
            pltpu.VMEM((mine, rows, 2 * inner), BF16),
            pltpu.VMEM((mine, rows, inner), BF16),
            pltpu.VMEM((owners, mine * CAP, width), BF16),
            pltpu.VMEM((owners, mine * CAP, width), BF16),
            pltpu.VMEM((owners, mine * CAP, tokens), BF16),
            pltpu.VMEM((owners, mine * CAP, tokens), BF16),
            pltpu.VMEM((owners, mine * CAP, tokens), BF16),
            pltpu.VMEM((rows, 1), F32),
            pltpu.VMEM((rows, 1), F32),
            pltpu.VMEM((owners, 8, tokens), F32),
            pltpu.VMEM((owners, tokens, width), BF16),
            pltpu.VMEM((owners, tokens, width), BF16),
            pltpu.VMEM((mine, *wide), BF16),
            pltpu.VMEM((mine, *wide), BF16),
            pltpu.VMEM((mine, *tall), BF16),
            dma((owners,)),
            dma((owners,)),
            dma((owners,)),
            dma((owners,)),
            dma((3 * mine,)),
            dma((3 * mine,)),
            dma((1,)),
        ],
        name="run_experts",
        compiler_params=pltpu.CompilerParams(
            collective_id=cid, has_side_effects=True, vmem_limit_bytes=67_043_328
        ),
    )(moe_all, grad_all, table_all, gate_weight, up_weight, down_weight)


CHIP_AXES = ("dp", "side", "expert")


def sum_body(sizes, *refs):
    query_in, key_in, value_in, output_in, narrow_in = refs[:5]
    query_out, key_out, value_out, output_out, narrow_out = refs[5:10]
    load, near, sums, got, whole = refs[10:15]
    near_send, near_recv, send_sems, recv_sems, give_sems, take_sems, pass_sems, land_sems = refs[15:]
    core = lax.rem(lax.axis_index("context"), 2)
    partner = {"context": lax.axis_index("context") + 1 - 2 * core}
    me, total = own_index(CHIP_AXES, sizes), group_size(CHIP_AXES, sizes)
    plane = total // sizes["dp"]
    rows = load.shape[1]
    some, wide = rows // 2, query_in.shape[1]
    half = wide // 2

    def place(step):
        target = lax.rem(me + step, total)
        return target, coords_of(CHIP_AXES, sizes, target)

    def remote(src, dst, send, recv, peer):
        return pltpu.make_async_remote_copy(
            src_ref=src, dst_ref=dst, send_sem=send, recv_sem=recv, device_id=peer, device_id_type=MESH_ID
        )

    def reduce_copy(step):
        target, peer = place(step)
        return remote(sums.at[target], got.at[me], send_sems.at[step], recv_sems.at[step], peer)

    def gather_copy(step):
        _, peer = place(step)
        own = whole.at[core, me]
        return remote(own, own, give_sems.at[step], take_sems.at[step], peer)

    def pass_copy(step):
        source = whole.at[core, lax.rem(me - step + total, total)]
        return remote(source, source, pass_sems.at[step], land_sems.at[step], partner)

    def near_copy(turn):
        chunks = pl.ds(lax.rem(lax.axis_index("dp") + turn, sizes["dp"]) * plane, plane)
        return remote(load.at[chunks], near.at[chunks], near_send.at[turn], near_recv.at[turn], partner)

    def each(start, stop, body):
        def run(step, carry):
            body(step)
            return carry

        lax.fori_loop(start, stop, run, 0)

    def pack(number, chunk):
        here = pl.ds(pl.multiple_of(chunk * rows, rows), rows)
        there = pl.ds(pl.multiple_of(chunk * some, some), some)
        if number == 0:
            parts = [query_in[here, :]]
        else:
            parts = [key_in[here, :], value_in[here, :]]
        start = number * wide
        output = jnp.concatenate(
            [output_in[there, start : start + half], output_in[there, start + half : start + wide]], axis=0
        )
        return jnp.concatenate([*parts, output, narrow_in[here, :]], axis=1)

    def unpack(number, chunk):
        here = pl.ds(pl.multiple_of(chunk * rows, rows), rows)
        there = pl.ds(pl.multiple_of(chunk * some, some), some)
        block = whole[number, chunk].astype(F32)
        if number == 0:
            query_out[here, :] = block[:, :wide]
            narrow_out[here, :] = block[:, wide + half :]
        else:
            key_out[here, :] = block[:, :half]
            value_out[here, :] = block[:, half:wide]
        start = number * wide
        output_out[there, start : start + half] = block[:some, wide : wide + half]
        output_out[there, start + half : start + wide] = block[some:, wide : wide + half]

    barrier = pltpu.get_barrier_semaphore()
    pl.semaphore_signal(barrier, inc=1, device_id=partner, device_id_type=MESH_ID)
    each(
        1,
        total,
        lambda step: pl.semaphore_signal(
            barrier, inc=1, device_id=place(step)[1], device_id_type=MESH_ID
        ),
    )
    for number in range(2):

        @pl.when(core == 1 - number)
        def _(number=number):
            def fill(chunk):
                load[chunk] = pack(number, chunk).astype(BF16)

            each(0, total, fill)

    pl.semaphore_wait(barrier, total)
    for turn in range(sizes["dp"]):
        near_copy(turn).start()

    for turn in range(sizes["dp"]):
        near_copy(turn).wait()
        base = lax.rem(lax.axis_index("dp") + turn, sizes["dp"]) * plane
        for number in range(2):

            @pl.when(core == number)
            def _(number=number, base=base):
                def add(chunk):
                    sums[chunk] = (pack(number, chunk) + near[chunk].astype(F32)).astype(BF16)

                each(base, base + plane, add)

        def send(i, base=base):
            target = base + lax.rem(me + i, plane)

            @pl.when(target != me)
            def _():
                reduce_copy(lax.rem(target - me + total, total)).start()

        each(0, plane, send)

    got[me] = sums[me]
    each(1, total, lambda step: reduce_copy(step).wait())
    result = lax.fori_loop(
        0, total, lambda i, held: held + got[i].astype(F32), jnp.zeros(got.shape[1:], F32)
    )
    whole[core, me] = result.astype(BF16)
    each(1, total, lambda step: gather_copy(step).start())
    pass_copy(0).start()

    def forward(step):
        gather_copy(step).wait_recv()
        pass_copy(step).start()

    each(1, total, forward)
    each(1, total, lambda step: gather_copy(step).wait_send())
    each(0, total, lambda step: pass_copy(step).wait())
    for number in range(2):
        each(0, total, functools.partial(unpack, number))


def sum_everywhere(cid, sizes, *arrays):
    total = group_size(CHIP_AXES, sizes)
    depth, wide = arrays[0].shape
    half = (total, depth // total, wide + wide // 2 + arrays[4].shape[1])
    dma = pltpu.SemaphoreType.DMA
    vmem = pl.BlockSpec(memory_space=pltpu.VMEM)
    return pl.pallas_call(
        functools.partial(sum_body, sizes),
        out_shape=[jax.ShapeDtypeStruct(array.shape, F32) for array in arrays],
        in_specs=[vmem] * 5,
        out_specs=[vmem] * 5,
        scratch_shapes=[pltpu.VMEM(half, BF16)] * 4
        + [pltpu.VMEM((2, *half), BF16)]
        + [dma((sizes["dp"],))] * 2
        + [dma((total,))] * 6,
        name="sum_everywhere",
        compiler_params=pltpu.CompilerParams(
            collective_id=cid, has_side_effects=True, vmem_limit_bytes=60_000_000
        ),
    )(*arrays)


def rope_tables(positions, head_size):
    half_dim = head_size // 2
    frequency = ROPE_BASE ** (-2.0 * jnp.arange(half_dim, dtype=F32) / head_size)
    angles = positions.astype(F32)[:, None] * frequency[None, :]
    angles = jnp.concatenate([angles, angles], axis=1)
    return (jnp.cos(angles), jnp.sin(angles))


def rotate(values, cosine, sine_table):
    half_dim = values.shape[-1] // 2
    turned = jnp.concatenate([-values[..., half_dim:], values[..., :half_dim]], axis=-1)
    return values * cosine[:, None, :] + turned * sine_table[:, None, :]


def rotate_back(grads, cosine, sine_table):
    half_dim = grads.shape[-1] // 2
    scaled = grads * sine_table[:, None, :]
    turned = jnp.concatenate([scaled[..., half_dim:], -scaled[..., :half_dim]], axis=-1)
    return grads * cosine[:, None, :] + turned


def norm_forward(values, gain_vec):
    inverse = lax.rsqrt(jnp.mean(values * values, axis=-1, keepdims=True) + EPSILON)
    normed = values * inverse
    return (inverse, normed, (normed * gain_vec).astype(BF16))


def norm_backward(grad_out, normed, inverse, gain_vec):
    gain_grad = jnp.sum(grad_out * normed, axis=0)
    scaled = grad_out * gain_vec
    inner = jnp.mean(scaled * normed, axis=-1, keepdims=True)
    return (gain_grad, inverse * (scaled - normed * inner))


def local(
    sizes,
    inputs,
    prenorm_gain,
    query_weight,
    key_weight,
    value_weight,
    output_weight,
    midnorm_gain,
    router_weight,
    gate_weight,
    up_weight,
    down_weight,
    expert_ids,
    cotangent,
):
    tokens, width = inputs.shape[1:]
    owners = sizes["expert"]
    mine = gate_weight.shape[0]
    context, owner = lax.axis_index("context"), lax.axis_index("expert")
    block = context * owners + owner
    positions = block * tokens + jnp.arange(tokens, dtype=jnp.int32)
    cosine, sine_table = rope_tables(positions, HEAD_DIM)

    input_float = inputs[0].astype(F32)
    inverse_first, normed_first, attn_input = norm_forward(input_float, prenorm_gain)
    query_raw = dot(attn_input, query_weight).reshape(tokens, HEADS, HEAD_DIM)
    key_raw = dot(attn_input, key_weight).reshape(tokens, KV_HEADS, HEAD_DIM)
    value_raw = dot(attn_input, value_weight).reshape(tokens, KV_HEADS, HEAD_DIM)
    query_rot = rotate(query_raw, cosine, sine_table).astype(BF16)
    key_rot = rotate(key_raw, cosine, sine_table).astype(BF16)
    query_send = query_rot.reshape(tokens, KV_HEADS, 2 * HEAD_DIM).transpose(1, 0, 2)
    kv_send = jnp.concatenate([key_rot, value_raw.astype(BF16)], axis=2).transpose(1, 0, 2)
    kv_all, queries = exchange(
        0, sizes, "send_qkv", (kv_send, SEQ_AXES, pick_context), (query_send, ("context",), pick_target)
    )
    kv_all = kv_all.reshape(-1, 2 * HEAD_DIM)
    columns = 2 * tokens
    grad_all, mixtures, sums = exchange(
        7,
        sizes,
        "attention_forward",
        (cotangent[0], ("expert",), pick_whole),
        compute=attention_forward,
        data=(queries, kv_all),
        results=(
            jax.ShapeDtypeStruct(queries.shape, BF16),
            jax.ShapeDtypeStruct((KV_HEADS, 1, columns), F32),
        ),
        scratch=(pltpu.VMEM((kv_all.shape[0], columns), F32),),
    )
    (mixture,) = exchange(1, sizes, "send_mixture", (mixtures, ("context",), pick_target))
    mixture_flat = mixture.transpose(1, 0, 2).reshape(tokens, HEADS * HEAD_DIM)

    after_attn = input_float + dot(mixture_flat, output_weight)
    inverse_second, normed_second, moe_input = norm_forward(after_attn, midnorm_gain)
    logits = lax.dot_general(
        router_weight, moe_input, (((0,), (1,)), ((), ())), preferred_element_type=F32
    )
    numbers = jnp.arange(EXPERTS, dtype=jnp.int32)[:, None, None]
    chosen = jnp.any(expert_ids[0].T[None] == numbers, axis=1)
    masked = jnp.where(chosen, logits, -jnp.inf)
    powers = jnp.exp(masked - jnp.max(masked, axis=0, keepdims=True))
    gates = powers / jnp.sum(powers, axis=0, keepdims=True)
    gate_table = jnp.where(chosen, gates, -1.0)

    moe_all, table_all = exchange(
        2, sizes, "send_tokens", (moe_input, ("expert",), pick_whole), (gate_table, ("expert",), pick_whole)
    )
    own_g, own_u, own_d, other_g, other_u, other_d, moe_terms, grad_back, dot_back = run_experts(
        3, sizes, moe_all, grad_all, table_all, gate_weight, up_weight, down_weight
    )
    grad_gates = dot_back[:, :mine].reshape(EXPERTS, tokens)
    grad_logits = gates * (grad_gates - jnp.sum(gates * grad_gates, axis=0, keepdims=True))
    router_grad = jnp.einsum(
        "td,et->de", moe_input.astype(F32), grad_logits, precision=lax.Precision.HIGHEST
    )
    grad_moe_in = jnp.sum(grad_back.astype(F32), axis=0) + jnp.einsum(
        "et,de->td", grad_logits, router_weight.astype(F32), precision=lax.Precision.HIGHEST
    )
    grad_out = cotangent[0].astype(F32)
    midnorm_grad, grad_after = norm_backward(grad_moe_in, normed_second, inverse_second, midnorm_gain)
    grad_after = grad_out + grad_after
    grad_after_half = grad_after.astype(BF16)
    output_grad = t_dot(mixture_flat, grad_after_half)
    grad_mix = dot_t(grad_after_half, output_weight).astype(BF16)
    grad_mix = grad_mix.reshape(tokens, KV_HEADS, 2 * HEAD_DIM).transpose(1, 0, 2)
    (grad_mixtures,) = exchange(4, sizes, "send_grad_mixture", (grad_mix, ("context",), pick_target))
    moe_back, kv_back, grad_query, gate_sum, up_sum, down_sum = run_backward(
        8,
        sizes,
        (own_g, own_u, own_d),
        (other_g, other_u, other_d),
        moe_terms,
        (queries, kv_all, mixtures, grad_mixtures, sums),
    )
    outputs = (after_attn + jnp.sum(moe_back.astype(F32), axis=0)).astype(BF16)
    grad_kv = jnp.sum(kv_back.astype(F32).reshape(KV_HEADS, owners, tokens, 2 * HEAD_DIM), axis=1)
    grad_kv = grad_kv.transpose(1, 0, 2)
    grad_query = grad_query.transpose(1, 0, 2).reshape(tokens, HEADS, HEAD_DIM)
    query_back = rotate_back(grad_query, cosine, sine_table).reshape(tokens, -1).astype(BF16)
    key_back = rotate_back(grad_kv[..., :HEAD_DIM], cosine, sine_table).reshape(tokens, -1).astype(BF16)
    value_back = grad_kv[..., HEAD_DIM:].reshape(tokens, -1).astype(BF16)
    query_grad = t_dot(attn_input, query_back)
    key_grad = t_dot(attn_input, key_back)
    value_grad = t_dot(attn_input, value_back)
    grad_attn_in = (
        dot_t(query_back, query_weight) + dot_t(key_back, key_weight) + dot_t(value_back, value_weight)
    )
    prenorm_grad, grad_inputs = norm_backward(grad_attn_in, normed_first, inverse_first, prenorm_gain)
    grad_inputs = grad_after + grad_inputs
    narrow = jnp.concatenate([router_grad, prenorm_grad[:, None], midnorm_grad[:, None]], axis=1)
    narrow = jnp.pad(narrow, ((0, 0), (0, 128 - EXPERTS - 2)))
    query_grad, key_grad, value_grad, output_grad, narrow = sum_everywhere(
        9, sizes, query_grad, key_grad, value_grad, output_grad, narrow
    )
    dense = (
        narrow[:, EXPERTS],
        query_grad,
        key_grad,
        value_grad,
        output_grad,
        narrow[:, EXPERTS + 1],
        narrow[:, :EXPERTS],
    )
    return (outputs[None], grad_inputs[None], *dense, gate_sum, up_sum, down_sum)


def solution(mesh):
    split = P("dp", ("context", "expert"), None)
    owned = P("expert", None, None)
    summed = P("expert", ("dp", "context"), None)
    in_specs = (split, *([P()] * 7), owned, owned, owned, split, split)
    out_specs = (split, split, *([P()] * 7), summed, summed, summed)
    return jax.shard_map(
        functools.partial(local, dict(mesh.shape)),
        mesh=mesh,
        in_specs=in_specs,
        out_specs=out_specs,
        check_vma=False,
    )
```

```python
import functools

import jax
import jax.numpy as jnp
from jax import lax
from jax.experimental import pallas as pl
from jax.experimental.pallas import tpu as pltpu
from jax.sharding import PartitionSpec as P

HEADS = 8
KV_HEADS = 4
HEAD_DIM = 64
EXPERTS = 32
TOP = 8
CAP = 64
EPSILON = 1e-06
ROPE_BASE = 10000.0
F32 = jnp.float32
BF16 = jnp.bfloat16
MESH_ID = pl.DeviceIdType.MESH
SEQ_AXES = ("context", "expert")


def dot(left, right):
    return jnp.dot(left, right, preferred_element_type=F32)


def dot_t(left, right):
    return lax.dot_general(left, right, (((1,), (1,)), ((), ())), preferred_element_type=F32)


def t_dot(left, right):
    return lax.dot_general(left, right, (((0,), (0,)), ((), ())), preferred_element_type=F32)


def axis_size(sizes, name):
    return 2 if name == "side" else sizes[name]


def group_size(axes, sizes):
    total = 1
    for name in axes:
        total *= axis_size(sizes, name)
    return total


def own_index(axes, sizes):
    index = 0
    for name in axes:
        own = lax.axis_index("context") // 2 if name == "side" else lax.axis_index(name)
        index = index * axis_size(sizes, name) + own
    return index


def coords_of(axes, sizes, index):
    out = {}
    for name in reversed(axes):
        place = lax.rem(index, axis_size(sizes, name))
        if name == "side":
            out["context"] = place * 2 + lax.rem(lax.axis_index("context"), 2)
        else:
            out[name] = place
        index = index // axis_size(sizes, name)
    return out


def pick_whole(ref, target, peer):
    return ref


def pick_target(ref, target, peer):
    return ref.at[target]


def pick_context(ref, target, peer):
    return ref.at[peer["context"]]


def greet(all_axes, sizes):
    barrier = pltpu.get_barrier_semaphore()
    groups = []
    for axes in all_axes:
        if not any(set(axes) <= set(other) for other in groups):
            groups = [other for other in groups if not set(other) <= set(axes)] + [axes]
    signals = 0
    for axes in groups:
        me, total = own_index(axes, sizes), group_size(axes, sizes)
        for step in range(1, total):
            peer = coords_of(axes, sizes, lax.rem(me + step, total))
            pl.semaphore_signal(barrier, inc=1, device_id=peer, device_id_type=MESH_ID)
        signals += total - 1
    pl.semaphore_wait(barrier, signals)


def launch(sizes, axes, pick, keep, source, landing, send, recv):
    started = []
    me, total = own_index(axes, sizes), group_size(axes, sizes)
    for step in range(1, total):
        target = lax.rem(me + step, total)
        peer = coords_of(axes, sizes, target)
        copy = pltpu.make_async_remote_copy(
            src_ref=pick(source, target, peer),
            dst_ref=landing.at[me],
            send_sem=send.at[step],
            recv_sem=recv.at[step],
            device_id=peer,
            device_id_type=MESH_ID,
        )
        copy.start()
        started.append(copy)
    if keep:
        own = pltpu.make_async_copy(
            pick(source, me, coords_of(axes, sizes, me)), landing.at[me], send.at[0]
        )
        own.start()
        started.append(own)
    return started


def exchange_body(items, sizes, compute, more_ins, more_outs, *refs):
    count = len(items)
    ins, refs = refs[:count], refs[count:]
    data_ins, refs = refs[:more_ins], refs[more_ins:]
    outs, refs = refs[:count], refs[count:]
    data_outs, refs = refs[:more_outs], refs[more_outs:]
    sems, scratch = refs[: 2 * count], refs[2 * count :]

    greet([item[0] for item in items], sizes)
    waits = []
    for number, item in enumerate(items):
        pair = sems[2 * number : 2 * number + 2]
        waits += launch(sizes, *item, ins[number], outs[number], *pair)
    if compute is not None:
        compute(data_ins, data_outs, scratch)
    for copy in waits:
        copy.wait()


def exchange(cid, sizes, name, *specs, compute=None, data=(), results=(), scratch=(), cost=None):
    vmem, hbm = pl.BlockSpec(memory_space=pltpu.VMEM), pl.BlockSpec(memory_space=pl.ANY)
    items, shapes, spaces, sems = [], [], [], []
    for array, axes, pick, *large in specs:
        total = group_size(axes, sizes)
        chunk = array.shape if pick is pick_whole else array.shape[1:]
        shapes.append(jax.ShapeDtypeStruct((total, *chunk), array.dtype))
        spaces.append(hbm if large else vmem)
        items.append((axes, pick, not large))
        sems += [pltpu.SemaphoreType.DMA((total,)), pltpu.SemaphoreType.DMA((total,))]
    return pl.pallas_call(
        functools.partial(exchange_body, items, sizes, compute, len(data), len(results)),
        out_shape=[*shapes, *results],
        in_specs=[*spaces, *([vmem] * len(data))],
        out_specs=[*spaces, *([vmem] * len(results))],
        scratch_shapes=[*sems, *scratch],
        name=name,
        compiler_params=pltpu.CompilerParams(
            collective_id=cid, has_side_effects=True, vmem_limit_bytes=60_000_000
        ),
    )(*[spec[0] for spec in specs], *data)


def stack_heads(block, low):
    tokens = block.shape[0]
    zero = jnp.zeros((tokens, HEAD_DIM), block.dtype)
    parts = [block[:, :HEAD_DIM], block[:, HEAD_DIM:]]
    return jnp.concatenate(
        [jnp.concatenate([part, zero] if low else [zero, part], axis=1) for part in parts], axis=0
    )


def causal(shape, tokens):
    keys = lax.broadcasted_iota(jnp.int32, shape, 0)
    queries = lax.rem(lax.broadcasted_iota(jnp.int32, shape, 1), tokens)
    return keys - queries <= lax.axis_index("expert") * tokens


def identity(size):
    shape = (size, size)
    return lax.broadcasted_iota(jnp.int32, shape, 0) == lax.broadcasted_iota(jnp.int32, shape, 1)


def attention_forward(data, results, scratch):
    query_ref, kv_ref = data
    out_ref, sum_ref = results
    (score_ref,) = scratch
    blocks, tokens = query_ref.shape[:2]
    chunk, columns = 8 * tokens, 2 * tokens

    def block(number, carry):
        rows = stack_heads(query_ref[number], True) * (HEAD_DIM ** (-0.5))
        rows = rows.astype(BF16)

        def keys_of(j):
            return pl.ds(pl.multiple_of(j * chunk, chunk), chunk)

        def kv_of(j):
            return kv_ref[pl.ds(j * 8, 8)].reshape(chunk, 2 * HEAD_DIM)

        def first(j, top):
            scores = dot_t(kv_of(j), rows)
            score_ref[keys_of(j), :] = scores
            return jnp.maximum(top, jnp.max(scores, axis=0, keepdims=True))

        top = lax.fori_loop(0, number, first, jnp.full((1, columns), -jnp.inf, F32))
        scores = dot_t(kv_of(number), rows)
        scores = jnp.where(causal(scores.shape, tokens), scores, -jnp.inf)
        score_ref[keys_of(number), :] = scores
        top = jnp.maximum(top, jnp.max(scores, axis=0, keepdims=True))

        def second(j, held):
            total, mixed = held
            powers = jnp.exp(score_ref[keys_of(j), :] - top)
            total = total + jnp.sum(powers, axis=0, keepdims=True)
            return total, mixed + t_dot(powers.astype(BF16), kv_of(j))

        start = (jnp.zeros((1, columns), F32), jnp.zeros((columns, 2 * HEAD_DIM), F32))
        total, mixed = lax.fori_loop(0, number + 1, second, start)
        sum_ref[number] = top + jnp.log(total)
        inverse = jnp.sum(jnp.where(identity(columns), 1.0 / total, 0.0), axis=1, keepdims=True)
        mixed = (mixed * inverse)[:, HEAD_DIM:]
        out_ref[number] = jnp.concatenate([mixed[:tokens], mixed[tokens:]], axis=1).astype(BF16)
        return carry

    lax.fori_loop(0, blocks, block, 0)


def attention_backward(data, results, scratch):
    query_ref, kv_ref, mix_ref, grad_ref, sum_ref = data
    grad_query_ref, terms_ref = results
    (sum_kv,) = scratch
    blocks, tokens = query_ref.shape[:2]
    chunk, columns = 8 * tokens, 2 * tokens
    factor = HEAD_DIM ** (-0.5)
    sum_kv[...] = jnp.zeros_like(sum_kv)

    def block(number, carry):
        rows = (stack_heads(query_ref[number], True) * factor).astype(BF16)
        grads = stack_heads(grad_ref[number], False)
        both = jnp.concatenate([rows, grads], axis=0)
        pairs = dot_t(stack_heads(mix_ref[number], False), grads)
        delta = jnp.sum(jnp.where(identity(columns), pairs, 0.0), axis=0, keepdims=True)
        logsum = sum_ref[number]

        def unit(j, total, masked):
            keys = pl.ds(pl.multiple_of(j * chunk, chunk), chunk)
            kv = kv_ref[pl.ds(j * 8, 8)].reshape(chunk, 2 * HEAD_DIM)
            products = dot_t(kv, both)
            soft = jnp.exp(products[:, :columns] - logsum)
            if masked:
                soft = jnp.where(causal(soft.shape, tokens), soft, 0.0)
            scores = (soft * (products[:, columns:] - delta)).astype(BF16)
            sum_kv[keys, :] += dot(jnp.concatenate([scores, soft.astype(BF16)], axis=1), both)
            return total + t_dot(scores, kv)

        total = lax.fori_loop(
            0, number, lambda j, held: unit(j, held, False), jnp.zeros((columns, 2 * HEAD_DIM), F32)
        )
        total = unit(number, total, True)[:, :HEAD_DIM] * factor
        grad_query_ref[number] = jnp.concatenate([total[:tokens], total[tokens:]], axis=1)
        return carry

    lax.fori_loop(0, blocks, block, 0)
    terms_ref[...] = sum_kv[...].astype(BF16).reshape(terms_ref.shape)


def forward_body(sizes, *refs):
    kv_send, query_send, grad_ref = refs[:3]
    kv_all, queries, grad_all, mixtures, sums, mixture_back = refs[3:9]
    sems, scores = refs[9:17], refs[17]
    greet([SEQ_AXES], sizes)
    early = launch(sizes, ("context",), pick_target, True, query_send, queries, *sems[0:2])
    early += launch(sizes, SEQ_AXES, pick_context, True, kv_send, kv_all, *sems[2:4])
    late = launch(sizes, ("expert",), pick_whole, True, grad_ref, grad_all, *sems[4:6])
    for copy in early:
        copy.wait()
    attention_forward((queries, kv_all), (mixtures, sums), (scores,))
    late += launch(sizes, ("context",), pick_target, True, mixtures, mixture_back, *sems[6:8])
    for copy in late:
        copy.wait()


def run_forward(cid, sizes, kv_send, query_send, cotangent):
    heads, tokens, columns = query_send.shape
    total, owners = group_size(SEQ_AXES, sizes), sizes["expert"]
    vmem = pl.BlockSpec(memory_space=pltpu.VMEM)
    dma = pltpu.SemaphoreType.DMA
    return pl.pallas_call(
        functools.partial(forward_body, sizes),
        out_shape=[
            jax.ShapeDtypeStruct((total, tokens, columns), BF16),
            jax.ShapeDtypeStruct(query_send.shape, BF16),
            jax.ShapeDtypeStruct((owners, *cotangent.shape), BF16),
            jax.ShapeDtypeStruct(query_send.shape, BF16),
            jax.ShapeDtypeStruct((heads, 1, 2 * tokens), F32),
            jax.ShapeDtypeStruct(query_send.shape, BF16),
        ],
        in_specs=[vmem] * 3,
        out_specs=[vmem] * 6,
        scratch_shapes=[
            *[dma((n,)) for n in (heads, total, owners, heads) for _ in range(2)],
            pltpu.VMEM((total * tokens, 2 * tokens), F32),
        ],
        name="attention_forward",
        compiler_params=pltpu.CompilerParams(
            collective_id=cid, has_side_effects=True, vmem_limit_bytes=60_000_000
        ),
    )(kv_send, query_send, cotangent)


def backward_body(sizes, *refs):
    owns, others, y_ref, data, refs = refs[:3], refs[3:6], refs[6], refs[7:12], refs[12:]
    y_back, kv_back, query_back, *totals = refs[:6]
    sends, gots, sends_2, gots_2 = refs[6:9], refs[9:12], refs[12:15], refs[15:18]
    grad_query, terms, sum_kv = refs[18:21]
    sems = refs[21:]
    dp, side = lax.axis_index("dp"), lax.axis_index("context") // 2
    experts = owns[0].shape[0]
    firsts = (("dp",), ("dp",), ("side",))
    seconds = (("side",), ("side",), ("dp",))

    def chip_sum(i, expert, place):
        return owns[i][expert, place] + others[i][expert, place].astype(F32)

    for i, axes in enumerate(firsts):

        def fill(expert, carry, i=i, axes=axes):
            for d in range(4):
                for v in range(2):
                    terms_now = chip_sum(i, expert, 2 * d + v).astype(BF16)
                    if axes == ("dp",):
                        sends[i][d, expert, v] = terms_now
                    else:
                        sends[i][v, expert, d] = terms_now
            return carry

        lax.fori_loop(0, experts, fill, 0)
    greet([SEQ_AXES, ("dp",)], sizes)
    stage_1 = []
    for i, axes in enumerate(firsts):
        stage_1 += launch(sizes, axes, pick_target, False, sends[i], gots[i], *sems[2 * i : 2 * i + 2])
    rest = launch(sizes, ("expert",), pick_target, True, y_ref, y_back, *sems[6:8])

    attention_backward(data, (grad_query, terms), (sum_kv,))
    rest += launch(sizes, SEQ_AXES, pick_target, True, terms, kv_back, *sems[8:10])
    rest += launch(sizes, ("context",), pick_target, True, grad_query, query_back, *sems[10:12])
    for copy in stage_1:
        copy.wait()

    def part(i, expert, place):
        if firsts[i] == ("dp",):
            total = chip_sum(i, expert, 2 * dp + place)
            for step in range(1, 4):
                total = total + gots[i][lax.rem(dp + step, 4), expert, place].astype(F32)
            return total
        return chip_sum(i, expert, 2 * place + side) + gots[i][1 - side, expert, place].astype(F32)

    for i, axes in enumerate(seconds):

        def refill(expert, carry, i=i, axes=axes):
            for place in range(group_size(axes, sizes)):
                sends_2[i][place, expert] = part(i, expert, place).astype(BF16)
            return carry

        lax.fori_loop(0, experts, refill, 0)
    stage_2 = []
    for i, axes in enumerate(seconds):
        stage_2 += launch(
            sizes, axes, pick_target, False, sends_2[i], gots_2[i], *sems[12 + 2 * i : 14 + 2 * i]
        )
    for copy in stage_2:
        copy.wait()
    for i, axes in enumerate(seconds):
        me, total = own_index(axes, sizes), group_size(axes, sizes)

        def close(expert, carry, i=i, me=me, total=total):
            held = part(i, expert, me)
            for step in range(1, total):
                held = held + gots_2[i][lax.rem(me + step, total), expert].astype(F32)
            totals[i][expert] = held
            return carry

        lax.fori_loop(0, experts, close, 0)
    for copy in rest:
        copy.wait()


def run_backward(cid, sizes, owns, others, y_terms, data):
    queries, kv_all = data[:2]
    tokens = queries.shape[1]
    experts = owns[0].shape[0]
    vmem = pl.BlockSpec(memory_space=pltpu.VMEM)
    tiles = [own.shape[2:] for own in owns]
    stage_1 = [(4, experts, 2, *tiles[0]), (4, experts, 2, *tiles[1]), (2, experts, 4, *tiles[2])]
    stage_2 = [(2, experts, *tiles[0]), (2, experts, *tiles[1]), (4, experts, *tiles[2])]
    sizes_of = [4, 4, 2, sizes["expert"], group_size(SEQ_AXES, sizes), sizes["context"], 2, 2, 4]
    dma = pltpu.SemaphoreType.DMA
    return pl.pallas_call(
        functools.partial(backward_body, sizes),
        out_shape=[
            jax.ShapeDtypeStruct(y_terms.shape, BF16),
            jax.ShapeDtypeStruct(kv_all.shape, BF16),
            jax.ShapeDtypeStruct(queries.shape, F32),
            *[jax.ShapeDtypeStruct((experts, *tile), F32) for tile in tiles],
        ],
        in_specs=[vmem] * 12,
        out_specs=[vmem] * 6,
        scratch_shapes=[
            *[pltpu.VMEM(shape, BF16) for shape in stage_1 * 2 + stage_2 * 2],
            pltpu.VMEM(queries.shape, F32),
            pltpu.VMEM(kv_all.shape, BF16),
            pltpu.VMEM((kv_all.shape[0] * tokens, 2 * HEAD_DIM), F32),
            *[dma((n,)) for n in sizes_of for _ in range(2)],
        ],
        name="attention_backward",
        compiler_params=pltpu.CompilerParams(
            collective_id=cid, has_side_effects=True, vmem_limit_bytes=67_043_328
        ),
    )(*owns, *others, y_terms, *data)


def moe_copies(sizes, refs):
    moe_ref, table_ref, moe_land, table_land, d_send, d_back, dots, dot_back, g_sends, g_backs, sems = refs
    owners = sizes["expert"]
    owner, context = lax.axis_index("expert"), lax.axis_index("context")

    def pair_of(copies, target, number):
        return [
            pltpu.make_async_remote_copy(
                src_ref=src,
                dst_ref=dst,
                send_sem=send.at[number],
                recv_sem=recv.at[number],
                device_id={"expert": target},
                device_id_type=MESH_ID,
            )
            for src, dst, send, recv in copies
        ]

    def tokens_to(number):
        pairs = (
            (table_ref, table_land.at[number], sems[7], sems[8]),
            (moe_ref, moe_land.at[number], sems[9], sems[10]),
        )
        return pair_of(pairs, lax.rem(owner + number, owners), number)

    def results_of(number):
        target = lax.rem(owner + owners - number, owners)
        pairs = (
            (d_send.at[target], d_back.at[owner], sems[0], sems[1]),
            (dots.at[target], dot_back.at[owner], sems[2], sems[3]),
        )
        return pair_of(pairs, target, number)

    def own_results():
        return [
            pltpu.make_async_copy(d_send.at[owner], d_back.at[owner], sems[0].at[0]),
            pltpu.make_async_copy(dots.at[owner], dot_back.at[owner], sems[2].at[0]),
        ]

    def halves(number):
        partner = context + 1 - 2 * lax.rem(context, 2)
        return [
            pltpu.make_async_remote_copy(
                src_ref=g_sends[i].at[number],
                dst_ref=g_backs[i].at[number],
                send_sem=sems[4].at[3 * number + i],
                recv_sem=sems[5].at[3 * number + i],
                device_id={"context": partner},
                device_id_type=MESH_ID,
            )
            for i in range(3)
        ]

    return tokens_to, results_of, own_results, halves


def moe_body(
    sizes,
    moe_ref,
    table_ref,
    grad_ref,
    wg_ref,
    wu_ref,
    wd_ref,
    own_g,
    own_u,
    own_d,
    back_g,
    back_u,
    back_d,
    y_out,
    d_back,
    dot_back,
    moe_land,
    table_land,
    x_all,
    g_now,
    deo_all,
    dgu_all,
    eh_all,
    eo_all,
    dbuf_all,
    picks,
    highs,
    lows,
    gate_col,
    dot_col,
    dots,
    y_send,
    d_send,
    send_g,
    send_u,
    send_d,
    *sems,
):
    step = pl.program_id(0)
    owners = sizes["expert"]
    owner, context = lax.axis_index("expert"), lax.axis_index("context")
    core = lax.rem(context, 2)
    mine = 4
    group = owners // 2
    tokens, width = moe_ref.shape
    hidden_width = wg_ref.shape[2]
    rows = group * CAP
    barrier = pltpu.get_barrier_semaphore()
    tokens_to, results_of, own_results, halves = moe_copies(
        sizes,
        (
            moe_ref,
            table_ref,
            moe_land,
            table_land,
            d_send,
            d_back,
            dots,
            dot_back,
            (send_g, send_u, send_d),
            (back_g, back_u, back_d),
            sems,
        ),
    )

    @pl.when(step == 0)
    def _():
        for number in range(1, owners):
            pl.semaphore_signal(
                barrier,
                inc=1,
                device_id={"expert": lax.rem(owner + number, owners)},
                device_id_type=MESH_ID,
            )
        pl.semaphore_signal(
            barrier, inc=1, device_id={"context": context + 1 - 2 * core}, device_id_type=MESH_ID
        )
        pl.semaphore_wait(barrier, owners)
        for number in range(1, owners):
            for copy in tokens_to(number):
                copy.start()
        dots[...] = jnp.zeros_like(dots)
        moe_land[0] = moe_ref[...]
        table_land[0] = table_ref[...]
        for number in range(1, group):
            for copy in tokens_to(number):
                copy.wait_recv()

    @pl.when(step == mine)
    def _():
        for copy in own_results():
            copy.start()
        for number in range(1, group):
            for copy in results_of(number):
                copy.start()
        for number in range(group, owners):
            for copy in tokens_to(number):
                copy.wait_recv()

    @pl.when(step == 2 * mine)
    def _():
        for number in range(group, owners):
            for copy in results_of(number):
                copy.start()
        pltpu.make_async_copy(y_send, y_out, sems[6].at[0]).start()

    for number in range(mine):

        @pl.when(step == 2 * mine + 1 + number)
        def _(number=number):
            for copy in halves(number):
                copy.start()

    @pl.when(step < 2 * mine)
    def _():
        expert, tile = lax.rem(step, mine), step // mine
        place = pl.multiple_of(expert * CAP, CAP)
        spot = pl.ds(place, CAP)
        here = pl.ds(pl.multiple_of(tile * rows, rows), rows)
        part = pl.ds(tile * group, group)
        table = jnp.concatenate(
            [table_land[tile * group + j, pl.ds(owner * mine + expert, 1), :] for j in range(group)], axis=0
        )
        table = jnp.concatenate([table, table], axis=0)
        named = table >= 0.0
        above = lax.broadcasted_iota(jnp.int32, (tokens, tokens), 0)
        beside = lax.broadcasted_iota(jnp.int32, (tokens, tokens), 1)
        before = (above < beside).astype(F32).astype(BF16)
        slots = dot(named.astype(F32).astype(BF16), before)
        slots = jnp.where(named, slots, -1.0)
        counts = lax.broadcasted_iota(jnp.int32, (CAP, tokens), 0).astype(F32)
        for j in range(group):
            position = tile * group + j
            source = lax.rem(owner + owners - position, owners)
            chosen = counts == slots[j : j + 1]
            onehot = jnp.where(chosen, 1.0, 0.0).astype(BF16)
            weight = jnp.where(chosen, table[j : j + 1], 0.0)
            high = weight.astype(BF16)
            picks[position, spot, :] = onehot
            highs[position, spot, :] = high
            lows[position, spot, :] = (weight - high.astype(F32)).astype(BF16)
            gate_col[j * CAP : (j + 1) * CAP, :] = jnp.sum(weight, axis=1, keepdims=True)
            line = pl.ds(pl.multiple_of(tile * rows + j * CAP, CAP), CAP)
            x_all[expert, line, :] = dot(onehot, moe_land[position]).astype(BF16)
            g_now[j * CAP : (j + 1) * CAP, :] = dot(onehot, grad_ref[source]).astype(BF16)

        rows_in = x_all[expert, here, :]
        gate_act = dot(rows_in, wg_ref[0])
        up_act = dot(rows_in, wu_ref[0])
        sigma = jax.nn.sigmoid(gate_act)
        silu = gate_act * sigma
        hidden = (silu * up_act).astype(BF16)
        eh_all[expert, here, :] = hidden
        expert_out = dot(hidden, wd_ref[0]).astype(BF16)
        eo_all[part, spot, :] = expert_out.reshape(group, CAP, width)
        grads = g_now[...].astype(F32)
        dot_col[...] = jnp.sum(grads * expert_out.astype(F32), axis=1, keepdims=True)
        grad_expert = (gate_col[...] * grads).astype(BF16)
        deo_all[expert, here, :] = grad_expert
        grad_hidden = dot_t(grad_expert, wd_ref[0])
        slope = sigma * (1.0 + gate_act * (1.0 - sigma))
        grad_gate = (grad_hidden * up_act * slope).astype(BF16)
        grad_up = (grad_hidden * silu).astype(BF16)
        dgu_all[expert, here, :hidden_width] = grad_gate
        dgu_all[expert, here, hidden_width:] = grad_up
        grad_buffer = (dot_t(grad_gate, wg_ref[0]) + dot_t(grad_up, wu_ref[0])).astype(BF16)
        dbuf_all[part, spot, :] = grad_buffer.reshape(group, CAP, width)
        for j in range(group):
            position = tile * group + j
            source = lax.rem(owner + owners - position, owners)
            onehot = picks[position, spot, :].astype(F32)
            dots[source, pl.ds(expert, 1), :] = jnp.sum(
                onehot * dot_col[j * CAP : (j + 1) * CAP, :], axis=0, keepdims=True
            )

        @pl.when(expert == mine - 1)
        def _():
            def combine(j, carry):
                position = tile * group + j
                source = lax.rem(owner + owners - position, owners)
                d_send[source] = t_dot(picks[position], dbuf_all[position]).astype(BF16)
                moved = t_dot(highs[position], eo_all[position]) + t_dot(lows[position], eo_all[position])
                y_send[source] = moved.astype(BF16)
                return carry

            lax.fori_loop(0, group, combine, 0)

    @pl.when((step >= 2 * mine) & (step < 3 * mine))
    def _():
        number = step - 2 * mine
        blocks = width // 256
        per = width // 16

        def gate_rows(j, carry):
            columns = pl.ds(pl.multiple_of(j * 256, 256), 256)
            rows_in = x_all[number, :, columns]
            for half, own, send in ((0, own_g, send_g), (1, own_u, send_u)):
                grads = dgu_all[number, :, half * hidden_width : (half + 1) * hidden_width]
                terms = t_dot(rows_in, grads).reshape(128 // per, 2, per, hidden_width)
                first, second = terms[:, 0], terms[:, 1]
                places = pl.ds(j * (128 // per), 128 // per)
                own[0, places] = jnp.where(core == 0, first, second)
                send[number, places] = jnp.where(core == 0, second, first).astype(BF16)
            return carry

        lax.fori_loop(0, blocks, gate_rows, 0)
        less = hidden_width // 16

        def down_rows(j, carry):
            columns = pl.ds(pl.multiple_of(j * 256, 256), 256)
            terms = t_dot(eh_all[number, :, columns], deo_all[number])
            terms = terms.reshape(128 // less, 2, less, width)
            first, second = terms[:, 0], terms[:, 1]
            places = pl.ds(j * (128 // less), 128 // less)
            own_d[0, places] = jnp.where(core == 0, first, second)
            send_d[number, places] = jnp.where(core == 0, second, first).astype(BF16)
            return carry

        lax.fori_loop(0, hidden_width // 256, down_rows, 0)

    @pl.when(step == 3 * mine)
    def _():
        for number in range(1, owners):
            for copy in tokens_to(number):
                copy.wait_send()
            for copy in results_of(number):
                copy.wait()
        for copy in own_results():
            copy.wait()
        pltpu.make_async_copy(y_send, y_out, sems[6].at[0]).wait()
        for number in range(mine):
            for copy in halves(number):
                copy.wait()


def run_experts(cid, sizes, moe_input, table, grad_all, gate_weight, up_weight, down_weight):
    owners, tokens, width = grad_all.shape
    mine, _, inner = gate_weight.shape
    rows = owners * CAP
    part, less = width // 16, inner // 16

    def fixed(array):
        return pl.BlockSpec(array.shape, lambda i: (0,) * array.ndim, pipeline_mode=pl.Buffered(1))

    def expert_block(array):
        return pl.BlockSpec((1, *array.shape[1:]), lambda i: (lax.rem(jnp.minimum(i, 2 * mine - 1), mine), 0, 0))

    def own_block(*shape):
        return pl.BlockSpec((1, *shape), lambda i: (jnp.clip(i - 2 * mine, 0, mine - 1), 0, 0, 0))

    anywhere = pl.BlockSpec(memory_space=pl.ANY)
    wide, tall = (8, part, inner), (8, less, width)
    dma = pltpu.SemaphoreType.DMA
    return pl.pallas_call(
        functools.partial(moe_body, sizes),
        grid=(3 * mine + 1,),
        out_shape=[
            jax.ShapeDtypeStruct((mine, *wide), F32),
            jax.ShapeDtypeStruct((mine, *wide), F32),
            jax.ShapeDtypeStruct((mine, *tall), F32),
            jax.ShapeDtypeStruct((mine, *wide), BF16),
            jax.ShapeDtypeStruct((mine, *wide), BF16),
            jax.ShapeDtypeStruct((mine, *tall), BF16),
            jax.ShapeDtypeStruct((owners, tokens, width), BF16),
            jax.ShapeDtypeStruct((owners, tokens, width), BF16),
            jax.ShapeDtypeStruct((owners, 8, tokens), F32),
        ],
        in_specs=[
            fixed(moe_input),
            fixed(table),
            fixed(grad_all),
            expert_block(gate_weight),
            expert_block(up_weight),
            expert_block(down_weight),
        ],
        out_specs=[own_block(*wide), own_block(*wide), own_block(*tall), *([anywhere] * 6)],
        scratch_shapes=[
            pltpu.VMEM(grad_all.shape, BF16),
            pltpu.VMEM((owners, *table.shape), F32),
            pltpu.VMEM((mine, rows, width), BF16),
            pltpu.VMEM((rows // 2, width), BF16),
            pltpu.VMEM((mine, rows, width), BF16),
            pltpu.VMEM((mine, rows, 2 * inner), BF16),
            pltpu.VMEM((mine, rows, inner), BF16),
            pltpu.VMEM((owners, mine * CAP, width), BF16),
            pltpu.VMEM((owners, mine * CAP, width), BF16),
            pltpu.VMEM((owners, mine * CAP, tokens), BF16),
            pltpu.VMEM((owners, mine * CAP, tokens), BF16),
            pltpu.VMEM((owners, mine * CAP, tokens), BF16),
            pltpu.VMEM((rows // 2, 1), F32),
            pltpu.VMEM((rows // 2, 1), F32),
            pltpu.VMEM((owners, 8, tokens), F32),
            pltpu.VMEM((owners, tokens, width), BF16),
            pltpu.VMEM((owners, tokens, width), BF16),
            pltpu.VMEM((mine, *wide), BF16),
            pltpu.VMEM((mine, *wide), BF16),
            pltpu.VMEM((mine, *tall), BF16),
            dma((owners,)),
            dma((owners,)),
            dma((owners,)),
            dma((owners,)),
            dma((3 * mine,)),
            dma((3 * mine,)),
            dma((1,)),
            *[dma((owners,))] * 4,
        ],
        name="run_experts",
        compiler_params=pltpu.CompilerParams(
            collective_id=cid, has_side_effects=True, vmem_limit_bytes=67_043_328
        ),
    )(moe_input, table, grad_all, gate_weight, up_weight, down_weight)


CHIP_AXES = ("dp", "side", "expert")


def sum_body(sizes, *refs):
    query_in, key_in, value_in, output_in, narrow_in = refs[:5]
    whole, load, near, sums, got = refs[5:10]
    near_send, near_recv, send_sems, recv_sems, give_sems, take_sems, pass_sems, land_sems = refs[10:]
    core = lax.rem(lax.axis_index("context"), 2)
    partner = {"context": lax.axis_index("context") + 1 - 2 * core}
    me, total = own_index(CHIP_AXES, sizes), group_size(CHIP_AXES, sizes)
    plane = total // sizes["dp"]
    rows = load.shape[1]
    some, wide = rows // 2, query_in.shape[1]
    half = wide // 2

    def place(step):
        target = lax.rem(me + step, total)
        return target, coords_of(CHIP_AXES, sizes, target)

    def remote(src, dst, send, recv, peer):
        return pltpu.make_async_remote_copy(
            src_ref=src, dst_ref=dst, send_sem=send, recv_sem=recv, device_id=peer, device_id_type=MESH_ID
        )

    def reduce_copy(step):
        target, peer = place(step)
        return remote(sums.at[target], got.at[me], send_sems.at[step], recv_sems.at[step], peer)

    def gather_copy(step):
        _, peer = place(step)
        own = whole.at[core, me]
        return remote(own, own, give_sems.at[step], take_sems.at[step], peer)

    def pass_copy(step):
        source = whole.at[core, lax.rem(me - step + total, total)]
        return remote(source, source, pass_sems.at[step], land_sems.at[step], partner)

    def near_copy(turn):
        chunks = pl.ds(lax.rem(lax.axis_index("dp") + turn, sizes["dp"]) * plane, plane)
        return remote(load.at[chunks], near.at[chunks], near_send.at[turn], near_recv.at[turn], partner)

    def each(start, stop, body):
        def run(step, carry):
            body(step)
            return carry

        lax.fori_loop(start, stop, run, 0)

    def pack(number, chunk):
        here = pl.ds(pl.multiple_of(chunk * rows, rows), rows)
        there = pl.ds(pl.multiple_of(chunk * some, some), some)
        if number == 0:
            parts = [query_in[here, :]]
        else:
            parts = [key_in[here, :], value_in[here, :]]
        start = number * wide
        output = jnp.concatenate(
            [output_in[there, start : start + half], output_in[there, start + half : start + wide]], axis=0
        )
        return jnp.concatenate([*parts, output, narrow_in[here, :]], axis=1)

    barrier = pltpu.get_barrier_semaphore()
    pl.semaphore_signal(barrier, inc=1, device_id=partner, device_id_type=MESH_ID)
    each(
        1,
        total,
        lambda step: pl.semaphore_signal(
            barrier, inc=1, device_id=place(step)[1], device_id_type=MESH_ID
        ),
    )
    for number in range(2):

        @pl.when(core == 1 - number)
        def _(number=number):
            def fill(chunk):
                load[chunk] = pack(number, chunk).astype(BF16)

            each(0, total, fill)

    pl.semaphore_wait(barrier, total)
    for turn in range(sizes["dp"]):
        near_copy(turn).start()

    for turn in range(sizes["dp"]):
        near_copy(turn).wait()
        base = lax.rem(lax.axis_index("dp") + turn, sizes["dp"]) * plane
        for number in range(2):

            @pl.when(core == number)
            def _(number=number, base=base):
                def add(chunk):
                    sums[chunk] = (pack(number, chunk) + near[chunk].astype(F32)).astype(BF16)

                each(base, base + plane, add)

        def send(i, base=base):
            target = base + lax.rem(me + i, plane)

            @pl.when(target != me)
            def _():
                reduce_copy(lax.rem(target - me + total, total)).start()

        each(0, plane, send)

    got[me] = sums[me]
    each(1, total, lambda step: reduce_copy(step).wait())
    result = lax.fori_loop(
        0, total, lambda i, held: held + got[i].astype(F32), jnp.zeros(got.shape[1:], F32)
    )
    whole[core, me] = result.astype(BF16)
    each(1, total, lambda step: gather_copy(step).start())
    pass_copy(0).start()

    def forward(step):
        gather_copy(step).wait_recv()
        pass_copy(step).start()

    each(1, total, forward)
    each(1, total, lambda step: gather_copy(step).wait_send())
    each(0, total, lambda step: pass_copy(step).wait())


def unpack_body(whole, query_out, key_out, value_out, output_out, narrow_out):
    chunks, rows = whole.shape[1:3]
    some, wide = rows // 2, query_out.shape[1]
    half = wide // 2
    for chunk in range(chunks):
        here = slice(chunk * rows, (chunk + 1) * rows)
        there = slice(chunk * some, (chunk + 1) * some)
        for number in range(2):
            block = whole[number, chunk].astype(F32)
            if number == 0:
                query_out[here, :] = block[:, :wide]
                narrow_out[here, :] = block[:, wide + half :]
            else:
                key_out[here, :] = block[:, :half]
                value_out[here, :] = block[:, half:wide]
            start = number * wide
            output_out[there, start : start + half] = block[:some, wide : wide + half]
            output_out[there, start + half : start + wide] = block[some:, wide : wide + half]


def sum_everywhere(cid, sizes, *arrays):
    total = group_size(CHIP_AXES, sizes)
    depth, wide = arrays[0].shape
    half = (total, depth // total, wide + wide // 2 + arrays[4].shape[1])
    dma = pltpu.SemaphoreType.DMA
    vmem = pl.BlockSpec(memory_space=pltpu.VMEM)
    whole = pl.pallas_call(
        functools.partial(sum_body, sizes),
        out_shape=jax.ShapeDtypeStruct((2, *half), BF16),
        in_specs=[vmem] * 5,
        out_specs=vmem,
        scratch_shapes=[pltpu.VMEM(half, BF16)] * 4
        + [dma((sizes["dp"],))] * 2
        + [dma((total,))] * 6,
        name="sum_everywhere",
        compiler_params=pltpu.CompilerParams(
            collective_id=cid, has_side_effects=True, vmem_limit_bytes=60_000_000
        ),
    )(*arrays)
    parts = 4
    return pl.pallas_call(
        unpack_body,
        grid=(parts,),
        out_shape=[jax.ShapeDtypeStruct(array.shape, F32) for array in arrays],
        in_specs=[pl.BlockSpec((2, total // parts, *half[1:]), lambda i: (0, i, 0, 0))],
        out_specs=[
            pl.BlockSpec((array.shape[0] // parts, array.shape[1]), lambda i: (i, 0)) for array in arrays
        ],
        name="unpack_sums",
    )(whole)


def rope_tables(positions, head_size):
    half_dim = head_size // 2
    frequency = ROPE_BASE ** (-2.0 * jnp.arange(half_dim, dtype=F32) / head_size)
    angles = positions.astype(F32)[:, None] * frequency[None, :]
    angles = jnp.concatenate([angles, angles], axis=1)
    return (jnp.cos(angles), jnp.sin(angles))


def rotate(values, cosine, sine_table):
    half_dim = values.shape[-1] // 2
    turned = jnp.concatenate([-values[..., half_dim:], values[..., :half_dim]], axis=-1)
    return values * cosine[:, None, :] + turned * sine_table[:, None, :]


def rotate_back(grads, cosine, sine_table):
    half_dim = grads.shape[-1] // 2
    scaled = grads * sine_table[:, None, :]
    turned = jnp.concatenate([scaled[..., half_dim:], -scaled[..., :half_dim]], axis=-1)
    return grads * cosine[:, None, :] + turned


def norm_forward(values, gain_vec):
    inverse = lax.rsqrt(jnp.mean(values * values, axis=-1, keepdims=True) + EPSILON)
    normed = values * inverse
    return (inverse, normed, (normed * gain_vec).astype(BF16))


def norm_backward(grad_out, normed, inverse, gain_vec):
    gain_grad = jnp.sum(grad_out * normed, axis=0)
    scaled = grad_out * gain_vec
    inner = jnp.mean(scaled * normed, axis=-1, keepdims=True)
    return (gain_grad, inverse * (scaled - normed * inner))


def local(
    sizes,
    inputs,
    prenorm_gain,
    query_weight,
    key_weight,
    value_weight,
    output_weight,
    midnorm_gain,
    router_weight,
    gate_weight,
    up_weight,
    down_weight,
    expert_ids,
    cotangent,
):
    tokens, width = inputs.shape[1:]
    owners = sizes["expert"]
    mine = gate_weight.shape[0]
    context, owner = lax.axis_index("context"), lax.axis_index("expert")
    block = context * owners + owner
    positions = block * tokens + jnp.arange(tokens, dtype=jnp.int32)
    cosine, sine_table = rope_tables(positions, HEAD_DIM)

    input_float = inputs[0].astype(F32)
    inverse_first, normed_first, attn_input = norm_forward(input_float, prenorm_gain)
    query_raw = dot(attn_input, query_weight).reshape(tokens, HEADS, HEAD_DIM)
    key_raw = dot(attn_input, key_weight).reshape(tokens, KV_HEADS, HEAD_DIM)
    value_raw = dot(attn_input, value_weight).reshape(tokens, KV_HEADS, HEAD_DIM)
    query_rot = rotate(query_raw, cosine, sine_table).astype(BF16)
    key_rot = rotate(key_raw, cosine, sine_table).astype(BF16)
    query_send = query_rot.reshape(tokens, KV_HEADS, 2 * HEAD_DIM).transpose(1, 0, 2)
    kv_send = jnp.concatenate([key_rot, value_raw.astype(BF16)], axis=2).transpose(1, 0, 2)
    kv_all, queries, grad_all, mixtures, sums, mixture = run_forward(
        0, sizes, kv_send, query_send, cotangent[0]
    )
    mixture_flat = mixture.transpose(1, 0, 2).reshape(tokens, HEADS * HEAD_DIM)

    after_attn = input_float + dot(mixture_flat, output_weight)
    inverse_second, normed_second, moe_input = norm_forward(after_attn, midnorm_gain)
    logits = lax.dot_general(
        router_weight, moe_input, (((0,), (1,)), ((), ())), preferred_element_type=F32
    )
    numbers = jnp.arange(EXPERTS, dtype=jnp.int32)[:, None, None]
    chosen = jnp.any(expert_ids[0].T[None] == numbers, axis=1)
    masked = jnp.where(chosen, logits, -jnp.inf)
    powers = jnp.exp(masked - jnp.max(masked, axis=0, keepdims=True))
    gates = powers / jnp.sum(powers, axis=0, keepdims=True)
    gate_table = jnp.where(chosen, gates, -1.0)

    own_g, own_u, own_d, other_g, other_u, other_d, moe_terms, grad_back, dot_back = run_experts(
        3, sizes, moe_input, gate_table, grad_all, gate_weight, up_weight, down_weight
    )
    grad_gates = dot_back[:, :mine].reshape(EXPERTS, tokens)
    grad_logits = gates * (grad_gates - jnp.sum(gates * grad_gates, axis=0, keepdims=True))
    router_grad = jnp.einsum(
        "td,et->de", moe_input.astype(F32), grad_logits, precision=lax.Precision.HIGHEST
    )
    grad_moe_in = jnp.sum(grad_back.astype(F32), axis=0) + jnp.einsum(
        "et,de->td", grad_logits, router_weight.astype(F32), precision=lax.Precision.HIGHEST
    )
    grad_out = cotangent[0].astype(F32)
    midnorm_grad, grad_after = norm_backward(grad_moe_in, normed_second, inverse_second, midnorm_gain)
    grad_after = grad_out + grad_after
    grad_after_half = grad_after.astype(BF16)
    output_grad = t_dot(mixture_flat, grad_after_half)
    grad_mix = dot_t(grad_after_half, output_weight).astype(BF16)
    grad_mix = grad_mix.reshape(tokens, KV_HEADS, 2 * HEAD_DIM).transpose(1, 0, 2)
    (grad_mixtures,) = exchange(4, sizes, "send_grad_mixture", (grad_mix, ("context",), pick_target))
    moe_back, kv_back, grad_query, gate_sum, up_sum, down_sum = run_backward(
        8,
        sizes,
        (own_g, own_u, own_d),
        (other_g, other_u, other_d),
        moe_terms,
        (queries, kv_all, mixtures, grad_mixtures, sums),
    )
    outputs = (after_attn + jnp.sum(moe_back.astype(F32), axis=0)).astype(BF16)
    grad_kv = jnp.sum(kv_back.astype(F32).reshape(KV_HEADS, owners, tokens, 2 * HEAD_DIM), axis=1)
    grad_kv = grad_kv.transpose(1, 0, 2)
    grad_query = grad_query.transpose(1, 0, 2).reshape(tokens, HEADS, HEAD_DIM)
    query_back = rotate_back(grad_query, cosine, sine_table).reshape(tokens, -1).astype(BF16)
    key_back = rotate_back(grad_kv[..., :HEAD_DIM], cosine, sine_table).reshape(tokens, -1).astype(BF16)
    value_back = grad_kv[..., HEAD_DIM:].reshape(tokens, -1).astype(BF16)
    query_grad = t_dot(attn_input, query_back)
    key_grad = t_dot(attn_input, key_back)
    value_grad = t_dot(attn_input, value_back)
    grad_attn_in = (
        dot_t(query_back, query_weight) + dot_t(key_back, key_weight) + dot_t(value_back, value_weight)
    )
    prenorm_grad, grad_inputs = norm_backward(grad_attn_in, normed_first, inverse_first, prenorm_gain)
    grad_inputs = grad_after + grad_inputs
    narrow = jnp.concatenate([router_grad, prenorm_grad[:, None], midnorm_grad[:, None]], axis=1)
    narrow = jnp.pad(narrow, ((0, 0), (0, 128 - EXPERTS - 2)))
    query_grad, key_grad, value_grad, output_grad, narrow = sum_everywhere(
        9, sizes, query_grad, key_grad, value_grad, output_grad, narrow
    )
    dense = (
        narrow[:, EXPERTS],
        query_grad,
        key_grad,
        value_grad,
        output_grad,
        narrow[:, EXPERTS + 1],
        narrow[:, :EXPERTS],
    )
    return (outputs[None], grad_inputs[None], *dense, gate_sum, up_sum, down_sum)


def solution(mesh):
    split = P("dp", ("context", "expert"), None)
    owned = P("expert", None, None)
    summed = P("expert", ("dp", "context"), None)
    in_specs = (split, *([P()] * 7), owned, owned, owned, split, split)
    out_specs = (split, split, *([P()] * 7), summed, summed, summed)
    return jax.shard_map(
        functools.partial(local, dict(mesh.shape)),
        mesh=mesh,
        in_specs=in_specs,
        out_specs=out_specs,
        check_vma=False,
    )
```

```python
import functools

import jax
import jax.numpy as jnp
from jax import lax
from jax.experimental import pallas as pl
from jax.experimental.pallas import tpu as pltpu
from jax.sharding import PartitionSpec as P

HEADS = 8
KV_HEADS = 4
HEAD_DIM = 64
EXPERTS = 32
TOP = 8
CAP = 64
EPSILON = 1e-06
ROPE_BASE = 10000.0
F32 = jnp.float32
BF16 = jnp.bfloat16
MESH_ID = pl.DeviceIdType.MESH
SEQ_AXES = ("context", "expert")


def dot(left, right):
    return jnp.dot(left, right, preferred_element_type=F32)


def dot_t(left, right):
    return lax.dot_general(left, right, (((1,), (1,)), ((), ())), preferred_element_type=F32)


def t_dot(left, right):
    return lax.dot_general(left, right, (((0,), (0,)), ((), ())), preferred_element_type=F32)


def axis_size(sizes, name):
    return 2 if name == "side" else sizes[name]


def group_size(axes, sizes):
    total = 1
    for name in axes:
        total *= axis_size(sizes, name)
    return total


def own_index(axes, sizes):
    index = 0
    for name in axes:
        own = lax.axis_index("context") // 2 if name == "side" else lax.axis_index(name)
        index = index * axis_size(sizes, name) + own
    return index


def coords_of(axes, sizes, index):
    out = {}
    for name in reversed(axes):
        place = lax.rem(index, axis_size(sizes, name))
        if name == "side":
            out["context"] = place * 2 + lax.rem(lax.axis_index("context"), 2)
        else:
            out[name] = place
        index = index // axis_size(sizes, name)
    return out


def pick_whole(ref, target, peer):
    return ref


def pick_target(ref, target, peer):
    return ref.at[target]


def pick_context(ref, target, peer):
    return ref.at[peer["context"]]


def greet(all_axes, sizes):
    barrier = pltpu.get_barrier_semaphore()
    groups = []
    for axes in all_axes:
        if not any(set(axes) <= set(other) for other in groups):
            groups = [other for other in groups if not set(other) <= set(axes)] + [axes]
    signals = 0
    for axes in groups:
        me, total = own_index(axes, sizes), group_size(axes, sizes)
        for step in range(1, total):
            peer = coords_of(axes, sizes, lax.rem(me + step, total))
            pl.semaphore_signal(barrier, inc=1, device_id=peer, device_id_type=MESH_ID)
        signals += total - 1
    pl.semaphore_wait(barrier, signals)


def launch(sizes, axes, pick, keep, source, landing, send, recv):
    started = []
    me, total = own_index(axes, sizes), group_size(axes, sizes)
    for step in range(1, total):
        target = lax.rem(me + step, total)
        peer = coords_of(axes, sizes, target)
        copy = pltpu.make_async_remote_copy(
            src_ref=pick(source, target, peer),
            dst_ref=landing.at[me],
            send_sem=send.at[step],
            recv_sem=recv.at[step],
            device_id=peer,
            device_id_type=MESH_ID,
        )
        copy.start()
        started.append(copy)
    if keep:
        own = pltpu.make_async_copy(
            pick(source, me, coords_of(axes, sizes, me)), landing.at[me], send.at[0]
        )
        own.start()
        started.append(own)
    return started


def stack_heads(block, low):
    tokens = block.shape[0]
    zero = jnp.zeros((tokens, HEAD_DIM), block.dtype)
    parts = [block[:, :HEAD_DIM], block[:, HEAD_DIM:]]
    return jnp.concatenate(
        [jnp.concatenate([part, zero] if low else [zero, part], axis=1) for part in parts], axis=0
    )


def causal(shape, tokens):
    keys = lax.broadcasted_iota(jnp.int32, shape, 0)
    queries = lax.rem(lax.broadcasted_iota(jnp.int32, shape, 1), tokens)
    return keys - queries <= lax.axis_index("expert") * tokens


def identity(size):
    shape = (size, size)
    return lax.broadcasted_iota(jnp.int32, shape, 0) == lax.broadcasted_iota(jnp.int32, shape, 1)


def attention_forward(data, results, scratch):
    query_ref, kv_ref = data
    out_ref, sum_ref = results
    (score_ref,) = scratch
    blocks, tokens = query_ref.shape[:2]
    chunk, columns = 8 * tokens, 2 * tokens

    def block(number, carry):
        rows = stack_heads(query_ref[number], True) * (HEAD_DIM ** (-0.5))
        rows = rows.astype(BF16)

        def keys_of(j):
            return pl.ds(pl.multiple_of(j * chunk, chunk), chunk)

        def kv_of(j):
            return kv_ref[pl.ds(j * 8, 8)].reshape(chunk, 2 * HEAD_DIM)

        def first(j, top):
            scores = dot_t(kv_of(j), rows)
            score_ref[keys_of(j), :] = scores
            return jnp.maximum(top, jnp.max(scores, axis=0, keepdims=True))

        top = lax.fori_loop(0, number, first, jnp.full((1, columns), -jnp.inf, F32))
        scores = dot_t(kv_of(number), rows)
        scores = jnp.where(causal(scores.shape, tokens), scores, -jnp.inf)
        score_ref[keys_of(number), :] = scores
        top = jnp.maximum(top, jnp.max(scores, axis=0, keepdims=True))

        def second(j, held):
            total, mixed = held
            powers = jnp.exp(score_ref[keys_of(j), :] - top)
            total = total + jnp.sum(powers, axis=0, keepdims=True)
            return total, mixed + t_dot(powers.astype(BF16), kv_of(j))

        start = (jnp.zeros((1, columns), F32), jnp.zeros((columns, 2 * HEAD_DIM), F32))
        total, mixed = lax.fori_loop(0, number + 1, second, start)
        sum_ref[number] = top + jnp.log(total)
        inverse = jnp.sum(jnp.where(identity(columns), 1.0 / total, 0.0), axis=1, keepdims=True)
        mixed = (mixed * inverse)[:, HEAD_DIM:]
        out_ref[number] = jnp.concatenate([mixed[:tokens], mixed[tokens:]], axis=1).astype(BF16)
        return carry

    lax.fori_loop(0, blocks, block, 0)


def attention_backward(data, results, scratch):
    query_ref, kv_ref, mix_ref, grad_ref, sum_ref = data
    grad_query_ref, terms_ref = results
    (sum_kv,) = scratch
    blocks, tokens = query_ref.shape[:2]
    chunk, columns = 8 * tokens, 2 * tokens
    factor = HEAD_DIM ** (-0.5)
    sum_kv[...] = jnp.zeros_like(sum_kv)

    def block(number, carry):
        rows = (stack_heads(query_ref[number], True) * factor).astype(BF16)
        grads = stack_heads(grad_ref[number], False)
        both = jnp.concatenate([rows, grads], axis=0)
        pairs = dot_t(stack_heads(mix_ref[number], False), grads)
        delta = jnp.sum(jnp.where(identity(columns), pairs, 0.0), axis=0, keepdims=True)
        logsum = sum_ref[number]

        def unit(j, total, masked):
            keys = pl.ds(pl.multiple_of(j * chunk, chunk), chunk)
            kv = kv_ref[pl.ds(j * 8, 8)].reshape(chunk, 2 * HEAD_DIM)
            products = dot_t(kv, both)
            soft = jnp.exp(products[:, :columns] - logsum)
            if masked:
                soft = jnp.where(causal(soft.shape, tokens), soft, 0.0)
            scores = (soft * (products[:, columns:] - delta)).astype(BF16)
            sum_kv[keys, :] += dot(jnp.concatenate([scores, soft.astype(BF16)], axis=1), both)
            return total + t_dot(scores, kv)

        total = lax.fori_loop(
            0, number, lambda j, held: unit(j, held, False), jnp.zeros((columns, 2 * HEAD_DIM), F32)
        )
        total = unit(number, total, True)[:, :HEAD_DIM] * factor
        grad_query_ref[number] = jnp.concatenate([total[:tokens], total[tokens:]], axis=1)
        return carry

    lax.fori_loop(0, blocks, block, 0)
    terms_ref[...] = sum_kv[...].astype(BF16).reshape(terms_ref.shape)


def forward_body(sizes, *refs):
    kv_send, query_send, grad_ref = refs[:3]
    kv_all, queries, grad_all, mixtures, sums, mixture_back = refs[3:9]
    sems, scores = refs[9:17], refs[17]
    greet([SEQ_AXES], sizes)
    early = launch(sizes, ("context",), pick_target, True, query_send, queries, *sems[0:2])
    early += launch(sizes, SEQ_AXES, pick_context, True, kv_send, kv_all, *sems[2:4])
    late = launch(sizes, ("expert",), pick_whole, True, grad_ref, grad_all, *sems[4:6])
    for copy in early:
        copy.wait()
    attention_forward((queries, kv_all), (mixtures, sums), (scores,))
    late += launch(sizes, ("context",), pick_target, True, mixtures, mixture_back, *sems[6:8])
    for copy in late:
        copy.wait()


def run_forward(cid, sizes, kv_send, query_send, cotangent):
    heads, tokens, columns = query_send.shape
    total, owners = group_size(SEQ_AXES, sizes), sizes["expert"]
    vmem = pl.BlockSpec(memory_space=pltpu.VMEM)
    dma = pltpu.SemaphoreType.DMA
    return pl.pallas_call(
        functools.partial(forward_body, sizes),
        out_shape=[
            jax.ShapeDtypeStruct((total, tokens, columns), BF16),
            jax.ShapeDtypeStruct(query_send.shape, BF16),
            jax.ShapeDtypeStruct((owners, *cotangent.shape), BF16),
            jax.ShapeDtypeStruct(query_send.shape, BF16),
            jax.ShapeDtypeStruct((heads, 1, 2 * tokens), F32),
            jax.ShapeDtypeStruct(query_send.shape, BF16),
        ],
        in_specs=[vmem] * 3,
        out_specs=[vmem] * 6,
        scratch_shapes=[
            *[dma((n,)) for n in (heads, total, owners, heads) for _ in range(2)],
            pltpu.VMEM((total * tokens, 2 * tokens), F32),
        ],
        name="attention_forward",
        compiler_params=pltpu.CompilerParams(
            collective_id=cid, has_side_effects=True, vmem_limit_bytes=60_000_000
        ),
    )(kv_send, query_send, cotangent)


def backward_body(sizes, *refs):
    owns_hbm, others_hbm, y_ref, refs = refs[:3], refs[3:6], refs[6], refs[7:]
    queries, kv_all, mixtures, mix_send, sums, *refs = refs
    y_back, kv_back, query_back, *totals = refs[:6]
    sends, gots, sends_2, gots_2 = refs[6:9], refs[9:12], refs[12:15], refs[15:18]
    grad_query, terms, sum_kv, grad_mix = refs[18:22]
    owns, others, sems = refs[22:25], refs[25:28], refs[28:]
    dp, side = lax.axis_index("dp"), lax.axis_index("context") // 2
    experts = owns[0].shape[0]
    firsts = (("dp",), ("dp",), ("side",))
    seconds = (("side",), ("side",), ("dp",))
    loads = [
        (
            pltpu.make_async_copy(owns_hbm[i], owns[i], sems[20].at[i]),
            pltpu.make_async_copy(others_hbm[i], others[i], sems[20].at[3 + i]),
        )
        for i in range(3)
    ]
    for pair in loads:
        for copy in pair:
            copy.start()
    greet([SEQ_AXES, ("dp",)], sizes)
    mixes = launch(sizes, ("context",), pick_target, True, mix_send, grad_mix, *sems[18:20])
    rest = launch(sizes, ("expert",), pick_target, True, y_ref, y_back, *sems[6:8])

    def chip_sum(i, expert, place):
        return owns[i][expert, place] + others[i][expert, place].astype(F32)

    stage_1 = []
    for i, axes in enumerate(firsts):
        for copy in loads[i]:
            copy.wait()

        def fill(expert, carry, i=i, axes=axes):
            for d in range(4):
                for v in range(2):
                    terms_now = chip_sum(i, expert, 2 * d + v).astype(BF16)
                    if axes == ("dp",):
                        sends[i][d, expert, v] = terms_now
                    else:
                        sends[i][v, expert, d] = terms_now
            return carry

        lax.fori_loop(0, experts, fill, 0)
        stage_1 += launch(sizes, axes, pick_target, False, sends[i], gots[i], *sems[2 * i : 2 * i + 2])
    for copy in mixes:
        copy.wait()
    attention_backward((queries, kv_all, mixtures, grad_mix, sums), (grad_query, terms), (sum_kv,))
    rest += launch(sizes, SEQ_AXES, pick_target, True, terms, kv_back, *sems[8:10])
    rest += launch(sizes, ("context",), pick_target, True, grad_query, query_back, *sems[10:12])
    for copy in stage_1:
        copy.wait()

    def part(i, expert, place):
        if firsts[i] == ("dp",):
            total = chip_sum(i, expert, 2 * dp + place)
            for step in range(1, 4):
                total = total + gots[i][lax.rem(dp + step, 4), expert, place].astype(F32)
            return total
        return chip_sum(i, expert, 2 * place + side) + gots[i][1 - side, expert, place].astype(F32)

    for i, axes in enumerate(seconds):

        def refill(expert, carry, i=i, axes=axes):
            for place in range(group_size(axes, sizes)):
                sends_2[i][place, expert] = part(i, expert, place).astype(BF16)
            return carry

        lax.fori_loop(0, experts, refill, 0)
    stage_2 = []
    for i, axes in enumerate(seconds):
        stage_2 += launch(
            sizes, axes, pick_target, False, sends_2[i], gots_2[i], *sems[12 + 2 * i : 14 + 2 * i]
        )
    for copy in stage_2:
        copy.wait()
    for i, axes in enumerate(seconds):
        me, total = own_index(axes, sizes), group_size(axes, sizes)

        def close(expert, carry, i=i, me=me, total=total):
            held = part(i, expert, me)
            for step in range(1, total):
                held = held + gots_2[i][lax.rem(me + step, total), expert].astype(F32)
            totals[i][expert] = held
            return carry

        lax.fori_loop(0, experts, close, 0)
    for copy in rest:
        copy.wait()


def run_backward(cid, sizes, owns, others, y_terms, data):
    queries, kv_all = data[:2]
    tokens = queries.shape[1]
    experts = owns[0].shape[0]
    vmem = pl.BlockSpec(memory_space=pltpu.VMEM)
    tiles = [own.shape[2:] for own in owns]
    stage_1 = [(4, experts, 2, *tiles[0]), (4, experts, 2, *tiles[1]), (2, experts, 4, *tiles[2])]
    stage_2 = [(2, experts, *tiles[0]), (2, experts, *tiles[1]), (4, experts, *tiles[2])]
    context = sizes["context"]
    sizes_of = [4, 4, 2, sizes["expert"], group_size(SEQ_AXES, sizes), context, 2, 2, 4, context]
    dma = pltpu.SemaphoreType.DMA
    return pl.pallas_call(
        functools.partial(backward_body, sizes),
        out_shape=[
            jax.ShapeDtypeStruct(y_terms.shape, BF16),
            jax.ShapeDtypeStruct(kv_all.shape, BF16),
            jax.ShapeDtypeStruct(queries.shape, F32),
            *[jax.ShapeDtypeStruct((experts, *tile), F32) for tile in tiles],
        ],
        in_specs=[*([pl.BlockSpec(memory_space=pl.ANY)] * 6), *([vmem] * 6)],
        out_specs=[vmem] * 6,
        scratch_shapes=[
            *[pltpu.VMEM(shape, BF16) for shape in stage_1 * 2 + stage_2 * 2],
            pltpu.VMEM(queries.shape, F32),
            pltpu.VMEM(kv_all.shape, BF16),
            pltpu.VMEM((kv_all.shape[0] * tokens, 2 * HEAD_DIM), F32),
            pltpu.VMEM(queries.shape, BF16),
            *[pltpu.VMEM(own.shape, F32) for own in owns],
            *[pltpu.VMEM(own.shape, BF16) for own in owns],
            *[dma((n,)) for n in sizes_of for _ in range(2)],
            dma((6,)),
        ],
        name="attention_backward",
        compiler_params=pltpu.CompilerParams(
            collective_id=cid, has_side_effects=True, vmem_limit_bytes=67_043_328
        ),
    )(*owns, *others, y_terms, *data)


NEAR = ((0, 0), (1, 0), (0, 1), (0, 3), (0, 2), (1, 1), (1, 3), (1, 2))


def owner_at(owner, steps, sign):
    half = lax.rem(owner // 4 + steps[0], 2)
    return half * 4 + lax.rem(owner + 4 + sign * steps[1], 4)


def moe_copies(sizes, refs):
    moe_ref, table_ref, moe_land, table_land, d_send, d_back, dots, dot_back, g_sends, g_backs, sems = refs
    owner, context = lax.axis_index("expert"), lax.axis_index("context")

    def pair_of(copies, target, number):
        return [
            pltpu.make_async_remote_copy(
                src_ref=src,
                dst_ref=dst,
                send_sem=send.at[number],
                recv_sem=recv.at[number],
                device_id={"expert": target},
                device_id_type=MESH_ID,
            )
            for src, dst, send, recv in copies
        ]

    def tokens_to(number):
        pairs = (
            (table_ref, table_land.at[number], sems[7], sems[8]),
            (moe_ref, moe_land.at[number], sems[9], sems[10]),
        )
        return pair_of(pairs, owner_at(owner, NEAR[number], 1), number)

    def results_of(number):
        target = owner_at(owner, NEAR[number], -1)
        pairs = (
            (d_send.at[target], d_back.at[owner], sems[0], sems[1]),
            (dots.at[target], dot_back.at[owner], sems[2], sems[3]),
        )
        return pair_of(pairs, target, number)

    def own_results():
        return [
            pltpu.make_async_copy(d_send.at[owner], d_back.at[owner], sems[0].at[0]),
            pltpu.make_async_copy(dots.at[owner], dot_back.at[owner], sems[2].at[0]),
        ]

    def halves(number):
        partner = context + 1 - 2 * lax.rem(context, 2)
        return [
            pltpu.make_async_remote_copy(
                src_ref=g_sends[i].at[number],
                dst_ref=g_backs[i].at[number],
                send_sem=sems[4].at[3 * number + i],
                recv_sem=sems[5].at[3 * number + i],
                device_id={"context": partner},
                device_id_type=MESH_ID,
            )
            for i in range(3)
        ]

    return tokens_to, results_of, own_results, halves


def moe_body(
    sizes,
    moe_ref,
    table_ref,
    grad_ref,
    wg_ref,
    wu_ref,
    wd_ref,
    own_g,
    own_u,
    own_d,
    back_g,
    back_u,
    back_d,
    y_out,
    d_back,
    dot_back,
    moe_land,
    table_land,
    x_all,
    g_now,
    deo_all,
    dgu_all,
    eh_all,
    eo_all,
    dbuf_all,
    picks,
    highs,
    lows,
    gate_col,
    dot_col,
    dots,
    y_send,
    d_send,
    send_g,
    send_u,
    send_d,
    *sems,
):
    step = pl.program_id(0)
    owners = sizes["expert"]
    owner, context = lax.axis_index("expert"), lax.axis_index("context")
    core = lax.rem(context, 2)
    mine = 4
    group = owners // 2
    tokens, width = moe_ref.shape
    hidden_width = wg_ref.shape[2]
    rows = group * CAP
    barrier = pltpu.get_barrier_semaphore()
    tokens_to, results_of, own_results, halves = moe_copies(
        sizes,
        (
            moe_ref,
            table_ref,
            moe_land,
            table_land,
            d_send,
            d_back,
            dots,
            dot_back,
            (send_g, send_u, send_d),
            (back_g, back_u, back_d),
            sems,
        ),
    )

    @pl.when(step == 0)
    def _():
        for number in range(1, owners):
            pl.semaphore_signal(
                barrier,
                inc=1,
                device_id={"expert": lax.rem(owner + number, owners)},
                device_id_type=MESH_ID,
            )
        pl.semaphore_signal(
            barrier, inc=1, device_id={"context": context + 1 - 2 * core}, device_id_type=MESH_ID
        )
        pl.semaphore_wait(barrier, owners)
        for number in range(1, group):
            for copy in tokens_to(number):
                copy.start()
        dots[...] = jnp.zeros_like(dots)
        moe_land[0] = moe_ref[...]
        table_land[0] = table_ref[...]
        for number in range(1, group):
            for copy in tokens_to(number):
                copy.wait_recv()
        for number in range(group, owners):
            for copy in tokens_to(number):
                copy.start()

    @pl.when(step == mine)
    def _():
        for copy in own_results():
            copy.start()
        for number in range(1, group):
            for copy in results_of(number):
                copy.start()
        for number in range(group, owners):
            for copy in tokens_to(number):
                copy.wait_recv()

    @pl.when(step == 2 * mine)
    def _():
        for number in range(group, owners):
            for copy in results_of(number):
                copy.start()
        pltpu.make_async_copy(y_send, y_out, sems[6].at[0]).start()

    for number in range(mine):

        @pl.when(step == 2 * mine + 1 + number)
        def _(number=number):
            for copy in halves(number):
                copy.start()

    @pl.when(step < 2 * mine)
    def _():
        expert, tile = lax.rem(step, mine), step // mine
        place = pl.multiple_of(expert * CAP, CAP)
        spot = pl.ds(place, CAP)
        here = pl.ds(pl.multiple_of(tile * rows, rows), rows)
        part = pl.ds(tile * group, group)

        def source_of(j):
            near, far = owner_at(owner, NEAR[j], -1), owner_at(owner, NEAR[group + j], -1)
            return near + tile * (far - near)

        table = jnp.concatenate(
            [table_land[tile * group + j, pl.ds(owner * mine + expert, 1), :] for j in range(group)], axis=0
        )
        table = jnp.concatenate([table, table], axis=0)
        named = table >= 0.0
        above = lax.broadcasted_iota(jnp.int32, (tokens, tokens), 0)
        beside = lax.broadcasted_iota(jnp.int32, (tokens, tokens), 1)
        before = (above < beside).astype(F32).astype(BF16)
        slots = dot(named.astype(F32).astype(BF16), before)
        slots = jnp.where(named, slots, -1.0)
        counts = lax.broadcasted_iota(jnp.int32, (CAP, tokens), 0).astype(F32)
        for j in range(group):
            position = tile * group + j
            source = source_of(j)
            chosen = counts == slots[j : j + 1]
            onehot = jnp.where(chosen, 1.0, 0.0).astype(BF16)
            weight = jnp.where(chosen, table[j : j + 1], 0.0)
            high = weight.astype(BF16)
            picks[position, spot, :] = onehot
            highs[position, spot, :] = high
            lows[position, spot, :] = (weight - high.astype(F32)).astype(BF16)
            gate_col[j * CAP : (j + 1) * CAP, :] = jnp.sum(weight, axis=1, keepdims=True)
            line = pl.ds(pl.multiple_of(tile * rows + j * CAP, CAP), CAP)
            x_all[expert, line, :] = dot(onehot, moe_land[position]).astype(BF16)
            g_now[j * CAP : (j + 1) * CAP, :] = dot(onehot, grad_ref[source]).astype(BF16)

        rows_in = x_all[expert, here, :]
        gate_act = dot(rows_in, wg_ref[0])
        up_act = dot(rows_in, wu_ref[0])
        sigma = jax.nn.sigmoid(gate_act)
        silu = gate_act * sigma
        hidden = (silu * up_act).astype(BF16)
        eh_all[expert, here, :] = hidden
        expert_out = dot(hidden, wd_ref[0]).astype(BF16)
        eo_all[part, spot, :] = expert_out.reshape(group, CAP, width)
        grads = g_now[...].astype(F32)
        dot_col[...] = jnp.sum(grads * expert_out.astype(F32), axis=1, keepdims=True)
        grad_expert = (gate_col[...] * grads).astype(BF16)
        deo_all[expert, here, :] = grad_expert
        grad_hidden = dot_t(grad_expert, wd_ref[0])
        slope = sigma * (1.0 + gate_act * (1.0 - sigma))
        grad_gate = (grad_hidden * up_act * slope).astype(BF16)
        grad_up = (grad_hidden * silu).astype(BF16)
        dgu_all[expert, here, :hidden_width] = grad_gate
        dgu_all[expert, here, hidden_width:] = grad_up
        grad_buffer = (dot_t(grad_gate, wg_ref[0]) + dot_t(grad_up, wu_ref[0])).astype(BF16)
        dbuf_all[part, spot, :] = grad_buffer.reshape(group, CAP, width)
        for j in range(group):
            position = tile * group + j
            source = source_of(j)
            onehot = picks[position, spot, :].astype(F32)
            dots[source, pl.ds(expert, 1), :] = jnp.sum(
                onehot * dot_col[j * CAP : (j + 1) * CAP, :], axis=0, keepdims=True
            )

        @pl.when(expert == mine - 1)
        def _():
            for j in range(group):
                position, source = tile * group + j, source_of(j)
                d_send[source] = t_dot(picks[position], dbuf_all[position]).astype(BF16)
                moved = t_dot(highs[position], eo_all[position]) + t_dot(lows[position], eo_all[position])
                y_send[source] = moved.astype(BF16)

    @pl.when((step >= 2 * mine) & (step < 3 * mine))
    def _():
        number = step - 2 * mine
        blocks = width // 256
        per = width // 16

        def gate_rows(j, carry):
            columns = pl.ds(pl.multiple_of(j * 256, 256), 256)
            rows_in = x_all[number, :, columns]
            for half, own, send in ((0, own_g, send_g), (1, own_u, send_u)):
                grads = dgu_all[number, :, half * hidden_width : (half + 1) * hidden_width]
                terms = t_dot(rows_in, grads).reshape(128 // per, 2, per, hidden_width)
                first, second = terms[:, 0], terms[:, 1]
                places = pl.ds(j * (128 // per), 128 // per)
                own[0, places] = jnp.where(core == 0, first, second)
                send[number, places] = jnp.where(core == 0, second, first).astype(BF16)
            return carry

        lax.fori_loop(0, blocks, gate_rows, 0)
        less = hidden_width // 16

        def down_rows(j, carry):
            columns = pl.ds(pl.multiple_of(j * 256, 256), 256)
            terms = t_dot(eh_all[number, :, columns], deo_all[number])
            terms = terms.reshape(128 // less, 2, less, width)
            first, second = terms[:, 0], terms[:, 1]
            places = pl.ds(j * (128 // less), 128 // less)
            own_d[0, places] = jnp.where(core == 0, first, second)
            send_d[number, places] = jnp.where(core == 0, second, first).astype(BF16)
            return carry

        lax.fori_loop(0, hidden_width // 256, down_rows, 0)

    @pl.when(step == 3 * mine)
    def _():
        for number in range(1, owners):
            for copy in tokens_to(number):
                copy.wait_send()
            for copy in results_of(number):
                copy.wait()
        for copy in own_results():
            copy.wait()
        pltpu.make_async_copy(y_send, y_out, sems[6].at[0]).wait()
        for number in range(mine):
            for copy in halves(number):
                copy.wait()


def run_experts(cid, sizes, moe_input, table, grad_all, gate_weight, up_weight, down_weight):
    owners, tokens, width = grad_all.shape
    mine, _, inner = gate_weight.shape
    rows = owners * CAP
    part, less = width // 16, inner // 16

    def fixed(array):
        return pl.BlockSpec(array.shape, lambda i: (0,) * array.ndim, pipeline_mode=pl.Buffered(1))

    def expert_block(array):
        return pl.BlockSpec((1, *array.shape[1:]), lambda i: (lax.rem(jnp.minimum(i, 2 * mine - 1), mine), 0, 0))

    def own_block(*shape):
        return pl.BlockSpec((1, *shape), lambda i: (jnp.clip(i - 2 * mine, 0, mine - 1), 0, 0, 0))

    anywhere = pl.BlockSpec(memory_space=pl.ANY)
    wide, tall = (8, part, inner), (8, less, width)
    dma = pltpu.SemaphoreType.DMA
    return pl.pallas_call(
        functools.partial(moe_body, sizes),
        grid=(3 * mine + 1,),
        out_shape=[
            jax.ShapeDtypeStruct((mine, *wide), F32),
            jax.ShapeDtypeStruct((mine, *wide), F32),
            jax.ShapeDtypeStruct((mine, *tall), F32),
            jax.ShapeDtypeStruct((mine, *wide), BF16),
            jax.ShapeDtypeStruct((mine, *wide), BF16),
            jax.ShapeDtypeStruct((mine, *tall), BF16),
            jax.ShapeDtypeStruct((owners, tokens, width), BF16),
            jax.ShapeDtypeStruct((owners, tokens, width), BF16),
            jax.ShapeDtypeStruct((owners, 8, tokens), F32),
        ],
        in_specs=[
            fixed(moe_input),
            fixed(table),
            fixed(grad_all),
            expert_block(gate_weight),
            expert_block(up_weight),
            expert_block(down_weight),
        ],
        out_specs=[own_block(*wide), own_block(*wide), own_block(*tall), *([anywhere] * 6)],
        scratch_shapes=[
            pltpu.VMEM(grad_all.shape, BF16),
            pltpu.VMEM((owners, *table.shape), F32),
            pltpu.VMEM((mine, rows, width), BF16),
            pltpu.VMEM((rows // 2, width), BF16),
            pltpu.VMEM((mine, rows, width), BF16),
            pltpu.VMEM((mine, rows, 2 * inner), BF16),
            pltpu.VMEM((mine, rows, inner), BF16),
            pltpu.VMEM((owners, mine * CAP, width), BF16),
            pltpu.VMEM((owners, mine * CAP, width), BF16),
            pltpu.VMEM((owners, mine * CAP, tokens), BF16),
            pltpu.VMEM((owners, mine * CAP, tokens), BF16),
            pltpu.VMEM((owners, mine * CAP, tokens), BF16),
            pltpu.VMEM((rows // 2, 1), F32),
            pltpu.VMEM((rows // 2, 1), F32),
            pltpu.VMEM((owners, 8, tokens), F32),
            pltpu.VMEM((owners, tokens, width), BF16),
            pltpu.VMEM((owners, tokens, width), BF16),
            pltpu.VMEM((mine, *wide), BF16),
            pltpu.VMEM((mine, *wide), BF16),
            pltpu.VMEM((mine, *tall), BF16),
            dma((owners,)),
            dma((owners,)),
            dma((owners,)),
            dma((owners,)),
            dma((3 * mine,)),
            dma((3 * mine,)),
            dma((1,)),
            *[dma((owners,))] * 4,
        ],
        name="run_experts",
        compiler_params=pltpu.CompilerParams(
            collective_id=cid, has_side_effects=True, vmem_limit_bytes=67_043_328
        ),
    )(moe_input, table, grad_all, gate_weight, up_weight, down_weight)


CHIP_AXES = ("dp", "side", "expert")


def sum_body(sizes, *refs):
    query_in, key_in, value_in, output_in, narrow_in = refs[:5]
    whole, load, near, sums, got = refs[5:10]
    near_send, near_recv, send_sems, recv_sems, give_sems, take_sems, pass_sems, land_sems = refs[10:]
    core = lax.rem(lax.axis_index("context"), 2)
    partner = {"context": lax.axis_index("context") + 1 - 2 * core}
    me, total = own_index(CHIP_AXES, sizes), group_size(CHIP_AXES, sizes)
    plane = total // sizes["dp"]
    rows = load.shape[1]
    some, wide = rows // 2, query_in.shape[1]
    half = wide // 2

    def place(step):
        target = lax.rem(me + step, total)
        return target, coords_of(CHIP_AXES, sizes, target)

    def remote(src, dst, send, recv, peer):
        return pltpu.make_async_remote_copy(
            src_ref=src, dst_ref=dst, send_sem=send, recv_sem=recv, device_id=peer, device_id_type=MESH_ID
        )

    def reduce_copy(step):
        target, peer = place(step)
        return remote(sums.at[target], got.at[me], send_sems.at[step], recv_sems.at[step], peer)

    def gather_copy(step):
        _, peer = place(step)
        own = whole.at[core, me]
        return remote(own, own, give_sems.at[step], take_sems.at[step], peer)

    def pass_copy(step):
        source = whole.at[core, lax.rem(me - step + total, total)]
        return remote(source, source, pass_sems.at[step], land_sems.at[step], partner)

    def near_copy(turn):
        chunks = pl.ds(lax.rem(lax.axis_index("dp") + turn, sizes["dp"]) * plane, plane)
        return remote(load.at[chunks], near.at[chunks], near_send.at[turn], near_recv.at[turn], partner)

    def each(start, stop, body):
        def run(step, carry):
            body(step)
            return carry

        lax.fori_loop(start, stop, run, 0)

    def pack(number, chunk):
        here = pl.ds(pl.multiple_of(chunk * rows, rows), rows)
        there = pl.ds(pl.multiple_of(chunk * some, some), some)
        if number == 0:
            parts = [query_in[here, :]]
        else:
            parts = [key_in[here, :], value_in[here, :]]
        start = number * wide
        output = jnp.concatenate(
            [output_in[there, start : start + half], output_in[there, start + half : start + wide]], axis=0
        )
        return jnp.concatenate([*parts, output, narrow_in[here, :]], axis=1)

    barrier = pltpu.get_barrier_semaphore()
    pl.semaphore_signal(barrier, inc=1, device_id=partner, device_id_type=MESH_ID)
    each(
        1,
        total,
        lambda step: pl.semaphore_signal(
            barrier, inc=1, device_id=place(step)[1], device_id_type=MESH_ID
        ),
    )
    for turn in range(sizes["dp"]):
        base = lax.rem(lax.axis_index("dp") + turn, sizes["dp"]) * plane
        for number in range(2):

            @pl.when(core == 1 - number)
            def _(number=number, base=base):
                def fill(chunk):
                    load[chunk] = pack(number, chunk).astype(BF16)

                each(base, base + plane, fill)

        if turn == 0:
            pl.semaphore_wait(barrier, total)
        near_copy(turn).start()

    for turn in range(sizes["dp"]):
        near_copy(turn).wait()
        base = lax.rem(lax.axis_index("dp") + turn, sizes["dp"]) * plane
        for number in range(2):

            @pl.when(core == number)
            def _(number=number, base=base):
                def add(chunk):
                    sums[chunk] = (pack(number, chunk) + near[chunk].astype(F32)).astype(BF16)

                each(base, base + plane, add)

        def send(i, base=base):
            target = base + lax.rem(me + i, plane)

            @pl.when(target != me)
            def _():
                reduce_copy(lax.rem(target - me + total, total)).start()

        each(0, plane, send)

    got[me] = sums[me]
    each(1, total, lambda step: reduce_copy(step).wait())
    result = lax.fori_loop(
        0, total, lambda i, held: held + got[i].astype(F32), jnp.zeros(got.shape[1:], F32)
    )
    whole[core, me] = result.astype(BF16)
    each(1, total, lambda step: gather_copy(step).start())
    pass_copy(0).start()

    def forward(step):
        gather_copy(step).wait_recv()
        pass_copy(step).start()

    each(1, total, forward)
    each(1, total, lambda step: gather_copy(step).wait_send())
    each(0, total, lambda step: pass_copy(step).wait())


def unpack_body(whole, query_out, key_out, value_out, output_out, narrow_out):
    chunks, rows = whole.shape[1:3]
    some, wide = rows // 2, query_out.shape[1]
    half = wide // 2
    for chunk in range(chunks):
        here = slice(chunk * rows, (chunk + 1) * rows)
        there = slice(chunk * some, (chunk + 1) * some)
        for number in range(2):
            block = whole[number, chunk].astype(F32)
            if number == 0:
                query_out[here, :] = block[:, :wide]
                narrow_out[here, :] = block[:, wide + half :]
            else:
                key_out[here, :] = block[:, :half]
                value_out[here, :] = block[:, half:wide]
            start = number * wide
            output_out[there, start : start + half] = block[:some, wide : wide + half]
            output_out[there, start + half : start + wide] = block[some:, wide : wide + half]


def sum_everywhere(cid, sizes, *arrays):
    total = group_size(CHIP_AXES, sizes)
    depth, wide = arrays[0].shape
    half = (total, depth // total, wide + wide // 2 + arrays[4].shape[1])
    dma = pltpu.SemaphoreType.DMA
    vmem = pl.BlockSpec(memory_space=pltpu.VMEM)
    whole = pl.pallas_call(
        functools.partial(sum_body, sizes),
        out_shape=jax.ShapeDtypeStruct((2, *half), BF16),
        in_specs=[vmem] * 5,
        out_specs=vmem,
        scratch_shapes=[pltpu.VMEM(half, BF16)] * 4
        + [dma((sizes["dp"],))] * 2
        + [dma((total,))] * 6,
        name="sum_everywhere",
        compiler_params=pltpu.CompilerParams(
            collective_id=cid, has_side_effects=True, vmem_limit_bytes=60_000_000
        ),
    )(*arrays)
    parts = 4
    return pl.pallas_call(
        unpack_body,
        grid=(parts,),
        out_shape=[jax.ShapeDtypeStruct(array.shape, F32) for array in arrays],
        in_specs=[pl.BlockSpec((2, total // parts, *half[1:]), lambda i: (0, i, 0, 0))],
        out_specs=[
            pl.BlockSpec((array.shape[0] // parts, array.shape[1]), lambda i: (i, 0)) for array in arrays
        ],
        name="unpack_sums",
    )(whole)


def rope_tables(positions, head_size):
    half_dim = head_size // 2
    frequency = ROPE_BASE ** (-2.0 * jnp.arange(half_dim, dtype=F32) / head_size)
    angles = positions.astype(F32)[:, None] * frequency[None, :]
    angles = jnp.concatenate([angles, angles], axis=1)
    return (jnp.cos(angles), jnp.sin(angles))


def rotate(values, cosine, sine_table):
    half_dim = values.shape[-1] // 2
    turned = jnp.concatenate([-values[..., half_dim:], values[..., :half_dim]], axis=-1)
    return values * cosine[:, None, :] + turned * sine_table[:, None, :]


def rotate_back(grads, cosine, sine_table):
    half_dim = grads.shape[-1] // 2
    scaled = grads * sine_table[:, None, :]
    turned = jnp.concatenate([scaled[..., half_dim:], -scaled[..., :half_dim]], axis=-1)
    return grads * cosine[:, None, :] + turned


def norm_forward(values, gain_vec):
    inverse = lax.rsqrt(jnp.mean(values * values, axis=-1, keepdims=True) + EPSILON)
    normed = values * inverse
    return (inverse, normed, (normed * gain_vec).astype(BF16))


def norm_backward(grad_out, normed, inverse, gain_vec):
    gain_grad = jnp.sum(grad_out * normed, axis=0)
    scaled = grad_out * gain_vec
    inner = jnp.mean(scaled * normed, axis=-1, keepdims=True)
    return (gain_grad, inverse * (scaled - normed * inner))


def local(
    sizes,
    inputs,
    prenorm_gain,
    query_weight,
    key_weight,
    value_weight,
    output_weight,
    midnorm_gain,
    router_weight,
    gate_weight,
    up_weight,
    down_weight,
    expert_ids,
    cotangent,
):
    tokens, width = inputs.shape[1:]
    owners = sizes["expert"]
    mine = gate_weight.shape[0]
    context, owner = lax.axis_index("context"), lax.axis_index("expert")
    block = context * owners + owner
    positions = block * tokens + jnp.arange(tokens, dtype=jnp.int32)
    cosine, sine_table = rope_tables(positions, HEAD_DIM)

    input_float = inputs[0].astype(F32)
    inverse_first, normed_first, attn_input = norm_forward(input_float, prenorm_gain)
    query_raw = dot(attn_input, query_weight).reshape(tokens, HEADS, HEAD_DIM)
    key_raw = dot(attn_input, key_weight).reshape(tokens, KV_HEADS, HEAD_DIM)
    value_raw = dot(attn_input, value_weight).reshape(tokens, KV_HEADS, HEAD_DIM)
    query_rot = rotate(query_raw, cosine, sine_table).astype(BF16)
    key_rot = rotate(key_raw, cosine, sine_table).astype(BF16)
    query_send = query_rot.reshape(tokens, KV_HEADS, 2 * HEAD_DIM).transpose(1, 0, 2)
    kv_send = jnp.concatenate([key_rot, value_raw.astype(BF16)], axis=2).transpose(1, 0, 2)
    kv_all, queries, grad_all, mixtures, sums, mixture = run_forward(
        0, sizes, kv_send, query_send, cotangent[0]
    )
    mixture_flat = mixture.transpose(1, 0, 2).reshape(tokens, HEADS * HEAD_DIM)

    after_attn = input_float + dot(mixture_flat, output_weight)
    inverse_second, normed_second, moe_input = norm_forward(after_attn, midnorm_gain)
    logits = lax.dot_general(
        router_weight, moe_input, (((0,), (1,)), ((), ())), preferred_element_type=F32
    )
    numbers = jnp.arange(EXPERTS, dtype=jnp.int32)[:, None, None]
    chosen = jnp.any(expert_ids[0].T[None] == numbers, axis=1)
    masked = jnp.where(chosen, logits, -jnp.inf)
    powers = jnp.exp(masked - jnp.max(masked, axis=0, keepdims=True))
    gates = powers / jnp.sum(powers, axis=0, keepdims=True)
    gate_table = jnp.where(chosen, gates, -1.0)

    own_g, own_u, own_d, other_g, other_u, other_d, moe_terms, grad_back, dot_back = run_experts(
        3, sizes, moe_input, gate_table, grad_all, gate_weight, up_weight, down_weight
    )
    grad_gates = dot_back[:, :mine].reshape(EXPERTS, tokens)
    grad_logits = gates * (grad_gates - jnp.sum(gates * grad_gates, axis=0, keepdims=True))
    router_grad = jnp.einsum(
        "td,et->de", moe_input.astype(F32), grad_logits, precision=lax.Precision.HIGHEST
    )
    grad_moe_in = jnp.sum(grad_back.astype(F32), axis=0) + jnp.einsum(
        "et,de->td", grad_logits, router_weight.astype(F32), precision=lax.Precision.HIGHEST
    )
    grad_out = cotangent[0].astype(F32)
    midnorm_grad, grad_after = norm_backward(grad_moe_in, normed_second, inverse_second, midnorm_gain)
    grad_after = grad_out + grad_after
    grad_after_half = grad_after.astype(BF16)
    output_grad = t_dot(mixture_flat, grad_after_half)
    grad_mix = dot_t(grad_after_half, output_weight).astype(BF16)
    grad_mix = grad_mix.reshape(tokens, KV_HEADS, 2 * HEAD_DIM).transpose(1, 0, 2)
    moe_back, kv_back, grad_query, gate_sum, up_sum, down_sum = run_backward(
        8,
        sizes,
        (own_g, own_u, own_d),
        (other_g, other_u, other_d),
        moe_terms,
        (queries, kv_all, mixtures, grad_mix, sums),
    )
    outputs = (after_attn + jnp.sum(moe_back.astype(F32), axis=0)).astype(BF16)
    grad_kv = jnp.sum(kv_back.astype(F32).reshape(KV_HEADS, owners, tokens, 2 * HEAD_DIM), axis=1)
    grad_kv = grad_kv.transpose(1, 0, 2)
    grad_query = grad_query.transpose(1, 0, 2).reshape(tokens, HEADS, HEAD_DIM)
    query_back = rotate_back(grad_query, cosine, sine_table).reshape(tokens, -1).astype(BF16)
    key_back = rotate_back(grad_kv[..., :HEAD_DIM], cosine, sine_table).reshape(tokens, -1).astype(BF16)
    value_back = grad_kv[..., HEAD_DIM:].reshape(tokens, -1).astype(BF16)
    query_grad = t_dot(attn_input, query_back)
    key_grad = t_dot(attn_input, key_back)
    value_grad = t_dot(attn_input, value_back)
    grad_attn_in = (
        dot_t(query_back, query_weight) + dot_t(key_back, key_weight) + dot_t(value_back, value_weight)
    )
    prenorm_grad, grad_inputs = norm_backward(grad_attn_in, normed_first, inverse_first, prenorm_gain)
    grad_inputs = grad_after + grad_inputs
    narrow = jnp.concatenate([router_grad, prenorm_grad[:, None], midnorm_grad[:, None]], axis=1)
    narrow = jnp.pad(narrow, ((0, 0), (0, 128 - EXPERTS - 2)))
    query_grad, key_grad, value_grad, output_grad, narrow = sum_everywhere(
        9, sizes, query_grad, key_grad, value_grad, output_grad, narrow
    )
    dense = (
        narrow[:, EXPERTS],
        query_grad,
        key_grad,
        value_grad,
        output_grad,
        narrow[:, EXPERTS + 1],
        narrow[:, :EXPERTS],
    )
    return (outputs[None], grad_inputs[None], *dense, gate_sum, up_sum, down_sum)


def solution(mesh):
    split = P("dp", ("context", "expert"), None)
    owned = P("expert", None, None)
    summed = P("expert", ("dp", "context"), None)
    in_specs = (split, *([P()] * 7), owned, owned, owned, split, split)
    out_specs = (split, split, *([P()] * 7), summed, summed, summed)
    return jax.shard_map(
        functools.partial(local, dict(mesh.shape)),
        mesh=mesh,
        in_specs=in_specs,
        out_specs=out_specs,
        check_vma=False,
    )
```

```python
import functools

import jax
import jax.numpy as jnp
from jax import lax
from jax.experimental import pallas as pl
from jax.experimental.pallas import tpu as pltpu
from jax.sharding import PartitionSpec as P

HEADS = 8
KV_HEADS = 4
HEAD_DIM = 64
EXPERTS = 32
TOP = 8
CAP = 64
EPSILON = 1e-06
ROPE_BASE = 10000.0
F32 = jnp.float32
BF16 = jnp.bfloat16
MESH_ID = pl.DeviceIdType.MESH
SEQ_AXES = ("context", "expert")


def dot(left, right):
    return jnp.dot(left, right, preferred_element_type=F32)


def dot_t(left, right):
    return lax.dot_general(left, right, (((1,), (1,)), ((), ())), preferred_element_type=F32)


def t_dot(left, right):
    return lax.dot_general(left, right, (((0,), (0,)), ((), ())), preferred_element_type=F32)


PARTS = {"side": ("context", 2, 2), "half": ("expert", 2, 4), "place": ("expert", 4, 1)}


def axis_size(sizes, name):
    return PARTS[name][1] if name in PARTS else sizes[name]


def group_size(axes, sizes):
    total = 1
    for name in axes:
        total *= axis_size(sizes, name)
    return total


def part_index(name):
    if name not in PARTS:
        return lax.axis_index(name)
    axis, size, stride = PARTS[name]
    return lax.rem(lax.axis_index(axis) // stride, size)


def own_index(axes, sizes):
    index = 0
    for name in axes:
        index = index * axis_size(sizes, name) + part_index(name)
    return index


def coords_of(axes, sizes, index):
    out = {}
    for name in reversed(axes):
        place = lax.rem(index, axis_size(sizes, name))
        if name in PARTS:
            axis, _, stride = PARTS[name]
            out[axis] = lax.axis_index(axis) + (place - part_index(name)) * stride
        else:
            out[name] = place
        index = index // axis_size(sizes, name)
    return out


def pick_whole(ref, target, peer):
    return ref


def pick_target(ref, target, peer):
    return ref.at[target]


def pick_second(ref, target, peer):
    return ref.at[:, target]


def pick_context(ref, target, peer):
    return ref.at[peer["context"]]


def greet(all_axes, sizes):
    barrier = pltpu.get_barrier_semaphore()
    groups = []
    for axes in all_axes:
        if not any(set(axes) <= set(other) for other in groups):
            groups = [other for other in groups if not set(other) <= set(axes)] + [axes]
    signals = 0
    for axes in groups:
        me, total = own_index(axes, sizes), group_size(axes, sizes)
        for step in range(1, total):
            peer = coords_of(axes, sizes, lax.rem(me + step, total))
            pl.semaphore_signal(barrier, inc=1, device_id=peer, device_id_type=MESH_ID)
        signals += total - 1
    pl.semaphore_wait(barrier, signals)


def launch(sizes, axes, pick, keep, source, landing, send, recv):
    started = []
    me, total = own_index(axes, sizes), group_size(axes, sizes)
    for step in range(1, total):
        target = lax.rem(me + step, total)
        peer = coords_of(axes, sizes, target)
        copy = pltpu.make_async_remote_copy(
            src_ref=pick(source, target, peer),
            dst_ref=landing.at[me],
            send_sem=send.at[step],
            recv_sem=recv.at[step],
            device_id=peer,
            device_id_type=MESH_ID,
        )
        copy.start()
        started.append(copy)
    if keep:
        own = pltpu.make_async_copy(
            pick(source, me, coords_of(axes, sizes, me)), landing.at[me], send.at[0]
        )
        own.start()
        started.append(own)
    return started


def stack_heads(block, low):
    tokens = block.shape[0]
    zero = jnp.zeros((tokens, HEAD_DIM), block.dtype)
    parts = [block[:, :HEAD_DIM], block[:, HEAD_DIM:]]
    return jnp.concatenate(
        [jnp.concatenate([part, zero] if low else [zero, part], axis=1) for part in parts], axis=0
    )


def causal(shape, tokens):
    keys = lax.broadcasted_iota(jnp.int32, shape, 0)
    queries = lax.rem(lax.broadcasted_iota(jnp.int32, shape, 1), tokens)
    return keys - queries <= lax.axis_index("expert") * tokens


def identity(size):
    shape = (size, size)
    return lax.broadcasted_iota(jnp.int32, shape, 0) == lax.broadcasted_iota(jnp.int32, shape, 1)


def attention_forward(data, results, scratch):
    query_ref, kv_ref = data
    out_ref, sum_ref = results
    (score_ref,) = scratch
    blocks, tokens = query_ref.shape[:2]
    chunk, columns = 8 * tokens, 2 * tokens

    def block(number, carry):
        rows = stack_heads(query_ref[number], True) * (HEAD_DIM ** (-0.5))
        rows = rows.astype(BF16)

        def keys_of(j):
            return pl.ds(pl.multiple_of(j * chunk, chunk), chunk)

        def kv_of(j):
            return kv_ref[pl.ds(j * 8, 8)].reshape(chunk, 2 * HEAD_DIM)

        def first(j, top):
            scores = dot_t(kv_of(j), rows)
            score_ref[keys_of(j), :] = scores
            return jnp.maximum(top, jnp.max(scores, axis=0, keepdims=True))

        top = lax.fori_loop(0, number, first, jnp.full((1, columns), -jnp.inf, F32))
        scores = dot_t(kv_of(number), rows)
        scores = jnp.where(causal(scores.shape, tokens), scores, -jnp.inf)
        score_ref[keys_of(number), :] = scores
        top = jnp.maximum(top, jnp.max(scores, axis=0, keepdims=True))

        def second(j, held):
            total, mixed = held
            powers = jnp.exp(score_ref[keys_of(j), :] - top)
            total = total + jnp.sum(powers, axis=0, keepdims=True)
            return total, mixed + t_dot(powers.astype(BF16), kv_of(j))

        start = (jnp.zeros((1, columns), F32), jnp.zeros((columns, 2 * HEAD_DIM), F32))
        total, mixed = lax.fori_loop(0, number + 1, second, start)
        sum_ref[number] = top + jnp.log(total)
        inverse = jnp.sum(jnp.where(identity(columns), 1.0 / total, 0.0), axis=1, keepdims=True)
        mixed = (mixed * inverse)[:, HEAD_DIM:]
        out_ref[number] = jnp.concatenate([mixed[:tokens], mixed[tokens:]], axis=1).astype(BF16)
        return carry

    lax.fori_loop(0, blocks, block, 0)


def attention_backward(data, results, scratch):
    query_ref, kv_ref, mix_ref, grad_ref, sum_ref = data
    grad_query_ref, terms_ref = results
    (sum_kv,) = scratch
    blocks, tokens = query_ref.shape[:2]
    chunk, columns = 8 * tokens, 2 * tokens
    factor = HEAD_DIM ** (-0.5)
    sum_kv[...] = jnp.zeros_like(sum_kv)

    def block(number, carry):
        rows = (stack_heads(query_ref[number], True) * factor).astype(BF16)
        grads = stack_heads(grad_ref[number], False)
        both = jnp.concatenate([rows, grads], axis=0)
        pairs = dot_t(stack_heads(mix_ref[number], False), grads)
        delta = jnp.sum(jnp.where(identity(columns), pairs, 0.0), axis=0, keepdims=True)
        logsum = sum_ref[number]

        def unit(j, total, masked):
            keys = pl.ds(pl.multiple_of(j * chunk, chunk), chunk)
            kv = kv_ref[pl.ds(j * 8, 8)].reshape(chunk, 2 * HEAD_DIM)
            products = dot_t(kv, both)
            soft = jnp.exp(products[:, :columns] - logsum)
            if masked:
                soft = jnp.where(causal(soft.shape, tokens), soft, 0.0)
            scores = (soft * (products[:, columns:] - delta)).astype(BF16)
            sum_kv[keys, :] += dot(jnp.concatenate([scores, soft.astype(BF16)], axis=1), both)
            return total + t_dot(scores, kv)

        total = lax.fori_loop(
            0, number, lambda j, held: unit(j, held, False), jnp.zeros((columns, 2 * HEAD_DIM), F32)
        )
        total = unit(number, total, True)[:, :HEAD_DIM] * factor
        grad_query_ref[number] = jnp.concatenate([total[:tokens], total[tokens:]], axis=1)
        return carry

    lax.fori_loop(0, blocks, block, 0)
    terms_ref[...] = sum_kv[...].astype(BF16).reshape(terms_ref.shape)


def forward_body(sizes, *refs):
    kv_send, query_send, grad_ref = refs[:3]
    kv_all, queries, grad_all, mixtures, sums, mixture_back = refs[3:9]
    sems, scores = refs[9:17], refs[17]
    greet([SEQ_AXES], sizes)
    early = launch(sizes, ("context",), pick_target, True, query_send, queries, *sems[0:2])
    early += launch(sizes, SEQ_AXES, pick_context, True, kv_send, kv_all, *sems[2:4])
    late = launch(sizes, ("expert",), pick_whole, True, grad_ref, grad_all, *sems[4:6])
    for copy in early:
        copy.wait()
    attention_forward((queries, kv_all), (mixtures, sums), (scores,))
    late += launch(sizes, ("context",), pick_target, True, mixtures, mixture_back, *sems[6:8])
    for copy in late:
        copy.wait()


def run_forward(cid, sizes, kv_send, query_send, cotangent):
    heads, tokens, columns = query_send.shape
    total, owners = group_size(SEQ_AXES, sizes), sizes["expert"]
    vmem = pl.BlockSpec(memory_space=pltpu.VMEM)
    dma = pltpu.SemaphoreType.DMA
    return pl.pallas_call(
        functools.partial(forward_body, sizes),
        out_shape=[
            jax.ShapeDtypeStruct((total, tokens, columns), BF16),
            jax.ShapeDtypeStruct(query_send.shape, BF16),
            jax.ShapeDtypeStruct((owners, *cotangent.shape), BF16),
            jax.ShapeDtypeStruct(query_send.shape, BF16),
            jax.ShapeDtypeStruct((heads, 1, 2 * tokens), F32),
            jax.ShapeDtypeStruct(query_send.shape, BF16),
        ],
        in_specs=[vmem] * 3,
        out_specs=[vmem] * 6,
        scratch_shapes=[
            *[dma((n,)) for n in (heads, total, owners, heads) for _ in range(2)],
            pltpu.VMEM((total * tokens, 2 * tokens), F32),
        ],
        name="attention_forward",
        compiler_params=pltpu.CompilerParams(
            collective_id=cid, has_side_effects=True, vmem_limit_bytes=60_000_000
        ),
    )(kv_send, query_send, cotangent)


def backward_body(sizes, *refs):
    owns_hbm, others_hbm, y_ref, refs = refs[:3], refs[3:6], refs[6], refs[7:]
    queries, kv_all, mixtures, mix_send, sums, *refs = refs
    y_total, kv_back, query_back, *totals = refs[:6]
    sends, gots, sends_2, gots_2 = refs[6:9], refs[9:12], refs[12:15], refs[15:18]
    grad_query, terms, sum_kv, grad_mix = refs[18:22]
    owns, others, refs = refs[22:25], refs[25:28], refs[28:]
    y_land, y_pass, y_got, *sems = refs
    dp, side = lax.axis_index("dp"), lax.axis_index("context") // 2
    experts = owns[0].shape[0]
    firsts = (("dp",), ("dp",), ("side",))
    seconds = (("side",), ("side",), ("dp",))
    loads = [
        (
            pltpu.make_async_copy(owns_hbm[i], owns[i], sems[22].at[i]),
            pltpu.make_async_copy(others_hbm[i], others[i], sems[22].at[3 + i]),
        )
        for i in range(3)
    ]
    for pair in loads:
        for copy in pair:
            copy.start()
    greet([SEQ_AXES, ("dp",)], sizes)
    mixes = launch(sizes, ("context",), pick_target, True, mix_send, grad_mix, *sems[18:20])
    outputs = launch(sizes, ("place",), pick_second, True, y_ref, y_land, *sems[6:8])

    def chip_sum(i, expert, place):
        return owns[i][expert, place] + others[i][expert, place].astype(F32)

    stage_1 = []
    for i, axes in enumerate(firsts):
        for copy in loads[i]:
            copy.wait()

        def fill(expert, carry, i=i, axes=axes):
            for d in range(4):
                for v in range(2):
                    terms_now = chip_sum(i, expert, 2 * d + v).astype(BF16)
                    if axes == ("dp",):
                        sends[i][d, expert, v] = terms_now
                    else:
                        sends[i][v, expert, d] = terms_now
            return carry

        lax.fori_loop(0, experts, fill, 0)
        stage_1 += launch(sizes, axes, pick_target, False, sends[i], gots[i], *sems[2 * i : 2 * i + 2])
    for copy in mixes:
        copy.wait()
    attention_backward((queries, kv_all, mixtures, grad_mix, sums), (grad_query, terms), (sum_kv,))
    rest = launch(sizes, SEQ_AXES, pick_target, True, terms, kv_back, *sems[8:10])
    rest += launch(sizes, ("context",), pick_target, True, grad_query, query_back, *sems[10:12])
    half = part_index("half")
    for copy in outputs:
        copy.wait()

    def half_sum(number):
        total = y_land[0, number].astype(F32)
        for place in range(1, y_land.shape[0]):
            total = total + y_land[place, number].astype(F32)
        return total

    y_pass[1 - half] = half_sum(1 - half).astype(BF16)
    rest += launch(sizes, ("half",), pick_target, False, y_pass, y_got, *sems[20:22])
    for copy in stage_1:
        copy.wait()

    def part(i, expert, place):
        if firsts[i] == ("dp",):
            total = chip_sum(i, expert, 2 * dp + place)
            for step in range(1, 4):
                total = total + gots[i][lax.rem(dp + step, 4), expert, place].astype(F32)
            return total
        return chip_sum(i, expert, 2 * place + side) + gots[i][1 - side, expert, place].astype(F32)

    for i, axes in enumerate(seconds):

        def refill(expert, carry, i=i, axes=axes):
            for place in range(group_size(axes, sizes)):
                sends_2[i][place, expert] = part(i, expert, place).astype(BF16)
            return carry

        lax.fori_loop(0, experts, refill, 0)
    stage_2 = []
    for i, axes in enumerate(seconds):
        stage_2 += launch(
            sizes, axes, pick_target, False, sends_2[i], gots_2[i], *sems[12 + 2 * i : 14 + 2 * i]
        )
    for copy in stage_2:
        copy.wait()
    for i, axes in enumerate(seconds):
        me, total = own_index(axes, sizes), group_size(axes, sizes)

        def close(expert, carry, i=i, me=me, total=total):
            held = part(i, expert, me)
            for step in range(1, total):
                held = held + gots_2[i][lax.rem(me + step, total), expert].astype(F32)
            totals[i][expert] = held
            return carry

        lax.fori_loop(0, experts, close, 0)
    for copy in rest:
        copy.wait()
    y_total[...] = half_sum(half) + y_got[1 - half].astype(F32)


def run_backward(cid, sizes, owns, others, y_terms, data):
    queries, kv_all = data[:2]
    tokens = queries.shape[1]
    experts = owns[0].shape[0]
    vmem = pl.BlockSpec(memory_space=pltpu.VMEM)
    tiles = [own.shape[2:] for own in owns]
    stage_1 = [(4, experts, 2, *tiles[0]), (4, experts, 2, *tiles[1]), (2, experts, 4, *tiles[2])]
    stage_2 = [(2, experts, *tiles[0]), (2, experts, *tiles[1]), (4, experts, *tiles[2])]
    context = sizes["context"]
    sizes_of = [4, 4, 2, 4, group_size(SEQ_AXES, sizes), context, 2, 2, 4, context, 2]
    places, rows = y_terms.shape[1], y_terms.shape[2:]
    dma = pltpu.SemaphoreType.DMA
    return pl.pallas_call(
        functools.partial(backward_body, sizes),
        out_shape=[
            jax.ShapeDtypeStruct(rows, F32),
            jax.ShapeDtypeStruct(kv_all.shape, BF16),
            jax.ShapeDtypeStruct(queries.shape, F32),
            *[jax.ShapeDtypeStruct((experts, *tile), F32) for tile in tiles],
        ],
        in_specs=[*([pl.BlockSpec(memory_space=pl.ANY)] * 6), *([vmem] * 6)],
        out_specs=[vmem] * 6,
        scratch_shapes=[
            *[pltpu.VMEM(shape, BF16) for shape in stage_1 * 2 + stage_2 * 2],
            pltpu.VMEM(queries.shape, F32),
            pltpu.VMEM(kv_all.shape, BF16),
            pltpu.VMEM((kv_all.shape[0] * tokens, 2 * HEAD_DIM), F32),
            pltpu.VMEM(queries.shape, BF16),
            *[pltpu.VMEM(own.shape, F32) for own in owns],
            *[pltpu.VMEM(own.shape, BF16) for own in owns],
            pltpu.VMEM((places, 2, *rows), BF16),
            pltpu.VMEM((2, *rows), BF16),
            pltpu.VMEM((2, *rows), BF16),
            *[dma((n,)) for n in sizes_of for _ in range(2)],
            dma((6,)),
        ],
        name="attention_backward",
        compiler_params=pltpu.CompilerParams(
            collective_id=cid, has_side_effects=True, vmem_limit_bytes=67_043_328
        ),
    )(*owns, *others, y_terms, *data)


NEAR = ((0, 0), (1, 0), (0, 1), (0, 3), (0, 2), (1, 1), (1, 3), (1, 2))


def owner_at(owner, steps, sign):
    half = lax.rem(owner // 4 + steps[0], 2)
    return half * 4 + lax.rem(owner + 4 + sign * steps[1], 4)


def moe_copies(sizes, refs):
    moe_ref, table_ref, moe_land, table_land, d_send, d_back, dots, dot_back, g_sends, g_backs, sems = refs
    owner, context = lax.axis_index("expert"), lax.axis_index("context")

    def pair_of(copies, target, number):
        return [
            pltpu.make_async_remote_copy(
                src_ref=src,
                dst_ref=dst,
                send_sem=send.at[number],
                recv_sem=recv.at[number],
                device_id={"expert": target},
                device_id_type=MESH_ID,
            )
            for src, dst, send, recv in copies
        ]

    def tokens_to(number):
        pairs = (
            (table_ref, table_land.at[number], sems[7], sems[8]),
            (moe_ref, moe_land.at[number], sems[9], sems[10]),
        )
        return pair_of(pairs, owner_at(owner, NEAR[number], 1), number)

    def results_of(number):
        target = owner_at(owner, NEAR[number], -1)
        pairs = (
            (d_send.at[target], d_back.at[owner], sems[0], sems[1]),
            (dots.at[target], dot_back.at[owner], sems[2], sems[3]),
        )
        return pair_of(pairs, target, number)

    def own_results():
        return [
            pltpu.make_async_copy(d_send.at[owner], d_back.at[owner], sems[0].at[0]),
            pltpu.make_async_copy(dots.at[owner], dot_back.at[owner], sems[2].at[0]),
        ]

    def halves(number):
        partner = context + 1 - 2 * lax.rem(context, 2)
        return [
            pltpu.make_async_remote_copy(
                src_ref=g_sends[i].at[number],
                dst_ref=g_backs[i].at[number],
                send_sem=sems[4].at[3 * number + i],
                recv_sem=sems[5].at[3 * number + i],
                device_id={"context": partner},
                device_id_type=MESH_ID,
            )
            for i in range(3)
        ]

    return tokens_to, results_of, own_results, halves


def moe_body(
    sizes,
    moe_ref,
    table_ref,
    grad_ref,
    wg_ref,
    wu_ref,
    wd_ref,
    own_g,
    own_u,
    own_d,
    back_g,
    back_u,
    back_d,
    y_out,
    d_back,
    dot_back,
    moe_land,
    table_land,
    x_all,
    g_now,
    deo_all,
    dgu_all,
    eh_all,
    eo_all,
    dbuf_all,
    picks,
    highs,
    lows,
    gate_col,
    dot_col,
    dots,
    y_send,
    d_send,
    send_g,
    send_u,
    send_d,
    *sems,
):
    step = pl.program_id(0)
    owners = sizes["expert"]
    owner, context = lax.axis_index("expert"), lax.axis_index("context")
    core = lax.rem(context, 2)
    mine = 4
    group = owners // 2
    tokens, width = moe_ref.shape
    hidden_width = wg_ref.shape[2]
    rows = group * CAP
    barrier = pltpu.get_barrier_semaphore()
    tokens_to, results_of, own_results, halves = moe_copies(
        sizes,
        (
            moe_ref,
            table_ref,
            moe_land,
            table_land,
            d_send,
            d_back,
            dots,
            dot_back,
            (send_g, send_u, send_d),
            (back_g, back_u, back_d),
            sems,
        ),
    )

    @pl.when(step == 0)
    def _():
        for number in range(1, owners):
            pl.semaphore_signal(
                barrier,
                inc=1,
                device_id={"expert": lax.rem(owner + number, owners)},
                device_id_type=MESH_ID,
            )
        pl.semaphore_signal(
            barrier, inc=1, device_id={"context": context + 1 - 2 * core}, device_id_type=MESH_ID
        )
        pl.semaphore_wait(barrier, owners)
        for number in range(1, group):
            for copy in tokens_to(number):
                copy.start()
        dots[...] = jnp.zeros_like(dots)
        moe_land[0] = moe_ref[...]
        table_land[0] = table_ref[...]
        for number in range(1, group):
            for copy in tokens_to(number):
                copy.wait_recv()
        for number in range(group, owners):
            for copy in tokens_to(number):
                copy.start()

    @pl.when(step == mine)
    def _():
        for copy in own_results():
            copy.start()
        for number in range(1, group):
            for copy in results_of(number):
                copy.start()
        for number in range(group, owners):
            for copy in tokens_to(number):
                copy.wait_recv()

    @pl.when(step == 2 * mine)
    def _():
        for number in range(group, owners):
            for copy in results_of(number):
                copy.start()
        pltpu.make_async_copy(y_send, y_out, sems[6].at[0]).start()

    for number in range(mine):

        @pl.when(step == 2 * mine + 1 + number)
        def _(number=number):
            for copy in halves(number):
                copy.start()

    @pl.when(step < 2 * mine)
    def _():
        expert, tile = lax.rem(step, mine), step // mine
        place = pl.multiple_of(expert * CAP, CAP)
        spot = pl.ds(place, CAP)
        here = pl.ds(pl.multiple_of(tile * rows, rows), rows)
        part = pl.ds(tile * group, group)

        def source_of(j):
            near, far = owner_at(owner, NEAR[j], -1), owner_at(owner, NEAR[group + j], -1)
            return near + tile * (far - near)

        table = jnp.concatenate(
            [table_land[tile * group + j, pl.ds(owner * mine + expert, 1), :] for j in range(group)], axis=0
        )
        table = jnp.concatenate([table, table], axis=0)
        named = table >= 0.0
        above = lax.broadcasted_iota(jnp.int32, (tokens, tokens), 0)
        beside = lax.broadcasted_iota(jnp.int32, (tokens, tokens), 1)
        before = (above < beside).astype(F32).astype(BF16)
        slots = dot(named.astype(F32).astype(BF16), before)
        slots = jnp.where(named, slots, -1.0)
        counts = lax.broadcasted_iota(jnp.int32, (CAP, tokens), 0).astype(F32)
        for j in range(group):
            position = tile * group + j
            source = source_of(j)
            chosen = counts == slots[j : j + 1]
            onehot = jnp.where(chosen, 1.0, 0.0).astype(BF16)
            weight = jnp.where(chosen, table[j : j + 1], 0.0)
            high = weight.astype(BF16)
            picks[position, spot, :] = onehot
            highs[position, spot, :] = high
            lows[position, spot, :] = (weight - high.astype(F32)).astype(BF16)
            gate_col[j * CAP : (j + 1) * CAP, :] = jnp.sum(weight, axis=1, keepdims=True)
            line = pl.ds(pl.multiple_of(tile * rows + j * CAP, CAP), CAP)
            x_all[expert, line, :] = dot(onehot, moe_land[position]).astype(BF16)
            g_now[j * CAP : (j + 1) * CAP, :] = dot(onehot, grad_ref[source]).astype(BF16)

        rows_in = x_all[expert, here, :]
        gate_act = dot(rows_in, wg_ref[0])
        up_act = dot(rows_in, wu_ref[0])
        sigma = jax.nn.sigmoid(gate_act)
        silu = gate_act * sigma
        hidden = (silu * up_act).astype(BF16)
        eh_all[expert, here, :] = hidden
        expert_out = dot(hidden, wd_ref[0]).astype(BF16)
        eo_all[part, spot, :] = expert_out.reshape(group, CAP, width)
        grads = g_now[...].astype(F32)
        dot_col[...] = jnp.sum(grads * expert_out.astype(F32), axis=1, keepdims=True)
        grad_expert = (gate_col[...] * grads).astype(BF16)
        deo_all[expert, here, :] = grad_expert
        grad_hidden = dot_t(grad_expert, wd_ref[0])
        slope = sigma * (1.0 + gate_act * (1.0 - sigma))
        grad_gate = (grad_hidden * up_act * slope).astype(BF16)
        grad_up = (grad_hidden * silu).astype(BF16)
        dgu_all[expert, here, :hidden_width] = grad_gate
        dgu_all[expert, here, hidden_width:] = grad_up
        grad_buffer = (dot_t(grad_gate, wg_ref[0]) + dot_t(grad_up, wu_ref[0])).astype(BF16)
        dbuf_all[part, spot, :] = grad_buffer.reshape(group, CAP, width)
        for j in range(group):
            position = tile * group + j
            source = source_of(j)
            onehot = picks[position, spot, :].astype(F32)
            dots[source, pl.ds(expert, 1), :] = jnp.sum(
                onehot * dot_col[j * CAP : (j + 1) * CAP, :], axis=0, keepdims=True
            )

        @pl.when(expert == mine - 1)
        def _():
            for j in range(group):
                position, source = tile * group + j, source_of(j)
                d_send[source] = t_dot(picks[position], dbuf_all[position]).astype(BF16)
                moved = t_dot(highs[position], eo_all[position]) + t_dot(lows[position], eo_all[position])
                y_send[source] = moved.astype(BF16)

    @pl.when((step >= 2 * mine) & (step < 3 * mine))
    def _():
        number = step - 2 * mine
        blocks = width // 256
        per = width // 16

        def gate_rows(j, carry):
            columns = pl.ds(pl.multiple_of(j * 256, 256), 256)
            rows_in = x_all[number, :, columns]
            for half, own, send in ((0, own_g, send_g), (1, own_u, send_u)):
                grads = dgu_all[number, :, half * hidden_width : (half + 1) * hidden_width]
                terms = t_dot(rows_in, grads).reshape(128 // per, 2, per, hidden_width)
                first, second = terms[:, 0], terms[:, 1]
                places = pl.ds(j * (128 // per), 128 // per)
                own[0, places] = jnp.where(core == 0, first, second)
                send[number, places] = jnp.where(core == 0, second, first).astype(BF16)
            return carry

        lax.fori_loop(0, blocks, gate_rows, 0)
        less = hidden_width // 16

        def down_rows(j, carry):
            columns = pl.ds(pl.multiple_of(j * 256, 256), 256)
            terms = t_dot(eh_all[number, :, columns], deo_all[number])
            terms = terms.reshape(128 // less, 2, less, width)
            first, second = terms[:, 0], terms[:, 1]
            places = pl.ds(j * (128 // less), 128 // less)
            own_d[0, places] = jnp.where(core == 0, first, second)
            send_d[number, places] = jnp.where(core == 0, second, first).astype(BF16)
            return carry

        lax.fori_loop(0, hidden_width // 256, down_rows, 0)

    @pl.when(step == 3 * mine)
    def _():
        for number in range(1, owners):
            for copy in tokens_to(number):
                copy.wait_send()
            for copy in results_of(number):
                copy.wait()
        for copy in own_results():
            copy.wait()
        pltpu.make_async_copy(y_send, y_out, sems[6].at[0]).wait()
        for number in range(mine):
            for copy in halves(number):
                copy.wait()


def run_experts(cid, sizes, moe_input, table, grad_all, gate_weight, up_weight, down_weight):
    owners, tokens, width = grad_all.shape
    mine, _, inner = gate_weight.shape
    rows = owners * CAP
    part, less = width // 16, inner // 16

    def fixed(array):
        return pl.BlockSpec(array.shape, lambda i: (0,) * array.ndim, pipeline_mode=pl.Buffered(1))

    def expert_block(array):
        return pl.BlockSpec((1, *array.shape[1:]), lambda i: (lax.rem(jnp.minimum(i, 2 * mine - 1), mine), 0, 0))

    def own_block(*shape):
        return pl.BlockSpec((1, *shape), lambda i: (jnp.clip(i - 2 * mine, 0, mine - 1), 0, 0, 0))

    anywhere = pl.BlockSpec(memory_space=pl.ANY)
    wide, tall = (8, part, inner), (8, less, width)
    dma = pltpu.SemaphoreType.DMA
    return pl.pallas_call(
        functools.partial(moe_body, sizes),
        grid=(3 * mine + 1,),
        out_shape=[
            jax.ShapeDtypeStruct((mine, *wide), F32),
            jax.ShapeDtypeStruct((mine, *wide), F32),
            jax.ShapeDtypeStruct((mine, *tall), F32),
            jax.ShapeDtypeStruct((mine, *wide), BF16),
            jax.ShapeDtypeStruct((mine, *wide), BF16),
            jax.ShapeDtypeStruct((mine, *tall), BF16),
            jax.ShapeDtypeStruct((owners, tokens, width), BF16),
            jax.ShapeDtypeStruct((owners, tokens, width), BF16),
            jax.ShapeDtypeStruct((owners, 8, tokens), F32),
        ],
        in_specs=[
            fixed(moe_input),
            fixed(table),
            fixed(grad_all),
            expert_block(gate_weight),
            expert_block(up_weight),
            expert_block(down_weight),
        ],
        out_specs=[own_block(*wide), own_block(*wide), own_block(*tall), *([anywhere] * 6)],
        scratch_shapes=[
            pltpu.VMEM(grad_all.shape, BF16),
            pltpu.VMEM((owners, *table.shape), F32),
            pltpu.VMEM((mine, rows, width), BF16),
            pltpu.VMEM((rows // 2, width), BF16),
            pltpu.VMEM((mine, rows, width), BF16),
            pltpu.VMEM((mine, rows, 2 * inner), BF16),
            pltpu.VMEM((mine, rows, inner), BF16),
            pltpu.VMEM((owners, mine * CAP, width), BF16),
            pltpu.VMEM((owners, mine * CAP, width), BF16),
            pltpu.VMEM((owners, mine * CAP, tokens), BF16),
            pltpu.VMEM((owners, mine * CAP, tokens), BF16),
            pltpu.VMEM((owners, mine * CAP, tokens), BF16),
            pltpu.VMEM((rows // 2, 1), F32),
            pltpu.VMEM((rows // 2, 1), F32),
            pltpu.VMEM((owners, 8, tokens), F32),
            pltpu.VMEM((owners, tokens, width), BF16),
            pltpu.VMEM((owners, tokens, width), BF16),
            pltpu.VMEM((mine, *wide), BF16),
            pltpu.VMEM((mine, *wide), BF16),
            pltpu.VMEM((mine, *tall), BF16),
            dma((owners,)),
            dma((owners,)),
            dma((owners,)),
            dma((owners,)),
            dma((3 * mine,)),
            dma((3 * mine,)),
            dma((1,)),
            *[dma((owners,))] * 4,
        ],
        name="run_experts",
        compiler_params=pltpu.CompilerParams(
            collective_id=cid, has_side_effects=True, vmem_limit_bytes=67_043_328
        ),
    )(moe_input, table, grad_all, gate_weight, up_weight, down_weight)


CHIP_AXES = ("dp", "side", "expert")
PLANE_AXES = ("side", "expert")
CUT = 384


def sum_body(sizes, *refs):
    query_in, key_in, value_in, output_in, narrow_in = refs[:5]
    whole, load, near, sums, got = refs[5:10]
    near_send, near_recv, send_sems, recv_sems = refs[10:14]
    gather_sems = refs[14:]
    core = lax.rem(lax.axis_index("context"), 2)
    partner = {"context": lax.axis_index("context") + 1 - 2 * core}
    me, total = own_index(CHIP_AXES, sizes), group_size(CHIP_AXES, sizes)
    plane = total // sizes["dp"]
    rows = load.shape[1]
    some, wide = rows // 2, query_in.shape[1]
    half = wide // 2

    def place(step):
        target = lax.rem(me + step, total)
        return target, coords_of(CHIP_AXES, sizes, target)

    def remote(src, dst, send, recv, peer):
        return pltpu.make_async_remote_copy(
            src_ref=src, dst_ref=dst, send_sem=send, recv_sem=recv, device_id=peer, device_id_type=MESH_ID
        )

    def reduce_copy(step):
        target, peer = place(step)
        return remote(sums.at[target], got.at[me], send_sems.at[step], recv_sems.at[step], peer)

    dp, spot = lax.axis_index("dp"), own_index(PLANE_AXES, sizes)
    planes, cut = sizes["dp"], CUT
    low, high = pl.ds(0, cut), pl.ds(cut, whole.shape[4] - cut)

    def across(step, view, pair):
        peer = {"dp": lax.rem(dp + step, planes)}
        return remote(view, view, pair[0].at[step], pair[1].at[step], peer)

    def along(step, view, pair):
        peer = coords_of(PLANE_AXES, sizes, lax.rem(spot + step, plane))
        return remote(view, view, pair[0].at[step], pair[1].at[step], peer)

    def low_first(step):
        return across(step, whole.at[core, dp, spot, :, low], gather_sems[0:2])

    def low_second(step):
        return along(step, whole.at[core, :, spot, :, low], gather_sems[2:4])

    def low_pass(step):
        view = whole.at[core, :, lax.rem(spot - step + plane, plane), :, low]
        return remote(view, view, gather_sems[4].at[step], gather_sems[5].at[step], partner)

    def high_first(step):
        return along(step, whole.at[core, dp, spot, :, high], gather_sems[6:8])

    def high_second(step):
        return across(step, whole.at[core, dp, :, :, high], gather_sems[8:10])

    def high_pass(step):
        view = whole.at[core, lax.rem(dp - step + planes, planes), :, :, high]
        return remote(view, view, gather_sems[10].at[step], gather_sems[11].at[step], partner)

    def near_copy(turn):
        chunks = pl.ds(lax.rem(lax.axis_index("dp") + turn, sizes["dp"]) * plane, plane)
        return remote(load.at[chunks], near.at[chunks], near_send.at[turn], near_recv.at[turn], partner)

    def each(start, stop, body):
        def run(step, carry):
            body(step)
            return carry

        lax.fori_loop(start, stop, run, 0)

    def pack(number, chunk):
        here = pl.ds(pl.multiple_of(chunk * rows, rows), rows)
        there = pl.ds(pl.multiple_of(chunk * some, some), some)
        if number == 0:
            parts = [query_in[here, :]]
        else:
            parts = [key_in[here, :], value_in[here, :]]
        start = number * wide
        output = jnp.concatenate(
            [output_in[there, start : start + half], output_in[there, start + half : start + wide]], axis=0
        )
        return jnp.concatenate([*parts, output, narrow_in[here, :]], axis=1)

    barrier = pltpu.get_barrier_semaphore()
    pl.semaphore_signal(barrier, inc=1, device_id=partner, device_id_type=MESH_ID)
    each(
        1,
        total,
        lambda step: pl.semaphore_signal(
            barrier, inc=1, device_id=place(step)[1], device_id_type=MESH_ID
        ),
    )
    for turn in range(sizes["dp"]):
        base = lax.rem(lax.axis_index("dp") + turn, sizes["dp"]) * plane
        for number in range(2):

            @pl.when(core == 1 - number)
            def _(number=number, base=base):
                def fill(chunk):
                    load[chunk] = pack(number, chunk).astype(BF16)

                each(base, base + plane, fill)

        if turn == 0:
            pl.semaphore_wait(barrier, total)
        near_copy(turn).start()

    for turn in range(sizes["dp"]):
        near_copy(turn).wait()
        base = lax.rem(lax.axis_index("dp") + turn, sizes["dp"]) * plane
        for number in range(2):

            @pl.when(core == number)
            def _(number=number, base=base):
                def add(chunk):
                    sums[chunk] = (pack(number, chunk) + near[chunk].astype(F32)).astype(BF16)

                each(base, base + plane, add)

        def send(i, base=base):
            target = base + lax.rem(me + i, plane)

            @pl.when(target != me)
            def _():
                reduce_copy(lax.rem(target - me + total, total)).start()

        each(0, plane, send)

    got[me] = sums[me]
    each(1, total, lambda step: reduce_copy(step).wait())
    result = lax.fori_loop(
        0, total, lambda i, held: held + got[i].astype(F32), jnp.zeros(got.shape[1:], F32)
    )
    whole[core, dp, spot] = result.astype(BF16)
    each(1, planes, lambda step: low_first(step).start())
    each(1, plane, lambda step: high_first(step).start())
    each(1, planes, lambda step: low_first(step).wait_recv())
    each(1, plane, lambda step: low_second(step).start())
    low_pass(0).start()
    each(1, plane, lambda step: high_first(step).wait_recv())
    each(1, planes, lambda step: high_second(step).start())
    high_pass(0).start()

    def forward_low(step):
        low_second(step).wait_recv()
        low_pass(step).start()

    def forward_high(step):
        high_second(step).wait_recv()
        high_pass(step).start()

    each(1, plane, forward_low)
    each(1, planes, forward_high)
    each(1, planes, lambda step: low_first(step).wait_send())
    each(1, plane, lambda step: low_second(step).wait_send())
    each(1, plane, lambda step: high_first(step).wait_send())
    each(1, planes, lambda step: high_second(step).wait_send())
    each(0, plane, lambda step: low_pass(step).wait())
    each(0, planes, lambda step: high_pass(step).wait())


def unpack_body(whole, query_out, key_out, value_out, output_out, narrow_out):
    chunks, rows = whole.shape[1:3]
    some, wide = rows // 2, query_out.shape[1]
    half = wide // 2
    for chunk in range(chunks):
        here = slice(chunk * rows, (chunk + 1) * rows)
        there = slice(chunk * some, (chunk + 1) * some)
        for number in range(2):
            block = whole[number, chunk].astype(F32)
            if number == 0:
                query_out[here, :] = block[:, :wide]
                narrow_out[here, :] = block[:, wide + half :]
            else:
                key_out[here, :] = block[:, :half]
                value_out[here, :] = block[:, half:wide]
            start = number * wide
            output_out[there, start : start + half] = block[:some, wide : wide + half]
            output_out[there, start + half : start + wide] = block[some:, wide : wide + half]


def sum_everywhere(cid, sizes, *arrays):
    total = group_size(CHIP_AXES, sizes)
    depth, wide = arrays[0].shape
    half = (total, depth // total, wide + wide // 2 + arrays[4].shape[1])
    dma = pltpu.SemaphoreType.DMA
    vmem = pl.BlockSpec(memory_space=pltpu.VMEM)
    planes = sizes["dp"]
    plane = total // planes
    whole = pl.pallas_call(
        functools.partial(sum_body, sizes),
        out_shape=jax.ShapeDtypeStruct((2, planes, total // planes, *half[1:]), BF16),
        in_specs=[vmem] * 5,
        out_specs=vmem,
        scratch_shapes=[pltpu.VMEM(half, BF16)] * 4
        + [dma((planes,))] * 2
        + [dma((total,))] * 2
        + [dma((n,)) for n in (planes, plane, plane, plane, planes, planes) for _ in range(2)],
        name="sum_everywhere",
        compiler_params=pltpu.CompilerParams(
            collective_id=cid, has_side_effects=True, vmem_limit_bytes=60_000_000
        ),
    )(*arrays)
    parts = 4
    return pl.pallas_call(
        unpack_body,
        grid=(parts,),
        out_shape=[jax.ShapeDtypeStruct(array.shape, F32) for array in arrays],
        in_specs=[pl.BlockSpec((2, total // parts, *half[1:]), lambda i: (0, i, 0, 0))],
        out_specs=[
            pl.BlockSpec((array.shape[0] // parts, array.shape[1]), lambda i: (i, 0)) for array in arrays
        ],
        name="unpack_sums",
    )(whole.reshape(2, *half))


def rope_tables(positions, head_size):
    half_dim = head_size // 2
    frequency = ROPE_BASE ** (-2.0 * jnp.arange(half_dim, dtype=F32) / head_size)
    angles = positions.astype(F32)[:, None] * frequency[None, :]
    angles = jnp.concatenate([angles, angles], axis=1)
    return (jnp.cos(angles), jnp.sin(angles))


def rotate(values, cosine, sine_table):
    half_dim = values.shape[-1] // 2
    turned = jnp.concatenate([-values[..., half_dim:], values[..., :half_dim]], axis=-1)
    return values * cosine[:, None, :] + turned * sine_table[:, None, :]


def rotate_back(grads, cosine, sine_table):
    half_dim = grads.shape[-1] // 2
    scaled = grads * sine_table[:, None, :]
    turned = jnp.concatenate([scaled[..., half_dim:], -scaled[..., :half_dim]], axis=-1)
    return grads * cosine[:, None, :] + turned


def norm_forward(values, gain_vec):
    inverse = lax.rsqrt(jnp.mean(values * values, axis=-1, keepdims=True) + EPSILON)
    normed = values * inverse
    return (inverse, normed, (normed * gain_vec).astype(BF16))


def norm_backward(grad_out, normed, inverse, gain_vec):
    gain_grad = jnp.sum(grad_out * normed, axis=0)
    scaled = grad_out * gain_vec
    inner = jnp.mean(scaled * normed, axis=-1, keepdims=True)
    return (gain_grad, inverse * (scaled - normed * inner))


def local(
    sizes,
    inputs,
    prenorm_gain,
    query_weight,
    key_weight,
    value_weight,
    output_weight,
    midnorm_gain,
    router_weight,
    gate_weight,
    up_weight,
    down_weight,
    expert_ids,
    cotangent,
):
    tokens, width = inputs.shape[1:]
    owners = sizes["expert"]
    mine = gate_weight.shape[0]
    context, owner = lax.axis_index("context"), lax.axis_index("expert")
    block = context * owners + owner
    positions = block * tokens + jnp.arange(tokens, dtype=jnp.int32)
    cosine, sine_table = rope_tables(positions, HEAD_DIM)

    input_float = inputs[0].astype(F32)
    inverse_first, normed_first, attn_input = norm_forward(input_float, prenorm_gain)
    query_raw = dot(attn_input, query_weight).reshape(tokens, HEADS, HEAD_DIM)
    key_raw = dot(attn_input, key_weight).reshape(tokens, KV_HEADS, HEAD_DIM)
    value_raw = dot(attn_input, value_weight).reshape(tokens, KV_HEADS, HEAD_DIM)
    query_rot = rotate(query_raw, cosine, sine_table).astype(BF16)
    key_rot = rotate(key_raw, cosine, sine_table).astype(BF16)
    query_send = query_rot.reshape(tokens, KV_HEADS, 2 * HEAD_DIM).transpose(1, 0, 2)
    kv_send = jnp.concatenate([key_rot, value_raw.astype(BF16)], axis=2).transpose(1, 0, 2)
    kv_all, queries, grad_all, mixtures, sums, mixture = run_forward(
        0, sizes, kv_send, query_send, cotangent[0]
    )
    mixture_flat = mixture.transpose(1, 0, 2).reshape(tokens, HEADS * HEAD_DIM)

    after_attn = input_float + dot(mixture_flat, output_weight)
    inverse_second, normed_second, moe_input = norm_forward(after_attn, midnorm_gain)
    logits = lax.dot_general(
        router_weight, moe_input, (((0,), (1,)), ((), ())), preferred_element_type=F32
    )
    numbers = jnp.arange(EXPERTS, dtype=jnp.int32)[:, None, None]
    chosen = jnp.any(expert_ids[0].T[None] == numbers, axis=1)
    masked = jnp.where(chosen, logits, -jnp.inf)
    powers = jnp.exp(masked - jnp.max(masked, axis=0, keepdims=True))
    gates = powers / jnp.sum(powers, axis=0, keepdims=True)
    gate_table = jnp.where(chosen, gates, -1.0)

    own_g, own_u, own_d, other_g, other_u, other_d, moe_terms, grad_back, dot_back = run_experts(
        3, sizes, moe_input, gate_table, grad_all, gate_weight, up_weight, down_weight
    )
    grad_gates = dot_back[:, :mine].reshape(EXPERTS, tokens)
    grad_logits = gates * (grad_gates - jnp.sum(gates * grad_gates, axis=0, keepdims=True))
    router_grad = jnp.einsum(
        "td,et->de", moe_input.astype(F32), grad_logits, precision=lax.Precision.HIGHEST
    )
    grad_moe_in = jnp.sum(grad_back.astype(F32), axis=0) + jnp.einsum(
        "et,de->td", grad_logits, router_weight.astype(F32), precision=lax.Precision.HIGHEST
    )
    grad_out = cotangent[0].astype(F32)
    midnorm_grad, grad_after = norm_backward(grad_moe_in, normed_second, inverse_second, midnorm_gain)
    grad_after = grad_out + grad_after
    grad_after_half = grad_after.astype(BF16)
    output_grad = t_dot(mixture_flat, grad_after_half)
    grad_mix = dot_t(grad_after_half, output_weight).astype(BF16)
    grad_mix = grad_mix.reshape(tokens, KV_HEADS, 2 * HEAD_DIM).transpose(1, 0, 2)
    moe_out, kv_back, grad_query, gate_sum, up_sum, down_sum = run_backward(
        8,
        sizes,
        (own_g, own_u, own_d),
        (other_g, other_u, other_d),
        moe_terms.reshape(2, owners // 2, tokens, width),
        (queries, kv_all, mixtures, grad_mix, sums),
    )
    outputs = (after_attn + moe_out).astype(BF16)
    grad_kv = jnp.sum(kv_back.astype(F32).reshape(KV_HEADS, owners, tokens, 2 * HEAD_DIM), axis=1)
    grad_kv = grad_kv.transpose(1, 0, 2)
    grad_query = grad_query.transpose(1, 0, 2).reshape(tokens, HEADS, HEAD_DIM)
    query_back = rotate_back(grad_query, cosine, sine_table).reshape(tokens, -1).astype(BF16)
    key_back = rotate_back(grad_kv[..., :HEAD_DIM], cosine, sine_table).reshape(tokens, -1).astype(BF16)
    value_back = grad_kv[..., HEAD_DIM:].reshape(tokens, -1).astype(BF16)
    query_grad = t_dot(attn_input, query_back)
    key_grad = t_dot(attn_input, key_back)
    value_grad = t_dot(attn_input, value_back)
    grad_attn_in = (
        dot_t(query_back, query_weight) + dot_t(key_back, key_weight) + dot_t(value_back, value_weight)
    )
    prenorm_grad, grad_inputs = norm_backward(grad_attn_in, normed_first, inverse_first, prenorm_gain)
    grad_inputs = grad_after + grad_inputs
    narrow = jnp.concatenate([router_grad, prenorm_grad[:, None], midnorm_grad[:, None]], axis=1)
    narrow = jnp.pad(narrow, ((0, 0), (0, 128 - EXPERTS - 2)))
    query_grad, key_grad, value_grad, output_grad, narrow = sum_everywhere(
        9, sizes, query_grad, key_grad, value_grad, output_grad, narrow
    )
    dense = (
        narrow[:, EXPERTS],
        query_grad,
        key_grad,
        value_grad,
        output_grad,
        narrow[:, EXPERTS + 1],
        narrow[:, :EXPERTS],
    )
    return (outputs[None], grad_inputs[None], *dense, gate_sum, up_sum, down_sum)


def solution(mesh):
    split = P("dp", ("context", "expert"), None)
    owned = P("expert", None, None)
    summed = P("expert", ("dp", "context"), None)
    in_specs = (split, *([P()] * 7), owned, owned, owned, split, split)
    out_specs = (split, split, *([P()] * 7), summed, summed, summed)
    return jax.shard_map(
        functools.partial(local, dict(mesh.shape)),
        mesh=mesh,
        in_specs=in_specs,
        out_specs=out_specs,
        check_vma=False,
    )
```

```python
import functools

import jax
import jax.numpy as jnp
from jax import lax
from jax.experimental import pallas as pl
from jax.experimental.pallas import tpu as pltpu
from jax.sharding import PartitionSpec as P

HEADS = 8
KV_HEADS = 4
HEAD_DIM = 64
EXPERTS = 32
TOP = 8
CAP = 64
EPSILON = 1e-06
ROPE_BASE = 10000.0
F32 = jnp.float32
BF16 = jnp.bfloat16
MESH_ID = pl.DeviceIdType.MESH
SEQ_AXES = ("context", "expert")


def dot(left, right):
    return jnp.dot(left, right, preferred_element_type=F32)


def dot_t(left, right):
    return lax.dot_general(left, right, (((1,), (1,)), ((), ())), preferred_element_type=F32)


def t_dot(left, right):
    return lax.dot_general(left, right, (((0,), (0,)), ((), ())), preferred_element_type=F32)


PARTS = {"side": ("context", 2, 2), "half": ("expert", 2, 4), "place": ("expert", 4, 1)}


def axis_size(sizes, name):
    return PARTS[name][1] if name in PARTS else sizes[name]


def group_size(axes, sizes):
    total = 1
    for name in axes:
        total *= axis_size(sizes, name)
    return total


def part_index(name):
    if name not in PARTS:
        return lax.axis_index(name)
    axis, size, stride = PARTS[name]
    return lax.rem(lax.axis_index(axis) // stride, size)


def own_index(axes, sizes):
    index = 0
    for name in axes:
        index = index * axis_size(sizes, name) + part_index(name)
    return index


def coords_of(axes, sizes, index):
    out = {}
    for name in reversed(axes):
        place = lax.rem(index, axis_size(sizes, name))
        if name in PARTS:
            axis, _, stride = PARTS[name]
            out[axis] = lax.axis_index(axis) + (place - part_index(name)) * stride
        else:
            out[name] = place
        index = index // axis_size(sizes, name)
    return out


def pick_whole(ref, target, peer):
    return ref


def pick_target(ref, target, peer):
    return ref.at[target]


def pick_second(ref, target, peer):
    return ref.at[:, target]


def pick_context(ref, target, peer):
    return ref.at[peer["context"]]


def greet(all_axes, sizes):
    barrier = pltpu.get_barrier_semaphore()
    groups = []
    for axes in all_axes:
        if not any(set(axes) <= set(other) for other in groups):
            groups = [other for other in groups if not set(other) <= set(axes)] + [axes]
    signals = 0
    for axes in groups:
        me, total = own_index(axes, sizes), group_size(axes, sizes)
        for step in range(1, total):
            peer = coords_of(axes, sizes, lax.rem(me + step, total))
            pl.semaphore_signal(barrier, inc=1, device_id=peer, device_id_type=MESH_ID)
        signals += total - 1
    pl.semaphore_wait(barrier, signals)


def launch(sizes, axes, pick, keep, source, landing, send, recv):
    started = []
    me, total = own_index(axes, sizes), group_size(axes, sizes)
    for step in range(1, total):
        target = lax.rem(me + step, total)
        peer = coords_of(axes, sizes, target)
        copy = pltpu.make_async_remote_copy(
            src_ref=pick(source, target, peer),
            dst_ref=landing.at[me],
            send_sem=send.at[step],
            recv_sem=recv.at[step],
            device_id=peer,
            device_id_type=MESH_ID,
        )
        copy.start()
        started.append(copy)
    if keep:
        own = pltpu.make_async_copy(
            pick(source, me, coords_of(axes, sizes, me)), landing.at[me], send.at[0]
        )
        own.start()
        started.append(own)
    return started


def stack_heads(block, low):
    tokens = block.shape[0]
    zero = jnp.zeros((tokens, HEAD_DIM), block.dtype)
    parts = [block[:, :HEAD_DIM], block[:, HEAD_DIM:]]
    return jnp.concatenate(
        [jnp.concatenate([part, zero] if low else [zero, part], axis=1) for part in parts], axis=0
    )


def causal(shape, tokens):
    keys = lax.broadcasted_iota(jnp.int32, shape, 0)
    queries = lax.rem(lax.broadcasted_iota(jnp.int32, shape, 1), tokens)
    return keys - queries <= lax.axis_index("expert") * tokens


def identity(size):
    shape = (size, size)
    return lax.broadcasted_iota(jnp.int32, shape, 0) == lax.broadcasted_iota(jnp.int32, shape, 1)


def attention_forward(data, results, scratch):
    query_ref, kv_ref = data
    out_ref, sum_ref = results
    (score_ref,) = scratch
    blocks, tokens = query_ref.shape[:2]
    chunk, columns = 8 * tokens, 2 * tokens

    def block(number, carry):
        rows = stack_heads(query_ref[number], True) * (HEAD_DIM ** (-0.5))
        rows = rows.astype(BF16)

        def keys_of(j):
            return pl.ds(pl.multiple_of(j * chunk, chunk), chunk)

        def kv_of(j):
            return kv_ref[pl.ds(j * 8, 8)].reshape(chunk, 2 * HEAD_DIM)

        def first(j, top):
            scores = dot_t(kv_of(j), rows)
            score_ref[keys_of(j), :] = scores
            return jnp.maximum(top, jnp.max(scores, axis=0, keepdims=True))

        top = lax.fori_loop(0, number, first, jnp.full((1, columns), -jnp.inf, F32))
        scores = dot_t(kv_of(number), rows)
        scores = jnp.where(causal(scores.shape, tokens), scores, -jnp.inf)
        score_ref[keys_of(number), :] = scores
        top = jnp.maximum(top, jnp.max(scores, axis=0, keepdims=True))

        def second(j, held):
            total, mixed = held
            powers = jnp.exp(score_ref[keys_of(j), :] - top)
            total = total + jnp.sum(powers, axis=0, keepdims=True)
            return total, mixed + t_dot(powers.astype(BF16), kv_of(j))

        start = (jnp.zeros((1, columns), F32), jnp.zeros((columns, 2 * HEAD_DIM), F32))
        total, mixed = lax.fori_loop(0, number + 1, second, start)
        sum_ref[number] = top + jnp.log(total)
        inverse = jnp.sum(jnp.where(identity(columns), 1.0 / total, 0.0), axis=1, keepdims=True)
        mixed = (mixed * inverse)[:, HEAD_DIM:]
        out_ref[number] = jnp.concatenate([mixed[:tokens], mixed[tokens:]], axis=1).astype(BF16)
        return carry

    lax.fori_loop(0, blocks, block, 0)


def attention_backward(data, results, scratch):
    query_ref, kv_ref, mix_ref, grad_ref, sum_ref = data
    grad_query_ref, terms_ref = results
    (sum_kv,) = scratch
    blocks, tokens = query_ref.shape[:2]
    chunk, columns = 8 * tokens, 2 * tokens
    factor = HEAD_DIM ** (-0.5)
    sum_kv[...] = jnp.zeros_like(sum_kv)

    def block(number, carry):
        rows = (stack_heads(query_ref[number], True) * factor).astype(BF16)
        grads = stack_heads(grad_ref[number], False)
        both = jnp.concatenate([rows, grads], axis=0)
        pairs = dot_t(stack_heads(mix_ref[number], False), grads)
        delta = jnp.sum(jnp.where(identity(columns), pairs, 0.0), axis=0, keepdims=True)
        logsum = sum_ref[number]

        def unit(j, total, masked):
            keys = pl.ds(pl.multiple_of(j * chunk, chunk), chunk)
            kv = kv_ref[pl.ds(j * 8, 8)].reshape(chunk, 2 * HEAD_DIM)
            products = dot_t(kv, both)
            soft = jnp.exp(products[:, :columns] - logsum)
            if masked:
                soft = jnp.where(causal(soft.shape, tokens), soft, 0.0)
            scores = (soft * (products[:, columns:] - delta)).astype(BF16)
            sum_kv[keys, :] += dot(jnp.concatenate([scores, soft.astype(BF16)], axis=1), both)
            return total + t_dot(scores, kv)

        total = lax.fori_loop(
            0, number, lambda j, held: unit(j, held, False), jnp.zeros((columns, 2 * HEAD_DIM), F32)
        )
        total = unit(number, total, True)[:, :HEAD_DIM] * factor
        grad_query_ref[number] = jnp.concatenate([total[:tokens], total[tokens:]], axis=1)
        return carry

    lax.fori_loop(0, blocks, block, 0)
    terms_ref[...] = sum_kv[...].astype(BF16).reshape(terms_ref.shape)


def forward_body(sizes, *refs):
    kv_send, query_send, grad_ref = refs[:3]
    kv_all, queries, grad_all, mixtures, sums, mixture_back = refs[3:9]
    sems, scores = refs[9:21], refs[21]
    mix_sems = refs[22:24]
    greet([SEQ_AXES], sizes)
    early = launch(sizes, ("context",), pick_target, True, query_send, queries, *sems[0:2])
    early += launch(sizes, SEQ_AXES, pick_context, True, kv_send, kv_all, *sems[2:4])
    half, place = part_index("half"), part_index("place")
    some = grad_ref.shape[0] // 2
    upper, lower = pl.ds(0, some), pl.ds(some, some)

    def grad_copies(axis, source, landing, pair):
        found = []
        for step in range(1, axis_size(sizes, axis)):
            target = lax.rem(part_index(axis) + step, axis_size(sizes, axis))
            copy = pltpu.make_async_remote_copy(
                src_ref=source,
                dst_ref=landing,
                send_sem=pair[0].at[step],
                recv_sem=pair[1].at[step],
                device_id=coords_of((axis,), sizes, target),
                device_id_type=MESH_ID,
            )
            copy.start()
            found.append(copy)
        return found

    near = grad_copies("half", grad_ref.at[upper], grad_all.at[half, place, upper], sems[4:6])
    near += grad_copies("place", grad_ref.at[lower], grad_all.at[half, place, lower], sems[6:8])
    grad_all[half, place] = grad_ref[...]
    for copy in early + near:
        copy.wait()
    columns, line = grad_all.at[:, place, upper], grad_all.at[half, :, lower]
    late = grad_copies("place", columns, columns, sems[8:10])
    late += grad_copies("half", line, line, sems[10:12])
    attention_forward((queries, kv_all), (mixtures, sums), (scores,))
    late += launch(sizes, ("context",), pick_target, True, mixtures, mixture_back, *mix_sems)
    for copy in late:
        copy.wait()


def run_forward(cid, sizes, kv_send, query_send, cotangent):
    heads, tokens, columns = query_send.shape
    total, owners = group_size(SEQ_AXES, sizes), sizes["expert"]
    vmem = pl.BlockSpec(memory_space=pltpu.VMEM)
    dma = pltpu.SemaphoreType.DMA
    return pl.pallas_call(
        functools.partial(forward_body, sizes),
        out_shape=[
            jax.ShapeDtypeStruct((total, tokens, columns), BF16),
            jax.ShapeDtypeStruct(query_send.shape, BF16),
            jax.ShapeDtypeStruct((2, owners // 2, *cotangent.shape), BF16),
            jax.ShapeDtypeStruct(query_send.shape, BF16),
            jax.ShapeDtypeStruct((heads, 1, 2 * tokens), F32),
            jax.ShapeDtypeStruct(query_send.shape, BF16),
        ],
        in_specs=[vmem] * 3,
        out_specs=[vmem] * 6,
        scratch_shapes=[
            *[dma((n,)) for n in (heads, total, 2, owners // 2, owners // 2, 2) for _ in range(2)],
            pltpu.VMEM((total * tokens, 2 * tokens), F32),
            *[dma((heads,))] * 2,
        ],
        name="attention_forward",
        compiler_params=pltpu.CompilerParams(
            collective_id=cid, has_side_effects=True, vmem_limit_bytes=60_000_000
        ),
    )(kv_send, query_send, cotangent)


def backward_body(sizes, *refs):
    owns_hbm, others_hbm, y_ref, refs = refs[:3], refs[3:6], refs[6], refs[7:]
    queries, kv_all, mixtures, mix_send, sums, *refs = refs
    y_total, kv_back, query_back, *totals = refs[:6]
    sends, gots, sends_2, gots_2 = refs[6:9], refs[9:12], refs[12:15], refs[15:18]
    grad_query, terms, sum_kv, grad_mix = refs[18:22]
    owns, others, refs = refs[22:25], refs[25:28], refs[28:]
    y_land, y_pass, y_got, *sems = refs
    dp, side = lax.axis_index("dp"), lax.axis_index("context") // 2
    experts = owns[0].shape[0]
    firsts = (("dp",), ("dp",), ("side",))
    seconds = (("side",), ("side",), ("dp",))
    loads = [
        (
            pltpu.make_async_copy(owns_hbm[i], owns[i], sems[22].at[i]),
            pltpu.make_async_copy(others_hbm[i], others[i], sems[22].at[3 + i]),
        )
        for i in range(3)
    ]
    for pair in loads:
        for copy in pair:
            copy.start()
    greet([SEQ_AXES, ("dp",)], sizes)
    mixes = launch(sizes, ("context",), pick_target, True, mix_send, grad_mix, *sems[18:20])
    outputs = launch(sizes, ("place",), pick_second, True, y_ref, y_land, *sems[6:8])

    def chip_sum(i, expert, place):
        return owns[i][expert, place] + others[i][expert, place].astype(F32)

    stage_1 = []
    for i, axes in enumerate(firsts):
        for copy in loads[i]:
            copy.wait()

        def fill(expert, carry, i=i, axes=axes):
            for d in range(4):
                for v in range(2):
                    terms_now = chip_sum(i, expert, 2 * d + v).astype(BF16)
                    if axes == ("dp",):
                        sends[i][d, expert, v] = terms_now
                    else:
                        sends[i][v, expert, d] = terms_now
            return carry

        lax.fori_loop(0, experts, fill, 0)
        stage_1 += launch(sizes, axes, pick_target, False, sends[i], gots[i], *sems[2 * i : 2 * i + 2])
    for copy in mixes:
        copy.wait()
    attention_backward((queries, kv_all, mixtures, grad_mix, sums), (grad_query, terms), (sum_kv,))
    rest = launch(sizes, SEQ_AXES, pick_target, True, terms, kv_back, *sems[8:10])
    rest += launch(sizes, ("context",), pick_target, True, grad_query, query_back, *sems[10:12])
    half = part_index("half")
    for copy in outputs:
        copy.wait()

    def half_sum(number):
        total = y_land[0, number].astype(F32)
        for place in range(1, y_land.shape[0]):
            total = total + y_land[place, number].astype(F32)
        return total

    y_pass[1 - half] = half_sum(1 - half).astype(BF16)
    rest += launch(sizes, ("half",), pick_target, False, y_pass, y_got, *sems[20:22])
    for copy in stage_1:
        copy.wait()

    def part(i, expert, place):
        if firsts[i] == ("dp",):
            total = chip_sum(i, expert, 2 * dp + place)
            for step in range(1, 4):
                total = total + gots[i][lax.rem(dp + step, 4), expert, place].astype(F32)
            return total
        return chip_sum(i, expert, 2 * place + side) + gots[i][1 - side, expert, place].astype(F32)

    for i, axes in enumerate(seconds):

        def refill(expert, carry, i=i, axes=axes):
            for place in range(group_size(axes, sizes)):
                sends_2[i][place, expert] = part(i, expert, place).astype(BF16)
            return carry

        lax.fori_loop(0, experts, refill, 0)
    stage_2 = []
    for i, axes in enumerate(seconds):
        stage_2 += launch(
            sizes, axes, pick_target, False, sends_2[i], gots_2[i], *sems[12 + 2 * i : 14 + 2 * i]
        )
    for copy in stage_2:
        copy.wait()
    for i, axes in enumerate(seconds):
        me, total = own_index(axes, sizes), group_size(axes, sizes)

        def close(expert, carry, i=i, me=me, total=total):
            held = part(i, expert, me)
            for step in range(1, total):
                held = held + gots_2[i][lax.rem(me + step, total), expert].astype(F32)
            totals[i][expert] = held
            return carry

        lax.fori_loop(0, experts, close, 0)
    for copy in rest:
        copy.wait()
    y_total[...] = half_sum(half) + y_got[1 - half].astype(F32)


def run_backward(cid, sizes, owns, others, y_terms, data):
    queries, kv_all = data[:2]
    tokens = queries.shape[1]
    experts = owns[0].shape[0]
    vmem = pl.BlockSpec(memory_space=pltpu.VMEM)
    tiles = [own.shape[2:] for own in owns]
    stage_1 = [(4, experts, 2, *tiles[0]), (4, experts, 2, *tiles[1]), (2, experts, 4, *tiles[2])]
    stage_2 = [(2, experts, *tiles[0]), (2, experts, *tiles[1]), (4, experts, *tiles[2])]
    context = sizes["context"]
    sizes_of = [4, 4, 2, 4, group_size(SEQ_AXES, sizes), context, 2, 2, 4, context, 2]
    places, rows = y_terms.shape[1], y_terms.shape[2:]
    dma = pltpu.SemaphoreType.DMA
    return pl.pallas_call(
        functools.partial(backward_body, sizes),
        out_shape=[
            jax.ShapeDtypeStruct(rows, F32),
            jax.ShapeDtypeStruct(kv_all.shape, BF16),
            jax.ShapeDtypeStruct(queries.shape, F32),
            *[jax.ShapeDtypeStruct((experts, *tile), F32) for tile in tiles],
        ],
        in_specs=[*([pl.BlockSpec(memory_space=pl.ANY)] * 6), *([vmem] * 6)],
        out_specs=[vmem] * 6,
        scratch_shapes=[
            *[pltpu.VMEM(shape, BF16) for shape in stage_1 * 2 + stage_2 * 2],
            pltpu.VMEM(queries.shape, F32),
            pltpu.VMEM(kv_all.shape, BF16),
            pltpu.VMEM((kv_all.shape[0] * tokens, 2 * HEAD_DIM), F32),
            pltpu.VMEM(queries.shape, BF16),
            *[pltpu.VMEM(own.shape, F32) for own in owns],
            *[pltpu.VMEM(own.shape, BF16) for own in owns],
            pltpu.VMEM((places, 2, *rows), BF16),
            pltpu.VMEM((2, *rows), BF16),
            pltpu.VMEM((2, *rows), BF16),
            *[dma((n,)) for n in sizes_of for _ in range(2)],
            dma((6,)),
        ],
        name="attention_backward",
        compiler_params=pltpu.CompilerParams(
            collective_id=cid, has_side_effects=True, vmem_limit_bytes=67_043_328
        ),
    )(*owns, *others, y_terms, *data)


NEAR = ((0, 0), (1, 0), (0, 1), (0, 3), (0, 2), (1, 1), (1, 3), (1, 2))


def owner_at(owner, steps, sign):
    half = lax.rem(owner // 4 + steps[0], 2)
    return half * 4 + lax.rem(owner + 4 + sign * steps[1], 4)


def moe_copies(sizes, refs):
    moe_ref, table_ref, moe_land, table_land, d_send, d_back, dots, dot_back, g_sends, g_backs, sems = refs
    owner, context = lax.axis_index("expert"), lax.axis_index("context")

    def pair_of(copies, target, number):
        return [
            pltpu.make_async_remote_copy(
                src_ref=src,
                dst_ref=dst,
                send_sem=send.at[number],
                recv_sem=recv.at[number],
                device_id={"expert": target},
                device_id_type=MESH_ID,
            )
            for src, dst, send, recv in copies
        ]

    def tokens_to(number):
        pairs = (
            (table_ref, table_land.at[number], sems[7], sems[8]),
            (moe_ref, moe_land.at[number], sems[9], sems[10]),
        )
        return pair_of(pairs, owner_at(owner, NEAR[number], 1), number)

    def results_of(number):
        target = owner_at(owner, NEAR[number], -1)
        pairs = (
            (d_send.at[target], d_back.at[owner], sems[0], sems[1]),
            (dots.at[target], dot_back.at[owner], sems[2], sems[3]),
        )
        return pair_of(pairs, target, number)

    def own_results():
        return [
            pltpu.make_async_copy(d_send.at[owner], d_back.at[owner], sems[0].at[0]),
            pltpu.make_async_copy(dots.at[owner], dot_back.at[owner], sems[2].at[0]),
        ]

    def halves(number):
        partner = context + 1 - 2 * lax.rem(context, 2)
        return [
            pltpu.make_async_remote_copy(
                src_ref=g_sends[i].at[number],
                dst_ref=g_backs[i].at[number],
                send_sem=sems[4].at[3 * number + i],
                recv_sem=sems[5].at[3 * number + i],
                device_id={"context": partner},
                device_id_type=MESH_ID,
            )
            for i in range(3)
        ]

    return tokens_to, results_of, own_results, halves


def moe_body(
    sizes,
    moe_ref,
    table_ref,
    grad_ref,
    wg_ref,
    wu_ref,
    wd_ref,
    own_g,
    own_u,
    own_d,
    back_g,
    back_u,
    back_d,
    y_out,
    d_back,
    dot_back,
    moe_land,
    table_land,
    x_all,
    g_now,
    deo_all,
    dgu_all,
    eh_all,
    eo_all,
    dbuf_all,
    picks,
    highs,
    lows,
    gate_col,
    dot_col,
    dots,
    y_send,
    d_send,
    send_g,
    send_u,
    send_d,
    *sems,
):
    step = pl.program_id(0)
    owners = sizes["expert"]
    owner, context = lax.axis_index("expert"), lax.axis_index("context")
    core = lax.rem(context, 2)
    mine = 4
    group = owners // 2
    tokens, width = moe_ref.shape
    hidden_width = wg_ref.shape[2]
    rows = group * CAP
    barrier = pltpu.get_barrier_semaphore()
    tokens_to, results_of, own_results, halves = moe_copies(
        sizes,
        (
            moe_ref,
            table_ref,
            moe_land,
            table_land,
            d_send,
            d_back,
            dots,
            dot_back,
            (send_g, send_u, send_d),
            (back_g, back_u, back_d),
            sems,
        ),
    )

    @pl.when(step == 0)
    def _():
        for number in range(1, owners):
            pl.semaphore_signal(
                barrier,
                inc=1,
                device_id={"expert": lax.rem(owner + number, owners)},
                device_id_type=MESH_ID,
            )
        pl.semaphore_signal(
            barrier, inc=1, device_id={"context": context + 1 - 2 * core}, device_id_type=MESH_ID
        )
        pl.semaphore_wait(barrier, owners)
        for number in range(1, group):
            for copy in tokens_to(number):
                copy.start()
        dots[...] = jnp.zeros_like(dots)
        moe_land[0] = moe_ref[...]
        table_land[0] = table_ref[...]
        for number in range(1, group):
            for copy in tokens_to(number):
                copy.wait_recv()
        for number in range(group, owners):
            for copy in tokens_to(number):
                copy.start()

    @pl.when(step == mine)
    def _():
        for copy in own_results():
            copy.start()
        for number in range(1, group):
            for copy in results_of(number):
                copy.start()
        for number in range(group, owners):
            for copy in tokens_to(number):
                copy.wait_recv()

    @pl.when(step == 2 * mine)
    def _():
        for number in range(group, owners):
            for copy in results_of(number):
                copy.start()
        pltpu.make_async_copy(y_send, y_out, sems[6].at[0]).start()

    for number in range(mine):

        @pl.when(step == 2 * mine + 1 + number)
        def _(number=number):
            for copy in halves(number):
                copy.start()

    @pl.when(step < 2 * mine)
    def _():
        expert, tile = lax.rem(step, mine), step // mine
        place = pl.multiple_of(expert * CAP, CAP)
        spot = pl.ds(place, CAP)
        here = pl.ds(pl.multiple_of(tile * rows, rows), rows)
        part = pl.ds(tile * group, group)

        def source_of(j):
            near, far = owner_at(owner, NEAR[j], -1), owner_at(owner, NEAR[group + j], -1)
            return near + tile * (far - near)

        table = jnp.concatenate(
            [table_land[tile * group + j, pl.ds(owner * mine + expert, 1), :] for j in range(group)], axis=0
        )
        table = jnp.concatenate([table, table], axis=0)
        named = table >= 0.0
        above = lax.broadcasted_iota(jnp.int32, (tokens, tokens), 0)
        beside = lax.broadcasted_iota(jnp.int32, (tokens, tokens), 1)
        before = (above < beside).astype(F32).astype(BF16)
        slots = dot(named.astype(F32).astype(BF16), before)
        slots = jnp.where(named, slots, -1.0)
        counts = lax.broadcasted_iota(jnp.int32, (CAP, tokens), 0).astype(F32)
        for j in range(group):
            position = tile * group + j
            source = source_of(j)
            chosen = counts == slots[j : j + 1]
            onehot = jnp.where(chosen, 1.0, 0.0).astype(BF16)
            weight = jnp.where(chosen, table[j : j + 1], 0.0)
            high = weight.astype(BF16)
            picks[position, spot, :] = onehot
            highs[position, spot, :] = high
            lows[position, spot, :] = (weight - high.astype(F32)).astype(BF16)
            gate_col[j * CAP : (j + 1) * CAP, :] = jnp.sum(weight, axis=1, keepdims=True)
            line = pl.ds(pl.multiple_of(tile * rows + j * CAP, CAP), CAP)
            x_all[expert, line, :] = dot(onehot, moe_land[position]).astype(BF16)
            g_now[j * CAP : (j + 1) * CAP, :] = dot(onehot, grad_ref[source]).astype(BF16)

        rows_in = x_all[expert, here, :]
        gate_act = dot(rows_in, wg_ref[0])
        up_act = dot(rows_in, wu_ref[0])
        sigma = jax.nn.sigmoid(gate_act)
        silu = gate_act * sigma
        hidden = (silu * up_act).astype(BF16)
        eh_all[expert, here, :] = hidden
        expert_out = dot(hidden, wd_ref[0]).astype(BF16)
        eo_all[part, spot, :] = expert_out.reshape(group, CAP, width)
        grads = g_now[...].astype(F32)
        dot_col[...] = jnp.sum(grads * expert_out.astype(F32), axis=1, keepdims=True)
        grad_expert = (gate_col[...] * grads).astype(BF16)
        deo_all[expert, here, :] = grad_expert
        grad_hidden = dot_t(grad_expert, wd_ref[0])
        slope = sigma * (1.0 + gate_act * (1.0 - sigma))
        grad_gate = (grad_hidden * up_act * slope).astype(BF16)
        grad_up = (grad_hidden * silu).astype(BF16)
        dgu_all[expert, here, :hidden_width] = grad_gate
        dgu_all[expert, here, hidden_width:] = grad_up
        grad_buffer = (dot_t(grad_gate, wg_ref[0]) + dot_t(grad_up, wu_ref[0])).astype(BF16)
        dbuf_all[part, spot, :] = grad_buffer.reshape(group, CAP, width)
        for j in range(group):
            position = tile * group + j
            source = source_of(j)
            onehot = picks[position, spot, :].astype(F32)
            dots[source, pl.ds(expert, 1), :] = jnp.sum(
                onehot * dot_col[j * CAP : (j + 1) * CAP, :], axis=0, keepdims=True
            )

        @pl.when(expert == mine - 1)
        def _():
            for j in range(group):
                position, source = tile * group + j, source_of(j)
                d_send[source] = t_dot(picks[position], dbuf_all[position]).astype(BF16)
                moved = t_dot(highs[position], eo_all[position]) + t_dot(lows[position], eo_all[position])
                y_send[source] = moved.astype(BF16)

    @pl.when((step >= 2 * mine) & (step < 3 * mine))
    def _():
        number = step - 2 * mine
        blocks = width // 256
        per = width // 16

        def gate_rows(j, carry):
            columns = pl.ds(pl.multiple_of(j * 256, 256), 256)
            rows_in = x_all[number, :, columns]
            for half, own, send in ((0, own_g, send_g), (1, own_u, send_u)):
                grads = dgu_all[number, :, half * hidden_width : (half + 1) * hidden_width]
                terms = t_dot(rows_in, grads).reshape(128 // per, 2, per, hidden_width)
                first, second = terms[:, 0], terms[:, 1]
                places = pl.ds(j * (128 // per), 128 // per)
                own[0, places] = jnp.where(core == 0, first, second)
                send[number, places] = jnp.where(core == 0, second, first).astype(BF16)
            return carry

        lax.fori_loop(0, blocks, gate_rows, 0)
        less = hidden_width // 16

        def down_rows(j, carry):
            columns = pl.ds(pl.multiple_of(j * 256, 256), 256)
            terms = t_dot(eh_all[number, :, columns], deo_all[number])
            terms = terms.reshape(128 // less, 2, less, width)
            first, second = terms[:, 0], terms[:, 1]
            places = pl.ds(j * (128 // less), 128 // less)
            own_d[0, places] = jnp.where(core == 0, first, second)
            send_d[number, places] = jnp.where(core == 0, second, first).astype(BF16)
            return carry

        lax.fori_loop(0, hidden_width // 256, down_rows, 0)

    @pl.when(step == 3 * mine)
    def _():
        for number in range(1, owners):
            for copy in tokens_to(number):
                copy.wait_send()
            for copy in results_of(number):
                copy.wait()
        for copy in own_results():
            copy.wait()
        pltpu.make_async_copy(y_send, y_out, sems[6].at[0]).wait()
        for number in range(mine):
            for copy in halves(number):
                copy.wait()


def run_experts(cid, sizes, moe_input, table, grad_all, gate_weight, up_weight, down_weight):
    owners, tokens, width = grad_all.shape
    mine, _, inner = gate_weight.shape
    rows = owners * CAP
    part, less = width // 16, inner // 16

    def fixed(array):
        return pl.BlockSpec(array.shape, lambda i: (0,) * array.ndim, pipeline_mode=pl.Buffered(1))

    def expert_block(array):
        return pl.BlockSpec((1, *array.shape[1:]), lambda i: (lax.rem(jnp.minimum(i, 2 * mine - 1), mine), 0, 0))

    def own_block(*shape):
        return pl.BlockSpec((1, *shape), lambda i: (jnp.clip(i - 2 * mine, 0, mine - 1), 0, 0, 0))

    anywhere = pl.BlockSpec(memory_space=pl.ANY)
    wide, tall = (8, part, inner), (8, less, width)
    dma = pltpu.SemaphoreType.DMA
    return pl.pallas_call(
        functools.partial(moe_body, sizes),
        grid=(3 * mine + 1,),
        out_shape=[
            jax.ShapeDtypeStruct((mine, *wide), F32),
            jax.ShapeDtypeStruct((mine, *wide), F32),
            jax.ShapeDtypeStruct((mine, *tall), F32),
            jax.ShapeDtypeStruct((mine, *wide), BF16),
            jax.ShapeDtypeStruct((mine, *wide), BF16),
            jax.ShapeDtypeStruct((mine, *tall), BF16),
            jax.ShapeDtypeStruct((owners, tokens, width), BF16),
            jax.ShapeDtypeStruct((owners, tokens, width), BF16),
            jax.ShapeDtypeStruct((owners, 8, tokens), F32),
        ],
        in_specs=[
            fixed(moe_input),
            fixed(table),
            fixed(grad_all),
            expert_block(gate_weight),
            expert_block(up_weight),
            expert_block(down_weight),
        ],
        out_specs=[own_block(*wide), own_block(*wide), own_block(*tall), *([anywhere] * 6)],
        scratch_shapes=[
            pltpu.VMEM(grad_all.shape, BF16),
            pltpu.VMEM((owners, *table.shape), F32),
            pltpu.VMEM((mine, rows, width), BF16),
            pltpu.VMEM((rows // 2, width), BF16),
            pltpu.VMEM((mine, rows, width), BF16),
            pltpu.VMEM((mine, rows, 2 * inner), BF16),
            pltpu.VMEM((mine, rows, inner), BF16),
            pltpu.VMEM((owners, mine * CAP, width), BF16),
            pltpu.VMEM((owners, mine * CAP, width), BF16),
            pltpu.VMEM((owners, mine * CAP, tokens), BF16),
            pltpu.VMEM((owners, mine * CAP, tokens), BF16),
            pltpu.VMEM((owners, mine * CAP, tokens), BF16),
            pltpu.VMEM((rows // 2, 1), F32),
            pltpu.VMEM((rows // 2, 1), F32),
            pltpu.VMEM((owners, 8, tokens), F32),
            pltpu.VMEM((owners, tokens, width), BF16),
            pltpu.VMEM((owners, tokens, width), BF16),
            pltpu.VMEM((mine, *wide), BF16),
            pltpu.VMEM((mine, *wide), BF16),
            pltpu.VMEM((mine, *tall), BF16),
            dma((owners,)),
            dma((owners,)),
            dma((owners,)),
            dma((owners,)),
            dma((3 * mine,)),
            dma((3 * mine,)),
            dma((1,)),
            *[dma((owners,))] * 4,
        ],
        name="run_experts",
        compiler_params=pltpu.CompilerParams(
            collective_id=cid, has_side_effects=True, vmem_limit_bytes=67_043_328
        ),
    )(moe_input, table, grad_all, gate_weight, up_weight, down_weight)


CHIP_AXES = ("dp", "side", "expert")
PLANE_AXES = ("side", "expert")
CUT = 384


def sum_body(sizes, *refs):
    query_in, key_in, value_in, output_in, narrow_in = refs[:5]
    whole, load, near, sums = refs[5:9]
    low_land, low_mid, low_got, high_land, high_mid, high_got = refs[9:15]
    near_send, near_recv = refs[15:17]
    gather_sems, reduce_sems = refs[17:29], refs[29:]
    core = lax.rem(lax.axis_index("context"), 2)
    partner = {"context": lax.axis_index("context") + 1 - 2 * core}
    me, total = own_index(CHIP_AXES, sizes), group_size(CHIP_AXES, sizes)
    plane = total // sizes["dp"]
    rows = load.shape[1]
    some, wide = rows // 2, query_in.shape[1]
    half = wide // 2

    def place(step):
        target = lax.rem(me + step, total)
        return target, coords_of(CHIP_AXES, sizes, target)

    def remote(src, dst, send, recv, peer):
        return pltpu.make_async_remote_copy(
            src_ref=src, dst_ref=dst, send_sem=send, recv_sem=recv, device_id=peer, device_id_type=MESH_ID
        )

    dp, spot = lax.axis_index("dp"), own_index(PLANE_AXES, sizes)
    planes, cut = sizes["dp"], CUT
    low, high = pl.ds(0, cut), pl.ds(cut, whole.shape[4] - cut)

    def across(step, view, pair):
        peer = {"dp": lax.rem(dp + step, planes)}
        return remote(view, view, pair[0].at[step], pair[1].at[step], peer)

    def along(step, view, pair):
        peer = coords_of(PLANE_AXES, sizes, lax.rem(spot + step, plane))
        return remote(view, view, pair[0].at[step], pair[1].at[step], peer)

    def low_first(step):
        return across(step, whole.at[core, dp, spot, :, low], gather_sems[0:2])

    def low_second(step):
        return along(step, whole.at[core, :, spot, :, low], gather_sems[2:4])

    def low_pass(step):
        view = whole.at[core, :, lax.rem(spot - step + plane, plane), :, low]
        return remote(view, view, gather_sems[4].at[step], gather_sems[5].at[step], partner)

    def high_first(step):
        return along(step, whole.at[core, dp, spot, :, high], gather_sems[6:8])

    def high_second(step):
        return across(step, whole.at[core, dp, :, :, high], gather_sems[8:10])

    def high_pass(step):
        view = whole.at[core, lax.rem(dp - step + planes, planes), :, :, high]
        return remote(view, view, gather_sems[10].at[step], gather_sems[11].at[step], partner)

    def dp_at(step):
        return lax.rem(dp + step, planes)

    def spot_at(step):
        return lax.rem(spot + step, plane)

    def reduce_along(step, source, landing, pair):
        peer = coords_of(PLANE_AXES, sizes, spot_at(step))
        return remote(source, landing.at[spot], pair[0].at[step], pair[1].at[step], peer)

    def reduce_across(step, source, landing, pair):
        return remote(source, landing.at[dp], pair[0].at[step], pair[1].at[step], {"dp": dp_at(step)})

    def low_reduce(step):
        return reduce_along(step, sums.at[:, spot_at(step), :, low], low_land, reduce_sems[0:2])

    def low_finish(step):
        return reduce_across(step, low_mid.at[dp_at(step)], low_got, reduce_sems[2:4])

    def high_reduce(step):
        return reduce_across(step, sums.at[dp_at(step), :, :, high], high_land, reduce_sems[4:6])

    def high_finish(step):
        return reduce_along(step, high_mid.at[spot_at(step)], high_got, reduce_sems[6:8])

    def near_copy(turn):
        chunks = pl.ds(lax.rem(lax.axis_index("dp") + turn, sizes["dp"]) * plane, plane)
        return remote(load.at[chunks], near.at[chunks], near_send.at[turn], near_recv.at[turn], partner)

    def each(start, stop, body):
        def run(step, carry):
            body(step)
            return carry

        lax.fori_loop(start, stop, run, 0)

    def pack(number, chunk):
        here = pl.ds(pl.multiple_of(chunk * rows, rows), rows)
        there = pl.ds(pl.multiple_of(chunk * some, some), some)
        if number == 0:
            parts = [query_in[here, :]]
        else:
            parts = [key_in[here, :], value_in[here, :]]
        start = number * wide
        output = jnp.concatenate(
            [output_in[there, start : start + half], output_in[there, start + half : start + wide]], axis=0
        )
        return jnp.concatenate([*parts, output, narrow_in[here, :]], axis=1)

    barrier = pltpu.get_barrier_semaphore()
    pl.semaphore_signal(barrier, inc=1, device_id=partner, device_id_type=MESH_ID)
    each(
        1,
        total,
        lambda step: pl.semaphore_signal(
            barrier, inc=1, device_id=place(step)[1], device_id_type=MESH_ID
        ),
    )
    for turn in range(sizes["dp"]):
        base = lax.rem(lax.axis_index("dp") + turn, sizes["dp"]) * plane
        for number in range(2):

            @pl.when(core == 1 - number)
            def _(number=number, base=base):
                def fill(chunk):
                    load[chunk] = pack(number, chunk).astype(BF16)

                each(base, base + plane, fill)

        if turn == 0:
            pl.semaphore_wait(barrier, total)
        near_copy(turn).start()

    for turn in range(sizes["dp"]):
        near_copy(turn).wait()
        base = lax.rem(lax.axis_index("dp") + turn, sizes["dp"]) * plane
        for number in range(2):

            @pl.when(core == number)
            def _(number=number, base=base):
                def add(chunk, base=base, turn=turn):
                    place_now = lax.rem(lax.axis_index("dp") + turn, planes)
                    both = pack(number, chunk) + near[chunk].astype(F32)
                    sums[place_now, chunk - base] = both.astype(BF16)

                each(base, base + plane, add)

        if turn > 0:
            high_reduce(turn).start()

    each(1, plane, lambda step: low_reduce(step).start())
    each(1, planes, lambda step: high_reduce(step).wait())

    def high_add(i):
        held = sums[dp, i, :, high].astype(F32)
        for step in range(1, planes):
            held = held + high_land[dp_at(step), i].astype(F32)
        high_mid[i] = held.astype(BF16)

    each(0, plane, high_add)
    each(1, plane, lambda step: high_finish(step).start())
    each(1, plane, lambda step: low_reduce(step).wait())

    def low_add(i):
        held = sums[i, spot, :, low].astype(F32)
        for step in range(1, plane):
            held = held + low_land[spot_at(step), i].astype(F32)
        low_mid[i] = held.astype(BF16)

    each(0, planes, low_add)
    each(1, planes, lambda step: low_finish(step).start())
    each(1, plane, lambda step: high_finish(step).wait())
    each(1, planes, lambda step: low_finish(step).wait())
    result_low, result_high = low_mid[dp].astype(F32), high_mid[spot].astype(F32)
    for step in range(1, planes):
        result_low = result_low + low_got[dp_at(step)].astype(F32)
    for step in range(1, plane):
        result_high = result_high + high_got[spot_at(step)].astype(F32)
    result = jnp.concatenate([result_low, result_high], axis=1)
    whole[core, dp, spot] = result.astype(BF16)
    each(1, planes, lambda step: low_first(step).start())
    each(1, plane, lambda step: high_first(step).start())
    each(1, planes, lambda step: low_first(step).wait_recv())
    each(1, plane, lambda step: low_second(step).start())
    low_pass(0).start()
    each(1, plane, lambda step: high_first(step).wait_recv())
    each(1, planes, lambda step: high_second(step).start())
    high_pass(0).start()

    def forward_low(step):
        low_second(step).wait_recv()
        low_pass(step).start()

    def forward_high(step):
        high_second(step).wait_recv()
        high_pass(step).start()

    each(1, plane, forward_low)
    each(1, planes, forward_high)
    each(1, planes, lambda step: low_first(step).wait_send())
    each(1, plane, lambda step: low_second(step).wait_send())
    each(1, plane, lambda step: high_first(step).wait_send())
    each(1, planes, lambda step: high_second(step).wait_send())
    each(0, plane, lambda step: low_pass(step).wait())
    each(0, planes, lambda step: high_pass(step).wait())


def unpack_body(whole, query_out, key_out, value_out, output_out, narrow_out):
    chunks, rows = whole.shape[1:3]
    some, wide = rows // 2, query_out.shape[1]
    half = wide // 2
    for chunk in range(chunks):
        here = slice(chunk * rows, (chunk + 1) * rows)
        there = slice(chunk * some, (chunk + 1) * some)
        for number in range(2):
            block = whole[number, chunk].astype(F32)
            if number == 0:
                query_out[here, :] = block[:, :wide]
                narrow_out[here, :] = block[:, wide + half :]
            else:
                key_out[here, :] = block[:, :half]
                value_out[here, :] = block[:, half:wide]
            start = number * wide
            output_out[there, start : start + half] = block[:some, wide : wide + half]
            output_out[there, start + half : start + wide] = block[some:, wide : wide + half]


def sum_everywhere(cid, sizes, *arrays):
    total = group_size(CHIP_AXES, sizes)
    depth, wide = arrays[0].shape
    half = (total, depth // total, wide + wide // 2 + arrays[4].shape[1])
    dma = pltpu.SemaphoreType.DMA
    vmem = pl.BlockSpec(memory_space=pltpu.VMEM)
    planes = sizes["dp"]
    plane = total // planes
    rows, less, more = half[1], CUT, half[2] - CUT
    shapes = [
        (planes, plane, *half[1:]),
        (plane, planes, rows, less),
        (planes, rows, less),
        (planes, rows, less),
        (planes, plane, rows, more),
        (plane, rows, more),
        (plane, rows, more),
    ]
    whole = pl.pallas_call(
        functools.partial(sum_body, sizes),
        out_shape=jax.ShapeDtypeStruct((2, planes, total // planes, *half[1:]), BF16),
        in_specs=[vmem] * 5,
        out_specs=vmem,
        scratch_shapes=[pltpu.VMEM(half, BF16)] * 2
        + [pltpu.VMEM(shape, BF16) for shape in shapes]
        + [dma((planes,))] * 2
        + [dma((n,)) for n in (planes, plane, plane, plane, planes, planes) for _ in range(2)]
        + [dma((n,)) for n in (plane, planes, planes, plane) for _ in range(2)],
        name="sum_everywhere",
        compiler_params=pltpu.CompilerParams(
            collective_id=cid, has_side_effects=True, vmem_limit_bytes=60_000_000
        ),
    )(*arrays)
    parts = 4
    return pl.pallas_call(
        unpack_body,
        grid=(parts,),
        out_shape=[jax.ShapeDtypeStruct(array.shape, F32) for array in arrays],
        in_specs=[pl.BlockSpec((2, total // parts, *half[1:]), lambda i: (0, i, 0, 0))],
        out_specs=[
            pl.BlockSpec((array.shape[0] // parts, array.shape[1]), lambda i: (i, 0)) for array in arrays
        ],
        name="unpack_sums",
    )(whole.reshape(2, *half))


def rope_tables(positions, head_size):
    half_dim = head_size // 2
    frequency = ROPE_BASE ** (-2.0 * jnp.arange(half_dim, dtype=F32) / head_size)
    angles = positions.astype(F32)[:, None] * frequency[None, :]
    angles = jnp.concatenate([angles, angles], axis=1)
    return (jnp.cos(angles), jnp.sin(angles))


def rotate(values, cosine, sine_table):
    half_dim = values.shape[-1] // 2
    turned = jnp.concatenate([-values[..., half_dim:], values[..., :half_dim]], axis=-1)
    return values * cosine[:, None, :] + turned * sine_table[:, None, :]


def rotate_back(grads, cosine, sine_table):
    half_dim = grads.shape[-1] // 2
    scaled = grads * sine_table[:, None, :]
    turned = jnp.concatenate([scaled[..., half_dim:], -scaled[..., :half_dim]], axis=-1)
    return grads * cosine[:, None, :] + turned


def norm_forward(values, gain_vec):
    inverse = lax.rsqrt(jnp.mean(values * values, axis=-1, keepdims=True) + EPSILON)
    normed = values * inverse
    return (inverse, normed, (normed * gain_vec).astype(BF16))


def norm_backward(grad_out, normed, inverse, gain_vec):
    gain_grad = jnp.sum(grad_out * normed, axis=0)
    scaled = grad_out * gain_vec
    inner = jnp.mean(scaled * normed, axis=-1, keepdims=True)
    return (gain_grad, inverse * (scaled - normed * inner))


def local(
    sizes,
    inputs,
    prenorm_gain,
    query_weight,
    key_weight,
    value_weight,
    output_weight,
    midnorm_gain,
    router_weight,
    gate_weight,
    up_weight,
    down_weight,
    expert_ids,
    cotangent,
):
    tokens, width = inputs.shape[1:]
    owners = sizes["expert"]
    mine = gate_weight.shape[0]
    context, owner = lax.axis_index("context"), lax.axis_index("expert")
    block = context * owners + owner
    positions = block * tokens + jnp.arange(tokens, dtype=jnp.int32)
    cosine, sine_table = rope_tables(positions, HEAD_DIM)

    input_float = inputs[0].astype(F32)
    inverse_first, normed_first, attn_input = norm_forward(input_float, prenorm_gain)
    query_raw = dot(attn_input, query_weight).reshape(tokens, HEADS, HEAD_DIM)
    key_raw = dot(attn_input, key_weight).reshape(tokens, KV_HEADS, HEAD_DIM)
    value_raw = dot(attn_input, value_weight).reshape(tokens, KV_HEADS, HEAD_DIM)
    query_rot = rotate(query_raw, cosine, sine_table).astype(BF16)
    key_rot = rotate(key_raw, cosine, sine_table).astype(BF16)
    query_send = query_rot.reshape(tokens, KV_HEADS, 2 * HEAD_DIM).transpose(1, 0, 2)
    kv_send = jnp.concatenate([key_rot, value_raw.astype(BF16)], axis=2).transpose(1, 0, 2)
    kv_all, queries, grad_all, mixtures, sums, mixture = run_forward(
        0, sizes, kv_send, query_send, cotangent[0]
    )
    mixture_flat = mixture.transpose(1, 0, 2).reshape(tokens, HEADS * HEAD_DIM)

    after_attn = input_float + dot(mixture_flat, output_weight)
    inverse_second, normed_second, moe_input = norm_forward(after_attn, midnorm_gain)
    logits = lax.dot_general(
        router_weight, moe_input, (((0,), (1,)), ((), ())), preferred_element_type=F32
    )
    numbers = jnp.arange(EXPERTS, dtype=jnp.int32)[:, None, None]
    chosen = jnp.any(expert_ids[0].T[None] == numbers, axis=1)
    masked = jnp.where(chosen, logits, -jnp.inf)
    powers = jnp.exp(masked - jnp.max(masked, axis=0, keepdims=True))
    gates = powers / jnp.sum(powers, axis=0, keepdims=True)
    gate_table = jnp.where(chosen, gates, -1.0)

    own_g, own_u, own_d, other_g, other_u, other_d, moe_terms, grad_back, dot_back = run_experts(
        3, sizes, moe_input, gate_table, grad_all.reshape(owners, tokens, width), gate_weight, up_weight, down_weight
    )
    grad_gates = dot_back[:, :mine].reshape(EXPERTS, tokens)
    grad_logits = gates * (grad_gates - jnp.sum(gates * grad_gates, axis=0, keepdims=True))
    router_grad = jnp.einsum(
        "td,et->de", moe_input.astype(F32), grad_logits, precision=lax.Precision.HIGHEST
    )
    grad_moe_in = jnp.sum(grad_back.astype(F32), axis=0) + jnp.einsum(
        "et,de->td", grad_logits, router_weight.astype(F32), precision=lax.Precision.HIGHEST
    )
    grad_out = cotangent[0].astype(F32)
    midnorm_grad, grad_after = norm_backward(grad_moe_in, normed_second, inverse_second, midnorm_gain)
    grad_after = grad_out + grad_after
    grad_after_half = grad_after.astype(BF16)
    output_grad = t_dot(mixture_flat, grad_after_half)
    grad_mix = dot_t(grad_after_half, output_weight).astype(BF16)
    grad_mix = grad_mix.reshape(tokens, KV_HEADS, 2 * HEAD_DIM).transpose(1, 0, 2)
    moe_out, kv_back, grad_query, gate_sum, up_sum, down_sum = run_backward(
        8,
        sizes,
        (own_g, own_u, own_d),
        (other_g, other_u, other_d),
        moe_terms.reshape(2, owners // 2, tokens, width),
        (queries, kv_all, mixtures, grad_mix, sums),
    )
    outputs = (after_attn + moe_out).astype(BF16)
    grad_kv = jnp.sum(kv_back.astype(F32).reshape(KV_HEADS, owners, tokens, 2 * HEAD_DIM), axis=1)
    grad_kv = grad_kv.transpose(1, 0, 2)
    grad_query = grad_query.transpose(1, 0, 2).reshape(tokens, HEADS, HEAD_DIM)
    query_back = rotate_back(grad_query, cosine, sine_table).reshape(tokens, -1).astype(BF16)
    key_back = rotate_back(grad_kv[..., :HEAD_DIM], cosine, sine_table).reshape(tokens, -1).astype(BF16)
    value_back = grad_kv[..., HEAD_DIM:].reshape(tokens, -1).astype(BF16)
    query_grad = t_dot(attn_input, query_back)
    key_grad = t_dot(attn_input, key_back)
    value_grad = t_dot(attn_input, value_back)
    grad_attn_in = (
        dot_t(query_back, query_weight) + dot_t(key_back, key_weight) + dot_t(value_back, value_weight)
    )
    prenorm_grad, grad_inputs = norm_backward(grad_attn_in, normed_first, inverse_first, prenorm_gain)
    grad_inputs = grad_after + grad_inputs
    narrow = jnp.concatenate([router_grad, prenorm_grad[:, None], midnorm_grad[:, None]], axis=1)
    narrow = jnp.pad(narrow, ((0, 0), (0, 128 - EXPERTS - 2)))
    query_grad, key_grad, value_grad, output_grad, narrow = sum_everywhere(
        9, sizes, query_grad, key_grad, value_grad, output_grad, narrow
    )
    dense = (
        narrow[:, EXPERTS],
        query_grad,
        key_grad,
        value_grad,
        output_grad,
        narrow[:, EXPERTS + 1],
        narrow[:, :EXPERTS],
    )
    return (outputs[None], grad_inputs[None], *dense, gate_sum, up_sum, down_sum)


def solution(mesh):
    split = P("dp", ("context", "expert"), None)
    owned = P("expert", None, None)
    summed = P("expert", ("dp", "context"), None)
    in_specs = (split, *([P()] * 7), owned, owned, owned, split, split)
    out_specs = (split, split, *([P()] * 7), summed, summed, summed)
    return jax.shard_map(
        functools.partial(local, dict(mesh.shape)),
        mesh=mesh,
        in_specs=in_specs,
        out_specs=out_specs,
        check_vma=False,
    )
```

```python
import functools

import jax
import jax.numpy as jnp
from jax import lax
from jax.experimental import pallas as pl
from jax.experimental.pallas import tpu as pltpu
from jax.sharding import PartitionSpec as P

HEADS = 8
KV_HEADS = 4
HEAD_DIM = 64
EXPERTS = 32
TOP = 8
CAP = 64
EPSILON = 1e-06
ROPE_BASE = 10000.0
F32 = jnp.float32
BF16 = jnp.bfloat16
MESH_ID = pl.DeviceIdType.MESH
SEQ_AXES = ("context", "expert")


def dot(left, right):
    return jnp.dot(left, right, preferred_element_type=F32)


def dot_t(left, right):
    return lax.dot_general(left, right, (((1,), (1,)), ((), ())), preferred_element_type=F32)


def t_dot(left, right):
    return lax.dot_general(left, right, (((0,), (0,)), ((), ())), preferred_element_type=F32)


PARTS = {"side": ("context", 2, 2), "half": ("expert", 2, 4), "place": ("expert", 4, 1)}


def axis_size(sizes, name):
    return PARTS[name][1] if name in PARTS else sizes[name]


def group_size(axes, sizes):
    total = 1
    for name in axes:
        total *= axis_size(sizes, name)
    return total


def part_index(name):
    if name not in PARTS:
        return lax.axis_index(name)
    axis, size, stride = PARTS[name]
    return lax.rem(lax.axis_index(axis) // stride, size)


def own_index(axes, sizes):
    index = 0
    for name in axes:
        index = index * axis_size(sizes, name) + part_index(name)
    return index


def coords_of(axes, sizes, index):
    out = {}
    for name in reversed(axes):
        place = lax.rem(index, axis_size(sizes, name))
        if name in PARTS:
            axis, _, stride = PARTS[name]
            out[axis] = lax.axis_index(axis) + (place - part_index(name)) * stride
        else:
            out[name] = place
        index = index // axis_size(sizes, name)
    return out


def pick_whole(ref, target, peer):
    return ref


def pick_target(ref, target, peer):
    return ref.at[target]


def pick_second(ref, target, peer):
    return ref.at[:, target]


def pick_context(ref, target, peer):
    return ref.at[peer["context"]]


def greet(all_axes, sizes):
    barrier = pltpu.get_barrier_semaphore()
    groups = []
    for axes in all_axes:
        if not any(set(axes) <= set(other) for other in groups):
            groups = [other for other in groups if not set(other) <= set(axes)] + [axes]
    signals = 0
    for axes in groups:
        me, total = own_index(axes, sizes), group_size(axes, sizes)
        for step in range(1, total):
            peer = coords_of(axes, sizes, lax.rem(me + step, total))
            pl.semaphore_signal(barrier, inc=1, device_id=peer, device_id_type=MESH_ID)
        signals += total - 1
    pl.semaphore_wait(barrier, signals)


def launch(sizes, axes, pick, keep, source, landing, send, recv):
    started = []
    me, total = own_index(axes, sizes), group_size(axes, sizes)
    for step in range(1, total):
        target = lax.rem(me + step, total)
        peer = coords_of(axes, sizes, target)
        copy = pltpu.make_async_remote_copy(
            src_ref=pick(source, target, peer),
            dst_ref=landing.at[me],
            send_sem=send.at[step],
            recv_sem=recv.at[step],
            device_id=peer,
            device_id_type=MESH_ID,
        )
        copy.start()
        started.append(copy)
    if keep:
        own = pltpu.make_async_copy(
            pick(source, me, coords_of(axes, sizes, me)), landing.at[me], send.at[0]
        )
        own.start()
        started.append(own)
    return started


def stack_heads(block, low):
    tokens = block.shape[0]
    zero = jnp.zeros((tokens, HEAD_DIM), block.dtype)
    parts = [block[:, :HEAD_DIM], block[:, HEAD_DIM:]]
    return jnp.concatenate(
        [jnp.concatenate([part, zero] if low else [zero, part], axis=1) for part in parts], axis=0
    )


def causal(shape, tokens):
    keys = lax.broadcasted_iota(jnp.int32, shape, 0)
    queries = lax.rem(lax.broadcasted_iota(jnp.int32, shape, 1), tokens)
    return keys - queries <= lax.axis_index("expert") * tokens


def identity(size):
    shape = (size, size)
    return lax.broadcasted_iota(jnp.int32, shape, 0) == lax.broadcasted_iota(jnp.int32, shape, 1)


def attention_forward(data, results, scratch):
    query_ref, kv_ref = data
    out_ref, sum_ref = results
    (score_ref,) = scratch
    blocks, tokens = query_ref.shape[:2]
    chunk, columns = 8 * tokens, 2 * tokens

    def block(number, carry):
        rows = stack_heads(query_ref[number], True) * (HEAD_DIM ** (-0.5))
        rows = rows.astype(BF16)

        def keys_of(j):
            return pl.ds(pl.multiple_of(j * chunk, chunk), chunk)

        def kv_of(j):
            return kv_ref[pl.ds(j * 8, 8)].reshape(chunk, 2 * HEAD_DIM)

        def first(j, top):
            scores = dot_t(kv_of(j), rows)
            score_ref[keys_of(j), :] = scores
            return jnp.maximum(top, jnp.max(scores, axis=0, keepdims=True))

        top = lax.fori_loop(0, number, first, jnp.full((1, columns), -jnp.inf, F32))
        scores = dot_t(kv_of(number), rows)
        scores = jnp.where(causal(scores.shape, tokens), scores, -jnp.inf)
        score_ref[keys_of(number), :] = scores
        top = jnp.maximum(top, jnp.max(scores, axis=0, keepdims=True))

        def second(j, held):
            total, mixed = held
            powers = jnp.exp(score_ref[keys_of(j), :] - top)
            total = total + jnp.sum(powers, axis=0, keepdims=True)
            return total, mixed + t_dot(powers.astype(BF16), kv_of(j))

        start = (jnp.zeros((1, columns), F32), jnp.zeros((columns, 2 * HEAD_DIM), F32))
        total, mixed = lax.fori_loop(0, number + 1, second, start)
        sum_ref[number] = top + jnp.log(total)
        inverse = jnp.sum(jnp.where(identity(columns), 1.0 / total, 0.0), axis=1, keepdims=True)
        mixed = (mixed * inverse)[:, HEAD_DIM:]
        out_ref[number] = jnp.concatenate([mixed[:tokens], mixed[tokens:]], axis=1).astype(BF16)
        return carry

    lax.fori_loop(0, blocks, block, 0)


def attention_backward(data, results, scratch):
    query_ref, kv_ref, mix_ref, grad_ref, sum_ref = data
    grad_query_ref, terms_ref = results
    (sum_kv,) = scratch
    blocks, tokens = query_ref.shape[:2]
    chunk, columns = 8 * tokens, 2 * tokens
    factor = HEAD_DIM ** (-0.5)
    sum_kv[...] = jnp.zeros_like(sum_kv)

    def block(number, carry):
        rows = (stack_heads(query_ref[number], True) * factor).astype(BF16)
        grads = stack_heads(grad_ref[number], False)
        both = jnp.concatenate([rows, grads], axis=0)
        pairs = dot_t(stack_heads(mix_ref[number], False), grads)
        delta = jnp.sum(jnp.where(identity(columns), pairs, 0.0), axis=0, keepdims=True)
        logsum = sum_ref[number]

        def unit(j, total, masked):
            keys = pl.ds(pl.multiple_of(j * chunk, chunk), chunk)
            kv = kv_ref[pl.ds(j * 8, 8)].reshape(chunk, 2 * HEAD_DIM)
            products = dot_t(kv, both)
            soft = jnp.exp(products[:, :columns] - logsum)
            if masked:
                soft = jnp.where(causal(soft.shape, tokens), soft, 0.0)
            scores = (soft * (products[:, columns:] - delta)).astype(BF16)
            sum_kv[keys, :] += dot(jnp.concatenate([scores, soft.astype(BF16)], axis=1), both)
            return total + t_dot(scores, kv)

        total = lax.fori_loop(
            0, number, lambda j, held: unit(j, held, False), jnp.zeros((columns, 2 * HEAD_DIM), F32)
        )
        total = unit(number, total, True)[:, :HEAD_DIM] * factor
        grad_query_ref[number] = jnp.concatenate([total[:tokens], total[tokens:]], axis=1)
        return carry

    lax.fori_loop(0, blocks, block, 0)
    terms_ref[...] = sum_kv[...].astype(BF16).reshape(terms_ref.shape)


def forward_body(sizes, *refs):
    kv_send, query_send, grad_ref = refs[:3]
    kv_all, queries, grad_all, mixtures, sums, mixture_back = refs[3:9]
    sems, scores = refs[9:21], refs[21]
    mix_sems = refs[22:24]
    greet([SEQ_AXES], sizes)
    early = launch(sizes, ("context",), pick_target, True, query_send, queries, *sems[0:2])
    early += launch(sizes, SEQ_AXES, pick_context, True, kv_send, kv_all, *sems[2:4])
    half, place = part_index("half"), part_index("place")
    some = grad_ref.shape[0] // 2
    upper, lower = pl.ds(0, some), pl.ds(some, some)

    def grad_copies(axis, source, landing, pair):
        found = []
        for step in range(1, axis_size(sizes, axis)):
            target = lax.rem(part_index(axis) + step, axis_size(sizes, axis))
            copy = pltpu.make_async_remote_copy(
                src_ref=source,
                dst_ref=landing,
                send_sem=pair[0].at[step],
                recv_sem=pair[1].at[step],
                device_id=coords_of((axis,), sizes, target),
                device_id_type=MESH_ID,
            )
            copy.start()
            found.append(copy)
        return found

    near = grad_copies("half", grad_ref.at[upper], grad_all.at[half, place, upper], sems[4:6])
    near += grad_copies("place", grad_ref.at[lower], grad_all.at[half, place, lower], sems[6:8])
    grad_all[half, place] = grad_ref[...]
    for copy in early + near:
        copy.wait()
    columns, line = grad_all.at[:, place, upper], grad_all.at[half, :, lower]
    late = grad_copies("place", columns, columns, sems[8:10])
    late += grad_copies("half", line, line, sems[10:12])
    attention_forward((queries, kv_all), (mixtures, sums), (scores,))
    late += launch(sizes, ("context",), pick_target, True, mixtures, mixture_back, *mix_sems)
    for copy in late:
        copy.wait()


def run_forward(cid, sizes, kv_send, query_send, cotangent):
    heads, tokens, columns = query_send.shape
    total, owners = group_size(SEQ_AXES, sizes), sizes["expert"]
    vmem = pl.BlockSpec(memory_space=pltpu.VMEM)
    dma = pltpu.SemaphoreType.DMA
    return pl.pallas_call(
        functools.partial(forward_body, sizes),
        out_shape=[
            jax.ShapeDtypeStruct((total, tokens, columns), BF16),
            jax.ShapeDtypeStruct(query_send.shape, BF16),
            jax.ShapeDtypeStruct((2, owners // 2, *cotangent.shape), BF16),
            jax.ShapeDtypeStruct(query_send.shape, BF16),
            jax.ShapeDtypeStruct((heads, 1, 2 * tokens), F32),
            jax.ShapeDtypeStruct(query_send.shape, BF16),
        ],
        in_specs=[vmem] * 3,
        out_specs=[vmem] * 6,
        scratch_shapes=[
            *[dma((n,)) for n in (heads, total, 2, owners // 2, owners // 2, 2) for _ in range(2)],
            pltpu.VMEM((total * tokens, 2 * tokens), F32),
            *[dma((heads,))] * 2,
        ],
        name="attention_forward",
        compiler_params=pltpu.CompilerParams(
            collective_id=cid, has_side_effects=True, vmem_limit_bytes=60_000_000
        ),
    )(kv_send, query_send, cotangent)


def backward_body(sizes, *refs):
    owns_hbm, others_hbm, y_ref, refs = refs[:3], refs[3:6], refs[6], refs[7:]
    queries, kv_all, mixtures, mix_send, sums, *refs = refs
    y_total, kv_back, query_back, *totals = refs[:6]
    sends, gots, sends_2, gots_2 = refs[6:9], refs[9:12], refs[12:15], refs[15:18]
    grad_query, terms, sum_kv, grad_mix = refs[18:22]
    owns, others, refs = refs[22:25], refs[25:28], refs[28:]
    y_land, y_pass, y_got, *sems = refs
    dp, side = lax.axis_index("dp"), lax.axis_index("context") // 2
    experts = owns[0].shape[0]
    firsts = (("dp",), ("dp",), ("side",))
    seconds = (("side",), ("side",), ("dp",))
    loads = [
        (
            pltpu.make_async_copy(owns_hbm[i], owns[i], sems[22].at[i]),
            pltpu.make_async_copy(others_hbm[i], others[i], sems[22].at[3 + i]),
        )
        for i in range(3)
    ]
    for pair in loads:
        for copy in pair:
            copy.start()
    greet([SEQ_AXES, ("dp",)], sizes)
    mixes = launch(sizes, ("context",), pick_target, True, mix_send, grad_mix, *sems[18:20])
    outputs = launch(sizes, ("place",), pick_second, True, y_ref, y_land, *sems[6:8])

    def chip_sum(i, expert, place):
        return owns[i][expert, place] + others[i][expert, place].astype(F32)

    stage_1 = []
    for i, axes in enumerate(firsts):
        for copy in loads[i]:
            copy.wait()

        def fill(expert, carry, i=i, axes=axes):
            for d in range(4):
                for v in range(2):
                    terms_now = chip_sum(i, expert, 2 * d + v).astype(BF16)
                    if axes == ("dp",):
                        sends[i][d, expert, v] = terms_now
                    else:
                        sends[i][v, expert, d] = terms_now
            return carry

        lax.fori_loop(0, experts, fill, 0)
        stage_1 += launch(sizes, axes, pick_target, False, sends[i], gots[i], *sems[2 * i : 2 * i + 2])
    for copy in mixes:
        copy.wait()
    attention_backward((queries, kv_all, mixtures, grad_mix, sums), (grad_query, terms), (sum_kv,))
    rest = launch(sizes, SEQ_AXES, pick_target, True, terms, kv_back, *sems[8:10])
    rest += launch(sizes, ("context",), pick_target, True, grad_query, query_back, *sems[10:12])
    half = part_index("half")
    for copy in outputs:
        copy.wait()

    def half_sum(number):
        total = y_land[0, number].astype(F32)
        for place in range(1, y_land.shape[0]):
            total = total + y_land[place, number].astype(F32)
        return total

    y_pass[1 - half] = half_sum(1 - half).astype(BF16)
    rest += launch(sizes, ("half",), pick_target, False, y_pass, y_got, *sems[20:22])
    for copy in stage_1:
        copy.wait()

    def part(i, expert, place):
        if firsts[i] == ("dp",):
            total = chip_sum(i, expert, 2 * dp + place)
            for step in range(1, 4):
                total = total + gots[i][lax.rem(dp + step, 4), expert, place].astype(F32)
            return total
        return chip_sum(i, expert, 2 * place + side) + gots[i][1 - side, expert, place].astype(F32)

    for i, axes in enumerate(seconds):

        def refill(expert, carry, i=i, axes=axes):
            for place in range(group_size(axes, sizes)):
                sends_2[i][place, expert] = part(i, expert, place).astype(BF16)
            return carry

        lax.fori_loop(0, experts, refill, 0)
    stage_2 = []
    for i, axes in enumerate(seconds):
        stage_2 += launch(
            sizes, axes, pick_target, False, sends_2[i], gots_2[i], *sems[12 + 2 * i : 14 + 2 * i]
        )
    for copy in stage_2:
        copy.wait()
    for i, axes in enumerate(seconds):
        me, total = own_index(axes, sizes), group_size(axes, sizes)

        def close(expert, carry, i=i, me=me, total=total):
            held = part(i, expert, me)
            for step in range(1, total):
                held = held + gots_2[i][lax.rem(me + step, total), expert].astype(F32)
            totals[i][expert] = held
            return carry

        lax.fori_loop(0, experts, close, 0)
    for copy in rest:
        copy.wait()
    y_total[...] = half_sum(half) + y_got[1 - half].astype(F32)


def run_backward(cid, sizes, owns, others, y_terms, data):
    queries, kv_all = data[:2]
    tokens = queries.shape[1]
    experts = owns[0].shape[0]
    vmem = pl.BlockSpec(memory_space=pltpu.VMEM)
    tiles = [own.shape[2:] for own in owns]
    stage_1 = [(4, experts, 2, *tiles[0]), (4, experts, 2, *tiles[1]), (2, experts, 4, *tiles[2])]
    stage_2 = [(2, experts, *tiles[0]), (2, experts, *tiles[1]), (4, experts, *tiles[2])]
    context = sizes["context"]
    sizes_of = [4, 4, 2, 4, group_size(SEQ_AXES, sizes), context, 2, 2, 4, context, 2]
    places, rows = y_terms.shape[1], y_terms.shape[2:]
    dma = pltpu.SemaphoreType.DMA
    return pl.pallas_call(
        functools.partial(backward_body, sizes),
        out_shape=[
            jax.ShapeDtypeStruct(rows, F32),
            jax.ShapeDtypeStruct(kv_all.shape, BF16),
            jax.ShapeDtypeStruct(queries.shape, F32),
            *[jax.ShapeDtypeStruct((experts, *tile), F32) for tile in tiles],
        ],
        in_specs=[*([pl.BlockSpec(memory_space=pl.ANY)] * 6), *([vmem] * 6)],
        out_specs=[vmem] * 6,
        scratch_shapes=[
            *[pltpu.VMEM(shape, BF16) for shape in stage_1 * 2 + stage_2 * 2],
            pltpu.VMEM(queries.shape, F32),
            pltpu.VMEM(kv_all.shape, BF16),
            pltpu.VMEM((kv_all.shape[0] * tokens, 2 * HEAD_DIM), F32),
            pltpu.VMEM(queries.shape, BF16),
            *[pltpu.VMEM(own.shape, F32) for own in owns],
            *[pltpu.VMEM(own.shape, BF16) for own in owns],
            pltpu.VMEM((places, 2, *rows), BF16),
            pltpu.VMEM((2, *rows), BF16),
            pltpu.VMEM((2, *rows), BF16),
            *[dma((n,)) for n in sizes_of for _ in range(2)],
            dma((6,)),
        ],
        name="attention_backward",
        compiler_params=pltpu.CompilerParams(
            collective_id=cid, has_side_effects=True, vmem_limit_bytes=67_043_328
        ),
    )(*owns, *others, y_terms, *data)


NEAR = ((0, 0), (1, 0), (0, 1), (0, 3), (0, 2), (1, 1), (1, 3), (1, 2))


def owner_at(owner, steps, sign):
    half = lax.rem(owner // 4 + steps[0], 2)
    return half * 4 + lax.rem(owner + 4 + sign * steps[1], 4)


def moe_copies(sizes, refs):
    moe_ref, table_ref, moe_land, table_land, d_send, d_back, dots, dot_back, g_sends, g_backs, sems = refs
    owner, context = lax.axis_index("expert"), lax.axis_index("context")

    def pair_of(copies, target, number):
        return [
            pltpu.make_async_remote_copy(
                src_ref=src,
                dst_ref=dst,
                send_sem=send.at[number],
                recv_sem=recv.at[number],
                device_id={"expert": target},
                device_id_type=MESH_ID,
            )
            for src, dst, send, recv in copies
        ]

    def tokens_to(number):
        pairs = (
            (table_ref, table_land.at[number], sems[7], sems[8]),
            (moe_ref, moe_land.at[number], sems[9], sems[10]),
        )
        return pair_of(pairs, owner_at(owner, NEAR[number], 1), number)

    def results_of(number):
        target = owner_at(owner, NEAR[number], -1)
        pairs = (
            (d_send.at[target], d_back.at[owner], sems[0], sems[1]),
            (dots.at[target], dot_back.at[owner], sems[2], sems[3]),
        )
        return pair_of(pairs, target, number)

    def own_results():
        return [
            pltpu.make_async_copy(d_send.at[owner], d_back.at[owner], sems[0].at[0]),
            pltpu.make_async_copy(dots.at[owner], dot_back.at[owner], sems[2].at[0]),
        ]

    def halves(number):
        partner = context + 1 - 2 * lax.rem(context, 2)
        return [
            pltpu.make_async_remote_copy(
                src_ref=g_sends[i].at[number],
                dst_ref=g_backs[i].at[number],
                send_sem=sems[4].at[3 * number + i],
                recv_sem=sems[5].at[3 * number + i],
                device_id={"context": partner},
                device_id_type=MESH_ID,
            )
            for i in range(3)
        ]

    return tokens_to, results_of, own_results, halves


def moe_body(
    sizes,
    moe_ref,
    table_ref,
    grad_ref,
    wg_ref,
    wu_ref,
    wd_ref,
    own_g,
    own_u,
    own_d,
    back_g,
    back_u,
    back_d,
    y_out,
    d_back,
    dot_back,
    moe_land,
    table_land,
    x_all,
    g_now,
    deo_all,
    dgu_all,
    eh_all,
    eo_all,
    dbuf_all,
    picks,
    highs,
    lows,
    gate_col,
    dot_col,
    dots,
    y_send,
    d_send,
    send_g,
    send_u,
    send_d,
    *sems,
):
    step = pl.program_id(0)
    owners = sizes["expert"]
    owner, context = lax.axis_index("expert"), lax.axis_index("context")
    core = lax.rem(context, 2)
    mine = 4
    group = owners // 2
    tokens, width = moe_ref.shape
    hidden_width = wg_ref.shape[2]
    rows = group * CAP
    barrier = pltpu.get_barrier_semaphore()
    tokens_to, results_of, own_results, halves = moe_copies(
        sizes,
        (
            moe_ref,
            table_ref,
            moe_land,
            table_land,
            d_send,
            d_back,
            dots,
            dot_back,
            (send_g, send_u, send_d),
            (back_g, back_u, back_d),
            sems,
        ),
    )

    @pl.when(step == 0)
    def _():
        for number in range(1, owners):
            pl.semaphore_signal(
                barrier,
                inc=1,
                device_id={"expert": lax.rem(owner + number, owners)},
                device_id_type=MESH_ID,
            )
        pl.semaphore_signal(
            barrier, inc=1, device_id={"context": context + 1 - 2 * core}, device_id_type=MESH_ID
        )
        pl.semaphore_wait(barrier, owners)
        for number in range(1, group):
            for copy in tokens_to(number):
                copy.start()
        dots[...] = jnp.zeros_like(dots)
        moe_land[0] = moe_ref[...]
        table_land[0] = table_ref[...]
        for number in range(1, group):
            for copy in tokens_to(number):
                copy.wait_recv()
        for number in range(group, owners):
            for copy in tokens_to(number):
                copy.start()

    def combine_outputs(first):
        for position in range(first, first + group):
            moved = t_dot(highs[position], eo_all[position]) + t_dot(lows[position], eo_all[position])
            y_send[owner_at(owner, NEAR[position], -1)] = moved.astype(BF16)

    @pl.when(step == mine)
    def _():
        for copy in own_results():
            copy.start()
        for number in range(1, group):
            for copy in results_of(number):
                copy.start()
        for number in range(group, owners):
            for copy in tokens_to(number):
                copy.wait_recv()
        combine_outputs(0)

    @pl.when(step == 2 * mine)
    def _():
        for number in range(group, owners):
            for copy in results_of(number):
                copy.start()
        combine_outputs(group)

    @pl.when(step == 2 * mine + 1)
    def _():
        pltpu.make_async_copy(y_send, y_out, sems[6].at[0]).start()

    for number in range(mine):

        @pl.when(step == 2 * mine + 1 + number)
        def _(number=number):
            for copy in halves(number):
                copy.start()

    @pl.when(step < 2 * mine)
    def _():
        expert, tile = lax.rem(step, mine), step // mine
        place = pl.multiple_of(expert * CAP, CAP)
        spot = pl.ds(place, CAP)
        here = pl.ds(pl.multiple_of(tile * rows, rows), rows)
        part = pl.ds(tile * group, group)

        def source_of(j):
            near, far = owner_at(owner, NEAR[j], -1), owner_at(owner, NEAR[group + j], -1)
            return near + tile * (far - near)

        table = jnp.concatenate(
            [table_land[tile * group + j, pl.ds(owner * mine + expert, 1), :] for j in range(group)], axis=0
        )
        table = jnp.concatenate([table, table], axis=0)
        named = table >= 0.0
        above = lax.broadcasted_iota(jnp.int32, (tokens, tokens), 0)
        beside = lax.broadcasted_iota(jnp.int32, (tokens, tokens), 1)
        before = (above < beside).astype(F32).astype(BF16)
        slots = dot(named.astype(F32).astype(BF16), before)
        slots = jnp.where(named, slots, -1.0)
        counts = lax.broadcasted_iota(jnp.int32, (CAP, tokens), 0).astype(F32)
        for j in range(group):
            position = tile * group + j
            source = source_of(j)
            chosen = counts == slots[j : j + 1]
            onehot = jnp.where(chosen, 1.0, 0.0).astype(BF16)
            weight = jnp.where(chosen, table[j : j + 1], 0.0)
            high = weight.astype(BF16)
            picks[position, spot, :] = onehot
            highs[position, spot, :] = high
            lows[position, spot, :] = (weight - high.astype(F32)).astype(BF16)
            gate_col[j * CAP : (j + 1) * CAP, :] = jnp.sum(weight, axis=1, keepdims=True)
            line = pl.ds(pl.multiple_of(tile * rows + j * CAP, CAP), CAP)
            x_all[expert, line, :] = dot(onehot, moe_land[position]).astype(BF16)
            g_now[j * CAP : (j + 1) * CAP, :] = dot(onehot, grad_ref[source]).astype(BF16)

        rows_in = x_all[expert, here, :]
        gate_act = dot(rows_in, wg_ref[0])
        up_act = dot(rows_in, wu_ref[0])
        sigma = jax.nn.sigmoid(gate_act)
        silu = gate_act * sigma
        hidden = (silu * up_act).astype(BF16)
        eh_all[expert, here, :] = hidden
        expert_out = dot(hidden, wd_ref[0]).astype(BF16)
        eo_all[part, spot, :] = expert_out.reshape(group, CAP, width)
        grads = g_now[...].astype(F32)
        dot_col[...] = jnp.sum(grads * expert_out.astype(F32), axis=1, keepdims=True)
        grad_expert = (gate_col[...] * grads).astype(BF16)
        deo_all[expert, here, :] = grad_expert
        grad_hidden = dot_t(grad_expert, wd_ref[0])
        slope = sigma * (1.0 + gate_act * (1.0 - sigma))
        grad_gate = (grad_hidden * up_act * slope).astype(BF16)
        grad_up = (grad_hidden * silu).astype(BF16)
        dgu_all[expert, here, :hidden_width] = grad_gate
        dgu_all[expert, here, hidden_width:] = grad_up
        grad_buffer = (dot_t(grad_gate, wg_ref[0]) + dot_t(grad_up, wu_ref[0])).astype(BF16)
        dbuf_all[part, spot, :] = grad_buffer.reshape(group, CAP, width)
        for j in range(group):
            position = tile * group + j
            source = source_of(j)
            onehot = picks[position, spot, :].astype(F32)
            dots[source, pl.ds(expert, 1), :] = jnp.sum(
                onehot * dot_col[j * CAP : (j + 1) * CAP, :], axis=0, keepdims=True
            )

        @pl.when(expert == mine - 1)
        def _():
            for j in range(group):
                position, source = tile * group + j, source_of(j)
                d_send[source] = t_dot(picks[position], dbuf_all[position]).astype(BF16)

    @pl.when((step >= 2 * mine) & (step < 3 * mine))
    def _():
        number = step - 2 * mine
        blocks = width // 256
        per = width // 16

        def gate_rows(j, carry):
            columns = pl.ds(pl.multiple_of(j * 256, 256), 256)
            rows_in = x_all[number, :, columns]
            for half, own, send in ((0, own_g, send_g), (1, own_u, send_u)):
                grads = dgu_all[number, :, half * hidden_width : (half + 1) * hidden_width]
                terms = t_dot(rows_in, grads).reshape(128 // per, 2, per, hidden_width)
                first, second = terms[:, 0], terms[:, 1]
                places = pl.ds(j * (128 // per), 128 // per)
                own[0, places] = jnp.where(core == 0, first, second)
                send[number, places] = jnp.where(core == 0, second, first).astype(BF16)
            return carry

        lax.fori_loop(0, blocks, gate_rows, 0)
        less = hidden_width // 16

        def down_rows(j, carry):
            columns = pl.ds(pl.multiple_of(j * 256, 256), 256)
            terms = t_dot(eh_all[number, :, columns], deo_all[number])
            terms = terms.reshape(128 // less, 2, less, width)
            first, second = terms[:, 0], terms[:, 1]
            places = pl.ds(j * (128 // less), 128 // less)
            own_d[0, places] = jnp.where(core == 0, first, second)
            send_d[number, places] = jnp.where(core == 0, second, first).astype(BF16)
            return carry

        lax.fori_loop(0, hidden_width // 256, down_rows, 0)

    @pl.when(step == 3 * mine)
    def _():
        for number in range(1, owners):
            for copy in tokens_to(number):
                copy.wait_send()
            for copy in results_of(number):
                copy.wait()
        for copy in own_results():
            copy.wait()
        pltpu.make_async_copy(y_send, y_out, sems[6].at[0]).wait()
        for number in range(mine):
            for copy in halves(number):
                copy.wait()


def run_experts(cid, sizes, moe_input, table, grad_all, gate_weight, up_weight, down_weight):
    owners, tokens, width = grad_all.shape
    mine, _, inner = gate_weight.shape
    rows = owners * CAP
    part, less = width // 16, inner // 16

    def fixed(array):
        return pl.BlockSpec(array.shape, lambda i: (0,) * array.ndim, pipeline_mode=pl.Buffered(1))

    def expert_block(array):
        return pl.BlockSpec((1, *array.shape[1:]), lambda i: (lax.rem(jnp.minimum(i, 2 * mine - 1), mine), 0, 0))

    def own_block(*shape):
        return pl.BlockSpec((1, *shape), lambda i: (jnp.clip(i - 2 * mine, 0, mine - 1), 0, 0, 0))

    anywhere = pl.BlockSpec(memory_space=pl.ANY)
    wide, tall = (8, part, inner), (8, less, width)
    dma = pltpu.SemaphoreType.DMA
    return pl.pallas_call(
        functools.partial(moe_body, sizes),
        grid=(3 * mine + 1,),
        out_shape=[
            jax.ShapeDtypeStruct((mine, *wide), F32),
            jax.ShapeDtypeStruct((mine, *wide), F32),
            jax.ShapeDtypeStruct((mine, *tall), F32),
            jax.ShapeDtypeStruct((mine, *wide), BF16),
            jax.ShapeDtypeStruct((mine, *wide), BF16),
            jax.ShapeDtypeStruct((mine, *tall), BF16),
            jax.ShapeDtypeStruct((owners, tokens, width), BF16),
            jax.ShapeDtypeStruct((owners, tokens, width), BF16),
            jax.ShapeDtypeStruct((owners, 8, tokens), F32),
        ],
        in_specs=[
            fixed(moe_input),
            fixed(table),
            fixed(grad_all),
            expert_block(gate_weight),
            expert_block(up_weight),
            expert_block(down_weight),
        ],
        out_specs=[own_block(*wide), own_block(*wide), own_block(*tall), *([anywhere] * 6)],
        scratch_shapes=[
            pltpu.VMEM(grad_all.shape, BF16),
            pltpu.VMEM((owners, *table.shape), F32),
            pltpu.VMEM((mine, rows, width), BF16),
            pltpu.VMEM((rows // 2, width), BF16),
            pltpu.VMEM((mine, rows, width), BF16),
            pltpu.VMEM((mine, rows, 2 * inner), BF16),
            pltpu.VMEM((mine, rows, inner), BF16),
            pltpu.VMEM((owners, mine * CAP, width), BF16),
            pltpu.VMEM((owners, mine * CAP, width), BF16),
            pltpu.VMEM((owners, mine * CAP, tokens), BF16),
            pltpu.VMEM((owners, mine * CAP, tokens), BF16),
            pltpu.VMEM((owners, mine * CAP, tokens), BF16),
            pltpu.VMEM((rows // 2, 1), F32),
            pltpu.VMEM((rows // 2, 1), F32),
            pltpu.VMEM((owners, 8, tokens), F32),
            pltpu.VMEM((owners, tokens, width), BF16),
            pltpu.VMEM((owners, tokens, width), BF16),
            pltpu.VMEM((mine, *wide), BF16),
            pltpu.VMEM((mine, *wide), BF16),
            pltpu.VMEM((mine, *tall), BF16),
            dma((owners,)),
            dma((owners,)),
            dma((owners,)),
            dma((owners,)),
            dma((3 * mine,)),
            dma((3 * mine,)),
            dma((1,)),
            *[dma((owners,))] * 4,
        ],
        name="run_experts",
        compiler_params=pltpu.CompilerParams(
            collective_id=cid, has_side_effects=True, vmem_limit_bytes=67_043_328
        ),
    )(moe_input, table, grad_all, gate_weight, up_weight, down_weight)


CHIP_AXES = ("dp", "side", "expert")
PLANE_AXES = ("side", "expert")
CUT = 384


def sum_body(sizes, *refs):
    query_in, key_in, value_in, output_in, narrow_in = refs[:5]
    whole, load, near, sums = refs[5:9]
    low_land, low_mid, low_got, high_land, high_mid, high_got = refs[9:15]
    near_send, near_recv = refs[15:17]
    gather_sems, reduce_sems = refs[17:29], refs[29:]
    core = lax.rem(lax.axis_index("context"), 2)
    partner = {"context": lax.axis_index("context") + 1 - 2 * core}
    me, total = own_index(CHIP_AXES, sizes), group_size(CHIP_AXES, sizes)
    plane = total // sizes["dp"]
    rows = load.shape[1]
    some, wide = rows // 2, query_in.shape[1]
    half = wide // 2

    def place(step):
        target = lax.rem(me + step, total)
        return target, coords_of(CHIP_AXES, sizes, target)

    def remote(src, dst, send, recv, peer):
        return pltpu.make_async_remote_copy(
            src_ref=src, dst_ref=dst, send_sem=send, recv_sem=recv, device_id=peer, device_id_type=MESH_ID
        )

    dp, spot = lax.axis_index("dp"), own_index(PLANE_AXES, sizes)
    planes, cut = sizes["dp"], CUT
    low, high = pl.ds(0, cut), pl.ds(cut, whole.shape[4] - cut)

    def across(step, view, pair):
        peer = {"dp": lax.rem(dp + step, planes)}
        return remote(view, view, pair[0].at[step], pair[1].at[step], peer)

    def along(step, view, pair):
        peer = coords_of(PLANE_AXES, sizes, lax.rem(spot + step, plane))
        return remote(view, view, pair[0].at[step], pair[1].at[step], peer)

    def low_first(step):
        return across(step, whole.at[core, dp, spot, :, low], gather_sems[0:2])

    def low_second(step):
        return along(step, whole.at[core, :, spot, :, low], gather_sems[2:4])

    def low_pass(step):
        view = whole.at[core, :, lax.rem(spot - step + plane, plane), :, low]
        return remote(view, view, gather_sems[4].at[step], gather_sems[5].at[step], partner)

    def high_first(step):
        return along(step, whole.at[core, dp, spot, :, high], gather_sems[6:8])

    def high_second(step):
        return across(step, whole.at[core, dp, :, :, high], gather_sems[8:10])

    def high_pass(step):
        view = whole.at[core, lax.rem(dp - step + planes, planes), :, :, high]
        return remote(view, view, gather_sems[10].at[step], gather_sems[11].at[step], partner)

    def dp_at(step):
        return lax.rem(dp + step, planes)

    def spot_at(step):
        return lax.rem(spot + step, plane)

    def reduce_along(step, source, landing, pair):
        peer = coords_of(PLANE_AXES, sizes, spot_at(step))
        return remote(source, landing.at[spot], pair[0].at[step], pair[1].at[step], peer)

    def reduce_across(step, source, landing, pair):
        return remote(source, landing.at[dp], pair[0].at[step], pair[1].at[step], {"dp": dp_at(step)})

    def low_reduce(step):
        return reduce_along(step, sums.at[:, spot_at(step), :, low], low_land, reduce_sems[0:2])

    def low_finish(step):
        return reduce_across(step, low_mid.at[dp_at(step)], low_got, reduce_sems[2:4])

    def high_reduce(step):
        return reduce_across(step, sums.at[dp_at(step), :, :, high], high_land, reduce_sems[4:6])

    def high_finish(step):
        return reduce_along(step, high_mid.at[spot_at(step)], high_got, reduce_sems[6:8])

    def near_copy(turn):
        chunks = pl.ds(lax.rem(lax.axis_index("dp") + turn, sizes["dp"]) * plane, plane)
        return remote(load.at[chunks], near.at[chunks], near_send.at[turn], near_recv.at[turn], partner)

    def each(start, stop, body):
        def run(step, carry):
            body(step)
            return carry

        lax.fori_loop(start, stop, run, 0)

    def pack(number, chunk):
        here = pl.ds(pl.multiple_of(chunk * rows, rows), rows)
        there = pl.ds(pl.multiple_of(chunk * some, some), some)
        if number == 0:
            parts = [query_in[here, :]]
        else:
            parts = [key_in[here, :], value_in[here, :]]
        start = number * wide
        output = jnp.concatenate(
            [output_in[there, start : start + half], output_in[there, start + half : start + wide]], axis=0
        )
        return jnp.concatenate([*parts, output, narrow_in[here, :]], axis=1)

    barrier = pltpu.get_barrier_semaphore()
    pl.semaphore_signal(barrier, inc=1, device_id=partner, device_id_type=MESH_ID)
    each(
        1,
        total,
        lambda step: pl.semaphore_signal(
            barrier, inc=1, device_id=place(step)[1], device_id_type=MESH_ID
        ),
    )
    for turn in range(sizes["dp"]):
        base = lax.rem(lax.axis_index("dp") + turn, sizes["dp"]) * plane
        for number in range(2):

            @pl.when(core == 1 - number)
            def _(number=number, base=base):
                def fill(chunk):
                    load[chunk] = pack(number, chunk).astype(BF16)

                each(base, base + plane, fill)

        if turn == 0:
            pl.semaphore_wait(barrier, total)
        near_copy(turn).start()

    for turn in range(sizes["dp"]):
        near_copy(turn).wait()
        base = lax.rem(lax.axis_index("dp") + turn, sizes["dp"]) * plane
        for number in range(2):

            @pl.when(core == number)
            def _(number=number, base=base):
                def add(chunk, base=base, turn=turn):
                    place_now = lax.rem(lax.axis_index("dp") + turn, planes)
                    both = pack(number, chunk) + near[chunk].astype(F32)
                    sums[place_now, chunk - base] = both.astype(BF16)

                each(base, base + plane, add)

        if turn > 0:
            high_reduce(turn).start()

    each(1, plane, lambda step: low_reduce(step).start())
    each(1, planes, lambda step: high_reduce(step).wait())

    def high_add(i):
        held = sums[dp, i, :, high].astype(F32)
        for step in range(1, planes):
            held = held + high_land[dp_at(step), i].astype(F32)
        high_mid[i] = held.astype(BF16)

    each(0, plane, high_add)
    each(1, plane, lambda step: high_finish(step).start())
    each(1, plane, lambda step: low_reduce(step).wait())

    def low_add(i):
        held = sums[i, spot, :, low].astype(F32)
        for step in range(1, plane):
            held = held + low_land[spot_at(step), i].astype(F32)
        low_mid[i] = held.astype(BF16)

    each(0, planes, low_add)
    each(1, planes, lambda step: low_finish(step).start())
    each(1, plane, lambda step: high_finish(step).wait())
    each(1, planes, lambda step: low_finish(step).wait())
    result_low, result_high = low_mid[dp].astype(F32), high_mid[spot].astype(F32)
    for step in range(1, planes):
        result_low = result_low + low_got[dp_at(step)].astype(F32)
    for step in range(1, plane):
        result_high = result_high + high_got[spot_at(step)].astype(F32)
    result = jnp.concatenate([result_low, result_high], axis=1)
    whole[core, dp, spot] = result.astype(BF16)
    each(1, planes, lambda step: low_first(step).start())
    each(1, plane, lambda step: high_first(step).start())
    each(1, planes, lambda step: low_first(step).wait_recv())
    each(1, plane, lambda step: low_second(step).start())
    low_pass(0).start()
    each(1, plane, lambda step: high_first(step).wait_recv())
    each(1, planes, lambda step: high_second(step).start())
    high_pass(0).start()

    def forward_low(step):
        low_second(step).wait_recv()
        low_pass(step).start()

    def forward_high(step):
        high_second(step).wait_recv()
        high_pass(step).start()

    each(1, plane, forward_low)
    each(1, planes, forward_high)
    each(1, planes, lambda step: low_first(step).wait_send())
    each(1, plane, lambda step: low_second(step).wait_send())
    each(1, plane, lambda step: high_first(step).wait_send())
    each(1, planes, lambda step: high_second(step).wait_send())
    each(0, plane, lambda step: low_pass(step).wait())
    each(0, planes, lambda step: high_pass(step).wait())


def unpack_body(whole, query_out, key_out, value_out, output_out, narrow_out):
    chunks, rows = whole.shape[1:3]
    some, wide = rows // 2, query_out.shape[1]
    half = wide // 2
    for chunk in range(chunks):
        here = slice(chunk * rows, (chunk + 1) * rows)
        there = slice(chunk * some, (chunk + 1) * some)
        for number in range(2):
            block = whole[number, chunk].astype(F32)
            if number == 0:
                query_out[here, :] = block[:, :wide]
                narrow_out[here, :] = block[:, wide + half :]
            else:
                key_out[here, :] = block[:, :half]
                value_out[here, :] = block[:, half:wide]
            start = number * wide
            output_out[there, start : start + half] = block[:some, wide : wide + half]
            output_out[there, start + half : start + wide] = block[some:, wide : wide + half]


def sum_everywhere(cid, sizes, *arrays):
    total = group_size(CHIP_AXES, sizes)
    depth, wide = arrays[0].shape
    half = (total, depth // total, wide + wide // 2 + arrays[4].shape[1])
    dma = pltpu.SemaphoreType.DMA
    vmem = pl.BlockSpec(memory_space=pltpu.VMEM)
    planes = sizes["dp"]
    plane = total // planes
    rows, less, more = half[1], CUT, half[2] - CUT
    shapes = [
        (planes, plane, *half[1:]),
        (plane, planes, rows, less),
        (planes, rows, less),
        (planes, rows, less),
        (planes, plane, rows, more),
        (plane, rows, more),
        (plane, rows, more),
    ]
    whole = pl.pallas_call(
        functools.partial(sum_body, sizes),
        out_shape=jax.ShapeDtypeStruct((2, planes, total // planes, *half[1:]), BF16),
        in_specs=[vmem] * 5,
        out_specs=vmem,
        scratch_shapes=[pltpu.VMEM(half, BF16)] * 2
        + [pltpu.VMEM(shape, BF16) for shape in shapes]
        + [dma((planes,))] * 2
        + [dma((n,)) for n in (planes, plane, plane, plane, planes, planes) for _ in range(2)]
        + [dma((n,)) for n in (plane, planes, planes, plane) for _ in range(2)],
        name="sum_everywhere",
        compiler_params=pltpu.CompilerParams(
            collective_id=cid, has_side_effects=True, vmem_limit_bytes=60_000_000
        ),
    )(*arrays)
    parts = 4
    return pl.pallas_call(
        unpack_body,
        grid=(parts,),
        out_shape=[jax.ShapeDtypeStruct(array.shape, F32) for array in arrays],
        in_specs=[pl.BlockSpec((2, total // parts, *half[1:]), lambda i: (0, i, 0, 0))],
        out_specs=[
            pl.BlockSpec((array.shape[0] // parts, array.shape[1]), lambda i: (i, 0)) for array in arrays
        ],
        name="unpack_sums",
    )(whole.reshape(2, *half))


def rope_tables(positions, head_size):
    half_dim = head_size // 2
    frequency = ROPE_BASE ** (-2.0 * jnp.arange(half_dim, dtype=F32) / head_size)
    angles = positions.astype(F32)[:, None] * frequency[None, :]
    angles = jnp.concatenate([angles, angles], axis=1)
    return (jnp.cos(angles), jnp.sin(angles))


def rotate(values, cosine, sine_table):
    half_dim = values.shape[-1] // 2
    turned = jnp.concatenate([-values[..., half_dim:], values[..., :half_dim]], axis=-1)
    return values * cosine[:, None, :] + turned * sine_table[:, None, :]


def rotate_back(grads, cosine, sine_table):
    half_dim = grads.shape[-1] // 2
    scaled = grads * sine_table[:, None, :]
    turned = jnp.concatenate([scaled[..., half_dim:], -scaled[..., :half_dim]], axis=-1)
    return grads * cosine[:, None, :] + turned


def norm_forward(values, gain_vec):
    inverse = lax.rsqrt(jnp.mean(values * values, axis=-1, keepdims=True) + EPSILON)
    normed = values * inverse
    return (inverse, normed, (normed * gain_vec).astype(BF16))


def norm_backward(grad_out, normed, inverse, gain_vec):
    gain_grad = jnp.sum(grad_out * normed, axis=0)
    scaled = grad_out * gain_vec
    inner = jnp.mean(scaled * normed, axis=-1, keepdims=True)
    return (gain_grad, inverse * (scaled - normed * inner))


def local(
    sizes,
    inputs,
    prenorm_gain,
    query_weight,
    key_weight,
    value_weight,
    output_weight,
    midnorm_gain,
    router_weight,
    gate_weight,
    up_weight,
    down_weight,
    expert_ids,
    cotangent,
):
    tokens, width = inputs.shape[1:]
    owners = sizes["expert"]
    mine = gate_weight.shape[0]
    context, owner = lax.axis_index("context"), lax.axis_index("expert")
    block = context * owners + owner
    positions = block * tokens + jnp.arange(tokens, dtype=jnp.int32)
    cosine, sine_table = rope_tables(positions, HEAD_DIM)

    input_float = inputs[0].astype(F32)
    inverse_first, normed_first, attn_input = norm_forward(input_float, prenorm_gain)
    query_raw = dot(attn_input, query_weight).reshape(tokens, HEADS, HEAD_DIM)
    key_raw = dot(attn_input, key_weight).reshape(tokens, KV_HEADS, HEAD_DIM)
    value_raw = dot(attn_input, value_weight).reshape(tokens, KV_HEADS, HEAD_DIM)
    query_rot = rotate(query_raw, cosine, sine_table).astype(BF16)
    key_rot = rotate(key_raw, cosine, sine_table).astype(BF16)
    query_send = query_rot.reshape(tokens, KV_HEADS, 2 * HEAD_DIM).transpose(1, 0, 2)
    kv_send = jnp.concatenate([key_rot, value_raw.astype(BF16)], axis=2).transpose(1, 0, 2)
    kv_all, queries, grad_all, mixtures, sums, mixture = run_forward(
        0, sizes, kv_send, query_send, cotangent[0]
    )
    mixture_flat = mixture.transpose(1, 0, 2).reshape(tokens, HEADS * HEAD_DIM)

    after_attn = input_float + dot(mixture_flat, output_weight)
    inverse_second, normed_second, moe_input = norm_forward(after_attn, midnorm_gain)
    logits = lax.dot_general(
        router_weight, moe_input, (((0,), (1,)), ((), ())), preferred_element_type=F32
    )
    numbers = jnp.arange(EXPERTS, dtype=jnp.int32)[:, None, None]
    chosen = jnp.any(expert_ids[0].T[None] == numbers, axis=1)
    masked = jnp.where(chosen, logits, -jnp.inf)
    powers = jnp.exp(masked - jnp.max(masked, axis=0, keepdims=True))
    gates = powers / jnp.sum(powers, axis=0, keepdims=True)
    gate_table = jnp.where(chosen, gates, -1.0)

    own_g, own_u, own_d, other_g, other_u, other_d, moe_terms, grad_back, dot_back = run_experts(
        3, sizes, moe_input, gate_table, grad_all.reshape(owners, tokens, width), gate_weight, up_weight, down_weight
    )
    grad_gates = dot_back[:, :mine].reshape(EXPERTS, tokens)
    grad_logits = gates * (grad_gates - jnp.sum(gates * grad_gates, axis=0, keepdims=True))
    router_grad = jnp.einsum(
        "td,et->de", moe_input.astype(F32), grad_logits, precision=lax.Precision.HIGHEST
    )
    grad_moe_in = jnp.sum(grad_back.astype(F32), axis=0) + jnp.einsum(
        "et,de->td", grad_logits, router_weight.astype(F32), precision=lax.Precision.HIGHEST
    )
    grad_out = cotangent[0].astype(F32)
    midnorm_grad, grad_after = norm_backward(grad_moe_in, normed_second, inverse_second, midnorm_gain)
    grad_after = grad_out + grad_after
    grad_after_half = grad_after.astype(BF16)
    output_grad = t_dot(mixture_flat, grad_after_half)
    grad_mix = dot_t(grad_after_half, output_weight).astype(BF16)
    grad_mix = grad_mix.reshape(tokens, KV_HEADS, 2 * HEAD_DIM).transpose(1, 0, 2)
    moe_out, kv_back, grad_query, gate_sum, up_sum, down_sum = run_backward(
        8,
        sizes,
        (own_g, own_u, own_d),
        (other_g, other_u, other_d),
        moe_terms.reshape(2, owners // 2, tokens, width),
        (queries, kv_all, mixtures, grad_mix, sums),
    )
    outputs = (after_attn + moe_out).astype(BF16)
    grad_kv = jnp.sum(kv_back.astype(F32).reshape(KV_HEADS, owners, tokens, 2 * HEAD_DIM), axis=1)
    grad_kv = grad_kv.transpose(1, 0, 2)
    grad_query = grad_query.transpose(1, 0, 2).reshape(tokens, HEADS, HEAD_DIM)
    query_back = rotate_back(grad_query, cosine, sine_table).reshape(tokens, -1).astype(BF16)
    key_back = rotate_back(grad_kv[..., :HEAD_DIM], cosine, sine_table).reshape(tokens, -1).astype(BF16)
    value_back = grad_kv[..., HEAD_DIM:].reshape(tokens, -1).astype(BF16)
    query_grad = t_dot(attn_input, query_back)
    key_grad = t_dot(attn_input, key_back)
    value_grad = t_dot(attn_input, value_back)
    grad_attn_in = (
        dot_t(query_back, query_weight) + dot_t(key_back, key_weight) + dot_t(value_back, value_weight)
    )
    prenorm_grad, grad_inputs = norm_backward(grad_attn_in, normed_first, inverse_first, prenorm_gain)
    grad_inputs = grad_after + grad_inputs
    narrow = jnp.concatenate([router_grad, prenorm_grad[:, None], midnorm_grad[:, None]], axis=1)
    narrow = jnp.pad(narrow, ((0, 0), (0, 128 - EXPERTS - 2)))
    query_grad, key_grad, value_grad, output_grad, narrow = sum_everywhere(
        9, sizes, query_grad, key_grad, value_grad, output_grad, narrow
    )
    dense = (
        narrow[:, EXPERTS],
        query_grad,
        key_grad,
        value_grad,
        output_grad,
        narrow[:, EXPERTS + 1],
        narrow[:, :EXPERTS],
    )
    return (outputs[None], grad_inputs[None], *dense, gate_sum, up_sum, down_sum)


def solution(mesh):
    split = P("dp", ("context", "expert"), None)
    owned = P("expert", None, None)
    summed = P("expert", ("dp", "context"), None)
    in_specs = (split, *([P()] * 7), owned, owned, owned, split, split)
    out_specs = (split, split, *([P()] * 7), summed, summed, summed)
    return jax.shard_map(
        functools.partial(local, dict(mesh.shape)),
        mesh=mesh,
        in_specs=in_specs,
        out_specs=out_specs,
        check_vma=False,
    )
```
